32 devices in a mesh: seq: 8 (over z, x), wsh: 4 (over y, core).
Axes of the slice: x: 2, y: 2, z: 4, core: 2. Of those that a mesh axis runs over, the one named last changes fastest.
Arguments:
- tokens: bfloat16 [4096, 2048], P(('seq', 'wsh')), may hold values from -6 to 6
- first_layer_values: bfloat16 [4096, 2048], P(('seq', 'wsh')), may hold values from -6 to 6
- teacher: bfloat16 [4096, 2048], P(('seq', 'wsh')), may hold values from -6 to 6
- valid: int32 [4096], P(('seq', 'wsh')), may hold values from 0 to 1, as said below
- destination: int32 [4096], P(('seq', 'wsh')), may hold values from 0 to 4095, as said below
- lengths: int32 [4, 4], P('wsh'), may hold values from 1 to 512, 1024 in all within a row
- receptance_matrix: bfloat16 [2048, 2048], P('wsh'), may hold values from -0.125 to 0.125
- key_matrix: bfloat16 [2048, 2048], P('wsh'), may hold values from -0.125 to 0.125
- value_matrix: bfloat16 [2048, 2048], P('wsh'), may hold values from -0.125 to 0.125
- output_matrix: bfloat16 [2048, 2048], P('wsh'), may hold values from -0.125 to 0.125
- lowrank_down_weight: bfloat16 [2048, 512], P('wsh'), may hold values from -0.125 to 0.125
- lowrank_up_weight: bfloat16 [2048, 512], P('wsh'), may hold values from -0.5 to 0.5
- channel_key_weight: bfloat16 [8192, 2048], P('wsh'), may hold values from -0.125 to 0.125
- channel_value_weight: bfloat16 [8192, 2048], P('wsh'), may hold values from -0.0546875 to 0.0546875
- vectors: float32 [2048, 19], replicated, may hold values from -8 to 1.5
Outputs:
- output: bfloat16 [4096, 2048], P(('seq', 'wsh'))
- grad_tokens: bfloat16 [4096, 2048], P(('seq', 'wsh'))
- grad_first_values: bfloat16 [4096, 2048], P(('seq', 'wsh'))
- grad_receptance: float32 [2048, 2048], P(('seq', 'wsh'))
- grad_key: float32 [2048, 2048], P(('seq', 'wsh'))
- grad_value: float32 [2048, 2048], P(('seq', 'wsh'))
- grad_output_weight: float32 [2048, 2048], P(('seq', 'wsh'))
- grad_lora_down: float32 [2048, 512], P(('seq', 'wsh'))
- grad_lora_up: float32 [2048, 512], P(('seq', 'wsh'))
- grad_ffn_key: float32 [8192, 2048], P(('seq', 'wsh'))
- grad_ffn_value: float32 [8192, 2048], P(('seq', 'wsh'))
- grad_vectors: float32 [2048, 19], P(('seq', 'wsh'))
The draws below stay inside these ranges and needn't reach their ends.
Inputs may be any that keep to these rules, and one draw needn't show every extreme that they name: `destination`: A permutation of the rows. The rows of a block of 128 go to blocks of the same group, exactly 16 of them to each block of that group. `lengths`: each row sums to 1024; its largest entry is 512. `valid`: the first row of every block of 128 rows is 1.
All inputs are finite; a program needn't handle non-finite values.
Results may differ from the reference program's by a relative error of at most 0.013.
The reference program's roundings to bfloat16 on the way count: a program that leaves them out, or rounds other values in their place, can miss the bound.
Values may be sent and summed in bfloat16 or wider, within the bound.
A program may use at most 448 MiB of HBM per device.

```python
import math
import jax
import jax.numpy as jnp
import numpy as np
from jax import lax

LEADER_NUMBER = 32
PER_LEADER_DIMS = 64
MODEL_WIDTH = 2048
FF = 8192
RW = 96
RA = 96
RV = 64
RG = 256
RANK_COLUMNS = 512
TOK_DEV = 128
SEQS = 4
BLOCK = 64
PARAMS = 19
GROUP = 1024
LONGEST = 512
TOKENS = 4096
N_SEQ = 8
N_WSH = 4


LOWER = np.array([0.7, -0.3, 0.0, 0.0, 0.0, 0.0, 0.0, 0.0, -8.0, -1.0, -1.0, 0.5, 0.5, -1.0, 0.5, -0.3, 0.7, -0.3, 0.0], np.float32)


UPPER = np.array([1.3, 0.3, 1.0, 1.0, 1.0, 1.0, 1.0, 1.0, 1.0, 1.0, 1.0, 1.5, 1.5, 1.0, 1.5, 0.3, 1.3, 0.3, 1.0], np.float32)


def draw_vectors(key, part):
    unit = jax.random.uniform(key, (MODEL_WIDTH, PARAMS), jnp.float32)
    return jnp.asarray(LOWER) + (jnp.asarray(UPPER) - jnp.asarray(LOWER)) * unit


def draw_valid(key, part):
    devices = TOKENS // TOK_DEV
    row_ids = jnp.arange(TOKENS, dtype=jnp.int32)
    block_ids = row_ids // TOK_DEV
    threshold = 300 + 600 * block_ids // max(devices - 1, 1)
    rolled = jax.random.randint(key, (TOKENS,), 0, 1000, dtype=jnp.int32)
    return jnp.where((rolled < threshold) | (row_ids % TOK_DEV == 0), 1, 0).astype(jnp.int32)


def draw_destination(key, part):
    peer_rows = TOK_DEV // N_SEQ
    key_list = jax.random.split(key, 2 * N_WSH * N_SEQ)
    shuffles = jax.vmap(lambda one_key: jax.random.permutation(one_key, TOK_DEV))(key_list).reshape(2, N_WSH, N_SEQ, TOK_DEV)
    grid_wsh, grid_seq, grid_dest, grid_slot = jnp.meshgrid(jnp.arange(N_WSH), jnp.arange(N_SEQ), jnp.arange(N_SEQ), jnp.arange(peer_rows), indexing='ij')
    local_row = shuffles[0][grid_wsh, grid_seq, grid_dest * peer_rows + grid_slot]
    slot_index = shuffles[1][grid_wsh, grid_dest, grid_seq * peer_rows + grid_slot]
    source_index = (grid_seq * N_WSH + grid_wsh) * TOK_DEV + local_row
    target_index = (grid_dest * N_WSH + grid_wsh) * TOK_DEV + slot_index
    return jnp.zeros((TOKENS,), jnp.int32).at[source_index.reshape(-1)].set(target_index.reshape(-1).astype(jnp.int32))


def block_levels(stream_key, shape, cuts, smallest, high):
    loudness, own = 1.0, jax.random.fold_in(stream_key, 6)
    for dim, shards_of in cuts:
        heights = jnp.exp(jax.random.uniform(jax.random.fold_in(own, dim), (shards_of,), jnp.float32, smallest / len(cuts), high / len(cuts)))
        loudness = loudness * jnp.repeat(heights, shape[dim] // shards_of).reshape([-1 if axis == dim else 1 for axis in range(len(shape))])
    return loudness


def split_up(number_of, total, limit, slope):
    portions = [(1 << 20) // math.isqrt(rank ** slope) + 1 for rank in range(2, number_of + 1)]
    surplus, counts = total - limit - (number_of - 1), [1] * (number_of - 1)
    while surplus > 0:
        free = [i for i in range(number_of - 1) if counts[i] < limit]
        whole, budget = sum([portions[i] for i in free]), surplus
        for i in free:
            extra = min(limit - counts[i], max(1, budget * portions[i] // whole), surplus)
            counts[i] = counts[i] + extra
            surplus = surplus - extra
    return np.array([limit] + counts)


def uneven_parts(key, number_of, total, limit, lean):
    if number_of == 2:
        one = jax.random.randint(key, (), max(1, total - limit), min(limit, total - 1) + 1)
        return jnp.stack([one, total - one])
    sizes = jnp.asarray(split_up(number_of, total, limit, lean), jnp.int32)
    couples = (number_of - 1) // 2
    giver, taker = sizes[1:1 + 2 * couples:2], sizes[2:2 + 2 * couples:2]
    room = jnp.minimum(giver - 1, limit - taker)
    moved = jax.random.randint(jax.random.fold_in(key, 1), (couples,), 0, 1 << 20) % (room + 1)
    sizes = sizes.at[1:1 + 2 * couples:2].set(giver - moved).at[2:2 + 2 * couples:2].set(taker + moved)
    return sizes[jax.random.permutation(jax.random.fold_in(key, 2), number_of)]


def bell_draw(stream_key, extent, scale, limit, cuts=(), kind=jnp.bfloat16):
    values = scale * jax.random.normal(stream_key, extent, jnp.float32)
    if cuts:
        values = values * block_levels(stream_key, extent, cuts, -0.22, 0.18)
    return jnp.clip(values, -limit, limit).astype(kind)


def setup_inputs(seed: int = 0) -> dict:
    seeds = jax.random.split(jax.random.key(seed), 16)
    return {
        "tokens": bell_draw(seeds[0], (TOKENS, MODEL_WIDTH), 1.0, 6.0, ((0, 32),)),
        "first_layer_values": bell_draw(seeds[1], (TOKENS, MODEL_WIDTH), 1.0, 6.0, ((0, 32),)),
        "teacher": bell_draw(seeds[2], (TOKENS, MODEL_WIDTH), 1.0, 6.0, ((0, 32),)),
        "valid": draw_valid(jax.random.fold_in(seeds[15], 71), 0),
        "destination": draw_destination(jax.random.fold_in(seeds[15], 71), 0),
        "lengths": jax.vmap(lambda own: uneven_parts(own, SEQS, GROUP, LONGEST, 2))(jax.random.split(seeds[5], N_WSH)).reshape((N_WSH, SEQS)).astype(jnp.int32),
        "receptance_matrix": bell_draw(seeds[6], (MODEL_WIDTH, MODEL_WIDTH), MODEL_WIDTH ** -0.5, 0.125, ((0, 4),)),
        "key_matrix": bell_draw(seeds[7], (MODEL_WIDTH, MODEL_WIDTH), MODEL_WIDTH ** -0.5, 0.125, ((0, 4),)),
        "value_matrix": bell_draw(seeds[8], (MODEL_WIDTH, MODEL_WIDTH), MODEL_WIDTH ** -0.5, 0.125, ((0, 4),)),
        "output_matrix": bell_draw(seeds[9], (MODEL_WIDTH, MODEL_WIDTH), MODEL_WIDTH ** -0.5, 0.125, ((0, 4),)),
        "lowrank_down_weight": bell_draw(seeds[10], (MODEL_WIDTH, RANK_COLUMNS), MODEL_WIDTH ** -0.5, 0.125, ((0, 4),)),
        "lowrank_up_weight": bell_draw(seeds[11], (MODEL_WIDTH, RANK_COLUMNS), (RANK_COLUMNS // 4) ** -0.5, 0.5, ((0, 4),)),
        "channel_key_weight": bell_draw(seeds[12], (FF, MODEL_WIDTH), MODEL_WIDTH ** -0.5, 0.125, ((0, 4),)),
        "channel_value_weight": bell_draw(seeds[13], (FF, MODEL_WIDTH), (FF * 3 // 2) ** -0.5, 0.0546875, ((0, 4),)),
        "vectors": draw_vectors(jax.random.fold_in(seeds[15], 71), 0),
    }


@jax.custom_vjp
def low(v):
    return lax.optimization_barrier(v.astype(jnp.bfloat16)).astype(jnp.float32)

@jax.custom_vjp
def low_back(v):
    return v

def low_keep(v):
    return (low(v), None)

def low_pass(kept, grad):
    return (grad,)

def back_keep(v):
    return (v, None)

def back_low(kept, grad):
    return (low(grad),)
low.defvjp(low_keep, low_pass)
low_back.defvjp(back_keep, back_low)

def matrix_product(left_side, right_side):
    return jnp.dot(left_side, right_side, precision=lax.Precision.HIGHEST, preferred_element_type=jnp.float32)

def layer_norm(values, gain_row, bias_row):
    centered = values - lax.optimization_barrier(jnp.mean(values, -1, keepdims=True))
    return centered * lax.rsqrt(lax.optimization_barrier(jnp.mean(centered * centered, -1, keepdims=True)) + 1e-05) * gain_row + bias_row

def shifted(values, starts):
    return jnp.concatenate([jnp.zeros_like(values[:1]), values[:-1]], 0) * (1.0 - starts)[:, None]

def shape_front(keys_raw, values_raw, decay_up, rate_up, value_up, first_in, vectors):
    number_lines = keys_raw.shape[0]
    decay_log = -jax.nn.softplus(-(vectors[:, 8] + decay_up)) - 0.5
    learn_rate = jax.nn.sigmoid(vectors[:, 9] + rate_up)
    blended_payload = values_raw + (first_in - values_raw) * jax.nn.sigmoid(vectors[:, 10] + value_up)
    scaled = (keys_raw * vectors[:, 11]).reshape(number_lines, LEADER_NUMBER, PER_LEADER_DIMS)
    key_dir = (scaled * lax.rsqrt(lax.optimization_barrier(jnp.sum(scaled * scaled, -1, keepdims=True)) + 1e-06)).reshape(number_lines, -1)
    key_mod = keys_raw * (1.0 + (learn_rate - 1.0) * vectors[:, 12])
    return (decay_log, key_mod, blended_payload, key_dir, learn_rate)

def shape_post(head_out, recept, key_mod, blended_payload, sigmoid_opening, vectors):
    number_lines = head_out.shape[0]
    grouped = head_out.reshape(number_lines, LEADER_NUMBER, PER_LEADER_DIMS)
    centered = grouped - lax.optimization_barrier(jnp.mean(grouped, -1, keepdims=True))
    standardized_lines = centered * lax.rsqrt(lax.optimization_barrier(jnp.mean(centered * centered, -1, keepdims=True)) + PER_LEADER_DIMS * 1e-05)
    standardized_lines = standardized_lines.reshape(number_lines, -1) * vectors[:, 14] + vectors[:, 15]
    coefficient_sum = lax.optimization_barrier(jnp.sum((recept * key_mod * vectors[:, 13]).reshape(number_lines, LEADER_NUMBER, PER_LEADER_DIMS), -1, keepdims=True))
    extra_reward_share = (coefficient_sum * blended_payload.reshape(number_lines, LEADER_NUMBER, PER_LEADER_DIMS)).reshape(number_lines, -1)
    return (standardized_lines + extra_reward_share) * sigmoid_opening

def recurrence(pieces, starts):
    number_lines = starts.shape[0]
    blocks = number_lines // BLOCK
    shaped = tuple((piece.reshape(blocks, BLOCK, LEADER_NUMBER, PER_LEADER_DIMS) for piece in pieces)) + (starts.reshape(blocks, BLOCK),)

    def token_step(state_now, token_items):
        recept, decay_log, key_mod, blended_payload, key_dir, learn_rate, start_flag = token_items
        state_now = state_now * (1.0 - start_flag)
        decay_rate = jnp.exp(-jnp.exp(decay_log))
        removed = jnp.einsum('hvk,hk->hv', state_now, -key_dir, precision=lax.Precision.HIGHEST)
        state_now = state_now * decay_rate[:, None, :] + removed[:, :, None] * (key_dir * learn_rate)[:, None, :] + blended_payload[:, :, None] * key_mod[:, None, :]
        return (state_now, jnp.einsum('hvk,hk->hv', state_now, recept, precision=lax.Precision.HIGHEST))

    def block_step(state_now, block_items):
        return lax.scan(token_step, state_now, block_items)
    initial = jnp.zeros((LEADER_NUMBER, PER_LEADER_DIMS, PER_LEADER_DIMS), jnp.float32)
    final_state, outputs = lax.scan(jax.checkpoint(block_step), initial, shaped)
    return outputs.reshape(number_lines, LEADER_NUMBER * PER_LEADER_DIMS)

def forward_group(tokens, first_in, starts, layer_parameters):
    receptance_projection, key_projection, value_projection, output_projection, lowrank_down_weight, lowrank_up_weight, channel_key_weight, channel_value_weight, vectors = layer_parameters
    group_bounds = [0, RW, RW + RA, RW + RA + RV, RW + RA + RV + RG]
    standardized_lines = layer_norm(tokens, vectors[:, 0], vectors[:, 1])
    delta_row = shifted(standardized_lines, starts) - standardized_lines
    mixed = [low(standardized_lines + delta_row * vectors[:, 2 + piece_count]) for piece_count in range(6)]
    recept = low_back(matrix_product(mixed[0], receptance_projection))
    keys_raw = low_back(matrix_product(mixed[2], key_projection))
    values_raw = low_back(matrix_product(mixed[3], value_projection))

    def downward(source_rows, piece_count):
        return low_back(matrix_product(source_rows, lowrank_down_weight[:, group_bounds[piece_count]:group_bounds[piece_count + 1]]))

    def upward(hidden_rows, piece_count):
        return low_back(matrix_product(hidden_rows, lowrank_up_weight[:, group_bounds[piece_count]:group_bounds[piece_count + 1]].T))
    decay_up = upward(low(jnp.tanh(downward(mixed[1], 0))), 0)
    rate_up = upward(low(downward(mixed[4], 1)), 1)
    value_up = upward(low(downward(mixed[3], 2)), 2)
    sigmoid_opening = upward(low(jax.nn.sigmoid(downward(mixed[5], 3))), 3)
    decay_log, key_mod, blended_payload, key_dir, learn_rate = shape_front(keys_raw, values_raw, decay_up, rate_up, value_up, first_in, vectors)
    copies = [low(low_back(piece)) for piece in (recept, decay_log, key_mod, blended_payload, key_dir, learn_rate)]
    head_out = low(low_back(recurrence(copies, starts)))
    mixed_out = low(shape_post(head_out, recept, key_mod, blended_payload, sigmoid_opening, vectors))
    residual = tokens + low_back(matrix_product(mixed_out, output_projection))
    normed_two = layer_norm(residual, vectors[:, 16], vectors[:, 17])
    channel_in = low(normed_two + (shifted(normed_two, starts) - normed_two) * vectors[:, 18])
    hidden_rows = low(jnp.square(jax.nn.relu(low_back(matrix_product(channel_in, channel_key_weight.T)))))
    return residual + low_back(matrix_product(hidden_rows, channel_value_weight))

def reference(tokens, first_layer_values, teacher, valid, destination, lengths, receptance_matrix, key_matrix, value_matrix, output_matrix, lowrank_down_weight, lowrank_up_weight, channel_key_weight, channel_value_weight, vectors):
    total_rows = tokens.shape[0]
    inverse = jnp.zeros((total_rows,), jnp.int32).at[destination.astype(jnp.int32)].set(jnp.arange(total_rows, dtype=jnp.int32))
    offsets = (jnp.cumsum(lengths, 1) - lengths).astype(jnp.int32)
    places = jnp.arange(GROUP, dtype=jnp.int32)
    starts = jnp.any(places[None, :, None] == offsets[:, None, :], 2).astype(jnp.float32)

    def to_groups(array):
        return array[inverse].reshape(N_SEQ, N_WSH, TOK_DEV, -1).transpose(1, 0, 2, 3).reshape(N_WSH, GROUP, -1)

    def from_groups(array):
        return array.reshape(N_WSH, N_SEQ, TOK_DEV, -1).transpose(1, 0, 2, 3).reshape(total_rows, -1)[destination]

    def forward_all(tokens_in, first_in, *layer_parameters):

        def group_fn(group_items):
            return forward_group(group_items[0], group_items[1], group_items[2], layer_parameters)
        group_out = lax.map(jax.checkpoint(group_fn), (to_groups(tokens_in), to_groups(first_in), starts))
        return from_groups(group_out)
    weight_tuple = [matrix_operand.astype(jnp.float32) for matrix_operand in (receptance_matrix, key_matrix, value_matrix, output_matrix, lowrank_down_weight, lowrank_up_weight, channel_key_weight, channel_value_weight)]
    result, pullback = jax.vjp(forward_all, tokens.astype(jnp.float32), first_layer_values.astype(jnp.float32), *weight_tuple, vectors)
    mask_rows = valid.astype(jnp.float32)
    valid_count = jnp.sum(mask_rows)
    cotangent = (result - teacher.astype(jnp.float32)) * (mask_rows * (total_rows / valid_count))[:, None]
    gradients = pullback(cotangent)
    return (result.astype(jnp.bfloat16), gradients[0].astype(jnp.bfloat16), gradients[1].astype(jnp.bfloat16), gradients[2], gradients[3], gradients[4], gradients[5], gradients[6], gradients[7], gradients[8], gradients[9], gradients[10])
```

```python
import functools

import jax
import jax.numpy as jnp
from jax import lax
from jax.experimental import pallas as pl
from jax.experimental.pallas import tpu as pltpu
from jax.sharding import PartitionSpec as P

HEAD = 64
BLOCK = 64
RANKS = (96, 96, 64, 256)
PADDED = (128, 128, 128, 256)
OFFSETS = (0, 128, 256, 384)
WIDE = 640
EXTRA = 128
DIGIT = 64

F32 = jnp.float32
BF16 = jnp.bfloat16

NN = (((1,), (0,)), ((), ()))
NT = (((1,), (1,)), ((), ()))
TN = (((0,), (0,)), ((), ()))


def dot(a, b, dims=NN):
    return lax.dot_general(a, b, dims, preferred_element_type=F32)


def halves(x):
    high = x.astype(BF16)
    return high, (x - high.astype(F32)).astype(BF16)


def dot3(a, b, dims=NN):
    a_high, a_low = halves(a)
    b_high, b_low = halves(b)
    return dot(a_high, b_high, dims) + (dot(a_high, b_low, dims) + dot(a_low, b_high, dims))


def sum_left(mask, x):
    high, low = halves(x)
    low_two = (x - high.astype(F32) - low.astype(F32)).astype(BF16)
    return dot(mask, high) + (dot(mask, low) + dot(mask, low_two))


def head_sum(x, ones):
    high, low = halves(x)
    return dot(high, ones) + dot(low, ones)


def low(x):
    return x.astype(BF16).astype(F32)


def iotas(rows, columns):
    return (
        lax.broadcasted_iota(jnp.int32, (rows, columns), 0),
        lax.broadcasted_iota(jnp.int32, (rows, columns), 1),
    )


def head_ones(width):
    i, j = iotas(width, width)
    return jnp.where((i >> 6) == (j >> 6), 1.0, 0.0).astype(BF16)


def front(keys, values, hidden, up, first, vec, ones):
    z = vec[0:1] + dot(hidden[:, 0:128], up[0:128])
    decay_log = -(jnp.maximum(-z, 0.0) + jnp.log1p(jnp.exp(-jnp.abs(z)))) - 0.5
    rate = jax.nn.sigmoid(vec[1:2] + dot(hidden[:, 128:256], up[128:256]))
    blend = jax.nn.sigmoid(vec[2:3] + dot(hidden[:, 256:384], up[256:384]))
    gate = dot(hidden[:, 384:640], up[384:640])
    mixed_value = values + (first - values) * blend
    scaled = keys * vec[3:4]
    scale = lax.rsqrt(head_sum(scaled * scaled, ones) + 1e-06)
    key_dir = scaled * scale
    key_mod = keys * (1.0 + (rate - 1.0) * vec[4:5])
    return z, decay_log, rate, blend, gate, mixed_value, scale, key_dir, key_mod


def block_masks(segments):
    i, j = iotas(BLOCK, BLOCK)
    across = jnp.broadcast_to(segments[0:1], (BLOCK, BLOCK))
    down = across.T
    before = jnp.broadcast_to(segments[1:2], (BLOCK, BLOCK))
    last = jnp.broadcast_to(segments[2:3], (BLOCK, BLOCK))
    same = across == down
    strict = jnp.where(same & (i > j), 1.0, 0.0)
    closed = jnp.where(same & (i >= j), 1.0, 0.0)
    carry = jnp.where(down == before, 1.0, 0.0)
    tail = jnp.where(down == last, 1.0, 0.0)
    keep = jnp.where(segments[2:3] == segments[1:2], 1.0, 0.0)
    quad = jnp.concatenate(
        [jnp.concatenate([strict, strict], 1), jnp.concatenate([closed, closed], 1)], 0
    )
    return quad, carry, tail, keep


def tile_heads(x, heads):
    return jnp.concatenate([x] * heads, 1) if heads > 1 else x


def join(pieces, axis):
    return jnp.concatenate(pieces, axis) if len(pieces) > 1 else pieces[0]


def decayed(decay_low, key_low, dir_low, rate_low, recept_low, carry, tail):
    i, j = iotas(BLOCK, BLOCK)
    lower = jnp.where(i >= j, 1.0, 0.0).astype(BF16)
    log_step = -jnp.exp(decay_low)
    total = sum_left(lower, log_step)
    before = jnp.exp(total - log_step)
    grown = jnp.exp(total)
    shrunk = jnp.exp(-total)
    end = total[BLOCK - 1 : BLOCK]
    tail_decay = jnp.exp(end - total) * tail
    alpha = -dir_low * before
    beta_plain = dir_low * rate_low
    beta = beta_plain * shrunk
    key = key_low * shrunk
    recept = recept_low * grown
    return dict(
        log_step=log_step, before=before, grown=grown, shrunk=shrunk, end=jnp.exp(end), tail=tail_decay,
        alpha=alpha, beta_plain=beta_plain, beta=beta, key=key, recept=recept,
        beta_end=beta_plain * tail_decay, key_end=key_low * tail_decay,
        alpha_in=alpha * carry, recept_in=recept * carry,
    )


def unit_inverse(lower_part):
    i, j = iotas(BLOCK, BLOCK)

    def within(size):
        return (i // size) == (j // size)

    small = jnp.where(within(8), lower_part, 0.0)
    two = dot3(small, small)
    four = dot3(two, two)
    inverse = jnp.where(i == j, 1.0, 0.0) + small
    inverse = inverse + dot3(inverse, two)
    inverse = inverse + dot3(inverse, four)
    for size in (16, 32, 64):
        off = jnp.where(within(size) & ~within(size // 2), lower_part, 0.0)
        inverse = inverse + dot3(inverse, dot3(off, inverse))
    return inverse


def post_norm(head_low, ones):
    centered = head_low - head_sum(head_low, ones) * (1.0 / HEAD)
    spread = lax.rsqrt(head_sum(centered * centered, ones) * (1.0 / HEAD) + HEAD * 1e-05)
    return centered * spread, spread


def forward_kernel(
    count, recept_ref, keys_ref, values_ref, hidden_ref, first_ref, up_ref, vec_ref, segment_ref,
    mixed_ref, head_ref, state_ref, inverse_ref, removed_ref, state,
):
    width = recept_ref.shape[1]
    heads = width // HEAD

    @pl.when(pl.program_id(0) == 0)
    def _():
        state[...] = jnp.zeros_like(state)

    ones = head_ones(width)
    vec = vec_ref[...]
    up = up_ref[...]
    for block in range(count):
        rows = slice(block * BLOCK, (block + 1) * BLOCK)
        recept, keys, values = recept_ref[rows], keys_ref[rows], values_ref[rows]
        _, decay_log, rate, _, gate, mixed_value, _, key_dir, key_mod = front(
            keys, values, hidden_ref[rows], up, first_ref[rows].astype(F32), vec, ones
        )
        quad, carry, tail, keep = block_masks(segment_ref[block * 8 : block * 8 + 8])
        parts = decayed(
            low(decay_log), low(key_mod), low(key_dir), low(rate), low(recept),
            tile_heads(carry, heads), tile_heads(tail, heads),
        )
        value_low = low(mixed_value)
        entering = state[...]
        state_ref[rows] = entering
        leaving, outs, inverses, removals = [], [], [], []
        for head in range(heads):
            cols = slice(head * HEAD, (head + 1) * HEAD)
            own = value_low[:, cols]
            now = entering[:, cols]
            pairs = quad * dot3(
                jnp.concatenate([parts["alpha"][:, cols], parts["recept"][:, cols]], 0),
                jnp.concatenate([parts["beta"][:, cols], parts["key"][:, cols]], 0),
                NT,
            )
            inverse = unit_inverse(pairs[:BLOCK, :BLOCK])
            inward = dot3(
                jnp.concatenate([parts["alpha_in"][:, cols], parts["recept_in"][:, cols]], 0), now, NT
            )
            by_value = dot3(pairs[:, BLOCK:], own)
            removed = dot3(inverse, inward[:BLOCK] + by_value[:BLOCK])
            outs.append(inward[BLOCK:] + by_value[BLOCK:] + dot3(pairs[BLOCK:, :BLOCK], removed))
            leaving.append(
                now * (parts["end"][:, cols] * keep)
                + dot3(
                    jnp.concatenate([removed, own], 0),
                    jnp.concatenate([parts["beta_end"][:, cols], parts["key_end"][:, cols]], 0),
                    TN,
                )
            )
            inverses.append(inverse)
            removals.append(removed)
        state[...] = join(leaving, 1)
        inverse_ref[rows] = join(inverses, 1)
        removed_ref[rows] = join(removals, 1)
        head_low = join(outs, 1).astype(BF16)
        head_ref[rows] = head_low
        normed, _ = post_norm(head_low.astype(F32), ones)
        bonus = head_sum(recept * key_mod * vec[5:6], ones) * mixed_value
        mixed_ref[rows] = ((normed * vec[6:7] + vec[7:8] + bonus) * gate).astype(BF16)


def backward_kernel(
    count, grad_ref, recept_ref, keys_ref, values_ref, hidden_ref, first_ref, up_ref, vec_ref, segment_ref,
    head_ref, state_ref, inverse_ref, removed_ref,
    recept_out, keys_out, values_out, ups_out, first_out, vec_out, state,
):
    width = recept_ref.shape[1]
    heads = width // HEAD

    @pl.when(pl.program_id(0) == 0)
    def _():
        state[...] = jnp.zeros_like(state)
        vec_out[...] = jnp.zeros_like(vec_out)

    ones = head_ones(width)
    vec = vec_ref[...]
    up = up_ref[...]
    i, j = iotas(BLOCK, BLOCK)
    upper = jnp.where(i <= j, 1.0, 0.0).astype(BF16)
    for block in range(count - 1, -1, -1):
        rows = slice(block * BLOCK, (block + 1) * BLOCK)
        recept, keys, values = recept_ref[rows], keys_ref[rows], values_ref[rows]
        first = first_ref[rows].astype(F32)
        z, decay_log, rate, blend, gate, mixed_value, scale, key_dir, key_mod = front(
            keys, values, hidden_ref[rows], up, first, vec, ones
        )
        quad, carry, tail, keep = block_masks(segment_ref[block * 8 : block * 8 + 8])
        carry_wide = tile_heads(carry, heads)
        rate_low, dir_low = low(rate), low(key_dir)
        parts = decayed(
            low(decay_log), low(key_mod), dir_low, rate_low, low(recept), carry_wide, tile_heads(tail, heads)
        )
        value_low = low(mixed_value)

        grad = grad_ref[rows].astype(F32)
        normed, spread = post_norm(head_ref[rows].astype(F32), ones)
        product = recept * key_mod
        coefficient = head_sum(product * vec[5:6], ones)
        grad_gate = grad * (normed * vec[6:7] + vec[7:8] + coefficient * mixed_value)
        opened = grad * gate
        grad_normed = opened * vec[6:7]
        grad_head = spread * (
            grad_normed
            - head_sum(grad_normed, ones) * (1.0 / HEAD)
            - normed * (head_sum(grad_normed * normed, ones) * (1.0 / HEAD))
        )
        grad_coefficient = head_sum(opened * mixed_value, ones)
        grad_mixed_value = opened * coefficient
        weighted = grad_coefficient * vec[5:6]
        grad_recept = weighted * key_mod
        grad_key_mod = weighted * recept
        head_grad = low(grad_head)

        entering, removed_all, inverse_all = state_ref[rows], removed_ref[rows], inverse_ref[rows]
        after = state[...]
        leaving, g_alpha, g_recept, g_beta, g_key, g_beta_end, g_key_end, g_value, g_end = (
            [], [], [], [], [], [], [], [], [],
        )
        for head in range(heads):
            cols = slice(head * HEAD, (head + 1) * HEAD)
            own, now, later = value_low[:, cols], entering[:, cols], after[:, cols]
            removed, inverse, out_grad = removed_all[:, cols], inverse_all[:, cols], head_grad[:, cols]
            left = jnp.concatenate([parts["alpha"][:, cols], parts["recept"][:, cols]], 0)
            right = jnp.concatenate([parts["beta"][:, cols], parts["key"][:, cols]], 0)
            ends = jnp.concatenate([parts["beta_end"][:, cols], parts["key_end"][:, cols]], 0)
            pairs = quad * dot3(left, right, NT)
            from_end = dot3(ends, later, NT)
            grad_removed = dot3(pairs[BLOCK:, :BLOCK], out_grad, TN) + from_end[:BLOCK]
            grad_inner = dot3(inverse, grad_removed, TN)
            both = jnp.concatenate([grad_inner, out_grad], 0)
            sources = jnp.concatenate([removed, own], 0)
            grad_pairs = quad * dot3(both, sources, NT)
            carry_two = jnp.concatenate([carry, carry], 0)
            grad_left = dot3(grad_pairs, right) + carry_two * dot3(both, now)
            grad_right = dot3(grad_pairs, left, TN)
            grad_ends = dot3(sources, later)
            g_value.append(dot3(pairs[:, BLOCK:], both, TN) + from_end[BLOCK:])
            kept = later * (parts["end"][:, cols] * keep)
            leaving.append(kept + dot3(both, carry_two * left, TN))
            g_end.append(jnp.sum(now * kept, 0, keepdims=True))
            g_alpha.append(grad_left[:BLOCK])
            g_recept.append(grad_left[BLOCK:])
            g_beta.append(grad_right[:BLOCK])
            g_key.append(grad_right[BLOCK:])
            g_beta_end.append(grad_ends[:BLOCK])
            g_key_end.append(grad_ends[BLOCK:])
        state[...] = join(leaving, 1)
        d_alpha, d_recept, d_beta, d_key = join(g_alpha, 1), join(g_recept, 1), join(g_beta, 1), join(g_key, 1)
        d_beta_end, d_key_end = join(g_beta_end, 1), join(g_key_end, 1)
        ended = parts["beta_end"] * d_beta_end + parts["key_end"] * d_key_end
        alphas = parts["alpha"] * d_alpha
        d_total = parts["recept"] * d_recept - parts["beta"] * d_beta - parts["key"] * d_key - ended + alphas
        d_step = sum_left(upper, d_total) + (jnp.sum(ended, 0, keepdims=True) + join(g_end, 1)) - alphas
        d_beta_plain = d_beta * parts["shrunk"] + d_beta_end * parts["tail"]
        copy_recept = low(d_recept * parts["grown"])
        copy_decay = low(d_step * parts["log_step"])
        copy_key = low(d_key * parts["shrunk"] + d_key_end * parts["tail"])
        copy_value = low(join(g_value, 1))
        copy_dir = low(d_beta_plain * rate_low - d_alpha * parts["before"])
        copy_rate = low(d_beta_plain * dir_low)

        grad_recept = grad_recept + copy_recept
        grad_key_mod = grad_key_mod + copy_key
        grad_mixed_value = grad_mixed_value + copy_value
        grad_z = copy_decay * jax.nn.sigmoid(-z)
        factor = 1.0 + (rate - 1.0) * vec[4:5]
        keyed = grad_key_mod * keys
        grad_rate = copy_rate + keyed * vec[4:5]
        grad_scaled = scale * (copy_dir - key_dir * head_sum(copy_dir * key_dir, ones))
        grad_keys = grad_key_mod * factor + grad_scaled * vec[3:4]
        grad_rate_up = grad_rate * rate * (1.0 - rate)
        grad_blend = grad_mixed_value * (first - values)
        grad_value_up = grad_blend * blend * (1.0 - blend)
        recept_out[rows] = grad_recept.astype(BF16)
        keys_out[rows] = grad_keys.astype(BF16)
        values_out[rows] = (grad_mixed_value * (1.0 - blend)).astype(BF16)
        first_out[rows] = (grad_mixed_value * blend).astype(BF16)
        ups_out[0, rows] = grad_z.astype(BF16)
        ups_out[1, rows] = grad_rate_up.astype(BF16)
        ups_out[2, rows] = grad_value_up.astype(BF16)
        ups_out[3, rows] = grad_gate.astype(BF16)

        def total(x):
            return jnp.sum(x, 0, keepdims=True)

        vec_out[...] += jnp.concatenate(
            [
                total(grad_z), total(grad_rate_up), total(grad_value_up), total(grad_scaled * keys),
                total(keyed * (rate - 1.0)), total(grad_coefficient * product),
                total(opened * normed), total(opened),
            ],
            0,
        )


def per_step(rows):
    return 2 if (rows // BLOCK) % 2 == 0 else 1


def run_forward(recept, keys, values, hidden, first, up, vec, segments):
    rows, width = recept.shape
    count = per_step(rows)
    step = count * BLOCK

    def spec(columns):
        return pl.BlockSpec((step, columns), lambda i: (i, 0))

    def whole(array):
        return pl.BlockSpec(array.shape, lambda i: (0, 0))

    return pl.pallas_call(
        functools.partial(forward_kernel, count),
        grid=(rows // step,),
        in_specs=[
            spec(width), spec(width), spec(width), spec(WIDE), spec(width), whole(up), whole(vec),
            pl.BlockSpec((count * 8, BLOCK), lambda i: (i, 0)),
        ],
        out_specs=[spec(width)] * 5,
        out_shape=[jax.ShapeDtypeStruct((rows, width), d) for d in (BF16, BF16, F32, F32, F32)],
        scratch_shapes=[pltpu.VMEM((BLOCK, width), F32)],
        compiler_params=pltpu.CompilerParams(vmem_limit_bytes=48 << 20),
        name="mix_forward",
    )(recept, keys, values, hidden, first, up, vec, segments)


def run_backward(grad, recept, keys, values, hidden, first, up, vec, segments, saved):
    rows, width = recept.shape
    count = per_step(rows)
    step = count * BLOCK
    last = rows // step - 1

    def spec(columns):
        return pl.BlockSpec((step, columns), lambda i: (last - i, 0))

    def whole(array):
        return pl.BlockSpec(array.shape, lambda i: (0, 0))

    return pl.pallas_call(
        functools.partial(backward_kernel, count),
        grid=(rows // step,),
        in_specs=[
            spec(width), spec(width), spec(width), spec(width), spec(WIDE), spec(width), whole(up), whole(vec),
            pl.BlockSpec((count * 8, BLOCK), lambda i: (last - i, 0)),
            spec(width), spec(width), spec(width), spec(width),
        ],
        out_specs=[
            spec(width), spec(width), spec(width),
            pl.BlockSpec((4, step, width), lambda i: (0, last - i, 0)),
            spec(width), pl.BlockSpec((8, width), lambda i: (0, 0)),
        ],
        out_shape=[
            jax.ShapeDtypeStruct((rows, width), BF16), jax.ShapeDtypeStruct((rows, width), BF16),
            jax.ShapeDtypeStruct((rows, width), BF16), jax.ShapeDtypeStruct((4, rows, width), BF16),
            jax.ShapeDtypeStruct((rows, width), BF16), jax.ShapeDtypeStruct((8, width), F32),
        ],
        scratch_shapes=[pltpu.VMEM((BLOCK, width), F32)],
        compiler_params=pltpu.CompilerParams(vmem_limit_bytes=48 << 20),
        name="mix_backward",
    )(grad, recept, keys, values, hidden, first, up, vec, segments, *saved)


def norm_stats(values):
    centered = values - jnp.mean(values, -1, keepdims=True)
    scale = lax.rsqrt(jnp.mean(centered * centered, -1, keepdims=True) + 1e-05)
    return centered * scale, scale


def norm_back(grad, standard, scale, gain):
    scaled = grad * gain
    return scale * (
        scaled
        - jnp.mean(scaled, -1, keepdims=True)
        - standard * jnp.mean(scaled * standard, -1, keepdims=True)
    )


def pad_ranks(matrix):
    pieces, start = [], 0
    for rank, padded in zip(RANKS, PADDED):
        pieces.append(jnp.pad(matrix[:, start : start + rank], ((0, 0), (0, padded - rank))))
        start += rank
    return jnp.concatenate(pieces, 1)


def unpad_ranks(matrix):
    return jnp.concatenate([matrix[..., o : o + r] for o, r in zip(OFFSETS, RANKS)], -1)


def from_behind(x, axis, by):
    size = lax.axis_size(axis)
    pairs = [(i, i + by) for i in range(size) if 0 <= i + by < size]
    return lax.ppermute(x, axis, pairs)


def exchange(x, axis):
    return lax.all_to_all(x, axis, split_axis=0, concat_axis=0, tiled=True)


def local(
    tokens, first_layer_values, teacher, valid, destination, lengths,
    receptance_matrix, key_matrix, value_matrix, output_matrix,
    lowrank_down_weight, lowrank_up_weight, channel_key_weight, channel_value_weight, vectors,
):
    rows, width = tokens.shape
    seqs, parts = lax.axis_size("seq"), lax.axis_size("wsh")
    me = lax.axis_index("seq")
    group = rows * seqs
    own_width = width // seqs
    shard = width // parts
    piece = shard // seqs
    column = me * own_width

    dest_seq = destination // rows // parts
    position = dest_seq * rows + destination % rows
    digits = jnp.stack([position // DIGIT, position % DIGIT, valid], 1).astype(BF16)
    tail = jnp.pad(digits, ((0, 0), (0, EXTRA - 3)))
    given = lax.all_gather(jnp.concatenate([tokens, tail], 1), "seq", axis=0, tiled=True)
    info = given[:, width : width + 3].astype(F32)
    places = (info[:, 0] * DIGIT + info[:, 1]).astype(jnp.int32)
    numbers = jnp.arange(group, dtype=jnp.int32)
    permute = (numbers[:, None] == places[None, :]).astype(BF16)
    total_valid = jnp.sum(lax.all_gather(jnp.sum(info[:, 2]).reshape(1), "wsh", axis=0, tiled=True))

    index = jnp.arange(rows, dtype=jnp.int32)
    same_dest = (dest_seq[:, None] == dest_seq[None, :]) & (index[None, :] < index[:, None])
    slot = dest_seq * (rows // seqs) + jnp.sum(same_dest.astype(jnp.int32), 1)
    arrange = (index[:, None] == slot[None, :]).astype(BF16)
    mine = (places // rows) == me
    arrival = jnp.cumsum(mine.astype(jnp.int32)) - 1
    own_rows = ((index[:, None] + me * rows) == places[None, :]).astype(BF16)
    settle = dot(own_rows, (mine[:, None] & (arrival[:, None] == index[None, :])).astype(BF16)).astype(BF16)

    def deal(array):
        moved = exchange(dot(arrange, array).astype(BF16).reshape(seqs, rows // seqs, width), "seq")
        return dot(settle, moved.reshape(rows, width))

    def undeal(array):
        back = dot(settle, array.astype(BF16), TN).astype(BF16)
        moved = exchange(back.reshape(seqs, rows // seqs, width), "seq")
        return dot(arrange, moved.reshape(rows, width), TN).astype(BF16)

    target = deal(teacher)
    first_given = exchange(
        first_layer_values.reshape(rows, seqs, own_width).transpose(1, 0, 2), "seq"
    ).reshape(group, own_width)
    first = dot(permute, first_given).astype(BF16)

    offsets = jnp.cumsum(lengths[0]) - lengths[0]
    starts = jnp.any(numbers[:, None] == offsets[None, :], 1).astype(F32)
    segment_ids = jnp.cumsum(starts).reshape(-1, BLOCK)
    before = segment_ids[:, :1] - starts.reshape(-1, BLOCK)[:, :1]
    segments = jnp.stack(
        [segment_ids, jnp.broadcast_to(before, segment_ids.shape), jnp.broadcast_to(segment_ids[:, -1:], segment_ids.shape)]
        + [jnp.zeros_like(segment_ids)] * 5,
        1,
    ).reshape(-1, BLOCK)
    flowing = (1.0 - starts)[:, None]

    def own_columns(matrix):
        return lax.dynamic_slice_in_dim(matrix, column, own_width, 1)

    weights = lax.all_gather(
        jnp.concatenate(
            [own_columns(receptance_matrix), own_columns(key_matrix), own_columns(value_matrix), pad_ranks(lowrank_down_weight)], 1
        ),
        "wsh", axis=0, tiled=True,
    )
    w_recept, w_key = weights[:, :own_width], weights[:, own_width : 2 * own_width]
    w_value, down = weights[:, 2 * own_width : 3 * own_width], weights[:, 3 * own_width :]
    up_piece = lax.dynamic_slice_in_dim(lowrank_up_weight, column % shard, own_width, 0)
    ups = lax.all_gather(up_piece, "wsh", axis=0, tiled=False)
    up = pad_ranks(lax.dynamic_index_in_dim(ups, column // shard, 0, keepdims=False))
    w_out = lax.all_gather(output_matrix, "wsh", axis=0, tiled=True)
    vec = lax.dynamic_slice_in_dim(vectors, column, own_width, 0)[:, 8:16].T

    balanced = dot(permute, given[:, :width])
    standard, scale_one = norm_stats(balanced)
    normed = standard * vectors[:, 0] + vectors[:, 1]
    previous = jnp.concatenate([jnp.zeros_like(normed[:1]), normed[:-1]], 0) * flowing
    delta = previous - normed
    mixed = [(normed + delta * vectors[:, 2 + c]).astype(BF16) for c in range(6)]
    recept = dot(mixed[0], w_recept)
    keys = dot(mixed[2], w_key)
    values = dot(mixed[3], w_value)
    downs = [dot(mixed[c], down[:, o : o + n]) for c, o, n in zip((1, 4, 3, 5), OFFSETS, PADDED)]
    decay_tanh, gate_sigmoid = jnp.tanh(downs[0]), jax.nn.sigmoid(downs[3])
    hidden = jnp.concatenate(
        [decay_tanh.astype(BF16), downs[1].astype(BF16), downs[2].astype(BF16), gate_sigmoid.astype(BF16)], 1
    )
    inputs = (recept, keys, values, hidden, first, up.T, vec, segments)
    mixed_out, *saved = run_forward(*inputs)

    mixed_rows = exchange(mixed_out.reshape(seqs, rows, own_width), "seq").transpose(1, 0, 2).reshape(rows, width)
    own = lax.dynamic_slice_in_dim(balanced, me * rows, rows, 0)
    own_starts = lax.dynamic_slice_in_dim(starts, me * rows, rows, 0)
    own_flowing = (1.0 - own_starts)[:, None]
    own_valid = dot(own_rows, given[:, width : width + EXTRA])[:, 2]
    residual = own + dot(mixed_rows, w_out)
    standard_two, scale_two = norm_stats(residual)
    normed_two = standard_two * vectors[:, 16] + vectors[:, 17]
    carried_two = from_behind(normed_two[-1:], "seq", 1)
    delta_two = jnp.concatenate([carried_two, normed_two[:-1]], 0) * own_flowing - normed_two
    channel = lax.all_gather(
        (normed_two + delta_two * vectors[:, 18]).astype(BF16), "wsh", axis=0, tiled=True
    )
    active = jax.nn.relu(dot(channel, channel_key_weight, NT))
    hidden_rows = jnp.square(active).astype(BF16)
    result = residual + lax.psum_scatter(
        dot(hidden_rows, channel_value_weight), "wsh", scatter_dimension=0, tiled=True
    )
    total_tokens = group * parts
    cotangent = (result - target) * (own_valid * (total_tokens / total_valid))[:, None]
    cot = lax.all_gather(cotangent.astype(BF16), "wsh", axis=0, tiled=True)

    grad_pre = (dot(cot, channel_value_weight, NT) * 2.0 * active).astype(BF16)
    grad_channel = lax.psum_scatter(dot(grad_pre, channel_key_weight), "wsh", scatter_dimension=0, tiled=True)
    blocks = [(s * parts + w, w * seqs + s) for s in range(seqs) for w in range(parts)]

    def ffn_grad(left, right):
        part = lax.psum_scatter(dot(left, right, TN).astype(BF16), "seq", scatter_dimension=0, tiled=True)
        return lax.ppermute(part, ("seq", "wsh"), blocks).astype(F32)

    grad_ffn_value = ffn_grad(hidden_rows, cot)
    grad_ffn_key = ffn_grad(grad_pre, channel)
    grad_vec_mix_two = jnp.sum(grad_channel * delta_two, 0)
    shifted = grad_channel * vectors[:, 18] * own_flowing
    behind = from_behind(shifted[:1], "seq", -1)
    grad_normed_two = grad_channel * (1.0 - vectors[:, 18]) + jnp.concatenate([shifted[1:], behind], 0)
    grad_residual = cotangent + norm_back(grad_normed_two, standard_two, scale_two, vectors[:, 16])
    grad_low = grad_residual.astype(BF16)

    grad_posted = dot(grad_low, w_out, NT).astype(BF16)
    grad_heads = exchange(grad_posted.reshape(rows, seqs, own_width).transpose(1, 0, 2), "seq").reshape(group, own_width)
    recept_low, keys_low, values_low, ups_low, grad_first, grad_vec_heads = run_backward(grad_heads, *inputs, saved)
    grad_low_all = lax.all_gather(grad_low, "seq", axis=0, tiled=True)
    hid = [dot(ups_low[k], up[:, o : o + n]) for k, (o, n) in enumerate(zip(OFFSETS, PADDED))]
    down_lows = [
        (hid[0] * (1.0 - jnp.square(decay_tanh))).astype(BF16),
        hid[1].astype(BF16),
        hid[2].astype(BF16),
        (hid[3] * gate_sigmoid * (1.0 - gate_sigmoid)).astype(BF16),
    ]
    down_cols = [down[:, o : o + n] for o, n in zip(OFFSETS, PADDED)]
    grad_mix = [
        dot(recept_low, w_recept, NT),
        dot(down_lows[0], down_cols[0], NT),
        dot(keys_low, w_key, NT),
        dot(values_low, w_value, NT) + dot(down_lows[2], down_cols[2], NT),
        dot(down_lows[1], down_cols[1], NT),
        dot(down_lows[3], down_cols[3], NT),
    ]
    grad_vec_mix = [jnp.sum(g * delta, 0) for g in grad_mix]
    kept = sum(g * (1.0 - vectors[:, 2 + c]) for c, g in enumerate(grad_mix))
    sent = sum(g * vectors[:, 2 + c] for c, g in enumerate(grad_mix)) * flowing
    grad_normed = kept + jnp.concatenate([sent[1:], jnp.zeros_like(sent[:1])], 0)
    grad_vec_one = [jnp.sum(grad_normed * standard, 0), jnp.sum(grad_normed, 0)]
    grad_balanced = norm_back(grad_normed, standard, scale_one, vectors[:, 0])
    mine_rows = lax.dynamic_slice_in_dim(grad_balanced, me * rows, rows, 0) + grad_residual
    grad_balanced = lax.dynamic_update_slice_in_dim(grad_balanced, mine_rows, me * rows, 0)
    grad_given = dot(permute, grad_balanced.astype(BF16), TN).astype(BF16)
    grad_tokens = lax.psum_scatter(grad_given, "seq", scatter_dimension=0, tiled=True)
    first_back = exchange(dot(permute, grad_first, TN).astype(BF16).reshape(seqs, rows, own_width), "seq")
    grad_first_rows = first_back.transpose(1, 0, 2).reshape(rows, width)

    wide = jnp.concatenate(
        [dot(mixed[0], recept_low, TN), dot(mixed[2], keys_low, TN), dot(mixed[3], values_low, TN)]
        + [dot(mixed[c], l, TN)[:, :r] for c, l, r in zip((1, 4, 3, 5), down_lows, RANKS)],
        1,
    ).astype(BF16)
    ordered = wide.reshape(seqs, parts, piece, -1).transpose(1, 0, 2, 3).reshape(parts * seqs * piece, -1)
    wide_part = lax.psum_scatter(ordered, "wsh", scatter_dimension=0, tiled=True)
    wide_all = exchange(wide_part.reshape(seqs, piece, -1), "seq").astype(F32)

    def square(number):
        taken = wide_all[:, :, number * own_width : (number + 1) * own_width]
        return taken.transpose(1, 0, 2).reshape(piece, width)

    grad_down = jnp.sum(wide_all[:, :, 3 * own_width :], 0)
    tall = jnp.concatenate(
        [dot(mixed_out, grad_low_all, TN)]
        + [dot(ups_low[k], hidden[:, o : o + r], TN) for k, (o, r) in enumerate(zip(OFFSETS, RANKS))],
        1,
    ).astype(BF16)
    tall_part = lax.psum_scatter(tall, "wsh", scatter_dimension=0, tiled=True).astype(F32)

    heads_part = lax.dynamic_update_slice_in_dim(jnp.zeros((width, 8), F32), grad_vec_heads.T, column, 0)
    grad_vectors = jnp.concatenate(
        [
            jnp.stack(grad_vec_one + grad_vec_mix, 1),
            heads_part,
            jnp.stack([jnp.sum(grad_normed_two * standard_two, 0), jnp.sum(grad_normed_two, 0), grad_vec_mix_two], 1),
        ],
        1,
    )
    vec_part = jnp.sum(exchange(grad_vectors.reshape(seqs, parts * piece, -1), "seq"), 0)
    vec_part = jnp.sum(exchange(vec_part.reshape(parts, piece, -1), "wsh"), 0)
    return (
        undeal(result), grad_tokens, grad_first_rows,
        square(0), square(1), square(2),
        tall_part[:, :width], grad_down, tall_part[:, width:],
        grad_ffn_key, grad_ffn_value, vec_part,
    )


def solution(mesh):
    both, shard = P(("seq", "wsh"), None), P("wsh", None)
    flat = P(("seq", "wsh"))
    return jax.shard_map(
        local,
        mesh=mesh,
        in_specs=(both, both, both, flat, flat) + (shard,) * 9 + (P(),),
        out_specs=(both,) * 12,
        check_vma=False,
    )
```

```python
import functools

import jax
import jax.numpy as jnp
from jax import lax
from jax.experimental import pallas as pl
from jax.experimental.pallas import tpu as pltpu
from jax.sharding import PartitionSpec as P

HEAD = 64
BLOCK = 64
RANKS = (96, 96, 64, 256)
PADDED = (128, 128, 128, 256)
OFFSETS = (0, 128, 256, 384)
WIDE = 640
EXTRA = 128
DIGIT = 64

F32 = jnp.float32
BF16 = jnp.bfloat16

NN = (((1,), (0,)), ((), ()))
NT = (((1,), (1,)), ((), ()))
TN = (((0,), (0,)), ((), ()))


def dot(a, b, dims=NN):
    return lax.dot_general(a, b, dims, preferred_element_type=F32)


def halves(x):
    high = x.astype(BF16)
    return high, (x - high.astype(F32)).astype(BF16)


def dot3(a, b, dims=NN):
    a_high, a_low = halves(a)
    b_high, b_low = halves(b)
    return dot(a_high, b_high, dims) + (dot(a_high, b_low, dims) + dot(a_low, b_high, dims))


def sum_left(mask, x):
    high, low = halves(x)
    low_two = (x - high.astype(F32) - low.astype(F32)).astype(BF16)
    return dot(mask, high) + (dot(mask, low) + dot(mask, low_two))


def head_sum(x, ones):
    high, low = halves(x)
    return dot(high, ones) + dot(low, ones)


def low(x):
    return x.astype(BF16).astype(F32)


def iotas(rows, columns):
    return (
        lax.broadcasted_iota(jnp.int32, (rows, columns), 0),
        lax.broadcasted_iota(jnp.int32, (rows, columns), 1),
    )


def head_ones(width):
    i, j = iotas(width, width)
    return jnp.where((i >> 6) == (j >> 6), 1.0, 0.0).astype(BF16)


def front(keys, values, hidden, up, first, vec, ones):
    z = vec[0:1] + dot(hidden[:, 0:128], up[0:128])
    decay_log = -(jnp.maximum(-z, 0.0) + jnp.log1p(jnp.exp(-jnp.abs(z)))) - 0.5
    rate = jax.nn.sigmoid(vec[1:2] + dot(hidden[:, 128:256], up[128:256]))
    blend = jax.nn.sigmoid(vec[2:3] + dot(hidden[:, 256:384], up[256:384]))
    gate = dot(hidden[:, 384:640], up[384:640])
    mixed_value = values + (first - values) * blend
    scaled = keys * vec[3:4]
    scale = lax.rsqrt(head_sum(scaled * scaled, ones) + 1e-06)
    key_dir = scaled * scale
    key_mod = keys * (1.0 + (rate - 1.0) * vec[4:5])
    return z, decay_log, rate, blend, gate, mixed_value, scale, key_dir, key_mod


def block_masks(segments):
    i, j = iotas(BLOCK, BLOCK)
    across = jnp.broadcast_to(segments[0:1], (BLOCK, BLOCK))
    down = across.T
    before = jnp.broadcast_to(segments[1:2], (BLOCK, BLOCK))
    last = jnp.broadcast_to(segments[2:3], (BLOCK, BLOCK))
    same = across == down
    strict = jnp.where(same & (i > j), 1.0, 0.0)
    closed = jnp.where(same & (i >= j), 1.0, 0.0)
    carry = jnp.where(down == before, 1.0, 0.0)
    tail = jnp.where(down == last, 1.0, 0.0)
    keep = jnp.where(segments[2:3] == segments[1:2], 1.0, 0.0)
    quad = jnp.concatenate(
        [jnp.concatenate([strict, strict], 1), jnp.concatenate([closed, closed], 1)], 0
    )
    return quad, carry, tail, keep


def tile_heads(x, heads):
    return jnp.concatenate([x] * heads, 1) if heads > 1 else x


def join(pieces, axis):
    return jnp.concatenate(pieces, axis) if len(pieces) > 1 else pieces[0]


def decayed(decay_low, key_low, dir_low, rate_low, recept_low, carry, tail):
    i, j = iotas(BLOCK, BLOCK)
    lower = jnp.where(i >= j, 1.0, 0.0).astype(BF16)
    log_step = -jnp.exp(decay_low)
    total = sum_left(lower, log_step)
    before = jnp.exp(total - log_step)
    grown = jnp.exp(total)
    shrunk = jnp.exp(-total)
    end = total[BLOCK - 1 : BLOCK]
    tail_decay = jnp.exp(end - total) * tail
    alpha = -dir_low * before
    beta_plain = dir_low * rate_low
    beta = beta_plain * shrunk
    key = key_low * shrunk
    recept = recept_low * grown
    return dict(
        log_step=log_step, before=before, grown=grown, shrunk=shrunk, end=jnp.exp(end), tail=tail_decay,
        alpha=alpha, beta_plain=beta_plain, beta=beta, key=key, recept=recept,
        beta_end=beta_plain * tail_decay, key_end=key_low * tail_decay,
        alpha_in=alpha * carry, recept_in=recept * carry,
    )


def unit_inverses(lowers):
    i, j = iotas(BLOCK, BLOCK)
    eye = jnp.where(i == j, 1.0, 0.0)

    def within(size):
        return (i // size) == (j // size)

    smalls = [jnp.where(within(4), x, 0.0) for x in lowers]
    low_smalls = [x.astype(BF16) for x in smalls]
    twos = [dot(x, x) for x in low_smalls]
    inverses = [eye + x for x in smalls]
    inverses = [x + dot(x.astype(BF16), y.astype(BF16)) for x, y in zip(inverses, twos)]
    for size in (8, 16, 32, 64):
        mask = within(size) & ~within(size // 2)
        offs = [jnp.where(mask, x, 0.0).astype(BF16) for x in lowers]
        lows = [x.astype(BF16) for x in inverses]
        inner = [dot(x, y).astype(BF16) for x, y in zip(offs, lows)]
        inverses = [x + dot(y, z) for x, y, z in zip(inverses, lows, inner)]
    errors = [eye - x + dot3(y, x) for x, y in zip(inverses, lowers)]
    return [x + dot(x.astype(BF16), y.astype(BF16)) for x, y in zip(inverses, errors)]


def post_norm(head_low, ones):
    centered = head_low - head_sum(head_low, ones) * (1.0 / HEAD)
    spread = lax.rsqrt(head_sum(centered * centered, ones) * (1.0 / HEAD) + HEAD * 1e-05)
    return centered * spread, spread


def forward_kernel(
    count, recept_ref, keys_ref, values_ref, hidden_ref, first_ref, up_ref, vec_ref, segment_ref,
    mixed_ref, head_ref, state_ref, inverse_ref, removed_ref, state,
):
    width = recept_ref.shape[1]
    heads = width // HEAD

    @pl.when(pl.program_id(0) == 0)
    def _():
        state[...] = jnp.zeros_like(state)

    ones = head_ones(width)
    vec = vec_ref[...]
    up = up_ref[...]
    columns = [slice(head * HEAD, (head + 1) * HEAD) for head in range(heads)]
    done = []
    for block in range(count):
        rows = slice(block * BLOCK, (block + 1) * BLOCK)
        recept, keys, values = recept_ref[rows], keys_ref[rows], values_ref[rows]
        _, decay_log, rate, _, gate, mixed_value, _, key_dir, key_mod = front(
            keys, values, hidden_ref[rows], up, first_ref[rows].astype(F32), vec, ones
        )
        quad, carry, tail, keep = block_masks(segment_ref[block * 8 : block * 8 + 8])
        parts = decayed(
            low(decay_log), low(key_mod), low(key_dir), low(rate), low(recept),
            tile_heads(carry, heads), tile_heads(tail, heads),
        )
        lefts = [jnp.concatenate([parts["alpha"][:, c], parts["recept"][:, c]], 0) for c in columns]
        rights = [jnp.concatenate([parts["beta"][:, c], parts["key"][:, c]], 0) for c in columns]
        pairs = [quad * dot3(x, y, NT) for x, y in zip(lefts, rights)]
        done.append((rows, recept, key_mod, gate, mixed_value, keep, parts, pairs))
    inverses = unit_inverses([x[:BLOCK, :BLOCK] for item in done for x in item[-1]])
    for block, (rows, recept, key_mod, gate, mixed_value, keep, parts, pairs) in enumerate(done):
        mine = inverses[block * heads : (block + 1) * heads]
        value_low = low(mixed_value)
        owns = [value_low[:, c] for c in columns]
        by_values = [dot3(x[:, BLOCK:], y) for x, y in zip(pairs, owns)]
        ends = [jnp.concatenate([parts["beta_end"][:, c], parts["key_end"][:, c]], 0) for c in columns]
        inners = [jnp.concatenate([parts["alpha_in"][:, c], parts["recept_in"][:, c]], 0) for c in columns]
        entering = state[...]
        state_ref[rows] = entering
        nows = [entering[:, c] for c in columns]
        inwards = [dot3(x, y, NT) for x, y in zip(inners, nows)]
        removals = [dot3(x, y[:BLOCK] + z[:BLOCK]) for x, y, z in zip(mine, inwards, by_values)]
        outs = [
            y[BLOCK:] + z[BLOCK:] + dot3(x[BLOCK:, :BLOCK], r)
            for x, y, z, r in zip(pairs, inwards, by_values, removals)
        ]
        leaving = [
            x * (parts["end"][:, c] * keep) + dot3(jnp.concatenate([r, v], 0), e, TN)
            for x, c, r, v, e in zip(nows, columns, removals, owns, ends)
        ]
        state[...] = join(leaving, 1)
        inverse_ref[rows] = join(mine, 1)
        removed_ref[rows] = join(removals, 1)
        head_low = join(outs, 1).astype(BF16)
        head_ref[rows] = head_low
        normed, _ = post_norm(head_low.astype(F32), ones)
        bonus = head_sum(recept * key_mod * vec[5:6], ones) * mixed_value
        mixed_ref[rows] = ((normed * vec[6:7] + vec[7:8] + bonus) * gate).astype(BF16)


def backward_kernel(
    count, grad_ref, recept_ref, keys_ref, values_ref, hidden_ref, first_ref, up_ref, vec_ref, segment_ref,
    head_ref, state_ref, inverse_ref, removed_ref,
    recept_out, keys_out, values_out, ups_out, first_out, vec_out, state,
):
    width = recept_ref.shape[1]
    heads = width // HEAD

    @pl.when(pl.program_id(0) == 0)
    def _():
        state[...] = jnp.zeros_like(state)
        vec_out[...] = jnp.zeros_like(vec_out)

    ones = head_ones(width)
    vec = vec_ref[...]
    up = up_ref[...]
    i, j = iotas(BLOCK, BLOCK)
    upper = jnp.where(i <= j, 1.0, 0.0).astype(BF16)
    columns = [slice(head * HEAD, (head + 1) * HEAD) for head in range(heads)]
    order = range(count - 1, -1, -1)
    kept = {}
    for block in order:
        rows = slice(block * BLOCK, (block + 1) * BLOCK)
        recept, keys, values = recept_ref[rows], keys_ref[rows], values_ref[rows]
        first = first_ref[rows].astype(F32)
        z, decay_log, rate, blend, gate, mixed_value, scale, key_dir, key_mod = front(
            keys, values, hidden_ref[rows], up, first, vec, ones
        )
        quad, carry, tail, keep = block_masks(segment_ref[block * 8 : block * 8 + 8])
        rate_low, dir_low = low(rate), low(key_dir)
        parts = decayed(
            low(decay_log), low(key_mod), dir_low, rate_low, low(recept),
            tile_heads(carry, heads), tile_heads(tail, heads),
        )
        value_low = low(mixed_value)

        grad = grad_ref[rows].astype(F32)
        normed, spread = post_norm(head_ref[rows].astype(F32), ones)
        product = recept * key_mod
        coefficient = head_sum(product * vec[5:6], ones)
        grad_gate = grad * (normed * vec[6:7] + vec[7:8] + coefficient * mixed_value)
        opened = grad * gate
        grad_normed = opened * vec[6:7]
        grad_head = spread * (
            grad_normed
            - head_sum(grad_normed, ones) * (1.0 / HEAD)
            - normed * (head_sum(grad_normed * normed, ones) * (1.0 / HEAD))
        )
        grad_coefficient = head_sum(opened * mixed_value, ones)
        weighted = grad_coefficient * vec[5:6]
        head_grad = low(grad_head)

        lefts = [jnp.concatenate([parts["alpha"][:, c], parts["recept"][:, c]], 0) for c in columns]
        rights = [jnp.concatenate([parts["beta"][:, c], parts["key"][:, c]], 0) for c in columns]
        ends = [jnp.concatenate([parts["beta_end"][:, c], parts["key_end"][:, c]], 0) for c in columns]
        inners = [jnp.concatenate([parts["alpha_in"][:, c], parts["recept_in"][:, c]], 0) for c in columns]
        pairs = [quad * dot3(x, y, NT) for x, y in zip(lefts, rights)]
        out_grads = [head_grad[:, c] for c in columns]
        through = [dot3(x[BLOCK:, :BLOCK], y, TN) for x, y in zip(pairs, out_grads)]
        kept[block] = dict(
            rows=rows, recept=recept, keys=keys, values=values, first=first, z=z, rate=rate, blend=blend,
            mixed_value=mixed_value, scale=scale, key_dir=key_dir, key_mod=key_mod, quad=quad, carry=carry, keep=keep,
            rate_low=rate_low, dir_low=dir_low, parts=parts, value_low=value_low, normed=normed, product=product,
            grad_gate=grad_gate, opened=opened, grad_coefficient=grad_coefficient,
            grad_mixed_value=opened * coefficient, grad_recept=weighted * key_mod, grad_key_mod=weighted * recept,
            lefts=lefts, rights=rights, ends=ends, inners=inners, pairs=pairs, out_grads=out_grads, through=through,
        )
    for block in order:
        k = kept[block]
        after, entering, inverse_all = state[...], state_ref[k["rows"]], inverse_ref[k["rows"]]
        laters, nows = [after[:, c] for c in columns], [entering[:, c] for c in columns]
        from_ends = [dot3(x, y, NT) for x, y in zip(k["ends"], laters)]
        inner_grads = [
            dot3(inverse_all[:, c], x + y[:BLOCK], TN) for c, x, y in zip(columns, k["through"], from_ends)
        ]
        boths = [jnp.concatenate([x, y], 0) for x, y in zip(inner_grads, k["out_grads"])]
        stays = [x * (k["parts"]["end"][:, c] * k["keep"]) for x, c in zip(laters, columns)]
        state[...] = join([x + dot3(y, z, TN) for x, y, z in zip(stays, boths, k["inners"])], 1)
        k.update(
            laters=laters, nows=nows, from_ends=from_ends, boths=boths,
            end_sum=join([jnp.sum(x * y, 0, keepdims=True) for x, y in zip(nows, stays)], 1),
        )
    vec_total = jnp.zeros_like(vec)
    for block in order:
        k = kept[block]
        rows, parts, quad = k["rows"], k["parts"], k["quad"]
        removed_all = removed_ref[rows]
        carry_two = jnp.concatenate([k["carry"], k["carry"]], 0)
        sources = [jnp.concatenate([removed_all[:, c], k["value_low"][:, c]], 0) for c in columns]
        grad_pairs = [quad * dot3(x, y, NT) for x, y in zip(k["boths"], sources)]
        grad_values = [
            dot3(x[:, BLOCK:], y, TN) + z[BLOCK:] for x, y, z in zip(k["pairs"], k["boths"], k["from_ends"])
        ]
        grad_ends = [dot3(x, y) for x, y in zip(sources, k["laters"])]
        to_state = [carry_two * dot3(x, y) for x, y in zip(k["boths"], k["nows"])]
        grad_lefts = [dot3(x, y) + z for x, y, z in zip(grad_pairs, k["rights"], to_state)]
        grad_rights = [dot3(x, y, TN) for x, y in zip(grad_pairs, k["lefts"])]
        d_alpha, d_recept = join([x[:BLOCK] for x in grad_lefts], 1), join([x[BLOCK:] for x in grad_lefts], 1)
        d_beta, d_key = join([x[:BLOCK] for x in grad_rights], 1), join([x[BLOCK:] for x in grad_rights], 1)
        d_beta_end, d_key_end = join([x[:BLOCK] for x in grad_ends], 1), join([x[BLOCK:] for x in grad_ends], 1)
        ended = parts["beta_end"] * d_beta_end + parts["key_end"] * d_key_end
        alphas = parts["alpha"] * d_alpha
        d_total = parts["recept"] * d_recept - parts["beta"] * d_beta - parts["key"] * d_key - ended + alphas
        d_step = sum_left(upper, d_total) + (jnp.sum(ended, 0, keepdims=True) + k["end_sum"]) - alphas
        d_beta_plain = d_beta * parts["shrunk"] + d_beta_end * parts["tail"]
        copy_decay = low(d_step * parts["log_step"])
        copy_dir = low(d_beta_plain * k["rate_low"] - d_alpha * parts["before"])
        copy_rate = low(d_beta_plain * k["dir_low"])

        keys, values, rate, blend = k["keys"], k["values"], k["rate"], k["blend"]
        grad_recept = k["grad_recept"] + low(d_recept * parts["grown"])
        grad_key_mod = k["grad_key_mod"] + low(d_key * parts["shrunk"] + d_key_end * parts["tail"])
        grad_mixed_value = k["grad_mixed_value"] + low(join(grad_values, 1))
        grad_z = copy_decay * jax.nn.sigmoid(-k["z"])
        factor = 1.0 + (rate - 1.0) * vec[4:5]
        keyed = grad_key_mod * keys
        grad_rate = copy_rate + keyed * vec[4:5]
        grad_scaled = k["scale"] * (copy_dir - k["key_dir"] * head_sum(copy_dir * k["key_dir"], ones))
        grad_keys = grad_key_mod * factor + grad_scaled * vec[3:4]
        grad_rate_up = grad_rate * rate * (1.0 - rate)
        grad_value_up = grad_mixed_value * (k["first"] - values) * blend * (1.0 - blend)
        recept_out[rows] = grad_recept.astype(BF16)
        keys_out[rows] = grad_keys.astype(BF16)
        values_out[rows] = (grad_mixed_value * (1.0 - blend)).astype(BF16)
        first_out[rows] = (grad_mixed_value * blend).astype(BF16)
        ups_out[0, rows] = grad_z.astype(BF16)
        ups_out[1, rows] = grad_rate_up.astype(BF16)
        ups_out[2, rows] = grad_value_up.astype(BF16)
        ups_out[3, rows] = k["grad_gate"].astype(BF16)

        def total(x):
            return jnp.sum(x, 0, keepdims=True)

        vec_total = vec_total + jnp.concatenate(
            [
                total(grad_z), total(grad_rate_up), total(grad_value_up), total(grad_scaled * keys),
                total(keyed * (rate - 1.0)), total(k["grad_coefficient"] * k["product"]),
                total(k["opened"] * k["normed"]), total(k["opened"]),
            ],
            0,
        )
    vec_out[...] += vec_total


def per_step(rows, most):
    return most if (rows // BLOCK) % most == 0 else 1


def run_forward(recept, keys, values, hidden, first, up, vec, segments):
    rows, width = recept.shape
    count = per_step(rows, 4)
    step = count * BLOCK

    def spec(columns):
        return pl.BlockSpec((step, columns), lambda i: (i, 0))

    def whole(array):
        return pl.BlockSpec(array.shape, lambda i: (0, 0))

    return pl.pallas_call(
        functools.partial(forward_kernel, count),
        grid=(rows // step,),
        in_specs=[
            spec(width), spec(width), spec(width), spec(WIDE), spec(width), whole(up), whole(vec),
            pl.BlockSpec((count * 8, BLOCK), lambda i: (i, 0)),
        ],
        out_specs=[spec(width)] * 5,
        out_shape=[jax.ShapeDtypeStruct((rows, width), d) for d in (BF16, BF16, F32, F32, F32)],
        scratch_shapes=[pltpu.VMEM((BLOCK, width), F32)],
        compiler_params=pltpu.CompilerParams(vmem_limit_bytes=48 << 20),
        name="mix_forward",
    )(recept, keys, values, hidden, first, up, vec, segments)


def run_backward(grad, recept, keys, values, hidden, first, up, vec, segments, saved):
    rows, width = recept.shape
    count = per_step(rows, 2)
    step = count * BLOCK
    last = rows // step - 1

    def spec(columns):
        return pl.BlockSpec((step, columns), lambda i: (last - i, 0))

    def whole(array):
        return pl.BlockSpec(array.shape, lambda i: (0, 0))

    return pl.pallas_call(
        functools.partial(backward_kernel, count),
        grid=(rows // step,),
        in_specs=[
            spec(width), spec(width), spec(width), spec(width), spec(WIDE), spec(width), whole(up), whole(vec),
            pl.BlockSpec((count * 8, BLOCK), lambda i: (last - i, 0)),
            spec(width), spec(width), spec(width), spec(width),
        ],
        out_specs=[
            spec(width), spec(width), spec(width),
            pl.BlockSpec((4, step, width), lambda i: (0, last - i, 0)),
            spec(width), pl.BlockSpec((8, width), lambda i: (0, 0)),
        ],
        out_shape=[
            jax.ShapeDtypeStruct((rows, width), BF16), jax.ShapeDtypeStruct((rows, width), BF16),
            jax.ShapeDtypeStruct((rows, width), BF16), jax.ShapeDtypeStruct((4, rows, width), BF16),
            jax.ShapeDtypeStruct((rows, width), BF16), jax.ShapeDtypeStruct((8, width), F32),
        ],
        scratch_shapes=[pltpu.VMEM((BLOCK, width), F32)],
        compiler_params=pltpu.CompilerParams(vmem_limit_bytes=48 << 20),
        name="mix_backward",
    )(grad, recept, keys, values, hidden, first, up, vec, segments, *saved)


def mix_norm(block_ref, stats_ref, vec_ref):
    stats = stats_ref[...]
    flowing = stats[:, 2:3]
    standard = (block_ref[...].astype(F32) - stats[:, 0:1]) * stats[:, 1:2]
    normed = standard * vec_ref[0:1] + vec_ref[1:2]
    delta = pltpu.roll(normed, 1, 0) * flowing - normed
    return standard, normed, delta, flowing


def project_kernel(
    width, number_ref, block_ref, stats_ref, vec_ref, weight_ref,
    recept_ref, keys_ref, values_ref, downs_ref, hidden_ref,
):
    base = 3 * width
    _, normed, delta, _ = mix_norm(block_ref, stats_ref, vec_ref)
    weight = weight_ref[...]
    uses = (
        ((recept_ref, 0, width, 0),),
        ((downs_ref, base + OFFSETS[0], PADDED[0], OFFSETS[0]),),
        ((keys_ref, width, width, 0),),
        ((values_ref, 2 * width, width, 0), (downs_ref, base + OFFSETS[2], PADDED[2], OFFSETS[2])),
        ((downs_ref, base + OFFSETS[1], PADDED[1], OFFSETS[1]),),
        ((downs_ref, base + OFFSETS[3], PADDED[3], OFFSETS[3]),),
    )

    @pl.when(pl.program_id(0) == 0)
    def _():
        for ref in (recept_ref, keys_ref, values_ref, downs_ref):
            ref[...] = jnp.zeros_like(ref)

    for c, targets in enumerate(uses):
        mixed = (normed + delta * vec_ref[2 + c : 3 + c]).astype(BF16)
        for ref, start, size, at in targets:
            ref[:, at : at + size] += dot(mixed, weight[:, start : start + size])

    @pl.when(pl.program_id(0) == pl.num_programs(0) - 1)
    def _():
        hidden_ref[:, 0:128] = jnp.tanh(downs_ref[:, 0:128]).astype(BF16)
        hidden_ref[:, 128:384] = downs_ref[:, 128:384].astype(BF16)
        hidden_ref[:, 384:640] = jax.nn.sigmoid(downs_ref[:, 384:640]).astype(BF16)


def unproject_kernel(
    width, parts, piece, number_ref, block_ref, stats_ref, vec_ref, weight_ref,
    recept_ref, keys_ref, values_ref, ups_ref, hidden_ref, downs_ref, up_ref,
    grad_ref, sums_ref, vec_out, wide_ref, up_out, down_lows,
):
    rows = block_ref.shape[0]
    base = 3 * width

    @pl.when(pl.program_id(0) == 0)
    def _():
        sums_ref[...] = jnp.zeros_like(sums_ref)
        for k, (at, size) in enumerate(zip(OFFSETS, PADDED)):
            cols = slice(at, at + size)
            grad = dot(ups_ref[k], up_ref[cols], NT)
            if k == 0:
                grad = grad * (1.0 - jnp.square(jnp.tanh(downs_ref[:, cols])))
            if k == 3:
                opening = jax.nn.sigmoid(downs_ref[:, cols])
                grad = grad * opening * (1.0 - opening)
            down_lows[:, cols] = grad.astype(BF16)
            up_out[:, cols] = dot(ups_ref[k], hidden_ref[:, cols], TN).astype(BF16)

    standard, normed, delta, flowing = mix_norm(block_ref, stats_ref, vec_ref)
    weight = weight_ref[...]

    def down(k):
        return (down_lows[:, OFFSETS[k] : OFFSETS[k] + PADDED[k]], base + OFFSETS[k], PADDED[k])

    uses = (
        ((recept_ref[...], 0, width),),
        (down(0),),
        ((keys_ref[...], width, width),),
        ((values_ref[...], 2 * width, width), down(2)),
        (down(1),),
        (down(3),),
    )
    kept, sent, vec_rows = None, None, []
    per_seq = parts * piece
    for c, sources in enumerate(uses):
        share = vec_ref[2 + c : 3 + c]
        mixed = (normed + delta * share).astype(BF16)
        grad = None
        for source, start, size in sources:
            part = dot(source, weight[:, start : start + size], NT)
            grad = part if grad is None else grad + part
            product = dot(mixed, source, TN).astype(BF16)
            for number in range(product.shape[0] // per_seq):
                for w in range(parts):
                    at = number * per_seq + w * piece
                    wide_ref[w, number, :, start : start + size] = product[at : at + piece]
        vec_rows.append(jnp.sum(grad * delta, 0, keepdims=True))
        moved = grad * share
        kept = grad - moved if kept is None else kept + (grad - moved)
        sent = moved if sent is None else sent + moved
    grad = kept + pltpu.roll(sent * flowing, rows - 1, 0)
    vec_out[...] = jnp.concatenate(
        [jnp.sum(grad * standard, 0, keepdims=True), jnp.sum(grad, 0, keepdims=True)] + vec_rows, 0
    )
    scaled = grad * vec_ref[0:1]
    sums_ref[:, 0:1] += jnp.sum(scaled, 1, keepdims=True)
    sums_ref[:, 1:2] += jnp.sum(scaled * standard, 1, keepdims=True)
    grad_ref[...] = scaled


def mix_specs(rows, width, own_width, parts):
    block = 256 if rows <= 1024 else 128
    per_shard = width // parts // block

    def columns(height):
        return pl.BlockSpec((height, block), lambda j, n: (0, j))

    def whole(shape):
        return pl.BlockSpec(shape, lambda j, n: (0,) * len(shape))

    def weights(array):
        size = array.shape[1] if rows > 1024 else 3 * own_width + WIDE
        return pl.BlockSpec((block, size), lambda j, n: (((j // per_shard) ^ n[0]) * per_shard + j % per_shard, 0))

    return block, columns, whole, weights


def run_project(number, balanced, stats, vec, weights, own_width, parts):
    rows, width = balanced.shape
    block, columns, whole, weight_spec = mix_specs(rows, width, own_width, parts)
    shapes = [(rows, own_width)] * 3 + [(rows, WIDE)] * 2
    return pl.pallas_call(
        functools.partial(project_kernel, own_width),
        grid_spec=pltpu.PrefetchScalarGridSpec(
            num_scalar_prefetch=1,
            grid=(width // block,),
            in_specs=[columns(rows), whole(stats.shape), columns(8), weight_spec(weights)],
            out_specs=[whole(s) for s in shapes],
        ),
        out_shape=[jax.ShapeDtypeStruct(s, d) for s, d in zip(shapes, (F32, F32, F32, F32, BF16))],
        compiler_params=pltpu.CompilerParams(vmem_limit_bytes=60 << 20),
        name="mix_project",
    )(number, balanced, stats, vec, weights)


def run_unproject(number, balanced, stats, vec, weights, lows, ups, hidden, downs, up, parts):
    rows, width = balanced.shape
    own_width = lows[0].shape[1]
    seqs = width // own_width
    piece = own_width // parts
    block, columns, whole, weight_spec = mix_specs(rows, width, own_width, parts)
    taken = block // own_width
    total = 3 * own_width + WIDE
    return pl.pallas_call(
        functools.partial(unproject_kernel, own_width, parts, piece),
        grid_spec=pltpu.PrefetchScalarGridSpec(
            num_scalar_prefetch=1,
            grid=(width // block,),
            in_specs=[columns(rows), whole(stats.shape), columns(8), weight_spec(weights)]
            + [whole(a.shape) for a in (*lows, ups, hidden, downs, up)],
            out_specs=[
                columns(rows), whole((rows, 2)), columns(8),
                pl.BlockSpec((parts, taken, piece, total), lambda j, n: (0, j, 0, 0)),
                whole((own_width, WIDE)),
            ],
            scratch_shapes=[pltpu.VMEM((rows, WIDE), BF16)],
        ),
        out_shape=[
            jax.ShapeDtypeStruct((rows, width), F32), jax.ShapeDtypeStruct((rows, 2), F32),
            jax.ShapeDtypeStruct((8, width), F32), jax.ShapeDtypeStruct((parts, seqs, piece, total), BF16),
            jax.ShapeDtypeStruct((own_width, WIDE), BF16),
        ],
        compiler_params=pltpu.CompilerParams(vmem_limit_bytes=60 << 20),
        name="mix_unproject",
    )(number, balanced, stats, vec, weights, *lows, ups, hidden, downs, up)


def norm_stats(values):
    centered = values - jnp.mean(values, -1, keepdims=True)
    scale = lax.rsqrt(jnp.mean(centered * centered, -1, keepdims=True) + 1e-05)
    return centered * scale, scale


def norm_back(grad, standard, scale, gain):
    scaled = grad * gain
    return scale * (
        scaled
        - jnp.mean(scaled, -1, keepdims=True)
        - standard * jnp.mean(scaled * standard, -1, keepdims=True)
    )


def pad_ranks(matrix):
    pieces, start = [], 0
    for rank, padded in zip(RANKS, PADDED):
        pieces.append(jnp.pad(matrix[:, start : start + rank], ((0, 0), (0, padded - rank))))
        start += rank
    return jnp.concatenate(pieces, 1)


def unpad_ranks(matrix):
    return jnp.concatenate([matrix[..., o : o + r] for o, r in zip(OFFSETS, RANKS)], -1)


def from_behind(x, axis, by):
    size = lax.axis_size(axis)
    pairs = [(i, i + by) for i in range(size) if 0 <= i + by < size]
    return lax.ppermute(x, axis, pairs)


def exchange(x, axis):
    return lax.all_to_all(x, axis, split_axis=0, concat_axis=0, tiled=True)


def swap(x, by):
    size = lax.axis_size("wsh")
    return lax.ppermute(x, "wsh", [(i, i ^ by) for i in range(size)])


def gather_near(x):
    if lax.axis_size("wsh") != 4:
        return lax.all_gather(x, "wsh", axis=0, tiled=True)
    across = swap(x, 2)
    beside = swap(x, 1)
    return jnp.concatenate([x, beside, across, swap(across, 1)], 0)


def scalar_sum(x):
    if lax.axis_size("wsh") != 4:
        return jnp.sum(lax.all_gather(x.reshape(1), "wsh", axis=0, tiled=True))
    x = jnp.full((8, 128), x)
    x = x + swap(x, 1)
    return (x + swap(x, 2))[0, 0]


def near_sum(x):
    if lax.axis_size("wsh") != 4:
        return lax.psum_scatter(x, "wsh", scatter_dimension=0, tiled=True)
    rows = x.shape[0] // 4
    beside = swap(jnp.concatenate([x[rows : 2 * rows], x[3 * rows :]], 0), 1)
    far = x[2 * rows : 3 * rows] + beside[rows:]
    return x[:rows] + beside[:rows] + swap(far.astype(BF16), 2).astype(F32)


def block_sum(x):
    if lax.axis_size("wsh") != 4:
        return lax.psum_scatter(x, "wsh", scatter_dimension=0, tiled=False).astype(F32)
    number = lax.axis_index("wsh")

    def block(by):
        return lax.dynamic_index_in_dim(x, number ^ by, 0, keepdims=False)

    beside = swap(jnp.stack([block(1), block(3)]), 1).astype(F32)
    far = block(2).astype(F32) + beside[1]
    return block(0).astype(F32) + beside[0] + swap(far.astype(BF16), 2).astype(F32)


def local(
    tokens, first_layer_values, teacher, valid, destination, lengths,
    receptance_matrix, key_matrix, value_matrix, output_matrix,
    lowrank_down_weight, lowrank_up_weight, channel_key_weight, channel_value_weight, vectors,
):
    rows, width = tokens.shape
    seqs, parts = lax.axis_size("seq"), lax.axis_size("wsh")
    me = lax.axis_index("seq")
    group = rows * seqs
    own_width = width // seqs
    shard = width // parts
    piece = shard // seqs
    column = me * own_width

    dest_seq = destination // rows // parts
    position = dest_seq * rows + destination % rows
    digits = jnp.stack([position // DIGIT, position % DIGIT, valid], 1).astype(BF16)
    tail = jnp.pad(digits, ((0, 0), (0, EXTRA - 3)))
    given = lax.all_gather(jnp.concatenate([tokens, tail], 1), "seq", axis=0, tiled=True)
    info = given[:, width : width + 3].astype(F32)
    places = (info[:, 0] * DIGIT + info[:, 1]).astype(jnp.int32)
    numbers = jnp.arange(group, dtype=jnp.int32)
    permute = (numbers[:, None] == places[None, :]).astype(BF16)
    total_valid = scalar_sum(jnp.sum(info[:, 2]))

    index = jnp.arange(rows, dtype=jnp.int32)
    same_dest = (dest_seq[:, None] == dest_seq[None, :]) & (index[None, :] < index[:, None])
    slot = dest_seq * (rows // seqs) + jnp.sum(same_dest.astype(jnp.int32), 1)
    arrange = (index[:, None] == slot[None, :]).astype(BF16)
    mine = (places // rows) == me
    arrival = jnp.cumsum(mine.astype(jnp.int32)) - 1
    own_rows = ((index[:, None] + me * rows) == places[None, :]).astype(BF16)
    settle = dot(own_rows, (mine[:, None] & (arrival[:, None] == index[None, :])).astype(BF16)).astype(BF16)

    def deal(array):
        moved = exchange(dot(arrange, array).astype(BF16).reshape(seqs, rows // seqs, width), "seq")
        return dot(settle, moved.reshape(rows, width))

    def undeal(array):
        back = dot(settle, array.astype(BF16), TN).astype(BF16)
        moved = exchange(back.reshape(seqs, rows // seqs, width), "seq")
        return dot(arrange, moved.reshape(rows, width), TN).astype(BF16)

    target = deal(teacher)
    first_given = exchange(
        first_layer_values.reshape(rows, seqs, own_width).transpose(1, 0, 2), "seq"
    ).reshape(group, own_width)
    first = dot(permute, first_given).astype(BF16)

    offsets = jnp.cumsum(lengths[0]) - lengths[0]
    starts = jnp.any(numbers[:, None] == offsets[None, :], 1).astype(F32)
    segment_ids = jnp.cumsum(starts).reshape(-1, BLOCK)
    before = segment_ids[:, :1] - starts.reshape(-1, BLOCK)[:, :1]
    segments = jnp.stack(
        [segment_ids, jnp.broadcast_to(before, segment_ids.shape), jnp.broadcast_to(segment_ids[:, -1:], segment_ids.shape)]
        + [jnp.zeros_like(segment_ids)] * 5,
        1,
    ).reshape(-1, BLOCK)
    flowing = (1.0 - starts)[:, None]

    def own_columns(matrix):
        return lax.dynamic_slice_in_dim(matrix, column, own_width, 1)

    near = parts == 4
    number = lax.axis_index("wsh") if near else 0
    up_piece = lax.dynamic_slice_in_dim(lowrank_up_weight, column % shard, own_width, 0)
    total = 3 * own_width + WIDE
    weights = gather_near(
        jnp.concatenate(
            [
                own_columns(receptance_matrix), own_columns(key_matrix), own_columns(value_matrix),
                pad_ranks(lowrank_down_weight), up_piece.reshape(shard, -1),
            ],
            1,
        )
    )
    up = pad_ranks(
        lax.dynamic_slice(
            weights, (((column // shard) ^ number) * shard, total), (shard, weights.shape[1] - total)
        ).reshape(own_width, -1)
    ).T
    number = jnp.full((1,), number, jnp.int32)
    w_out = lax.all_gather(output_matrix, "wsh", axis=0, tiled=True)
    vec = lax.dynamic_slice_in_dim(vectors, column, own_width, 0)[:, 8:16].T

    balanced = dot(permute, given[:, :width]).astype(BF16)
    wide_rows = balanced.astype(F32)
    mean = jnp.mean(wide_rows, -1, keepdims=True)
    scale_one = lax.rsqrt(jnp.mean(jnp.square(wide_rows - mean), -1, keepdims=True) + 1e-05)
    stats = jnp.concatenate([mean, scale_one, flowing, flowing], 1)
    mix_vec = vectors[:, :8].T
    recept, keys, values, downs, hidden = run_project(number, balanced, stats, mix_vec, weights, own_width, parts)
    inputs = (recept, keys, values, hidden, first, up, vec, segments)
    mixed_out, *saved = run_forward(*inputs)

    mixed_rows = exchange(mixed_out.reshape(seqs, rows, own_width), "seq").transpose(1, 0, 2).reshape(rows, width)
    own = lax.dynamic_slice_in_dim(balanced, me * rows, rows, 0).astype(F32)
    own_starts = lax.dynamic_slice_in_dim(starts, me * rows, rows, 0)
    own_flowing = (1.0 - own_starts)[:, None]
    own_valid = dot(own_rows, given[:, width : width + EXTRA])[:, 2]
    residual = own + dot(mixed_rows, w_out)
    standard_two, scale_two = norm_stats(residual)
    normed_two = standard_two * vectors[:, 16] + vectors[:, 17]
    carried_two = from_behind(normed_two[-1:], "seq", 1)
    delta_two = jnp.concatenate([carried_two, normed_two[:-1]], 0) * own_flowing - normed_two
    channel = gather_near((normed_two + delta_two * vectors[:, 18]).astype(BF16))
    active = jax.nn.relu(dot(channel, channel_key_weight, NT))
    hidden_rows = jnp.square(active).astype(BF16)
    result = residual + near_sum(dot(hidden_rows, channel_value_weight))
    total_tokens = group * parts
    cotangent = (result - target) * (own_valid * (total_tokens / total_valid))[:, None]
    cot = gather_near(cotangent.astype(BF16))

    blocks = [(s * parts + w, w * seqs + s) for s in range(seqs) for w in range(parts)]

    def ffn_grad(part):
        part = lax.psum_scatter(part, "seq", scatter_dimension=0, tiled=True)
        return lax.ppermute(part, ("seq", "wsh"), blocks).astype(F32)

    value_part, cot = lax.optimization_barrier((dot(hidden_rows, cot, TN).astype(BF16), cot))
    grad_ffn_value = ffn_grad(value_part)
    grad_pre = (dot(cot, channel_value_weight, NT) * 2.0 * active).astype(BF16)
    channel_part = dot(grad_pre, channel_key_weight)
    key_part, grad_channel = lax.optimization_barrier((dot(grad_pre, channel, TN).astype(BF16), near_sum(channel_part)))
    grad_ffn_key = ffn_grad(key_part)
    grad_vec_mix_two = jnp.sum(grad_channel * delta_two, 0)
    shifted = grad_channel * vectors[:, 18] * own_flowing
    behind = from_behind(shifted[:1], "seq", -1)
    grad_normed_two = grad_channel * (1.0 - vectors[:, 18]) + jnp.concatenate([shifted[1:], behind], 0)
    grad_residual = cotangent + norm_back(grad_normed_two, standard_two, scale_two, vectors[:, 16])
    grad_low = grad_residual.astype(BF16)

    lefts = exchange(mixed_rows.reshape(rows, seqs, parts, piece).transpose(2, 0, 1, 3), "wsh")
    if near:
        lefts = jnp.stack([lax.dynamic_index_in_dim(lefts, number[0] ^ k, 0, keepdims=False) for k in range(4)])
    out_part = dot(lefts.reshape(rows * parts, -1), gather_near(grad_low), TN).astype(BF16)
    grad_out = lax.psum_scatter(out_part, "seq", scatter_dimension=0, tiled=True).astype(F32)

    grad_posted = dot(grad_low, w_out, NT).astype(BF16)
    grad_heads = exchange(grad_posted.reshape(rows, seqs, own_width).transpose(1, 0, 2), "seq").reshape(group, own_width)
    recept_low, keys_low, values_low, ups_low, grad_first, grad_vec_heads = run_backward(grad_heads, *inputs, saved)
    scaled_grad, sums, vec_mix, wide, up_grad = run_unproject(
        number, balanced, stats, mix_vec, weights, (recept_low, keys_low, values_low), ups_low, hidden, downs, up, parts
    )
    standard = (balanced.astype(F32) - mean) * scale_one
    grad_balanced = scale_one * (scaled_grad - sums[:, :1] * (1.0 / width) - standard * (sums[:, 1:] * (1.0 / width)))
    mine_rows = lax.dynamic_slice_in_dim(grad_balanced, me * rows, rows, 0) + grad_residual
    grad_balanced = lax.dynamic_update_slice_in_dim(grad_balanced, mine_rows, me * rows, 0)
    grad_given = dot(permute, grad_balanced.astype(BF16), TN).astype(BF16)
    grad_tokens = jnp.sum(exchange(grad_given.reshape(seqs, rows, width), "seq").astype(F32), 0).astype(BF16)
    first_back = exchange(dot(permute, grad_first, TN).astype(BF16).reshape(seqs, rows, own_width), "seq")
    grad_first_rows = first_back.transpose(1, 0, 2).reshape(rows, width)

    wide_all = exchange(block_sum(wide).astype(BF16), "seq").astype(F32)

    def square(at):
        taken = wide_all[:, :, at * own_width : (at + 1) * own_width]
        return taken.transpose(1, 0, 2).reshape(piece, width)

    grad_down = unpad_ranks(jnp.sum(wide_all[:, :, 3 * own_width :], 0))
    up_part = unpad_ranks(block_sum(up_grad.reshape(parts, piece, WIDE)))

    heads_part = lax.dynamic_update_slice_in_dim(jnp.zeros((width, 8), F32), grad_vec_heads.T, column, 0)
    grad_vectors = jnp.concatenate(
        [
            vec_mix.T,
            heads_part,
            jnp.stack([jnp.sum(grad_normed_two * standard_two, 0), jnp.sum(grad_normed_two, 0), grad_vec_mix_two], 1),
        ],
        1,
    )
    vec_part = jnp.sum(exchange(grad_vectors.reshape(seqs, parts * piece, -1), "seq"), 0)
    vec_part = jnp.sum(exchange(vec_part.reshape(parts, piece, -1), "wsh"), 0)
    return (
        undeal(result), grad_tokens, grad_first_rows,
        square(0), square(1), square(2),
        grad_out, grad_down, up_part,
        grad_ffn_key, grad_ffn_value, vec_part,
    )


def solution(mesh):
    both, shard = P(("seq", "wsh"), None), P("wsh", None)
    flat = P(("seq", "wsh"))
    return jax.shard_map(
        local,
        mesh=mesh,
        in_specs=(both, both, both, flat, flat) + (shard,) * 9 + (P(),),
        out_specs=(both,) * 12,
        check_vma=False,
    )
```

```python
import functools

import jax
import jax.numpy as jnp
from jax import lax
from jax.experimental import pallas as pl
from jax.experimental.pallas import tpu as pltpu
from jax.sharding import PartitionSpec as P

HEAD = 64
BLOCK = 64
RANKS = (96, 96, 64, 256)
PADDED = (128, 128, 128, 256)
OFFSETS = (0, 128, 256, 384)
WIDE = 640
EXTRA = 128
DIGIT = 64

F32 = jnp.float32
BF16 = jnp.bfloat16

NN = (((1,), (0,)), ((), ()))
NT = (((1,), (1,)), ((), ()))
TN = (((0,), (0,)), ((), ()))


def dot(a, b, dims=NN):
    return lax.dot_general(a, b, dims, preferred_element_type=F32)


def halves(x):
    high = x.astype(BF16)
    return high, (x - high.astype(F32)).astype(BF16)


def dot3(a, b, dims=NN):
    a_high, a_low = halves(a)
    b_high, b_low = halves(b)
    return dot(a_high, b_high, dims) + (dot(a_high, b_low, dims) + dot(a_low, b_high, dims))


def sum_left(mask, x):
    high, low = halves(x)
    low_two = (x - high.astype(F32) - low.astype(F32)).astype(BF16)
    return dot(mask, high) + (dot(mask, low) + dot(mask, low_two))


def head_sum(x, ones):
    high, low = halves(x)
    return dot(high, ones) + dot(low, ones)


def low(x):
    return x.astype(BF16).astype(F32)


def iotas(rows, columns):
    return (
        lax.broadcasted_iota(jnp.int32, (rows, columns), 0),
        lax.broadcasted_iota(jnp.int32, (rows, columns), 1),
    )


def head_ones(width):
    i, j = iotas(width, width)
    return jnp.where((i >> 6) == (j >> 6), 1.0, 0.0).astype(BF16)


def front(keys, values, hidden, up, first, vec, ones):
    z = vec[0:1] + dot(hidden[:, 0:128], up[0:128])
    decay_log = -(jnp.maximum(-z, 0.0) + jnp.log1p(jnp.exp(-jnp.abs(z)))) - 0.5
    rate = jax.nn.sigmoid(vec[1:2] + dot(hidden[:, 128:256], up[128:256]))
    blend = jax.nn.sigmoid(vec[2:3] + dot(hidden[:, 256:384], up[256:384]))
    gate = dot(hidden[:, 384:640], up[384:640])
    mixed_value = values + (first - values) * blend
    scaled = keys * vec[3:4]
    scale = lax.rsqrt(head_sum(scaled * scaled, ones) + 1e-06)
    key_dir = scaled * scale
    key_mod = keys * (1.0 + (rate - 1.0) * vec[4:5])
    return z, decay_log, rate, blend, gate, mixed_value, scale, key_dir, key_mod


def block_masks(segments):
    i, j = iotas(BLOCK, BLOCK)
    across = jnp.broadcast_to(segments[0:1], (BLOCK, BLOCK))
    down = across.T
    before = jnp.broadcast_to(segments[1:2], (BLOCK, BLOCK))
    last = jnp.broadcast_to(segments[2:3], (BLOCK, BLOCK))
    same = across == down
    strict = jnp.where(same & (i > j), 1.0, 0.0)
    closed = jnp.where(same & (i >= j), 1.0, 0.0)
    carry = jnp.where(down == before, 1.0, 0.0)
    tail = jnp.where(down == last, 1.0, 0.0)
    keep = jnp.where(segments[2:3] == segments[1:2], 1.0, 0.0)
    quad = jnp.concatenate(
        [jnp.concatenate([strict, strict], 1), jnp.concatenate([closed, closed], 1)], 0
    )
    return quad, carry, tail, keep


def tile_heads(x, heads):
    return jnp.concatenate([x] * heads, 1) if heads > 1 else x


def join(pieces, axis):
    return jnp.concatenate(pieces, axis) if len(pieces) > 1 else pieces[0]


def decayed(decay_low, key_low, dir_low, rate_low, recept_low, carry, tail):
    i, j = iotas(BLOCK, BLOCK)
    lower = jnp.where(i >= j, 1.0, 0.0).astype(BF16)
    log_step = -jnp.exp(decay_low)
    total = sum_left(lower, log_step)
    before = jnp.exp(total - log_step)
    grown = jnp.exp(total)
    shrunk = jnp.exp(-total)
    end = total[BLOCK - 1 : BLOCK]
    tail_decay = jnp.exp(end - total) * tail
    alpha = -dir_low * before
    beta_plain = dir_low * rate_low
    beta = beta_plain * shrunk
    key = key_low * shrunk
    recept = recept_low * grown
    return dict(
        log_step=log_step, before=before, grown=grown, shrunk=shrunk, end=jnp.exp(end), tail=tail_decay,
        alpha=alpha, beta_plain=beta_plain, beta=beta, key=key, recept=recept,
        beta_end=beta_plain * tail_decay, key_end=key_low * tail_decay,
        alpha_in=alpha * carry, recept_in=recept * carry,
    )


def unit_inverses(lowers):
    i, j = iotas(BLOCK, BLOCK)
    eye = jnp.where(i == j, 1.0, 0.0)

    def within(size):
        return (i // size) == (j // size)

    smalls = [jnp.where(within(4), x, 0.0) for x in lowers]
    low_smalls = [x.astype(BF16) for x in smalls]
    twos = [dot(x, x) for x in low_smalls]
    inverses = [eye + x for x in smalls]
    inverses = [x + dot(x.astype(BF16), y.astype(BF16)) for x, y in zip(inverses, twos)]
    for size in (8, 16, 32, 64):
        mask = within(size) & ~within(size // 2)
        offs = [jnp.where(mask, x, 0.0).astype(BF16) for x in lowers]
        lows = [x.astype(BF16) for x in inverses]
        inner = [dot(x, y).astype(BF16) for x, y in zip(offs, lows)]
        inverses = [x + dot(y, z) for x, y, z in zip(inverses, lows, inner)]
    errors = [eye - x + dot3(y, x) for x, y in zip(inverses, lowers)]
    return [x + dot(x.astype(BF16), y.astype(BF16)) for x, y in zip(inverses, errors)]


def post_norm(head_low, ones):
    centered = head_low - head_sum(head_low, ones) * (1.0 / HEAD)
    spread = lax.rsqrt(head_sum(centered * centered, ones) * (1.0 / HEAD) + HEAD * 1e-05)
    return centered * spread, spread


def forward_kernel(
    count, recept_ref, keys_ref, values_ref, hidden_ref, first_ref, up_ref, vec_ref, segment_ref,
    mixed_ref, head_ref, state_ref, inverse_ref, removed_ref, state,
):
    width = recept_ref.shape[1]
    heads = width // HEAD

    @pl.when(pl.program_id(0) == 0)
    def _():
        state[...] = jnp.zeros_like(state)

    ones = head_ones(width)
    vec = vec_ref[...]
    up = up_ref[...]
    columns = [slice(head * HEAD, (head + 1) * HEAD) for head in range(heads)]
    done = []
    for block in range(count):
        rows = slice(block * BLOCK, (block + 1) * BLOCK)
        recept, keys, values = recept_ref[rows], keys_ref[rows], values_ref[rows]
        _, decay_log, rate, _, gate, mixed_value, _, key_dir, key_mod = front(
            keys, values, hidden_ref[rows], up, first_ref[rows].astype(F32), vec, ones
        )
        quad, carry, tail, keep = block_masks(segment_ref[block * 8 : block * 8 + 8])
        parts = decayed(
            low(decay_log), low(key_mod), low(key_dir), low(rate), low(recept),
            tile_heads(carry, heads), tile_heads(tail, heads),
        )
        lefts = [jnp.concatenate([parts["alpha"][:, c], parts["recept"][:, c]], 0) for c in columns]
        rights = [jnp.concatenate([parts["beta"][:, c], parts["key"][:, c]], 0) for c in columns]
        pairs = [quad * dot3(x, y, NT) for x, y in zip(lefts, rights)]
        done.append((rows, recept, key_mod, gate, mixed_value, keep, parts, pairs))
    inverses = unit_inverses([x[:BLOCK, :BLOCK] for item in done for x in item[-1]])
    for block, (rows, recept, key_mod, gate, mixed_value, keep, parts, pairs) in enumerate(done):
        mine = inverses[block * heads : (block + 1) * heads]
        value_low = low(mixed_value)
        owns = [value_low[:, c] for c in columns]
        by_values = [dot3(x[:, BLOCK:], y) for x, y in zip(pairs, owns)]
        ends = [jnp.concatenate([parts["beta_end"][:, c], parts["key_end"][:, c]], 0) for c in columns]
        inners = [jnp.concatenate([parts["alpha_in"][:, c], parts["recept_in"][:, c]], 0) for c in columns]
        entering = state[...]
        state_ref[rows] = entering
        nows = [entering[:, c] for c in columns]
        inwards = [dot3(x, y, NT) for x, y in zip(inners, nows)]
        removals = [dot3(x, y[:BLOCK] + z[:BLOCK]) for x, y, z in zip(mine, inwards, by_values)]
        outs = [
            y[BLOCK:] + z[BLOCK:] + dot3(x[BLOCK:, :BLOCK], r)
            for x, y, z, r in zip(pairs, inwards, by_values, removals)
        ]
        leaving = [
            x * (parts["end"][:, c] * keep) + dot3(jnp.concatenate([r, v], 0), e, TN)
            for x, c, r, v, e in zip(nows, columns, removals, owns, ends)
        ]
        state[...] = join(leaving, 1)
        inverse_ref[rows] = join(mine, 1)
        removed_ref[rows] = join(removals, 1)
        head_low = join(outs, 1).astype(BF16)
        head_ref[rows] = head_low
        normed, _ = post_norm(head_low.astype(F32), ones)
        bonus = head_sum(recept * key_mod * vec[5:6], ones) * mixed_value
        mixed_ref[rows] = ((normed * vec[6:7] + vec[7:8] + bonus) * gate).astype(BF16)


def backward_kernel(
    count, grad_ref, recept_ref, keys_ref, values_ref, hidden_ref, first_ref, up_ref, vec_ref, segment_ref,
    head_ref, state_ref, inverse_ref, removed_ref,
    recept_out, keys_out, values_out, ups_out, first_out, vec_out, state,
):
    width = recept_ref.shape[1]
    heads = width // HEAD

    @pl.when(pl.program_id(0) == 0)
    def _():
        state[...] = jnp.zeros_like(state)
        vec_out[...] = jnp.zeros_like(vec_out)

    ones = head_ones(width)
    vec = vec_ref[...]
    up = up_ref[...]
    i, j = iotas(BLOCK, BLOCK)
    upper = jnp.where(i <= j, 1.0, 0.0).astype(BF16)
    columns = [slice(head * HEAD, (head + 1) * HEAD) for head in range(heads)]
    order = range(count - 1, -1, -1)
    kept = {}
    for block in order:
        rows = slice(block * BLOCK, (block + 1) * BLOCK)
        recept, keys, values = recept_ref[rows], keys_ref[rows], values_ref[rows]
        first = first_ref[rows].astype(F32)
        z, decay_log, rate, blend, gate, mixed_value, scale, key_dir, key_mod = front(
            keys, values, hidden_ref[rows], up, first, vec, ones
        )
        quad, carry, tail, keep = block_masks(segment_ref[block * 8 : block * 8 + 8])
        rate_low, dir_low = low(rate), low(key_dir)
        parts = decayed(
            low(decay_log), low(key_mod), dir_low, rate_low, low(recept),
            tile_heads(carry, heads), tile_heads(tail, heads),
        )
        value_low = low(mixed_value)

        grad = grad_ref[rows].astype(F32)
        normed, spread = post_norm(head_ref[rows].astype(F32), ones)
        product = recept * key_mod
        coefficient = head_sum(product * vec[5:6], ones)
        grad_gate = grad * (normed * vec[6:7] + vec[7:8] + coefficient * mixed_value)
        opened = grad * gate
        grad_normed = opened * vec[6:7]
        grad_head = spread * (
            grad_normed
            - head_sum(grad_normed, ones) * (1.0 / HEAD)
            - normed * (head_sum(grad_normed * normed, ones) * (1.0 / HEAD))
        )
        grad_coefficient = head_sum(opened * mixed_value, ones)
        weighted = grad_coefficient * vec[5:6]
        head_grad = low(grad_head)

        lefts = [jnp.concatenate([parts["alpha"][:, c], parts["recept"][:, c]], 0) for c in columns]
        rights = [jnp.concatenate([parts["beta"][:, c], parts["key"][:, c]], 0) for c in columns]
        ends = [jnp.concatenate([parts["beta_end"][:, c], parts["key_end"][:, c]], 0) for c in columns]
        inners = [jnp.concatenate([parts["alpha_in"][:, c], parts["recept_in"][:, c]], 0) for c in columns]
        pairs = [quad * dot3(x, y, NT) for x, y in zip(lefts, rights)]
        out_grads = [head_grad[:, c] for c in columns]
        through = [dot3(x[BLOCK:, :BLOCK], y, TN) for x, y in zip(pairs, out_grads)]
        kept[block] = dict(
            rows=rows, recept=recept, keys=keys, values=values, first=first, z=z, rate=rate, blend=blend,
            mixed_value=mixed_value, scale=scale, key_dir=key_dir, key_mod=key_mod, quad=quad, carry=carry, keep=keep,
            rate_low=rate_low, dir_low=dir_low, parts=parts, value_low=value_low, normed=normed, product=product,
            grad_gate=grad_gate, opened=opened, grad_coefficient=grad_coefficient,
            grad_mixed_value=opened * coefficient, grad_recept=weighted * key_mod, grad_key_mod=weighted * recept,
            lefts=lefts, rights=rights, ends=ends, inners=inners, pairs=pairs, out_grads=out_grads, through=through,
        )
    for block in order:
        k = kept[block]
        after, entering, inverse_all = state[...], state_ref[k["rows"]], inverse_ref[k["rows"]]
        laters, nows = [after[:, c] for c in columns], [entering[:, c] for c in columns]
        from_ends = [dot3(x, y, NT) for x, y in zip(k["ends"], laters)]
        inner_grads = [
            dot3(inverse_all[:, c], x + y[:BLOCK], TN) for c, x, y in zip(columns, k["through"], from_ends)
        ]
        boths = [jnp.concatenate([x, y], 0) for x, y in zip(inner_grads, k["out_grads"])]
        stays = [x * (k["parts"]["end"][:, c] * k["keep"]) for x, c in zip(laters, columns)]
        state[...] = join([x + dot3(y, z, TN) for x, y, z in zip(stays, boths, k["inners"])], 1)
        k.update(
            laters=laters, nows=nows, from_ends=from_ends, boths=boths,
            end_sum=join([jnp.sum(x * y, 0, keepdims=True) for x, y in zip(nows, stays)], 1),
        )
    vec_total = jnp.zeros_like(vec)
    for block in order:
        k = kept[block]
        rows, parts, quad = k["rows"], k["parts"], k["quad"]
        removed_all = removed_ref[rows]
        carry_two = jnp.concatenate([k["carry"], k["carry"]], 0)
        sources = [jnp.concatenate([removed_all[:, c], k["value_low"][:, c]], 0) for c in columns]
        grad_pairs = [quad * dot3(x, y, NT) for x, y in zip(k["boths"], sources)]
        grad_values = [
            dot3(x[:, BLOCK:], y, TN) + z[BLOCK:] for x, y, z in zip(k["pairs"], k["boths"], k["from_ends"])
        ]
        grad_ends = [dot3(x, y) for x, y in zip(sources, k["laters"])]
        to_state = [carry_two * dot3(x, y) for x, y in zip(k["boths"], k["nows"])]
        grad_lefts = [dot3(x, y) + z for x, y, z in zip(grad_pairs, k["rights"], to_state)]
        grad_rights = [dot3(x, y, TN) for x, y in zip(grad_pairs, k["lefts"])]
        d_alpha, d_recept = join([x[:BLOCK] for x in grad_lefts], 1), join([x[BLOCK:] for x in grad_lefts], 1)
        d_beta, d_key = join([x[:BLOCK] for x in grad_rights], 1), join([x[BLOCK:] for x in grad_rights], 1)
        d_beta_end, d_key_end = join([x[:BLOCK] for x in grad_ends], 1), join([x[BLOCK:] for x in grad_ends], 1)
        ended = parts["beta_end"] * d_beta_end + parts["key_end"] * d_key_end
        alphas = parts["alpha"] * d_alpha
        d_total = parts["recept"] * d_recept - parts["beta"] * d_beta - parts["key"] * d_key - ended + alphas
        d_step = sum_left(upper, d_total) + (jnp.sum(ended, 0, keepdims=True) + k["end_sum"]) - alphas
        d_beta_plain = d_beta * parts["shrunk"] + d_beta_end * parts["tail"]
        copy_decay = low(d_step * parts["log_step"])
        copy_dir = low(d_beta_plain * k["rate_low"] - d_alpha * parts["before"])
        copy_rate = low(d_beta_plain * k["dir_low"])

        keys, values, rate, blend = k["keys"], k["values"], k["rate"], k["blend"]
        grad_recept = k["grad_recept"] + low(d_recept * parts["grown"])
        grad_key_mod = k["grad_key_mod"] + low(d_key * parts["shrunk"] + d_key_end * parts["tail"])
        grad_mixed_value = k["grad_mixed_value"] + low(join(grad_values, 1))
        grad_z = copy_decay * jax.nn.sigmoid(-k["z"])
        factor = 1.0 + (rate - 1.0) * vec[4:5]
        keyed = grad_key_mod * keys
        grad_rate = copy_rate + keyed * vec[4:5]
        grad_scaled = k["scale"] * (copy_dir - k["key_dir"] * head_sum(copy_dir * k["key_dir"], ones))
        grad_keys = grad_key_mod * factor + grad_scaled * vec[3:4]
        grad_rate_up = grad_rate * rate * (1.0 - rate)
        grad_value_up = grad_mixed_value * (k["first"] - values) * blend * (1.0 - blend)
        recept_out[rows] = grad_recept.astype(BF16)
        keys_out[rows] = grad_keys.astype(BF16)
        values_out[rows] = (grad_mixed_value * (1.0 - blend)).astype(BF16)
        first_out[rows] = (grad_mixed_value * blend).astype(BF16)
        ups_out[0, rows] = grad_z.astype(BF16)
        ups_out[1, rows] = grad_rate_up.astype(BF16)
        ups_out[2, rows] = grad_value_up.astype(BF16)
        ups_out[3, rows] = k["grad_gate"].astype(BF16)

        def total(x):
            return jnp.sum(x, 0, keepdims=True)

        vec_total = vec_total + jnp.concatenate(
            [
                total(grad_z), total(grad_rate_up), total(grad_value_up), total(grad_scaled * keys),
                total(keyed * (rate - 1.0)), total(k["grad_coefficient"] * k["product"]),
                total(k["opened"] * k["normed"]), total(k["opened"]),
            ],
            0,
        )
    vec_out[...] += vec_total


def kernel_cost(rows, width, passes):
    return pl.CostEstimate(flops=2 * rows * width * width, bytes_accessed=4 * rows * width * passes, transcendentals=0)


def per_step(rows, most):
    return most if (rows // BLOCK) % most == 0 else 1


def run_forward(recept, keys, values, hidden, first, up, vec, segments):
    rows, width = recept.shape
    count = per_step(rows, 4)
    step = count * BLOCK

    def spec(columns):
        return pl.BlockSpec((step, columns), lambda i: (i, 0))

    def whole(array):
        return pl.BlockSpec(array.shape, lambda i: (0, 0))

    return pl.pallas_call(
        functools.partial(forward_kernel, count),
        grid=(rows // step,),
        in_specs=[
            spec(width), spec(width), spec(width), spec(WIDE), spec(width), whole(up), whole(vec),
            pl.BlockSpec((count * 8, BLOCK), lambda i: (i, 0)),
        ],
        out_specs=[spec(width)] * 5,
        out_shape=[jax.ShapeDtypeStruct((rows, width), d) for d in (BF16, BF16, F32, F32, F32)],
        scratch_shapes=[pltpu.VMEM((BLOCK, width), F32)],
        compiler_params=pltpu.CompilerParams(vmem_limit_bytes=48 << 20),
        cost_estimate=kernel_cost(rows, width, 110),
        name="mix_forward",
    )(recept, keys, values, hidden, first, up, vec, segments)


def run_backward(grad, recept, keys, values, hidden, first, up, vec, segments, saved):
    rows, width = recept.shape
    count = per_step(rows, 2)
    step = count * BLOCK
    last = rows // step - 1

    def spec(columns):
        return pl.BlockSpec((step, columns), lambda i: (last - i, 0))

    def whole(array):
        return pl.BlockSpec(array.shape, lambda i: (0, 0))

    return pl.pallas_call(
        functools.partial(backward_kernel, count),
        grid=(rows // step,),
        in_specs=[
            spec(width), spec(width), spec(width), spec(width), spec(WIDE), spec(width), whole(up), whole(vec),
            pl.BlockSpec((count * 8, BLOCK), lambda i: (last - i, 0)),
            spec(width), spec(width), spec(width), spec(width),
        ],
        out_specs=[
            spec(width), spec(width), spec(width),
            pl.BlockSpec((4, step, width), lambda i: (0, last - i, 0)),
            spec(width), pl.BlockSpec((8, width), lambda i: (0, 0)),
        ],
        out_shape=[
            jax.ShapeDtypeStruct((rows, width), BF16), jax.ShapeDtypeStruct((rows, width), BF16),
            jax.ShapeDtypeStruct((rows, width), BF16), jax.ShapeDtypeStruct((4, rows, width), BF16),
            jax.ShapeDtypeStruct((rows, width), BF16), jax.ShapeDtypeStruct((8, width), F32),
        ],
        scratch_shapes=[pltpu.VMEM((BLOCK, width), F32)],
        compiler_params=pltpu.CompilerParams(vmem_limit_bytes=48 << 20),
        cost_estimate=kernel_cost(rows, width, 150),
        name="mix_backward",
    )(grad, recept, keys, values, hidden, first, up, vec, segments, *saved)


def mix_norm(block_ref, stats_ref, vec_ref):
    stats = stats_ref[...]
    flowing = stats[:, 2:3]
    standard = (block_ref[...].astype(F32) - stats[:, 0:1]) * stats[:, 1:2]
    normed = standard * vec_ref[0:1] + vec_ref[1:2]
    delta = pltpu.roll(normed, 1, 0) * flowing - normed
    return standard, normed, delta, flowing


def project_kernel(
    width, number_ref, block_ref, stats_ref, vec_ref, weight_ref,
    recept_ref, keys_ref, values_ref, downs_ref, hidden_ref,
):
    base = 3 * width
    _, normed, delta, _ = mix_norm(block_ref, stats_ref, vec_ref)
    weight = weight_ref[...]
    uses = (
        ((recept_ref, 0, width, 0),),
        ((downs_ref, base + OFFSETS[0], PADDED[0], OFFSETS[0]),),
        ((keys_ref, width, width, 0),),
        ((values_ref, 2 * width, width, 0), (downs_ref, base + OFFSETS[2], PADDED[2], OFFSETS[2])),
        ((downs_ref, base + OFFSETS[1], PADDED[1], OFFSETS[1]),),
        ((downs_ref, base + OFFSETS[3], PADDED[3], OFFSETS[3]),),
    )

    @pl.when(pl.program_id(0) == 0)
    def _():
        for ref in (recept_ref, keys_ref, values_ref, downs_ref):
            ref[...] = jnp.zeros_like(ref)

    for c, targets in enumerate(uses):
        mixed = (normed + delta * vec_ref[2 + c : 3 + c]).astype(BF16)
        for ref, start, size, at in targets:
            ref[:, at : at + size] += dot(mixed, weight[:, start : start + size])

    @pl.when(pl.program_id(0) == pl.num_programs(0) - 1)
    def _():
        hidden_ref[:, 0:128] = jnp.tanh(downs_ref[:, 0:128]).astype(BF16)
        hidden_ref[:, 128:384] = downs_ref[:, 128:384].astype(BF16)
        hidden_ref[:, 384:640] = jax.nn.sigmoid(downs_ref[:, 384:640]).astype(BF16)


def unproject_kernel(
    width, parts, piece, number_ref, block_ref, stats_ref, vec_ref, weight_ref,
    recept_ref, keys_ref, values_ref, ups_ref, hidden_ref, downs_ref, up_ref,
    grad_ref, sums_ref, vec_out, wide_ref, up_out, down_lows,
):
    rows = block_ref.shape[0]
    base = 3 * width

    @pl.when(pl.program_id(0) == 0)
    def _():
        sums_ref[...] = jnp.zeros_like(sums_ref)
        for k, (at, size) in enumerate(zip(OFFSETS, PADDED)):
            cols = slice(at, at + size)
            grad = dot(ups_ref[k], up_ref[cols], NT)
            if k == 0:
                grad = grad * (1.0 - jnp.square(jnp.tanh(downs_ref[:, cols])))
            if k == 3:
                opening = jax.nn.sigmoid(downs_ref[:, cols])
                grad = grad * opening * (1.0 - opening)
            down_lows[:, cols] = grad.astype(BF16)
            up_out[:, cols] = dot(ups_ref[k], hidden_ref[:, cols], TN).astype(BF16)

    standard, normed, delta, flowing = mix_norm(block_ref, stats_ref, vec_ref)
    weight = weight_ref[...]

    def down(k):
        return (down_lows[:, OFFSETS[k] : OFFSETS[k] + PADDED[k]], base + OFFSETS[k], PADDED[k])

    uses = (
        ((recept_ref[...], 0, width),),
        (down(0),),
        ((keys_ref[...], width, width),),
        ((values_ref[...], 2 * width, width), down(2)),
        (down(1),),
        (down(3),),
    )
    kept, sent, vec_rows = None, None, []
    per_seq = parts * piece
    for c, sources in enumerate(uses):
        share = vec_ref[2 + c : 3 + c]
        mixed = (normed + delta * share).astype(BF16)
        grad = None
        for source, start, size in sources:
            part = dot(source, weight[:, start : start + size], NT)
            grad = part if grad is None else grad + part
            product = dot(mixed, source, TN).astype(BF16)
            for number in range(product.shape[0] // per_seq):
                for w in range(parts):
                    at = number * per_seq + w * piece
                    wide_ref[w, number, :, start : start + size] = product[at : at + piece]
        vec_rows.append(jnp.sum(grad * delta, 0, keepdims=True))
        moved = grad * share
        kept = grad - moved if kept is None else kept + (grad - moved)
        sent = moved if sent is None else sent + moved
    grad = kept + pltpu.roll(sent * flowing, rows - 1, 0)
    vec_out[...] = jnp.concatenate(
        [jnp.sum(grad * standard, 0, keepdims=True), jnp.sum(grad, 0, keepdims=True)] + vec_rows, 0
    )
    scaled = grad * vec_ref[0:1]
    sums_ref[:, 0:1] += jnp.sum(scaled, 1, keepdims=True)
    sums_ref[:, 1:2] += jnp.sum(scaled * standard, 1, keepdims=True)
    grad_ref[...] = scaled


def mix_specs(rows, width, own_width, parts):
    block = 256 if rows <= 1024 else 128
    per_shard = width // parts // block

    def columns(height):
        return pl.BlockSpec((height, block), lambda j, n: (0, j))

    def whole(shape):
        return pl.BlockSpec(shape, lambda j, n: (0,) * len(shape))

    def weights(array):
        size = array.shape[1] if rows > 1024 else 3 * own_width + WIDE
        return pl.BlockSpec((block, size), lambda j, n: (((j // per_shard) ^ n[0]) * per_shard + j % per_shard, 0))

    return block, columns, whole, weights


def run_project(number, balanced, stats, vec, weights, own_width, parts):
    rows, width = balanced.shape
    block, columns, whole, weight_spec = mix_specs(rows, width, own_width, parts)
    shapes = [(rows, own_width)] * 3 + [(rows, WIDE)] * 2
    return pl.pallas_call(
        functools.partial(project_kernel, own_width),
        grid_spec=pltpu.PrefetchScalarGridSpec(
            num_scalar_prefetch=1,
            grid=(width // block,),
            in_specs=[columns(rows), whole(stats.shape), columns(8), weight_spec(weights)],
            out_specs=[whole(s) for s in shapes],
        ),
        out_shape=[jax.ShapeDtypeStruct(s, d) for s, d in zip(shapes, (F32, F32, F32, F32, BF16))],
        compiler_params=pltpu.CompilerParams(vmem_limit_bytes=60 << 20),
        cost_estimate=kernel_cost(rows, own_width, 60),
        name="mix_project",
    )(number, balanced, stats, vec, weights)


def run_unproject(number, balanced, stats, vec, weights, lows, ups, hidden, downs, up, parts):
    rows, width = balanced.shape
    own_width = lows[0].shape[1]
    seqs = width // own_width
    piece = own_width // parts
    block, columns, whole, weight_spec = mix_specs(rows, width, own_width, parts)
    taken = block // own_width
    total = 3 * own_width + WIDE
    return pl.pallas_call(
        functools.partial(unproject_kernel, own_width, parts, piece),
        grid_spec=pltpu.PrefetchScalarGridSpec(
            num_scalar_prefetch=1,
            grid=(width // block,),
            in_specs=[columns(rows), whole(stats.shape), columns(8), weight_spec(weights)]
            + [whole(a.shape) for a in (*lows, ups, hidden, downs, up)],
            out_specs=[
                columns(rows), whole((rows, 2)), columns(8),
                pl.BlockSpec((parts, taken, piece, total), lambda j, n: (0, j, 0, 0)),
                whole((own_width, WIDE)),
            ],
            scratch_shapes=[pltpu.VMEM((rows, WIDE), BF16)],
        ),
        out_shape=[
            jax.ShapeDtypeStruct((rows, width), F32), jax.ShapeDtypeStruct((rows, 2), F32),
            jax.ShapeDtypeStruct((8, width), F32), jax.ShapeDtypeStruct((parts, seqs, piece, total), BF16),
            jax.ShapeDtypeStruct((own_width, WIDE), BF16),
        ],
        compiler_params=pltpu.CompilerParams(vmem_limit_bytes=60 << 20),
        cost_estimate=kernel_cost(rows, own_width, 120),
        name="mix_unproject",
    )(number, balanced, stats, vec, weights, *lows, ups, hidden, downs, up)


def norm_stats(values):
    centered = values - jnp.mean(values, -1, keepdims=True)
    scale = lax.rsqrt(jnp.mean(centered * centered, -1, keepdims=True) + 1e-05)
    return centered * scale, scale


def norm_back(grad, standard, scale, gain):
    scaled = grad * gain
    return scale * (
        scaled
        - jnp.mean(scaled, -1, keepdims=True)
        - standard * jnp.mean(scaled * standard, -1, keepdims=True)
    )


def pad_ranks(matrix):
    pieces, start = [], 0
    for rank, padded in zip(RANKS, PADDED):
        pieces.append(jnp.pad(matrix[:, start : start + rank], ((0, 0), (0, padded - rank))))
        start += rank
    return jnp.concatenate(pieces, 1)


def unpad_ranks(matrix):
    return jnp.concatenate([matrix[..., o : o + r] for o, r in zip(OFFSETS, RANKS)], -1)


def from_behind(x, axis, by):
    size = lax.axis_size(axis)
    pairs = [(i, i + by) for i in range(size) if 0 <= i + by < size]
    return lax.ppermute(x, axis, pairs)


def exchange(x, axis):
    return lax.all_to_all(x, axis, split_axis=0, concat_axis=0, tiled=True)


def swap(x, by):
    size = lax.axis_size("wsh")
    return lax.ppermute(x, "wsh", [(i, i ^ by) for i in range(size)])


def gather_near(x):
    if lax.axis_size("wsh") != 4:
        return lax.all_gather(x, "wsh", axis=0, tiled=True)
    across = swap(x, 2)
    beside = swap(x, 1)
    return jnp.concatenate([x, beside, across, swap(across, 1)], 0)


def beside(x):
    return lax.ppermute(x, "seq", [(i, i ^ 1) for i in range(lax.axis_size("seq"))])


def own_half(x, me):
    half = x.shape[1] // 2
    side = me % 2
    return (
        lax.dynamic_slice_in_dim(x, side * half, half, 1),
        beside(lax.dynamic_slice_in_dim(x, (1 - side) * half, half, 1)),
    )


def scalar_sum(x):
    if lax.axis_size("wsh") != 4:
        return jnp.sum(lax.all_gather(x.reshape(1), "wsh", axis=0, tiled=True))
    x = jnp.full((8, 128), x)
    x = x + swap(x, 1)
    return (x + swap(x, 2))[0, 0]


def near_sum(x):
    if lax.axis_size("wsh") != 4:
        return lax.psum_scatter(x, "wsh", scatter_dimension=0, tiled=True)
    rows = x.shape[0] // 4
    beside = swap(jnp.concatenate([x[rows : 2 * rows], x[3 * rows :]], 0), 1)
    far = x[2 * rows : 3 * rows] + beside[rows:]
    return x[:rows] + beside[:rows] + swap(far.astype(BF16), 2).astype(F32)


def block_sum(x):
    if lax.axis_size("wsh") != 4:
        return lax.psum_scatter(x, "wsh", scatter_dimension=0, tiled=False).astype(F32)
    number = lax.axis_index("wsh")

    def block(by):
        return lax.dynamic_index_in_dim(x, number ^ by, 0, keepdims=False)

    beside = swap(jnp.stack([block(1), block(3)]), 1).astype(F32)
    far = block(2).astype(F32) + beside[1]
    return block(0).astype(F32) + beside[0] + swap(far.astype(BF16), 2).astype(F32)


def local(
    tokens, first_layer_values, teacher, valid, destination, lengths,
    receptance_matrix, key_matrix, value_matrix, output_matrix,
    lowrank_down_weight, lowrank_up_weight, channel_key_weight, channel_value_weight, vectors,
):
    rows, width = tokens.shape
    seqs, parts = lax.axis_size("seq"), lax.axis_size("wsh")
    me = lax.axis_index("seq")
    group = rows * seqs
    own_width = width // seqs
    shard = width // parts
    piece = shard // seqs
    column = me * own_width

    dest_seq = destination // rows // parts
    position = dest_seq * rows + destination % rows
    digits = jnp.stack([position // DIGIT, position % DIGIT, valid], 1).astype(BF16)
    tail = jnp.pad(digits, ((0, 0), (0, EXTRA - 3)))
    given = lax.all_gather(jnp.concatenate([tokens, tail], 1), "seq", axis=0, tiled=True)
    info = given[:, width : width + 3].astype(F32)
    places = (info[:, 0] * DIGIT + info[:, 1]).astype(jnp.int32)
    numbers = jnp.arange(group, dtype=jnp.int32)
    permute = (numbers[:, None] == places[None, :]).astype(BF16)
    total_valid = scalar_sum(jnp.sum(info[:, 2]))

    index = jnp.arange(rows, dtype=jnp.int32)
    same_dest = (dest_seq[:, None] == dest_seq[None, :]) & (index[None, :] < index[:, None])
    slot = dest_seq * (rows // seqs) + jnp.sum(same_dest.astype(jnp.int32), 1)
    arrange = (index[:, None] == slot[None, :]).astype(BF16)
    mine = (places // rows) == me
    arrival = jnp.cumsum(mine.astype(jnp.int32)) - 1
    own_rows = ((index[:, None] + me * rows) == places[None, :]).astype(BF16)
    settle = dot(own_rows, (mine[:, None] & (arrival[:, None] == index[None, :])).astype(BF16)).astype(BF16)

    def deal(array):
        moved = exchange(dot(arrange, array).astype(BF16).reshape(seqs, rows // seqs, width), "seq")
        return dot(settle, moved.reshape(rows, width))

    def undeal(array):
        back = dot(settle, array.astype(BF16), TN).astype(BF16)
        moved = exchange(back.reshape(seqs, rows // seqs, width), "seq")
        return dot(arrange, moved.reshape(rows, width), TN).astype(BF16)

    first_given = exchange(
        first_layer_values.reshape(rows, seqs, own_width).transpose(1, 0, 2), "seq"
    ).reshape(group, own_width)
    first = dot(permute, first_given).astype(BF16)

    offsets = jnp.cumsum(lengths[0]) - lengths[0]
    starts = jnp.any(numbers[:, None] == offsets[None, :], 1).astype(F32)
    segment_ids = jnp.cumsum(starts).reshape(-1, BLOCK)
    before = segment_ids[:, :1] - starts.reshape(-1, BLOCK)[:, :1]
    segments = jnp.stack(
        [segment_ids, jnp.broadcast_to(before, segment_ids.shape), jnp.broadcast_to(segment_ids[:, -1:], segment_ids.shape)]
        + [jnp.zeros_like(segment_ids)] * 5,
        1,
    ).reshape(-1, BLOCK)
    flowing = (1.0 - starts)[:, None]

    def own_columns(matrix):
        return lax.dynamic_slice_in_dim(matrix, column, own_width, 1)

    near = parts == 4
    number = lax.axis_index("wsh") if near else 0
    up_piece = lax.dynamic_slice_in_dim(lowrank_up_weight, column % shard, own_width, 0)
    total = 3 * own_width + WIDE
    weights = gather_near(
        jnp.concatenate(
            [
                own_columns(receptance_matrix), own_columns(key_matrix), own_columns(value_matrix),
                pad_ranks(lowrank_down_weight), up_piece.reshape(shard, -1),
            ],
            1,
        )
    )
    up = pad_ranks(
        lax.dynamic_slice(
            weights, (((column // shard) ^ number) * shard, total), (shard, weights.shape[1] - total)
        ).reshape(own_width, -1)
    ).T
    number = jnp.full((1,), number, jnp.int32)
    w_out = lax.all_gather(output_matrix, "wsh", axis=0, tiled=True)
    vec = lax.dynamic_slice_in_dim(vectors, column, own_width, 0)[:, 8:16].T

    balanced = dot(permute, given[:, :width]).astype(BF16)
    wide_rows = balanced.astype(F32)
    mean = jnp.mean(wide_rows, -1, keepdims=True)
    scale_one = lax.rsqrt(jnp.mean(jnp.square(wide_rows - mean), -1, keepdims=True) + 1e-05)
    stats = jnp.concatenate([mean, scale_one, flowing, flowing], 1)
    mix_vec = vectors[:, :8].T
    recept, keys, values, downs, hidden = run_project(number, balanced, stats, mix_vec, weights, own_width, parts)
    teacher_late, recept = lax.optimization_barrier((teacher, recept))
    target = deal(teacher_late)
    inputs = (recept, keys, values, hidden, first, up, vec, segments)
    mixed_out, *saved = run_forward(*inputs)

    mixed_rows = exchange(mixed_out.reshape(seqs, rows, own_width), "seq").transpose(1, 0, 2).reshape(rows, width)
    own = lax.dynamic_slice_in_dim(balanced, me * rows, rows, 0).astype(F32)
    own_starts = lax.dynamic_slice_in_dim(starts, me * rows, rows, 0)
    own_flowing = (1.0 - own_starts)[:, None]
    own_valid = dot(own_rows, given[:, width : width + EXTRA])[:, 2]
    residual = own + dot(mixed_rows, w_out)
    standard_two, scale_two = norm_stats(residual)
    normed_two = standard_two * vectors[:, 16] + vectors[:, 17]
    carried_two = from_behind(normed_two[-1:], "seq", 1)
    delta_two = jnp.concatenate([carried_two, normed_two[:-1]], 0) * own_flowing - normed_two
    channel = gather_near((normed_two + delta_two * vectors[:, 18]).astype(BF16))
    active = jax.nn.relu(dot(channel, channel_key_weight, NT))
    hidden_rows = jnp.square(active).astype(BF16)
    result = residual + near_sum(dot(hidden_rows, channel_value_weight))
    total_tokens = group * parts
    cotangent = (result - target) * (own_valid * (total_tokens / total_valid))[:, None]
    cot = gather_near(cotangent.astype(BF16))

    paired = near and seqs == 8
    channel_other = beside(channel) if paired else None
    lefts_hidden = own_half(hidden_rows, me) if paired else (hidden_rows,)

    def token_product(left, right, right_other=None):
        if not paired:
            return dot(left[0], right, TN).astype(BF16)
        other = beside(right) if right_other is None else right_other
        return (dot(left[0], right, TN) + dot(left[1], other, TN)).astype(BF16)

    value_part = token_product(lefts_hidden, cot)
    grad_pre = (dot(cot, channel_value_weight, NT) * 2.0 * active).astype(BF16)
    channel_part = dot(grad_pre, channel_key_weight)
    grad_channel = near_sum(channel_part)
    key_part = token_product(own_half(grad_pre, me) if paired else (grad_pre,), channel, channel_other)
    grad_vec_mix_two = jnp.sum(grad_channel * delta_two, 0)
    shifted = grad_channel * vectors[:, 18] * own_flowing
    behind = from_behind(shifted[:1], "seq", -1)
    grad_normed_two = grad_channel * (1.0 - vectors[:, 18]) + jnp.concatenate([shifted[1:], behind], 0)
    grad_residual = cotangent + norm_back(grad_normed_two, standard_two, scale_two, vectors[:, 16])
    grad_low = grad_residual.astype(BF16)

    lefts = exchange(mixed_rows.reshape(rows, seqs, parts, piece).transpose(2, 0, 1, 3), "wsh")
    if near:
        lefts = jnp.stack([lax.dynamic_index_in_dim(lefts, number[0] ^ k, 0, keepdims=False) for k in range(4)])
    out_part = dot(lefts.reshape(rows * parts, -1), gather_near(grad_low), TN).astype(BF16)
    if paired:
        halves_out = out_part.reshape(seqs // 2, 2, piece, width)
        x_side = me % 2
        out_mine = lax.dynamic_index_in_dim(halves_out, x_side, 1, keepdims=False).astype(F32)
        out_other = beside(lax.dynamic_index_in_dim(halves_out, 1 - x_side, 1, keepdims=False))
        out_half = (out_mine + out_other.astype(F32)).astype(BF16)
        lines = [[0, 2, 4, 6], [1, 3, 5, 7]]
        turned = [
            ((z * 2 + x) * 4 + w, (w * 2 + x) * 4 + z) for z in range(4) for x in range(2) for w in range(4)
        ]

        def along(part):
            return lax.psum_scatter(part, "seq", scatter_dimension=0, tiled=True, axis_index_groups=lines)

        def turn(part):
            return lax.ppermute(part, ("seq", "wsh"), turned).astype(F32)

        grad_ffn_value = turn(along(value_part))
        both_parts = along(
            jnp.concatenate([key_part.reshape(4, -1, width), out_half], 1).reshape(-1, width)
        )
        grad_ffn_key = turn(both_parts[:-piece])
        grad_out = both_parts[-piece:].astype(F32)
    else:
        moves = [(s * parts + w, w * seqs + s) for s in range(seqs) for w in range(parts)]

        def ffn_grad(part):
            part = lax.psum_scatter(part, "seq", scatter_dimension=0, tiled=True)
            return lax.ppermute(part, ("seq", "wsh"), moves).astype(F32)

        grad_ffn_value, grad_ffn_key = ffn_grad(value_part), ffn_grad(key_part)
        grad_out = lax.psum_scatter(out_part, "seq", scatter_dimension=0, tiled=True).astype(F32)

    grad_posted = dot(grad_low, w_out, NT).astype(BF16)
    grad_heads = exchange(grad_posted.reshape(rows, seqs, own_width).transpose(1, 0, 2), "seq").reshape(group, own_width)
    recept_low, keys_low, values_low, ups_low, grad_first, grad_vec_heads = run_backward(grad_heads, *inputs, saved)
    scaled_grad, sums, vec_mix, wide, up_grad = run_unproject(
        number, balanced, stats, mix_vec, weights, (recept_low, keys_low, values_low), ups_low, hidden, downs, up, parts
    )
    standard = (balanced.astype(F32) - mean) * scale_one
    grad_balanced = scale_one * (scaled_grad - sums[:, :1] * (1.0 / width) - standard * (sums[:, 1:] * (1.0 / width)))
    mine_rows = lax.dynamic_slice_in_dim(grad_balanced, me * rows, rows, 0) + grad_residual
    grad_balanced = lax.dynamic_update_slice_in_dim(grad_balanced, mine_rows, me * rows, 0)
    grad_given = dot(permute, grad_balanced.astype(BF16), TN).astype(BF16)
    grad_tokens = jnp.sum(exchange(grad_given.reshape(seqs, rows, width), "seq").astype(F32), 0).astype(BF16)
    first_back = exchange(dot(permute, grad_first, TN).astype(BF16).reshape(seqs, rows, own_width), "seq")
    grad_first_rows = first_back.transpose(1, 0, 2).reshape(rows, width)

    wide_all = exchange(block_sum(wide).astype(BF16), "seq").astype(F32)

    def square(at):
        taken = wide_all[:, :, at * own_width : (at + 1) * own_width]
        return taken.transpose(1, 0, 2).reshape(piece, width)

    grad_down = unpad_ranks(jnp.sum(wide_all[:, :, 3 * own_width :], 0))
    up_part = unpad_ranks(block_sum(up_grad.reshape(parts, piece, WIDE)))

    heads_part = lax.dynamic_update_slice_in_dim(jnp.zeros((width, 8), F32), grad_vec_heads.T, column, 0)
    grad_vectors = jnp.concatenate(
        [
            vec_mix.T,
            heads_part,
            jnp.stack([jnp.sum(grad_normed_two * standard_two, 0), jnp.sum(grad_normed_two, 0), grad_vec_mix_two], 1),
        ],
        1,
    )
    vec_part = jnp.sum(exchange(grad_vectors.reshape(seqs, parts * piece, -1), "seq"), 0)
    vec_part = jnp.sum(exchange(vec_part.reshape(parts, piece, -1), "wsh"), 0)
    return (
        undeal(result), grad_tokens, grad_first_rows,
        square(0), square(1), square(2),
        grad_out, grad_down, up_part,
        grad_ffn_key, grad_ffn_value, vec_part,
    )


def solution(mesh):
    both, shard = P(("seq", "wsh"), None), P("wsh", None)
    flat = P(("seq", "wsh"))
    return jax.shard_map(
        local,
        mesh=mesh,
        in_specs=(both, both, both, flat, flat) + (shard,) * 9 + (P(),),
        out_specs=(both,) * 12,
        check_vma=False,
    )
```

```python
import functools

import jax
import jax.numpy as jnp
from jax import lax
from jax.experimental import pallas as pl
from jax.experimental.pallas import tpu as pltpu
from jax.sharding import PartitionSpec as P

HEAD = 64
BLOCK = 64
RANKS = (96, 96, 64, 256)
PADDED = (128, 128, 128, 256)
OFFSETS = (0, 128, 256, 384)
WIDE = 640
EXTRA = 128
DIGIT = 64

F32 = jnp.float32
BF16 = jnp.bfloat16

NN = (((1,), (0,)), ((), ()))
NT = (((1,), (1,)), ((), ()))
TN = (((0,), (0,)), ((), ()))


def dot(a, b, dims=NN):
    return lax.dot_general(a, b, dims, preferred_element_type=F32)


def halves(x):
    high = x.astype(BF16)
    return high, (x - high.astype(F32)).astype(BF16)


def dot3(a, b, dims=NN):
    a_high, a_low = halves(a)
    b_high, b_low = halves(b)
    return dot(a_high, b_high, dims) + (dot(a_high, b_low, dims) + dot(a_low, b_high, dims))


def sum_left(mask, x):
    high, low = halves(x)
    low_two = (x - high.astype(F32) - low.astype(F32)).astype(BF16)
    return dot(mask, high) + (dot(mask, low) + dot(mask, low_two))


def head_sum(x, ones):
    high, low = halves(x)
    return dot(high, ones) + dot(low, ones)


def low(x):
    return x.astype(BF16).astype(F32)


def iotas(rows, columns):
    return (
        lax.broadcasted_iota(jnp.int32, (rows, columns), 0),
        lax.broadcasted_iota(jnp.int32, (rows, columns), 1),
    )


def head_ones(width):
    i, j = iotas(width, width)
    return jnp.where((i >> 6) == (j >> 6), 1.0, 0.0).astype(BF16)


def front(keys, values, hidden, up, first, vec, ones):
    z = vec[0:1] + dot(hidden[:, 0:128], up[0:128])
    decay_log = -(jnp.maximum(-z, 0.0) + jnp.log1p(jnp.exp(-jnp.abs(z)))) - 0.5
    rate = jax.nn.sigmoid(vec[1:2] + dot(hidden[:, 128:256], up[128:256]))
    blend = jax.nn.sigmoid(vec[2:3] + dot(hidden[:, 256:384], up[256:384]))
    gate = dot(hidden[:, 384:640], up[384:640])
    mixed_value = values + (first - values) * blend
    scaled = keys * vec[3:4]
    scale = lax.rsqrt(head_sum(scaled * scaled, ones) + 1e-06)
    key_dir = scaled * scale
    key_mod = keys * (1.0 + (rate - 1.0) * vec[4:5])
    return z, decay_log, rate, blend, gate, mixed_value, scale, key_dir, key_mod


def block_masks(segments):
    i, j = iotas(BLOCK, BLOCK)
    across = jnp.broadcast_to(segments[0:1], (BLOCK, BLOCK))
    down = across.T
    before = jnp.broadcast_to(segments[1:2], (BLOCK, BLOCK))
    last = jnp.broadcast_to(segments[2:3], (BLOCK, BLOCK))
    same = across == down
    strict = jnp.where(same & (i > j), 1.0, 0.0)
    closed = jnp.where(same & (i >= j), 1.0, 0.0)
    carry = jnp.where(down == before, 1.0, 0.0)
    tail = jnp.where(down == last, 1.0, 0.0)
    keep = jnp.where(segments[2:3] == segments[1:2], 1.0, 0.0)
    quad = jnp.concatenate(
        [jnp.concatenate([strict, strict], 1), jnp.concatenate([closed, closed], 1)], 0
    )
    return quad, carry, tail, keep


def tile_heads(x, heads):
    return jnp.concatenate([x] * heads, 1) if heads > 1 else x


def join(pieces, axis):
    return jnp.concatenate(pieces, axis) if len(pieces) > 1 else pieces[0]


def decayed(decay_low, key_low, dir_low, rate_low, recept_low, carry, tail):
    i, j = iotas(BLOCK, BLOCK)
    lower = jnp.where(i >= j, 1.0, 0.0).astype(BF16)
    log_step = -jnp.exp(decay_low)
    total = sum_left(lower, log_step)
    before = jnp.exp(total - log_step)
    grown = jnp.exp(total)
    shrunk = jnp.exp(-total)
    end = total[BLOCK - 1 : BLOCK]
    tail_decay = jnp.exp(end - total) * tail
    alpha = -dir_low * before
    beta_plain = dir_low * rate_low
    beta = beta_plain * shrunk
    key = key_low * shrunk
    recept = recept_low * grown
    return dict(
        log_step=log_step, before=before, grown=grown, shrunk=shrunk, end=jnp.exp(end), tail=tail_decay,
        alpha=alpha, beta_plain=beta_plain, beta=beta, key=key, recept=recept,
        beta_end=beta_plain * tail_decay, key_end=key_low * tail_decay,
        alpha_in=alpha * carry, recept_in=recept * carry,
    )


def unit_inverses(lowers):
    i, j = iotas(BLOCK, BLOCK)
    eye = jnp.where(i == j, 1.0, 0.0)

    def within(size):
        return (i // size) == (j // size)

    smalls = [jnp.where(within(4), x, 0.0) for x in lowers]
    low_smalls = [x.astype(BF16) for x in smalls]
    twos = [dot(x, x) for x in low_smalls]
    inverses = [eye + x for x in smalls]
    inverses = [x + dot(x.astype(BF16), y.astype(BF16)) for x, y in zip(inverses, twos)]
    for size in (8, 16, 32, 64):
        mask = within(size) & ~within(size // 2)
        offs = [jnp.where(mask, x, 0.0).astype(BF16) for x in lowers]
        lows = [x.astype(BF16) for x in inverses]
        inner = [dot(x, y).astype(BF16) for x, y in zip(offs, lows)]
        inverses = [x + dot(y, z) for x, y, z in zip(inverses, lows, inner)]
    errors = [eye - x + dot3(y, x) for x, y in zip(inverses, lowers)]
    return [x + dot(x.astype(BF16), y.astype(BF16)) for x, y in zip(inverses, errors)]


def post_norm(head_low, ones):
    centered = head_low - head_sum(head_low, ones) * (1.0 / HEAD)
    spread = lax.rsqrt(head_sum(centered * centered, ones) * (1.0 / HEAD) + HEAD * 1e-05)
    return centered * spread, spread


def forward_kernel(
    count, recept_ref, keys_ref, values_ref, hidden_ref, first_ref, up_ref, vec_ref, segment_ref,
    mixed_ref, head_ref, state_ref, inverse_ref, removed_ref, state,
):
    width = recept_ref.shape[1]
    heads = width // HEAD

    @pl.when(pl.program_id(0) == 0)
    def _():
        state[...] = jnp.zeros_like(state)

    ones = head_ones(width)
    vec = vec_ref[...]
    up = up_ref[...]
    columns = [slice(head * HEAD, (head + 1) * HEAD) for head in range(heads)]
    done = []
    for block in range(count):
        rows = slice(block * BLOCK, (block + 1) * BLOCK)
        recept, keys, values = recept_ref[rows], keys_ref[rows], values_ref[rows]
        _, decay_log, rate, _, gate, mixed_value, _, key_dir, key_mod = front(
            keys, values, hidden_ref[rows], up, first_ref[rows].astype(F32), vec, ones
        )
        quad, carry, tail, keep = block_masks(segment_ref[block * 8 : block * 8 + 8])
        parts = decayed(
            low(decay_log), low(key_mod), low(key_dir), low(rate), low(recept),
            tile_heads(carry, heads), tile_heads(tail, heads),
        )
        lefts = [jnp.concatenate([parts["alpha"][:, c], parts["recept"][:, c]], 0) for c in columns]
        rights = [jnp.concatenate([parts["beta"][:, c], parts["key"][:, c]], 0) for c in columns]
        pairs = [quad * dot3(x, y, NT) for x, y in zip(lefts, rights)]
        done.append((rows, recept, key_mod, gate, mixed_value, keep, parts, pairs))
    inverses = unit_inverses([x[:BLOCK, :BLOCK] for item in done for x in item[-1]])
    for block, (rows, recept, key_mod, gate, mixed_value, keep, parts, pairs) in enumerate(done):
        mine = inverses[block * heads : (block + 1) * heads]
        value_low = low(mixed_value)
        owns = [value_low[:, c] for c in columns]
        by_values = [dot3(x[:, BLOCK:], y) for x, y in zip(pairs, owns)]
        ends = [jnp.concatenate([parts["beta_end"][:, c], parts["key_end"][:, c]], 0) for c in columns]
        inners = [jnp.concatenate([parts["alpha_in"][:, c], parts["recept_in"][:, c]], 0) for c in columns]
        entering = state[...]
        state_ref[rows] = entering
        nows = [entering[:, c] for c in columns]
        inwards = [dot3(x, y, NT) for x, y in zip(inners, nows)]
        removals = [dot3(x, y[:BLOCK] + z[:BLOCK]) for x, y, z in zip(mine, inwards, by_values)]
        outs = [
            y[BLOCK:] + z[BLOCK:] + dot3(x[BLOCK:, :BLOCK], r)
            for x, y, z, r in zip(pairs, inwards, by_values, removals)
        ]
        leaving = [
            x * (parts["end"][:, c] * keep) + dot3(jnp.concatenate([r, v], 0), e, TN)
            for x, c, r, v, e in zip(nows, columns, removals, owns, ends)
        ]
        state[...] = join(leaving, 1)
        inverse_ref[rows] = join(mine, 1)
        removed_ref[rows] = join(removals, 1)
        head_low = join(outs, 1).astype(BF16)
        head_ref[rows] = head_low
        normed, _ = post_norm(head_low.astype(F32), ones)
        bonus = head_sum(recept * key_mod * vec[5:6], ones) * mixed_value
        mixed_ref[rows] = ((normed * vec[6:7] + vec[7:8] + bonus) * gate).astype(BF16)


def backward_kernel(
    count, grad_ref, recept_ref, keys_ref, values_ref, hidden_ref, first_ref, up_ref, vec_ref, segment_ref,
    head_ref, state_ref, inverse_ref, removed_ref,
    recept_out, keys_out, values_out, ups_out, first_out, vec_out, state,
):
    width = recept_ref.shape[1]
    heads = width // HEAD

    @pl.when(pl.program_id(0) == 0)
    def _():
        state[...] = jnp.zeros_like(state)
        vec_out[...] = jnp.zeros_like(vec_out)

    ones = head_ones(width)
    vec = vec_ref[...]
    up = up_ref[...]
    i, j = iotas(BLOCK, BLOCK)
    upper = jnp.where(i <= j, 1.0, 0.0).astype(BF16)
    columns = [slice(head * HEAD, (head + 1) * HEAD) for head in range(heads)]
    order = range(count - 1, -1, -1)
    kept = {}
    for block in order:
        rows = slice(block * BLOCK, (block + 1) * BLOCK)
        recept, keys, values = recept_ref[rows], keys_ref[rows], values_ref[rows]
        first = first_ref[rows].astype(F32)
        z, decay_log, rate, blend, gate, mixed_value, scale, key_dir, key_mod = front(
            keys, values, hidden_ref[rows], up, first, vec, ones
        )
        quad, carry, tail, keep = block_masks(segment_ref[block * 8 : block * 8 + 8])
        rate_low, dir_low = low(rate), low(key_dir)
        parts = decayed(
            low(decay_log), low(key_mod), dir_low, rate_low, low(recept),
            tile_heads(carry, heads), tile_heads(tail, heads),
        )
        value_low = low(mixed_value)

        grad = grad_ref[rows].astype(F32)
        normed, spread = post_norm(head_ref[rows].astype(F32), ones)
        product = recept * key_mod
        coefficient = head_sum(product * vec[5:6], ones)
        grad_gate = grad * (normed * vec[6:7] + vec[7:8] + coefficient * mixed_value)
        opened = grad * gate
        grad_normed = opened * vec[6:7]
        grad_head = spread * (
            grad_normed
            - head_sum(grad_normed, ones) * (1.0 / HEAD)
            - normed * (head_sum(grad_normed * normed, ones) * (1.0 / HEAD))
        )
        grad_coefficient = head_sum(opened * mixed_value, ones)
        weighted = grad_coefficient * vec[5:6]
        head_grad = low(grad_head)

        lefts = [jnp.concatenate([parts["alpha"][:, c], parts["recept"][:, c]], 0) for c in columns]
        rights = [jnp.concatenate([parts["beta"][:, c], parts["key"][:, c]], 0) for c in columns]
        ends = [jnp.concatenate([parts["beta_end"][:, c], parts["key_end"][:, c]], 0) for c in columns]
        inners = [jnp.concatenate([parts["alpha_in"][:, c], parts["recept_in"][:, c]], 0) for c in columns]
        pairs = [quad * dot3(x, y, NT) for x, y in zip(lefts, rights)]
        out_grads = [head_grad[:, c] for c in columns]
        through = [dot3(x[BLOCK:, :BLOCK], y, TN) for x, y in zip(pairs, out_grads)]
        kept[block] = dict(
            rows=rows, recept=recept, keys=keys, values=values, first=first, z=z, rate=rate, blend=blend,
            mixed_value=mixed_value, scale=scale, key_dir=key_dir, key_mod=key_mod, quad=quad, carry=carry, keep=keep,
            rate_low=rate_low, dir_low=dir_low, parts=parts, value_low=value_low, normed=normed, product=product,
            grad_gate=grad_gate, opened=opened, grad_coefficient=grad_coefficient,
            grad_mixed_value=opened * coefficient, grad_recept=weighted * key_mod, grad_key_mod=weighted * recept,
            lefts=lefts, rights=rights, ends=ends, inners=inners, pairs=pairs, out_grads=out_grads, through=through,
        )
    for block in order:
        k = kept[block]
        after, entering, inverse_all = state[...], state_ref[k["rows"]], inverse_ref[k["rows"]]
        laters, nows = [after[:, c] for c in columns], [entering[:, c] for c in columns]
        from_ends = [dot3(x, y, NT) for x, y in zip(k["ends"], laters)]
        inner_grads = [
            dot3(inverse_all[:, c], x + y[:BLOCK], TN) for c, x, y in zip(columns, k["through"], from_ends)
        ]
        boths = [jnp.concatenate([x, y], 0) for x, y in zip(inner_grads, k["out_grads"])]
        stays = [x * (k["parts"]["end"][:, c] * k["keep"]) for x, c in zip(laters, columns)]
        state[...] = join([x + dot3(y, z, TN) for x, y, z in zip(stays, boths, k["inners"])], 1)
        k.update(
            laters=laters, nows=nows, from_ends=from_ends, boths=boths,
            end_sum=join([jnp.sum(x * y, 0, keepdims=True) for x, y in zip(nows, stays)], 1),
        )
    vec_total = jnp.zeros_like(vec)
    for block in order:
        k = kept[block]
        rows, parts, quad = k["rows"], k["parts"], k["quad"]
        removed_all = removed_ref[rows]
        carry_two = jnp.concatenate([k["carry"], k["carry"]], 0)
        sources = [jnp.concatenate([removed_all[:, c], k["value_low"][:, c]], 0) for c in columns]
        grad_pairs = [quad * dot3(x, y, NT) for x, y in zip(k["boths"], sources)]
        grad_values = [
            dot3(x[:, BLOCK:], y, TN) + z[BLOCK:] for x, y, z in zip(k["pairs"], k["boths"], k["from_ends"])
        ]
        grad_ends = [dot3(x, y) for x, y in zip(sources, k["laters"])]
        to_state = [carry_two * dot3(x, y) for x, y in zip(k["boths"], k["nows"])]
        grad_lefts = [dot3(x, y) + z for x, y, z in zip(grad_pairs, k["rights"], to_state)]
        grad_rights = [dot3(x, y, TN) for x, y in zip(grad_pairs, k["lefts"])]
        d_alpha, d_recept = join([x[:BLOCK] for x in grad_lefts], 1), join([x[BLOCK:] for x in grad_lefts], 1)
        d_beta, d_key = join([x[:BLOCK] for x in grad_rights], 1), join([x[BLOCK:] for x in grad_rights], 1)
        d_beta_end, d_key_end = join([x[:BLOCK] for x in grad_ends], 1), join([x[BLOCK:] for x in grad_ends], 1)
        ended = parts["beta_end"] * d_beta_end + parts["key_end"] * d_key_end
        alphas = parts["alpha"] * d_alpha
        d_total = parts["recept"] * d_recept - parts["beta"] * d_beta - parts["key"] * d_key - ended + alphas
        d_step = sum_left(upper, d_total) + (jnp.sum(ended, 0, keepdims=True) + k["end_sum"]) - alphas
        d_beta_plain = d_beta * parts["shrunk"] + d_beta_end * parts["tail"]
        copy_decay = low(d_step * parts["log_step"])
        copy_dir = low(d_beta_plain * k["rate_low"] - d_alpha * parts["before"])
        copy_rate = low(d_beta_plain * k["dir_low"])

        keys, values, rate, blend = k["keys"], k["values"], k["rate"], k["blend"]
        grad_recept = k["grad_recept"] + low(d_recept * parts["grown"])
        grad_key_mod = k["grad_key_mod"] + low(d_key * parts["shrunk"] + d_key_end * parts["tail"])
        grad_mixed_value = k["grad_mixed_value"] + low(join(grad_values, 1))
        grad_z = copy_decay * jax.nn.sigmoid(-k["z"])
        factor = 1.0 + (rate - 1.0) * vec[4:5]
        keyed = grad_key_mod * keys
        grad_rate = copy_rate + keyed * vec[4:5]
        grad_scaled = k["scale"] * (copy_dir - k["key_dir"] * head_sum(copy_dir * k["key_dir"], ones))
        grad_keys = grad_key_mod * factor + grad_scaled * vec[3:4]
        grad_rate_up = grad_rate * rate * (1.0 - rate)
        grad_value_up = grad_mixed_value * (k["first"] - values) * blend * (1.0 - blend)
        recept_out[rows] = grad_recept.astype(BF16)
        keys_out[rows] = grad_keys.astype(BF16)
        values_out[rows] = (grad_mixed_value * (1.0 - blend)).astype(BF16)
        first_out[rows] = (grad_mixed_value * blend).astype(BF16)
        ups_out[0, rows] = grad_z.astype(BF16)
        ups_out[1, rows] = grad_rate_up.astype(BF16)
        ups_out[2, rows] = grad_value_up.astype(BF16)
        ups_out[3, rows] = k["grad_gate"].astype(BF16)

        def total(x):
            return jnp.sum(x, 0, keepdims=True)

        vec_total = vec_total + jnp.concatenate(
            [
                total(grad_z), total(grad_rate_up), total(grad_value_up), total(grad_scaled * keys),
                total(keyed * (rate - 1.0)), total(k["grad_coefficient"] * k["product"]),
                total(k["opened"] * k["normed"]), total(k["opened"]),
            ],
            0,
        )
    vec_out[...] += vec_total


def kernel_cost(rows, width, passes):
    return pl.CostEstimate(flops=2 * rows * width * width, bytes_accessed=4 * rows * width * passes, transcendentals=0)


def per_step(rows, most):
    return most if (rows // BLOCK) % most == 0 else 1


def run_forward(recept, keys, values, hidden, first, up, vec, segments):
    rows, width = recept.shape
    count = per_step(rows, 4)
    step = count * BLOCK

    def spec(columns):
        return pl.BlockSpec((step, columns), lambda i: (i, 0))

    def whole(array):
        return pl.BlockSpec(array.shape, lambda i: (0, 0))

    return pl.pallas_call(
        functools.partial(forward_kernel, count),
        grid=(rows // step,),
        in_specs=[
            spec(width), spec(width), spec(width), spec(WIDE), spec(width), whole(up), whole(vec),
            pl.BlockSpec((count * 8, BLOCK), lambda i: (i, 0)),
        ],
        out_specs=[spec(width)] * 5,
        out_shape=[jax.ShapeDtypeStruct((rows, width), d) for d in (BF16, BF16, F32, F32, F32)],
        scratch_shapes=[pltpu.VMEM((BLOCK, width), F32)],
        compiler_params=pltpu.CompilerParams(vmem_limit_bytes=48 << 20),
        cost_estimate=kernel_cost(rows, width, 110),
        name="mix_forward",
    )(recept, keys, values, hidden, first, up, vec, segments)


def run_backward(grad, recept, keys, values, hidden, first, up, vec, segments, saved):
    rows, width = recept.shape
    count = per_step(rows, 2)
    step = count * BLOCK
    last = rows // step - 1

    def spec(columns):
        return pl.BlockSpec((step, columns), lambda i: (last - i, 0))

    def whole(array):
        return pl.BlockSpec(array.shape, lambda i: (0, 0))

    return pl.pallas_call(
        functools.partial(backward_kernel, count),
        grid=(rows // step,),
        in_specs=[
            spec(width), spec(width), spec(width), spec(width), spec(WIDE), spec(width), whole(up), whole(vec),
            pl.BlockSpec((count * 8, BLOCK), lambda i: (last - i, 0)),
            spec(width), spec(width), spec(width), spec(width),
        ],
        out_specs=[
            spec(width), spec(width), spec(width),
            pl.BlockSpec((4, step, width), lambda i: (0, last - i, 0)),
            spec(width), pl.BlockSpec((8, width), lambda i: (0, 0)),
        ],
        out_shape=[
            jax.ShapeDtypeStruct((rows, width), BF16), jax.ShapeDtypeStruct((rows, width), BF16),
            jax.ShapeDtypeStruct((rows, width), BF16), jax.ShapeDtypeStruct((4, rows, width), BF16),
            jax.ShapeDtypeStruct((rows, width), BF16), jax.ShapeDtypeStruct((8, width), F32),
        ],
        scratch_shapes=[pltpu.VMEM((BLOCK, width), F32)],
        compiler_params=pltpu.CompilerParams(vmem_limit_bytes=48 << 20),
        cost_estimate=kernel_cost(rows, width, 150),
        name="mix_backward",
    )(grad, recept, keys, values, hidden, first, up, vec, segments, *saved)


def mix_norm(block_ref, stats_ref, vec_ref):
    stats = stats_ref[...]
    flowing = stats[:, 2:3]
    standard = (block_ref[...].astype(F32) - stats[:, 0:1]) * stats[:, 1:2]
    normed = standard * vec_ref[0:1] + vec_ref[1:2]
    delta = pltpu.roll(normed, 1, 0) * flowing - normed
    return standard, normed, delta, flowing


def project_kernel(
    width, number_ref, block_ref, stats_ref, vec_ref, weight_ref,
    recept_ref, keys_ref, values_ref, downs_ref, hidden_ref,
):
    base = 3 * width
    _, normed, delta, _ = mix_norm(block_ref, stats_ref, vec_ref)
    weight = weight_ref[...]
    uses = (
        ((recept_ref, 0, width, 0),),
        ((downs_ref, base + OFFSETS[0], PADDED[0], OFFSETS[0]),),
        ((keys_ref, width, width, 0),),
        ((values_ref, 2 * width, width, 0), (downs_ref, base + OFFSETS[2], PADDED[2], OFFSETS[2])),
        ((downs_ref, base + OFFSETS[1], PADDED[1], OFFSETS[1]),),
        ((downs_ref, base + OFFSETS[3], PADDED[3], OFFSETS[3]),),
    )

    @pl.when(pl.program_id(0) == 0)
    def _():
        for ref in (recept_ref, keys_ref, values_ref, downs_ref):
            ref[...] = jnp.zeros_like(ref)

    for c, targets in enumerate(uses):
        mixed = (normed + delta * vec_ref[2 + c : 3 + c]).astype(BF16)
        for ref, start, size, at in targets:
            ref[:, at : at + size] += dot(mixed, weight[:, start : start + size])

    @pl.when(pl.program_id(0) == pl.num_programs(0) - 1)
    def _():
        hidden_ref[:, 0:128] = jnp.tanh(downs_ref[:, 0:128]).astype(BF16)
        hidden_ref[:, 128:384] = downs_ref[:, 128:384].astype(BF16)
        hidden_ref[:, 384:640] = jax.nn.sigmoid(downs_ref[:, 384:640]).astype(BF16)


def unproject_kernel(
    width, parts, piece, number_ref, block_ref, stats_ref, vec_ref, weight_ref,
    other_ref, recept_ref, keys_ref, values_ref, ups_ref, hidden_ref, downs_ref, up_ref,
    grad_ref, sums_ref, wide_ref, up_out, down_lows,
):
    rows = block_ref.shape[0]
    base = 3 * width

    @pl.when(pl.program_id(0) == 0)
    def _():
        sums_ref[...] = jnp.zeros_like(sums_ref)
        for k, (at, size) in enumerate(zip(OFFSETS, PADDED)):
            cols = slice(at, at + size)
            grad = dot(ups_ref[k], up_ref[cols], NT)
            if k == 0:
                grad = grad * (1.0 - jnp.square(jnp.tanh(downs_ref[:, cols])))
            if k == 3:
                opening = jax.nn.sigmoid(downs_ref[:, cols])
                grad = grad * opening * (1.0 - opening)
            down_lows[:, cols] = grad.astype(BF16)
            up_out[:, cols] = dot(ups_ref[k], hidden_ref[:, cols], TN).astype(BF16)

    standard, normed, delta, flowing = mix_norm(block_ref, stats_ref, vec_ref)
    weight = weight_ref[...]

    def down(k):
        return (down_lows[:, OFFSETS[k] : OFFSETS[k] + PADDED[k]], base + OFFSETS[k], PADDED[k])

    uses = (
        ((recept_ref[...], 0, width),),
        (down(0),),
        ((keys_ref[...], width, width),),
        ((values_ref[...], 2 * width, width), down(2)),
        (down(1),),
        (down(3),),
    )
    kept, sent, vec_rows = None, None, []
    per_seq = parts * piece
    for c, sources in enumerate(uses):
        share = vec_ref[2 + c : 3 + c]
        mixed = (normed + delta * share).astype(BF16)
        grad = None
        for source, start, size in sources:
            part = dot(source, weight[:, start : start + size], NT)
            grad = part if grad is None else grad + part
            product = dot(mixed, source, TN).astype(BF16)
            for number in range(product.shape[0] // per_seq):
                for w in range(parts):
                    at = number * per_seq + w * piece
                    wide_ref[w, number, :, start : start + size] = product[at : at + piece]
        vec_rows.append(jnp.sum(grad * delta, 0, keepdims=True))
        moved = grad * share
        kept = grad - moved if kept is None else kept + (grad - moved)
        sent = moved if sent is None else sent + moved
    grad = kept + pltpu.roll(sent * flowing, rows - 1, 0)
    vec_rows = jnp.concatenate(
        [jnp.sum(grad * standard, 0, keepdims=True), jnp.sum(grad, 0, keepdims=True)] + vec_rows, 0
    )
    spare = jnp.concatenate([vec_rows.T, other_ref[...]], 1).astype(BF16)
    for number in range(spare.shape[0] // per_seq):
        for w in range(parts):
            at = number * per_seq + w * piece
            wide_ref[w, number, :, base + RANKS[0] : base + PADDED[0]] = spare[at : at + piece]
    scaled = grad * vec_ref[0:1]
    sums_ref[:, 0:1] += jnp.sum(scaled, 1, keepdims=True)
    sums_ref[:, 1:2] += jnp.sum(scaled * standard, 1, keepdims=True)
    grad_ref[...] = scaled


def mix_specs(rows, width, own_width, parts):
    block = 256 if rows <= 1024 else 128
    per_shard = width // parts // block

    def columns(height):
        return pl.BlockSpec((height, block), lambda j, n: (0, j))

    def whole(shape):
        return pl.BlockSpec(shape, lambda j, n: (0,) * len(shape))

    def weights(array):
        size = array.shape[1] if rows > 1024 else 3 * own_width + WIDE
        return pl.BlockSpec((block, size), lambda j, n: (((j // per_shard) ^ n[0]) * per_shard + j % per_shard, 0))

    return block, columns, whole, weights


def run_project(number, balanced, stats, vec, weights, own_width, parts):
    rows, width = balanced.shape
    block, columns, whole, weight_spec = mix_specs(rows, width, own_width, parts)
    shapes = [(rows, own_width)] * 3 + [(rows, WIDE)] * 2
    return pl.pallas_call(
        functools.partial(project_kernel, own_width),
        grid_spec=pltpu.PrefetchScalarGridSpec(
            num_scalar_prefetch=1,
            grid=(width // block,),
            in_specs=[columns(rows), whole(stats.shape), columns(8), weight_spec(weights)],
            out_specs=[whole(s) for s in shapes],
        ),
        out_shape=[jax.ShapeDtypeStruct(s, d) for s, d in zip(shapes, (F32, F32, F32, F32, BF16))],
        compiler_params=pltpu.CompilerParams(vmem_limit_bytes=60 << 20),
        cost_estimate=kernel_cost(rows, own_width, 60),
        name="mix_project",
    )(number, balanced, stats, vec, weights)


def run_unproject(number, balanced, stats, vec, weights, others, lows, ups, hidden, downs, up, parts):
    rows, width = balanced.shape
    own_width = lows[0].shape[1]
    seqs = width // own_width
    piece = own_width // parts
    block, columns, whole, weight_spec = mix_specs(rows, width, own_width, parts)
    taken = block // own_width
    total = 3 * own_width + WIDE
    return pl.pallas_call(
        functools.partial(unproject_kernel, own_width, parts, piece),
        grid_spec=pltpu.PrefetchScalarGridSpec(
            num_scalar_prefetch=1,
            grid=(width // block,),
            in_specs=[
                columns(rows), whole(stats.shape), columns(8), weight_spec(weights),
                pl.BlockSpec((block, others.shape[1]), lambda j, n: (j, 0)),
            ]
            + [whole(a.shape) for a in (*lows, ups, hidden, downs, up)],
            out_specs=[
                columns(rows), whole((rows, 2)),
                pl.BlockSpec((parts, taken, piece, total), lambda j, n: (0, j, 0, 0)),
                whole((own_width, WIDE)),
            ],
            scratch_shapes=[pltpu.VMEM((rows, WIDE), BF16)],
        ),
        out_shape=[
            jax.ShapeDtypeStruct((rows, width), F32), jax.ShapeDtypeStruct((rows, 2), F32),
            jax.ShapeDtypeStruct((parts, seqs, piece, total), BF16),
            jax.ShapeDtypeStruct((own_width, WIDE), BF16),
        ],
        compiler_params=pltpu.CompilerParams(vmem_limit_bytes=60 << 20),
        cost_estimate=kernel_cost(rows, own_width, 120),
        name="mix_unproject",
    )(number, balanced, stats, vec, weights, others, *lows, ups, hidden, downs, up)


def norm_stats(values):
    centered = values - jnp.mean(values, -1, keepdims=True)
    scale = lax.rsqrt(jnp.mean(centered * centered, -1, keepdims=True) + 1e-05)
    return centered * scale, scale


def norm_back(grad, standard, scale, gain):
    scaled = grad * gain
    return scale * (
        scaled
        - jnp.mean(scaled, -1, keepdims=True)
        - standard * jnp.mean(scaled * standard, -1, keepdims=True)
    )


def pad_ranks(matrix):
    pieces, start = [], 0
    for rank, padded in zip(RANKS, PADDED):
        pieces.append(jnp.pad(matrix[:, start : start + rank], ((0, 0), (0, padded - rank))))
        start += rank
    return jnp.concatenate(pieces, 1)


def unpad_ranks(matrix):
    return jnp.concatenate([matrix[..., o : o + r] for o, r in zip(OFFSETS, RANKS)], -1)


MESH_ID = pl.DeviceIdType.MESH


def places():
    s, w = lax.axis_index("seq"), lax.axis_index("wsh")
    side = s % 2
    return s, w, side, s // 2, (s + 1 - 2 * side, w), (s, w + 1 - 2 * (w % 2)), (s, w + 2 - 4 * (w // 2))


def greet(neighbours, number):
    barrier = pltpu.get_barrier_semaphore()
    for there, device in neighbours:
        if there is None:
            pl.semaphore_signal(barrier, inc=1, device_id=device, device_id_type=MESH_ID)
        else:

            @pl.when(there)
            def _(device=device):
                pl.semaphore_signal(barrier, inc=1, device_id=device, device_id_type=MESH_ID)

    pl.semaphore_wait(barrier, number)


def send(source, target, send_sem, recv_sem, device):
    return pltpu.make_async_remote_copy(
        src_ref=source, dst_ref=target, send_sem=send_sem, recv_sem=recv_sem, device_id=device, device_id_type=MESH_ID
    )


def line_ends(z):
    return jnp.where(z > 0, 1, 0) + jnp.where(z < 3, 1, 0)


def gather_kernel(own_ref, out_ref, copy_sem, right_send, right_recv, left_send, left_recv, x_send, x_recv):
    s, w, side, z, x_device, _, _ = places()
    up, down = (s + 2, w), (s - 2, w)
    copy = pltpu.make_async_copy(own_ref, out_ref.at[s], copy_sem)
    copy.start()
    greet(((None, x_device), (z < 3, up), (z > 0, down)), 1 + line_ends(z))

    def to_right(j, source, number):
        return send(source, out_ref.at[number], right_send.at[j], right_recv.at[j], up)

    def to_left(j, source, number):
        return send(source, out_ref.at[number], left_send.at[j], left_recv.at[j], down)

    def to_x(at, source, number):
        return send(source, out_ref.at[number], x_send.at[at], x_recv.at[at], x_device)

    @pl.when(z < 3)
    def _():
        to_right(0, own_ref, s).start()

    @pl.when(z > 0)
    def _():
        to_left(0, own_ref, s).start()

    to_x(z, own_ref, s).start()
    for j in (1, 2, 3):
        lower, upper = s - 2 * j, s + 2 * j

        @pl.when(z >= j)
        def _(j=j, lower=lower):
            block = out_ref.at[lower]
            to_right(j - 1, block, lower).wait_recv()

            @pl.when(z < 3)
            def _():
                to_right(j, block, lower).start()

            to_x(z - j, block, lower).start()

        @pl.when(z + j <= 3)
        def _(j=j, upper=upper):
            block = out_ref.at[upper]
            to_left(j - 1, block, upper).wait_recv()

            @pl.when(z > 0)
            def _():
                to_left(j, block, upper).start()

            to_x(z + j, block, upper).start()

    for number in range(4):
        done = to_x(number, own_ref, s)
        done.wait_send()
        done.wait_recv()
    for j in range(3):

        @pl.when((z >= j) & (z < 3))
        def _(j=j):
            to_right(j, own_ref, s).wait_send()

        @pl.when((z + j <= 3) & (z > 0))
        def _(j=j):
            to_left(j, own_ref, s).wait_send()

    copy.wait()


def gather_seq(own):
    seqs = lax.axis_size("seq")
    if seqs != 8 or lax.axis_size("wsh") != 4:
        return lax.all_gather(own, "seq", axis=0, tiled=False)
    sems = [pltpu.SemaphoreType.DMA((3,))] * 4 + [pltpu.SemaphoreType.DMA((4,))] * 2
    return pl.pallas_call(
        gather_kernel,
        in_specs=[pl.BlockSpec(memory_space=pl.ANY)],
        out_specs=pl.BlockSpec(memory_space=pl.ANY),
        out_shape=jax.ShapeDtypeStruct((seqs,) + own.shape, own.dtype),
        scratch_shapes=[pltpu.SemaphoreType.DMA] + sems,
        compiler_params=pltpu.CompilerParams(collective_id=1, has_side_effects=True),
        cost_estimate=pl.CostEstimate(flops=0, bytes_accessed=100 << 20, transcendentals=0),
        name="gather_seq",
    )(own)


def reduce_kernel(
    splits, x_ref, out_ref, x_buf, right_buf, left_buf, right_out, left_out,
    x_send, x_recv, right_send, right_recv, left_send, left_recv,
):
    s, w, side, z, x_device, _, _ = places()
    up, down = (s + 2, w), (s - 2, w)
    size = x_ref.shape[2] // splits
    columns = [slice(c * size, (c + 1) * size) for c in range(splits)]
    greet(((None, x_device), (z < 3, up), (z > 0, down)), 1 + line_ends(z))

    def to_x(target, c):
        return send(
            x_ref.at[target * 2 + 1 - side, :, columns[c]], x_buf.at[target, :, columns[c]],
            x_send.at[target, c], x_recv.at[target, c], x_device,
        )

    def start_x(target):
        for c in range(splits):
            to_x(target, c).start()

    def to_right(k, c):
        return send(
            right_out.at[k - 1, :, columns[c]], right_buf.at[k - 1, :, columns[c]],
            right_send.at[k - 1, c], right_recv.at[k - 1, c], up,
        )

    def to_left(k, c):
        return send(
            left_out.at[k - 1, :, columns[c]], left_buf.at[k - 1, :, columns[c]],
            left_send.at[k - 1, c], left_recv.at[k - 1, c], down,
        )

    def pair(target, c):
        to_x(target, c).wait_recv()
        return x_ref[target * 2 + side, :, columns[c]].astype(F32) + x_buf[target, :, columns[c]].astype(F32)

    for k in (3, 2, 1):

        @pl.when(z + k <= 3)
        def _(k=k):
            start_x(z + k)

        @pl.when(z >= k)
        def _(k=k):
            start_x(z - k)

    start_x(z)
    for k in (3, 2, 1):
        for c in range(splits):

            @pl.when(z + k <= 3)
            def _(k=k, c=c):
                right_out[k - 1, :, columns[c]] = pair(z + k, c).astype(BF16)
                if k < 3:

                    @pl.when(z > 0)
                    def _():
                        to_right(k + 1, c).wait_recv()
                        right_out[k - 1, :, columns[c]] = (
                            right_out[k - 1, :, columns[c]].astype(F32) + right_buf[k, :, columns[c]].astype(F32)
                        ).astype(BF16)

                to_right(k, c).start()

            @pl.when(z >= k)
            def _(k=k, c=c):
                left_out[k - 1, :, columns[c]] = pair(z - k, c).astype(BF16)
                if k < 3:

                    @pl.when(z < 3)
                    def _():
                        to_left(k + 1, c).wait_recv()
                        left_out[k - 1, :, columns[c]] = (
                            left_out[k - 1, :, columns[c]].astype(F32) + left_buf[k, :, columns[c]].astype(F32)
                        ).astype(BF16)

                to_left(k, c).start()

    for c in range(splits):
        out_ref[:, columns[c]] = pair(z, c)

        @pl.when(z > 0)
        def _(c=c):
            to_right(1, c).wait_recv()
            out_ref[:, columns[c]] += right_buf[0, :, columns[c]].astype(F32)

        @pl.when(z < 3)
        def _(c=c):
            to_left(1, c).wait_recv()
            out_ref[:, columns[c]] += left_buf[0, :, columns[c]].astype(F32)

    for c in range(splits):
        for target in range(4):
            to_x(target, c).wait_send()
        for k in (3, 2, 1):

            @pl.when(z + k <= 3)
            def _(k=k, c=c):
                to_right(k, c).wait_send()

            @pl.when(z >= k)
            def _(k=k, c=c):
                to_left(k, c).wait_send()


def reduce_seq(x):
    seqs, rows, width = x.shape
    if seqs != 8 or lax.axis_size("wsh") != 4:
        return jnp.sum(exchange(x, "seq").astype(F32), 0)
    splits = 2
    return pl.pallas_call(
        functools.partial(reduce_kernel, splits),
        in_specs=[pl.BlockSpec(memory_space=pltpu.VMEM)],
        out_specs=pl.BlockSpec(memory_space=pltpu.VMEM),
        out_shape=jax.ShapeDtypeStruct((rows, width), F32),
        scratch_shapes=[pltpu.VMEM((4, rows, width), BF16)]
        + [pltpu.VMEM((3, rows, width), BF16)] * 4
        + [pltpu.SemaphoreType.DMA((4, splits))] * 2
        + [pltpu.SemaphoreType.DMA((3, splits))] * 4,
        compiler_params=pltpu.CompilerParams(collective_id=2, has_side_effects=True, vmem_limit_bytes=40 << 20),
        cost_estimate=pl.CostEstimate(flops=0, bytes_accessed=120 << 20, transcendentals=0),
        name="reduce_seq",
    )(x)


def channel_kernel(
    forward, x_ref, first_hbm, second_hbm, active_hbm,
    sum_ref, all_hbm, mine_hbm, other_hbm, extra_hbm,
    first, second, rows_all, middle, active, part, core_buf, far_out, far_buf,
    load_sem, store_sem, core_send, core_recv, y_send, y_recv, x_send, x_recv, r_send, r_recv, f_send, f_recv,
):
    s, w, side, z, x_device, core_device, y_device = places()
    rows, width = x_ref.shape
    units = first.shape[0]
    half = units // 2
    loads = [
        pltpu.make_async_copy(first_hbm, first, load_sem.at[0]),
        pltpu.make_async_copy(second_hbm, second, load_sem.at[1]),
    ]
    if not forward:
        loads.append(pltpu.make_async_copy(active_hbm, active, load_sem.at[2]))
    for load in loads:
        load.start()
    rows_all[0:rows] = x_ref[...]
    greet(((None, x_device), (None, core_device), (None, y_device)), 3)

    def block(number):
        return rows_all.at[pl.ds(number * rows, rows)]

    to_core = [
        send(block(0), block(1), core_send.at[0], core_recv.at[0], core_device),
        send(block(2), block(3), core_send.at[1], core_recv.at[1], core_device),
    ]
    to_y = send(block(0), block(2), y_send, y_recv, y_device)
    if forward:
        to_x = [
            send(
                middle.at[1 - side, pl.ds(2 * n * rows, 2 * rows)], other_hbm.at[pl.ds(2 * n * rows, 2 * rows)],
                x_send.at[n], x_recv.at[n], x_device,
            )
            for n in range(2)
        ]
    else:
        to_x = [
            send(block(n), other_hbm.at[pl.ds(n * rows, rows)], x_send.at[n], x_recv.at[n], x_device) for n in range(4)
        ]
    sums_core = [
        send(part.at[pl.ds((2 * n + 1) * rows, rows)], core_buf.at[n], r_send.at[n], r_recv.at[n], core_device)
        for n in range(2)
    ]
    far = send(far_out, far_buf, f_send, f_recv, y_device)
    stores = [
        pltpu.make_async_copy(rows_all, all_hbm, store_sem.at[0]),
        pltpu.make_async_copy(middle.at[side], mine_hbm, store_sem.at[1]),
        pltpu.make_async_copy(active if forward else middle.at[1 - side], extra_hbm, store_sem.at[2]),
    ]

    def pass_on(number):
        if not forward:
            to_x[number].start()

    to_y.start()
    to_core[0].start()
    pass_on(0)
    tile = min(512, half)

    def multiply(number):
        two = pl.ds(2 * number * rows, 2 * rows)

        def up(t, carry):
            for side_units in range(2):
                at = pl.multiple_of(t * tile, tile)
                unit = pl.multiple_of(side_units * half + at, tile)
                raw = dot(rows_all[two, :], first[pl.ds(unit, tile), :], NT)
                if forward:
                    raw = jnp.maximum(raw, 0.0)
                    active[two, pl.ds(unit, tile)] = raw
                    mid = raw * raw
                else:
                    mid = raw * 2.0 * active[two, pl.ds(unit, tile)]
                middle[side_units, two, pl.ds(at, tile)] = mid.astype(BF16)
            return carry

        lax.fori_loop(0, half // tile, up, 0)
        if forward:
            to_x[number].start()
        if number == 0:
            loads[1].wait()

        def down(t, carry):
            at = pl.multiple_of(t * tile, tile)
            part[two, pl.ds(at, tile)] = dot(middle[0, two, :], second[0:half, pl.ds(at, tile)]) + dot(
                middle[1, two, :], second[half:units, pl.ds(at, tile)]
            )
            return carry

        lax.fori_loop(0, width // tile, down, 0)
        sums_core[number].start()

    loads[0].wait()
    if not forward:
        loads[2].wait()
    to_core[0].wait_recv()
    pass_on(1)
    multiply(0)
    to_y.wait_recv()
    to_core[1].start()
    pass_on(2)
    to_core[1].wait_recv()
    pass_on(3)
    stores[0].start()
    multiply(1)
    for store in stores[1:]:
        store.start()
    sums_core[1].wait_recv()
    far_out[...] = (part[2 * rows : 3 * rows] + core_buf[1]).astype(BF16)
    far.start()
    sums_core[0].wait_recv()
    sum_ref[...] = part[0:rows] + core_buf[0]
    far.wait_recv()
    sum_ref[...] += far_buf[...].astype(F32)
    for copy in to_x:
        copy.wait_recv()
    for copy in to_x + to_core + sums_core + [to_y, far]:
        copy.wait_send()
    for store in stores:
        store.wait()


def channel_stage(x, first, second, active):
    rows, width = x.shape
    units = first.shape[0]
    forward = active is None
    given = (x, first, second) if forward else (x, first, second, active)
    everything = pl.BlockSpec(memory_space=pl.ANY)
    shapes = [
        ((rows, width), F32), ((4 * rows, width), BF16), ((4 * rows, units // 2), BF16),
        ((4 * rows, units // 2 if forward else width), BF16),
        ((4 * rows, units), F32) if forward else ((4 * rows, units // 2), BF16),
    ]

    def body(*refs):
        refs = list(refs)
        if forward:
            refs.insert(3, None)
        channel_kernel(forward, *refs)

    dma = pltpu.SemaphoreType.DMA
    return pl.pallas_call(
        body,
        in_specs=[pl.BlockSpec(memory_space=pltpu.VMEM)] + [everything] * (len(given) - 1),
        out_specs=[pl.BlockSpec(memory_space=pltpu.VMEM)] + [everything] * (len(shapes) - 1),
        out_shape=[jax.ShapeDtypeStruct(s, d) for s, d in shapes],
        scratch_shapes=[
            pltpu.VMEM((units, width), BF16), pltpu.VMEM((units, width), BF16), pltpu.VMEM((4 * rows, width), BF16),
            pltpu.VMEM((2, 4 * rows, units // 2), BF16), pltpu.VMEM((4 * rows, units), F32),
            pltpu.VMEM((4 * rows, width), F32), pltpu.VMEM((2, rows, width), F32),
            pltpu.VMEM((rows, width), BF16), pltpu.VMEM((rows, width), BF16),
            dma((3,)), dma((3,)), dma((2,)), dma((2,)), dma, dma, dma((4,)), dma((4,)), dma((2,)), dma((2,)),
            dma, dma,
        ],
        compiler_params=pltpu.CompilerParams(
            collective_id=3 if forward else 4, has_side_effects=True, vmem_limit_bytes=60 << 20
        ),
        cost_estimate=pl.CostEstimate(flops=0, bytes_accessed=100 << 20, transcendentals=0),
        name="channel_forward" if forward else "channel_backward",
    )(*given)


def from_behind(x, axis, by):
    size = lax.axis_size(axis)
    pairs = [(i, i + by) for i in range(size) if 0 <= i + by < size]
    return lax.ppermute(x, axis, pairs)


def exchange(x, axis):
    return lax.all_to_all(x, axis, split_axis=0, concat_axis=0, tiled=True)


def swap(x, by):
    size = lax.axis_size("wsh")
    return lax.ppermute(x, "wsh", [(i, i ^ by) for i in range(size)])


def gather_near(x):
    if lax.axis_size("wsh") != 4:
        return lax.all_gather(x, "wsh", axis=0, tiled=True)
    across = swap(x, 2)
    beside = swap(x, 1)
    return jnp.concatenate([x, beside, across, swap(across, 1)], 0)


def beside(x):
    return lax.ppermute(x, "seq", [(i, i ^ 1) for i in range(lax.axis_size("seq"))])


def scalar_sum(x):
    if lax.axis_size("wsh") != 4:
        return jnp.sum(lax.all_gather(x.reshape(1), "wsh", axis=0, tiled=True))
    x = jnp.full((8, 128), x)
    x = x + swap(x, 1)
    return (x + swap(x, 2))[0, 0]


def near_sum(x):
    if lax.axis_size("wsh") != 4:
        return lax.psum_scatter(x, "wsh", scatter_dimension=0, tiled=True)
    rows = x.shape[0] // 4
    beside = swap(jnp.concatenate([x[rows : 2 * rows], x[3 * rows :]], 0), 1)
    far = x[2 * rows : 3 * rows] + beside[rows:]
    return x[:rows] + beside[:rows] + swap(far.astype(BF16), 2).astype(F32)


def block_sum(x):
    if lax.axis_size("wsh") != 4:
        return lax.psum_scatter(x, "wsh", scatter_dimension=0, tiled=False).astype(F32)
    kept, far = block_halves(x)
    return kept + swap(far, 2).astype(F32)


def block_halves(x):
    number = lax.axis_index("wsh")

    def block(by):
        return lax.dynamic_index_in_dim(x, number ^ by, 0, keepdims=False)

    beside = swap(jnp.stack([block(1), block(3)]), 1).astype(F32)
    return block(0).astype(F32) + beside[0], (block(2).astype(F32) + beside[1]).astype(BF16)


def local(
    tokens, first_layer_values, teacher, valid, destination, lengths,
    receptance_matrix, key_matrix, value_matrix, output_matrix,
    lowrank_down_weight, lowrank_up_weight, channel_key_weight, channel_value_weight, vectors,
):
    rows, width = tokens.shape
    seqs, parts = lax.axis_size("seq"), lax.axis_size("wsh")
    me = lax.axis_index("seq")
    group = rows * seqs
    own_width = width // seqs
    shard = width // parts
    piece = shard // seqs
    column = me * own_width

    dest_seq = destination // rows // parts
    position = dest_seq * rows + destination % rows
    digits = jnp.stack([position // DIGIT, position % DIGIT, valid], 1).astype(BF16)
    tail = jnp.pad(digits, ((0, 0), (0, EXTRA - 3)))
    given = gather_seq(jnp.concatenate([tokens, tail], 1)).reshape(group, -1)
    first_values, given = lax.optimization_barrier((first_layer_values, given))
    info = given[:, width : width + 3].astype(F32)
    places = (info[:, 0] * DIGIT + info[:, 1]).astype(jnp.int32)
    numbers = jnp.arange(group, dtype=jnp.int32)
    permute = (numbers[:, None] == places[None, :]).astype(BF16)
    total_valid = scalar_sum(jnp.sum(info[:, 2]))

    index = jnp.arange(rows, dtype=jnp.int32)
    same_dest = (dest_seq[:, None] == dest_seq[None, :]) & (index[None, :] < index[:, None])
    slot = dest_seq * (rows // seqs) + jnp.sum(same_dest.astype(jnp.int32), 1)
    arrange = (index[:, None] == slot[None, :]).astype(BF16)
    mine = (places // rows) == me
    arrival = jnp.cumsum(mine.astype(jnp.int32)) - 1
    own_rows = ((index[:, None] + me * rows) == places[None, :]).astype(BF16)
    settle = dot(own_rows, (mine[:, None] & (arrival[:, None] == index[None, :])).astype(BF16)).astype(BF16)

    first_given = exchange(
        first_values.reshape(rows, seqs, own_width).transpose(1, 0, 2), "seq"
    ).reshape(group, own_width)
    first = dot(permute, first_given).astype(BF16)

    offsets = jnp.cumsum(lengths[0]) - lengths[0]
    starts = jnp.any(numbers[:, None] == offsets[None, :], 1).astype(F32)
    segment_ids = jnp.cumsum(starts).reshape(-1, BLOCK)
    before = segment_ids[:, :1] - starts.reshape(-1, BLOCK)[:, :1]
    segments = jnp.stack(
        [segment_ids, jnp.broadcast_to(before, segment_ids.shape), jnp.broadcast_to(segment_ids[:, -1:], segment_ids.shape)]
        + [jnp.zeros_like(segment_ids)] * 5,
        1,
    ).reshape(-1, BLOCK)
    flowing = (1.0 - starts)[:, None]

    def own_columns(matrix):
        return lax.dynamic_slice_in_dim(matrix, column, own_width, 1)

    near = parts == 4
    number = lax.axis_index("wsh") if near else 0
    up_piece = lax.dynamic_slice_in_dim(lowrank_up_weight, column % shard, own_width, 0)
    total = 3 * own_width + WIDE
    weights = gather_near(
        jnp.concatenate(
            [
                own_columns(receptance_matrix), own_columns(key_matrix), own_columns(value_matrix),
                pad_ranks(lowrank_down_weight), up_piece.reshape(shard, -1),
            ],
            1,
        )
    )
    up = pad_ranks(
        lax.dynamic_slice(
            weights, (((column // shard) ^ number) * shard, total), (shard, weights.shape[1] - total)
        ).reshape(own_width, -1)
    ).T
    number = jnp.full((1,), number, jnp.int32)
    w_out = lax.all_gather(output_matrix, "wsh", axis=0, tiled=True)
    vec = lax.dynamic_slice_in_dim(vectors, column, own_width, 0)[:, 8:16].T

    balanced = dot(permute, given[:, :width]).astype(BF16)
    wide_rows = balanced.astype(F32)
    mean = jnp.mean(wide_rows, -1, keepdims=True)
    scale_one = lax.rsqrt(jnp.mean(jnp.square(wide_rows - mean), -1, keepdims=True) + 1e-05)
    stats = jnp.concatenate([mean, scale_one, flowing, flowing], 1)
    mix_vec = vectors[:, :8].T
    recept, keys, values, downs, hidden = run_project(number, balanced, stats, mix_vec, weights, own_width, parts)
    teacher_late, recept = lax.optimization_barrier((teacher, recept))
    teacher_rows = exchange(dot(arrange, teacher_late).astype(BF16).reshape(seqs, rows // seqs, width), "seq")
    inputs = (recept, keys, values, hidden, first, up, vec, segments)
    mixed_out, *saved = run_forward(*inputs)
    teacher_rows, mixed_out = lax.optimization_barrier((teacher_rows, mixed_out))
    target = dot(settle, teacher_rows.reshape(rows, width))

    mixed_rows = exchange(mixed_out.reshape(seqs, rows, own_width), "seq").transpose(1, 0, 2).reshape(rows, width)
    own = lax.dynamic_slice_in_dim(balanced, me * rows, rows, 0).astype(F32)
    own_starts = lax.dynamic_slice_in_dim(starts, me * rows, rows, 0)
    own_flowing = (1.0 - own_starts)[:, None]
    own_valid = dot(own_rows, given[:, width : width + EXTRA])[:, 2]
    residual = own + dot(mixed_rows, w_out)
    standard_two, scale_two = norm_stats(residual)
    normed_two = standard_two * vectors[:, 16] + vectors[:, 17]
    carried_two = from_behind(normed_two[-1:], "seq", 1)
    delta_two = jnp.concatenate([carried_two, normed_two[:-1]], 0) * own_flowing - normed_two
    channel_in = (normed_two + delta_two * vectors[:, 18]).astype(BF16)
    paired = near and seqs == 8
    if paired:
        summed, channel, hidden_mine, hidden_other, active = channel_stage(
            channel_in, channel_key_weight, channel_value_weight, None
        )
    else:
        channel = gather_near(channel_in)
        active = jax.nn.relu(dot(channel, channel_key_weight, NT))
        hidden_rows = jnp.square(active).astype(BF16)
        summed = near_sum(dot(hidden_rows, channel_value_weight))
    result = residual + summed
    total_tokens = group * parts
    cotangent = (result - target) * (own_valid * (total_tokens / total_valid))[:, None]
    cot_low = cotangent.astype(BF16)

    if paired:
        grad_channel, cot, pre_mine, cot_other, pre_spare = channel_stage(
            cot_low, channel_value_weight, channel_key_weight, active
        )
        channel_other, pre_other = beside(channel), beside(pre_spare)
    else:
        cot = gather_near(cot_low)
        grad_pre = (dot(cot, channel_value_weight, NT) * 2.0 * active).astype(BF16)
        grad_channel = near_sum(dot(grad_pre, channel_key_weight))
    grad_vec_mix_two = jnp.sum(grad_channel * delta_two, 0)
    shifted = grad_channel * vectors[:, 18] * own_flowing
    behind = from_behind(shifted[:1], "seq", -1)
    grad_normed_two = grad_channel * (1.0 - vectors[:, 18]) + jnp.concatenate([shifted[1:], behind], 0)
    grad_residual = cotangent + norm_back(grad_normed_two, standard_two, scale_two, vectors[:, 16])
    grad_low = grad_residual.astype(BF16)

    grad_posted = dot(grad_low, w_out, NT).astype(BF16)
    if paired:
        hidden_mine, grad_posted = lax.optimization_barrier((hidden_mine, grad_posted))
        value_part = (dot(hidden_mine, cot, TN) + dot(hidden_other, cot_other, TN)).astype(BF16)
    else:
        value_part = dot(hidden_rows, cot, TN).astype(BF16)
    grad_heads = exchange(grad_posted.reshape(rows, seqs, own_width).transpose(1, 0, 2), "seq").reshape(group, own_width)
    grad_heads, value_part, mixed_late = lax.optimization_barrier((grad_heads, value_part, mixed_rows))
    lefts = exchange(mixed_late.reshape(rows, seqs, parts, piece).transpose(2, 0, 1, 3), "wsh")
    near_grad = gather_near(grad_low)
    recept_low, keys_low, values_low, ups_low, grad_first, grad_vec_heads = run_backward(grad_heads, *inputs, saved)
    if paired:
        channel_other, pre_other, lefts, near_grad, recept_low = lax.optimization_barrier(
            (channel_other, pre_other, lefts, near_grad, recept_low)
        )
        key_part = (dot(pre_mine, channel, TN) + dot(pre_other, channel_other, TN)).astype(BF16)
    else:
        lefts, near_grad, recept_low = lax.optimization_barrier((lefts, near_grad, recept_low))
        key_part = dot(grad_pre, channel, TN).astype(BF16)
    if near:
        lefts = jnp.stack([lax.dynamic_index_in_dim(lefts, number[0] ^ k, 0, keepdims=False) for k in range(4)])
    out_part = dot(lefts.reshape(rows * parts, -1), near_grad, TN).astype(BF16)

    result_back = dot(settle, result.astype(BF16), TN).astype(BF16).reshape(seqs, rows // seqs, width)
    first_back = dot(permute, grad_first, TN).astype(BF16).reshape(seqs, rows // seqs, width)
    moved = exchange(jnp.concatenate([result_back, first_back], 1), "seq")
    recept_low, key_part, out_part = lax.optimization_barrier((recept_low, key_part, out_part))
    heads_part = lax.dynamic_update_slice_in_dim(jnp.zeros((width, 8), F32), grad_vec_heads.T, column, 0)
    vec_two = jnp.stack(
        [jnp.sum(grad_normed_two * standard_two, 0), jnp.sum(grad_normed_two, 0), grad_vec_mix_two], 1
    )
    others = jnp.concatenate([heads_part, jnp.pad(vec_two, ((0, 0), (0, 13)))], 1)
    scaled_grad, sums, wide, up_grad = run_unproject(
        number, balanced, stats, mix_vec, weights, others, (recept_low, keys_low, values_low), ups_low, hidden, downs, up, parts
    )
    moved, sums = lax.optimization_barrier((moved, sums))
    output = dot(arrange, moved[:, : rows // seqs].reshape(rows, width), TN).astype(BF16)
    grad_first_rows = moved[:, rows // seqs :].reshape(seqs, rows, own_width).transpose(1, 0, 2).reshape(rows, width)

    if paired:
        halves_out = out_part.reshape(seqs // 2, 2, piece, width)
        x_side = me % 2
        out_mine = lax.dynamic_index_in_dim(halves_out, x_side, 1, keepdims=False).astype(F32)
        out_other = beside(lax.dynamic_index_in_dim(halves_out, 1 - x_side, 1, keepdims=False))
        out_half = (out_mine + out_other.astype(F32)).astype(BF16).reshape(-1, width)
        lines = [[0, 2, 4, 6], [1, 3, 5, 7]]
        turned = [
            ((z * 2 + x) * 4 + w, (w * 2 + x) * 4 + z) for z in range(4) for x in range(2) for w in range(4)
        ]

        def along(part):
            return lax.psum_scatter(part, "seq", scatter_dimension=0, tiled=True, axis_index_groups=lines)

        def turn(part):
            return lax.ppermute(part, ("seq", "wsh"), turned).astype(F32)

        grad_ffn_value, grad_ffn_key = turn(along(value_part)), turn(along(key_part))
        grad_out = along(out_half).astype(F32)
    else:
        moves = [(s * parts + w, w * seqs + s) for s in range(seqs) for w in range(parts)]

        def ffn_grad(part):
            part = lax.psum_scatter(part, "seq", scatter_dimension=0, tiled=True)
            return lax.ppermute(part, ("seq", "wsh"), moves).astype(F32)

        grad_ffn_value, grad_ffn_key = ffn_grad(value_part), ffn_grad(key_part)
        grad_out = lax.psum_scatter(out_part, "seq", scatter_dimension=0, tiled=True).astype(F32)

    standard = (balanced.astype(F32) - mean) * scale_one
    grad_balanced = scale_one * (scaled_grad - sums[:, :1] * (1.0 / width) - standard * (sums[:, 1:] * (1.0 / width)))
    mine_rows = lax.dynamic_slice_in_dim(grad_balanced, me * rows, rows, 0) + grad_residual
    grad_balanced = lax.dynamic_update_slice_in_dim(grad_balanced, mine_rows, me * rows, 0)
    grad_given = dot(permute, grad_balanced.astype(BF16), TN).astype(BF16).reshape(seqs, rows, width)
    if near:
        kept_part, far = block_halves(wide)
        grad_given, far = lax.optimization_barrier((grad_given, far))
        wide_part = kept_part + swap(far, 2).astype(F32)
    else:
        wide_part = block_sum(wide)
    grad_tokens = reduce_seq(grad_given).astype(BF16)
    wide_part, grad_tokens = lax.optimization_barrier((wide_part, grad_tokens))
    wide_all = exchange(wide_part.astype(BF16), "seq").astype(F32)

    def square(at):
        taken = wide_all[:, :, at * own_width : (at + 1) * own_width]
        return taken.transpose(1, 0, 2).reshape(piece, width)

    narrow = jnp.sum(wide_all[:, :, 3 * own_width :], 0)
    grad_down = unpad_ranks(narrow)
    grad_vectors = narrow[:, RANKS[0] : RANKS[0] + vectors.shape[1]]
    up_part = unpad_ranks(block_sum(up_grad.reshape(parts, piece, WIDE)))

    return (
        output, grad_tokens, grad_first_rows,
        square(0), square(1), square(2),
        grad_out, grad_down, up_part,
        grad_ffn_key, grad_ffn_value, grad_vectors,
    )


def solution(mesh):
    both, shard = P(("seq", "wsh"), None), P("wsh", None)
    flat = P(("seq", "wsh"))
    return jax.shard_map(
        local,
        mesh=mesh,
        in_specs=(both, both, both, flat, flat) + (shard,) * 9 + (P(),),
        out_specs=(both,) * 12,
        check_vma=False,
    )
```

```python
import functools

import jax
import jax.numpy as jnp
from jax import lax
from jax.experimental import pallas as pl
from jax.experimental.pallas import tpu as pltpu
from jax.sharding import PartitionSpec as P

HEAD = 64
BLOCK = 64
RANKS = (96, 96, 64, 256)
PADDED = (128, 128, 128, 256)
OFFSETS = (0, 128, 256, 384)
WIDE = 640
EXTRA = 128
DIGIT = 64

F32 = jnp.float32
BF16 = jnp.bfloat16

NN = (((1,), (0,)), ((), ()))
NT = (((1,), (1,)), ((), ()))
TN = (((0,), (0,)), ((), ()))


def dot(a, b, dims=NN):
    return lax.dot_general(a, b, dims, preferred_element_type=F32)


def halves(x):
    high = x.astype(BF16)
    return high, (x - high.astype(F32)).astype(BF16)


def dot3(a, b, dims=NN):
    a_high, a_low = halves(a)
    b_high, b_low = halves(b)
    return dot(a_high, b_high, dims) + (dot(a_high, b_low, dims) + dot(a_low, b_high, dims))


def sum_left(mask, x):
    high, low = halves(x)
    low_two = (x - high.astype(F32) - low.astype(F32)).astype(BF16)
    return dot(mask, high) + (dot(mask, low) + dot(mask, low_two))


def head_sum(x, ones):
    high, low = halves(x)
    return dot(high, ones) + dot(low, ones)


def low(x):
    return x.astype(BF16).astype(F32)


def iotas(rows, columns):
    return (
        lax.broadcasted_iota(jnp.int32, (rows, columns), 0),
        lax.broadcasted_iota(jnp.int32, (rows, columns), 1),
    )


def head_ones(width):
    i, j = iotas(width, width)
    return jnp.where((i >> 6) == (j >> 6), 1.0, 0.0).astype(BF16)


def front(keys, values, hidden, up, first, vec, ones):
    z = vec[0:1] + dot(hidden[:, 0:128], up[0:128])
    decay_log = -(jnp.maximum(-z, 0.0) + jnp.log1p(jnp.exp(-jnp.abs(z)))) - 0.5
    rate = jax.nn.sigmoid(vec[1:2] + dot(hidden[:, 128:256], up[128:256]))
    blend = jax.nn.sigmoid(vec[2:3] + dot(hidden[:, 256:384], up[256:384]))
    gate = dot(hidden[:, 384:640], up[384:640])
    mixed_value = values + (first - values) * blend
    scaled = keys * vec[3:4]
    scale = lax.rsqrt(head_sum(scaled * scaled, ones) + 1e-06)
    key_dir = scaled * scale
    key_mod = keys * (1.0 + (rate - 1.0) * vec[4:5])
    return z, decay_log, rate, blend, gate, mixed_value, scale, key_dir, key_mod


def block_masks(segments):
    i, j = iotas(BLOCK, BLOCK)
    across = jnp.broadcast_to(segments[0:1], (BLOCK, BLOCK))
    down = across.T
    before = jnp.broadcast_to(segments[1:2], (BLOCK, BLOCK))
    last = jnp.broadcast_to(segments[2:3], (BLOCK, BLOCK))
    same = across == down
    strict = jnp.where(same & (i > j), 1.0, 0.0)
    closed = jnp.where(same & (i >= j), 1.0, 0.0)
    carry = jnp.where(down == before, 1.0, 0.0)
    tail = jnp.where(down == last, 1.0, 0.0)
    keep = jnp.where(segments[2:3] == segments[1:2], 1.0, 0.0)
    quad = jnp.concatenate(
        [jnp.concatenate([strict, strict], 1), jnp.concatenate([closed, closed], 1)], 0
    )
    return quad, carry, tail, keep


def tile_heads(x, heads):
    return jnp.concatenate([x] * heads, 1) if heads > 1 else x


def join(pieces, axis):
    return jnp.concatenate(pieces, axis) if len(pieces) > 1 else pieces[0]


def decayed(decay_low, key_low, dir_low, rate_low, recept_low, carry, tail):
    i, j = iotas(BLOCK, BLOCK)
    lower = jnp.where(i >= j, 1.0, 0.0).astype(BF16)
    log_step = -jnp.exp(decay_low)
    total = sum_left(lower, log_step)
    before = jnp.exp(total - log_step)
    grown = jnp.exp(total)
    shrunk = jnp.exp(-total)
    end = total[BLOCK - 1 : BLOCK]
    tail_decay = jnp.exp(end - total) * tail
    alpha = -dir_low * before
    beta_plain = dir_low * rate_low
    beta = beta_plain * shrunk
    key = key_low * shrunk
    recept = recept_low * grown
    return dict(
        log_step=log_step, before=before, grown=grown, shrunk=shrunk, end=jnp.exp(end), tail=tail_decay,
        alpha=alpha, beta_plain=beta_plain, beta=beta, key=key, recept=recept,
        beta_end=beta_plain * tail_decay, key_end=key_low * tail_decay,
        alpha_in=alpha * carry, recept_in=recept * carry,
    )


def unit_inverses(lowers):
    i, j = iotas(BLOCK, BLOCK)
    eye = jnp.where(i == j, 1.0, 0.0)

    def within(size):
        return (i // size) == (j // size)

    smalls = [jnp.where(within(4), x, 0.0) for x in lowers]
    low_smalls = [x.astype(BF16) for x in smalls]
    twos = [dot(x, x) for x in low_smalls]
    inverses = [eye + x for x in smalls]
    inverses = [x + dot(x.astype(BF16), y.astype(BF16)) for x, y in zip(inverses, twos)]
    for size in (8, 16, 32, 64):
        mask = within(size) & ~within(size // 2)
        offs = [jnp.where(mask, x, 0.0).astype(BF16) for x in lowers]
        lows = [x.astype(BF16) for x in inverses]
        inner = [dot(x, y).astype(BF16) for x, y in zip(offs, lows)]
        inverses = [x + dot(y, z) for x, y, z in zip(inverses, lows, inner)]
    errors = [eye - x + dot3(y, x) for x, y in zip(inverses, lowers)]
    return [x + dot(x.astype(BF16), y.astype(BF16)) for x, y in zip(inverses, errors)]


def post_norm(head_low, ones):
    centered = head_low - head_sum(head_low, ones) * (1.0 / HEAD)
    spread = lax.rsqrt(head_sum(centered * centered, ones) * (1.0 / HEAD) + HEAD * 1e-05)
    return centered * spread, spread


def forward_kernel(
    count, recept_ref, keys_ref, values_ref, hidden_ref, first_ref, up_ref, vec_ref, segment_ref,
    mixed_ref, head_ref, state_ref, inverse_ref, removed_ref, state,
):
    width = recept_ref.shape[1]
    heads = width // HEAD

    @pl.when(pl.program_id(0) == 0)
    def _():
        state[...] = jnp.zeros_like(state)

    ones = head_ones(width)
    vec = vec_ref[...]
    up = up_ref[...]
    columns = [slice(head * HEAD, (head + 1) * HEAD) for head in range(heads)]
    done = []
    for block in range(count):
        rows = slice(block * BLOCK, (block + 1) * BLOCK)
        recept, keys, values = recept_ref[rows], keys_ref[rows], values_ref[rows]
        _, decay_log, rate, _, gate, mixed_value, _, key_dir, key_mod = front(
            keys, values, hidden_ref[rows], up, first_ref[rows].astype(F32), vec, ones
        )
        quad, carry, tail, keep = block_masks(segment_ref[block * 8 : block * 8 + 8])
        parts = decayed(
            low(decay_log), low(key_mod), low(key_dir), low(rate), low(recept),
            tile_heads(carry, heads), tile_heads(tail, heads),
        )
        lefts = [jnp.concatenate([parts["alpha"][:, c], parts["recept"][:, c]], 0) for c in columns]
        rights = [jnp.concatenate([parts["beta"][:, c], parts["key"][:, c]], 0) for c in columns]
        pairs = [quad * dot3(x, y, NT) for x, y in zip(lefts, rights)]
        done.append((rows, recept, key_mod, gate, mixed_value, keep, parts, pairs))
    inverses = unit_inverses([x[:BLOCK, :BLOCK] for item in done for x in item[-1]])
    for block, (rows, recept, key_mod, gate, mixed_value, keep, parts, pairs) in enumerate(done):
        mine = inverses[block * heads : (block + 1) * heads]
        value_low = low(mixed_value)
        owns = [value_low[:, c] for c in columns]
        by_values = [dot3(x[:, BLOCK:], y) for x, y in zip(pairs, owns)]
        ends = [jnp.concatenate([parts["beta_end"][:, c], parts["key_end"][:, c]], 0) for c in columns]
        inners = [jnp.concatenate([parts["alpha_in"][:, c], parts["recept_in"][:, c]], 0) for c in columns]
        entering = state[...]
        state_ref[rows] = entering
        nows = [entering[:, c] for c in columns]
        inwards = [dot3(x, y, NT) for x, y in zip(inners, nows)]
        removals = [dot3(x, y[:BLOCK] + z[:BLOCK]) for x, y, z in zip(mine, inwards, by_values)]
        outs = [
            y[BLOCK:] + z[BLOCK:] + dot3(x[BLOCK:, :BLOCK], r)
            for x, y, z, r in zip(pairs, inwards, by_values, removals)
        ]
        leaving = [
            x * (parts["end"][:, c] * keep) + dot3(jnp.concatenate([r, v], 0), e, TN)
            for x, c, r, v, e in zip(nows, columns, removals, owns, ends)
        ]
        state[...] = join(leaving, 1)
        inverse_ref[rows] = join(mine, 1)
        removed_ref[rows] = join(removals, 1)
        head_low = join(outs, 1).astype(BF16)
        head_ref[rows] = head_low
        normed, _ = post_norm(head_low.astype(F32), ones)
        bonus = head_sum(recept * key_mod * vec[5:6], ones) * mixed_value
        mixed_ref[rows] = ((normed * vec[6:7] + vec[7:8] + bonus) * gate).astype(BF16)


def backward_kernel(
    count, grad_ref, recept_ref, keys_ref, values_ref, hidden_ref, first_ref, up_ref, vec_ref, segment_ref,
    head_ref, state_ref, inverse_ref, removed_ref,
    recept_out, keys_out, values_out, ups_out, first_out, vec_out, state,
):
    width = recept_ref.shape[1]
    heads = width // HEAD

    @pl.when(pl.program_id(0) == 0)
    def _():
        state[...] = jnp.zeros_like(state)
        vec_out[...] = jnp.zeros_like(vec_out)

    ones = head_ones(width)
    vec = vec_ref[...]
    up = up_ref[...]
    i, j = iotas(BLOCK, BLOCK)
    upper = jnp.where(i <= j, 1.0, 0.0).astype(BF16)
    columns = [slice(head * HEAD, (head + 1) * HEAD) for head in range(heads)]
    order = range(count - 1, -1, -1)
    kept = {}
    for block in order:
        rows = slice(block * BLOCK, (block + 1) * BLOCK)
        recept, keys, values = recept_ref[rows], keys_ref[rows], values_ref[rows]
        first = first_ref[rows].astype(F32)
        z, decay_log, rate, blend, gate, mixed_value, scale, key_dir, key_mod = front(
            keys, values, hidden_ref[rows], up, first, vec, ones
        )
        quad, carry, tail, keep = block_masks(segment_ref[block * 8 : block * 8 + 8])
        rate_low, dir_low = low(rate), low(key_dir)
        parts = decayed(
            low(decay_log), low(key_mod), dir_low, rate_low, low(recept),
            tile_heads(carry, heads), tile_heads(tail, heads),
        )
        value_low = low(mixed_value)

        grad = grad_ref[rows].astype(F32)
        normed, spread = post_norm(head_ref[rows].astype(F32), ones)
        product = recept * key_mod
        coefficient = head_sum(product * vec[5:6], ones)
        grad_gate = grad * (normed * vec[6:7] + vec[7:8] + coefficient * mixed_value)
        opened = grad * gate
        grad_normed = opened * vec[6:7]
        grad_head = spread * (
            grad_normed
            - head_sum(grad_normed, ones) * (1.0 / HEAD)
            - normed * (head_sum(grad_normed * normed, ones) * (1.0 / HEAD))
        )
        grad_coefficient = head_sum(opened * mixed_value, ones)
        weighted = grad_coefficient * vec[5:6]
        head_grad = low(grad_head)

        lefts = [jnp.concatenate([parts["alpha"][:, c], parts["recept"][:, c]], 0) for c in columns]
        rights = [jnp.concatenate([parts["beta"][:, c], parts["key"][:, c]], 0) for c in columns]
        ends = [jnp.concatenate([parts["beta_end"][:, c], parts["key_end"][:, c]], 0) for c in columns]
        inners = [jnp.concatenate([parts["alpha_in"][:, c], parts["recept_in"][:, c]], 0) for c in columns]
        pairs = [quad * dot3(x, y, NT) for x, y in zip(lefts, rights)]
        out_grads = [head_grad[:, c] for c in columns]
        through = [dot3(x[BLOCK:, :BLOCK], y, TN) for x, y in zip(pairs, out_grads)]
        kept[block] = dict(
            rows=rows, recept=recept, keys=keys, values=values, first=first, z=z, rate=rate, blend=blend,
            mixed_value=mixed_value, scale=scale, key_dir=key_dir, key_mod=key_mod, quad=quad, carry=carry, keep=keep,
            rate_low=rate_low, dir_low=dir_low, parts=parts, value_low=value_low, normed=normed, product=product,
            grad_gate=grad_gate, opened=opened, grad_coefficient=grad_coefficient,
            grad_mixed_value=opened * coefficient, grad_recept=weighted * key_mod, grad_key_mod=weighted * recept,
            lefts=lefts, rights=rights, ends=ends, inners=inners, pairs=pairs, out_grads=out_grads, through=through,
        )
    for block in order:
        k = kept[block]
        after, entering, inverse_all = state[...], state_ref[k["rows"]], inverse_ref[k["rows"]]
        laters, nows = [after[:, c] for c in columns], [entering[:, c] for c in columns]
        from_ends = [dot3(x, y, NT) for x, y in zip(k["ends"], laters)]
        inner_grads = [
            dot3(inverse_all[:, c], x + y[:BLOCK], TN) for c, x, y in zip(columns, k["through"], from_ends)
        ]
        boths = [jnp.concatenate([x, y], 0) for x, y in zip(inner_grads, k["out_grads"])]
        stays = [x * (k["parts"]["end"][:, c] * k["keep"]) for x, c in zip(laters, columns)]
        state[...] = join([x + dot3(y, z, TN) for x, y, z in zip(stays, boths, k["inners"])], 1)
        k.update(
            laters=laters, nows=nows, from_ends=from_ends, boths=boths,
            end_sum=join([jnp.sum(x * y, 0, keepdims=True) for x, y in zip(nows, stays)], 1),
        )
    vec_total = jnp.zeros_like(vec)
    for block in order:
        k = kept[block]
        rows, parts, quad = k["rows"], k["parts"], k["quad"]
        removed_all = removed_ref[rows]
        carry_two = jnp.concatenate([k["carry"], k["carry"]], 0)
        sources = [jnp.concatenate([removed_all[:, c], k["value_low"][:, c]], 0) for c in columns]
        grad_pairs = [quad * dot3(x, y, NT) for x, y in zip(k["boths"], sources)]
        grad_values = [
            dot3(x[:, BLOCK:], y, TN) + z[BLOCK:] for x, y, z in zip(k["pairs"], k["boths"], k["from_ends"])
        ]
        grad_ends = [dot3(x, y) for x, y in zip(sources, k["laters"])]
        to_state = [carry_two * dot3(x, y) for x, y in zip(k["boths"], k["nows"])]
        grad_lefts = [dot3(x, y) + z for x, y, z in zip(grad_pairs, k["rights"], to_state)]
        grad_rights = [dot3(x, y, TN) for x, y in zip(grad_pairs, k["lefts"])]
        d_alpha, d_recept = join([x[:BLOCK] for x in grad_lefts], 1), join([x[BLOCK:] for x in grad_lefts], 1)
        d_beta, d_key = join([x[:BLOCK] for x in grad_rights], 1), join([x[BLOCK:] for x in grad_rights], 1)
        d_beta_end, d_key_end = join([x[:BLOCK] for x in grad_ends], 1), join([x[BLOCK:] for x in grad_ends], 1)
        ended = parts["beta_end"] * d_beta_end + parts["key_end"] * d_key_end
        alphas = parts["alpha"] * d_alpha
        d_total = parts["recept"] * d_recept - parts["beta"] * d_beta - parts["key"] * d_key - ended + alphas
        d_step = sum_left(upper, d_total) + (jnp.sum(ended, 0, keepdims=True) + k["end_sum"]) - alphas
        d_beta_plain = d_beta * parts["shrunk"] + d_beta_end * parts["tail"]
        copy_decay = low(d_step * parts["log_step"])
        copy_dir = low(d_beta_plain * k["rate_low"] - d_alpha * parts["before"])
        copy_rate = low(d_beta_plain * k["dir_low"])

        keys, values, rate, blend = k["keys"], k["values"], k["rate"], k["blend"]
        grad_recept = k["grad_recept"] + low(d_recept * parts["grown"])
        grad_key_mod = k["grad_key_mod"] + low(d_key * parts["shrunk"] + d_key_end * parts["tail"])
        grad_mixed_value = k["grad_mixed_value"] + low(join(grad_values, 1))
        grad_z = copy_decay * jax.nn.sigmoid(-k["z"])
        factor = 1.0 + (rate - 1.0) * vec[4:5]
        keyed = grad_key_mod * keys
        grad_rate = copy_rate + keyed * vec[4:5]
        grad_scaled = k["scale"] * (copy_dir - k["key_dir"] * head_sum(copy_dir * k["key_dir"], ones))
        grad_keys = grad_key_mod * factor + grad_scaled * vec[3:4]
        grad_rate_up = grad_rate * rate * (1.0 - rate)
        grad_value_up = grad_mixed_value * (k["first"] - values) * blend * (1.0 - blend)
        recept_out[rows] = grad_recept.astype(BF16)
        keys_out[rows] = grad_keys.astype(BF16)
        values_out[rows] = (grad_mixed_value * (1.0 - blend)).astype(BF16)
        first_out[rows] = (grad_mixed_value * blend).astype(BF16)
        ups_out[0, rows] = grad_z.astype(BF16)
        ups_out[1, rows] = grad_rate_up.astype(BF16)
        ups_out[2, rows] = grad_value_up.astype(BF16)
        ups_out[3, rows] = k["grad_gate"].astype(BF16)

        def total(x):
            return jnp.sum(x, 0, keepdims=True)

        vec_total = vec_total + jnp.concatenate(
            [
                total(grad_z), total(grad_rate_up), total(grad_value_up), total(grad_scaled * keys),
                total(keyed * (rate - 1.0)), total(k["grad_coefficient"] * k["product"]),
                total(k["opened"] * k["normed"]), total(k["opened"]),
            ],
            0,
        )
    vec_out[...] += vec_total


def kernel_cost(rows, width, passes):
    return pl.CostEstimate(flops=2 * rows * width * width, bytes_accessed=4 * rows * width * passes, transcendentals=0)


def per_step(rows, most):
    return most if (rows // BLOCK) % most == 0 else 1


def run_forward(recept, keys, values, hidden, first, up, vec, segments):
    rows, width = recept.shape
    count = per_step(rows, 4)
    step = count * BLOCK

    def spec(columns):
        return pl.BlockSpec((step, columns), lambda i: (i, 0))

    def whole(array):
        return pl.BlockSpec(array.shape, lambda i: (0, 0))

    return pl.pallas_call(
        functools.partial(forward_kernel, count),
        grid=(rows // step,),
        in_specs=[
            spec(width), spec(width), spec(width), spec(WIDE), spec(width), whole(up), whole(vec),
            pl.BlockSpec((count * 8, BLOCK), lambda i: (i, 0)),
        ],
        out_specs=[spec(width)] * 5,
        out_shape=[jax.ShapeDtypeStruct((rows, width), d) for d in (BF16, BF16, F32, F32, F32)],
        scratch_shapes=[pltpu.VMEM((BLOCK, width), F32)],
        compiler_params=pltpu.CompilerParams(vmem_limit_bytes=48 << 20),
        cost_estimate=kernel_cost(rows, width, 110),
        name="mix_forward",
    )(recept, keys, values, hidden, first, up, vec, segments)


def run_backward(grad, recept, keys, values, hidden, first, up, vec, segments, saved):
    rows, width = recept.shape
    count = per_step(rows, 2)
    step = count * BLOCK
    last = rows // step - 1

    def spec(columns):
        return pl.BlockSpec((step, columns), lambda i: (last - i, 0))

    def whole(array):
        return pl.BlockSpec(array.shape, lambda i: (0, 0))

    return pl.pallas_call(
        functools.partial(backward_kernel, count),
        grid=(rows // step,),
        in_specs=[
            spec(width), spec(width), spec(width), spec(width), spec(WIDE), spec(width), whole(up), whole(vec),
            pl.BlockSpec((count * 8, BLOCK), lambda i: (last - i, 0)),
            spec(width), spec(width), spec(width), spec(width),
        ],
        out_specs=[
            spec(width), spec(width), spec(width),
            pl.BlockSpec((4, step, width), lambda i: (0, last - i, 0)),
            spec(width), pl.BlockSpec((8, width), lambda i: (0, 0)),
        ],
        out_shape=[
            jax.ShapeDtypeStruct((rows, width), BF16), jax.ShapeDtypeStruct((rows, width), BF16),
            jax.ShapeDtypeStruct((rows, width), BF16), jax.ShapeDtypeStruct((4, rows, width), BF16),
            jax.ShapeDtypeStruct((rows, width), BF16), jax.ShapeDtypeStruct((8, width), F32),
        ],
        scratch_shapes=[pltpu.VMEM((BLOCK, width), F32)],
        compiler_params=pltpu.CompilerParams(vmem_limit_bytes=48 << 20),
        cost_estimate=kernel_cost(rows, width, 150),
        name="mix_backward",
    )(grad, recept, keys, values, hidden, first, up, vec, segments, *saved)


def mix_norm(block_ref, stats_ref, vec_ref):
    stats = stats_ref[...]
    flowing = stats[:, 2:3]
    standard = (block_ref[...].astype(F32) - stats[:, 0:1]) * stats[:, 1:2]
    normed = standard * vec_ref[0:1] + vec_ref[1:2]
    delta = pltpu.roll(normed, 1, 0) * flowing - normed
    return standard, normed, delta, flowing


def project_kernel(
    width, block_ref, stats_ref, vec_ref, weight_ref,
    recept_ref, keys_ref, values_ref, downs_ref, hidden_ref,
):
    base = 3 * width
    _, normed, delta, _ = mix_norm(block_ref, stats_ref, vec_ref)
    weight = weight_ref[...]
    uses = (
        ((recept_ref, 0, width, 0),),
        ((downs_ref, base + OFFSETS[0], PADDED[0], OFFSETS[0]),),
        ((keys_ref, width, width, 0),),
        ((values_ref, 2 * width, width, 0), (downs_ref, base + OFFSETS[2], PADDED[2], OFFSETS[2])),
        ((downs_ref, base + OFFSETS[1], PADDED[1], OFFSETS[1]),),
        ((downs_ref, base + OFFSETS[3], PADDED[3], OFFSETS[3]),),
    )

    @pl.when(pl.program_id(0) == 0)
    def _():
        for ref in (recept_ref, keys_ref, values_ref, downs_ref):
            ref[...] = jnp.zeros_like(ref)

    for c, targets in enumerate(uses):
        mixed = (normed + delta * vec_ref[2 + c : 3 + c]).astype(BF16)
        for ref, start, size, at in targets:
            ref[:, at : at + size] += dot(mixed, weight[:, start : start + size])

    @pl.when(pl.program_id(0) == pl.num_programs(0) - 1)
    def _():
        hidden_ref[:, 0:128] = jnp.tanh(downs_ref[:, 0:128]).astype(BF16)
        hidden_ref[:, 128:384] = downs_ref[:, 128:384].astype(BF16)
        hidden_ref[:, 384:640] = jax.nn.sigmoid(downs_ref[:, 384:640]).astype(BF16)


def unproject_kernel(
    width, parts, piece, block_ref, stats_ref, vec_ref, weight_ref,
    other_ref, recept_ref, keys_ref, values_ref, ups_ref, hidden_ref, downs_ref, up_ref,
    grad_ref, sums_ref, wide_ref, up_out, down_lows,
):
    rows = block_ref.shape[0]
    base = 3 * width

    @pl.when(pl.program_id(0) == 0)
    def _():
        sums_ref[...] = jnp.zeros_like(sums_ref)
        for k, (at, size) in enumerate(zip(OFFSETS, PADDED)):
            cols = slice(at, at + size)
            grad = dot(ups_ref[k], up_ref[cols], NT)
            if k == 0:
                grad = grad * (1.0 - jnp.square(jnp.tanh(downs_ref[:, cols])))
            if k == 3:
                opening = jax.nn.sigmoid(downs_ref[:, cols])
                grad = grad * opening * (1.0 - opening)
            down_lows[:, cols] = grad.astype(BF16)
            up_out[:, cols] = dot(ups_ref[k], hidden_ref[:, cols], TN).astype(BF16)

    standard, normed, delta, flowing = mix_norm(block_ref, stats_ref, vec_ref)
    weight = weight_ref[...]

    def down(k):
        return (down_lows[:, OFFSETS[k] : OFFSETS[k] + PADDED[k]], base + OFFSETS[k], PADDED[k])

    uses = (
        ((recept_ref[...], 0, width),),
        (down(0),),
        ((keys_ref[...], width, width),),
        ((values_ref[...], 2 * width, width), down(2)),
        (down(1),),
        (down(3),),
    )
    kept, sent, vec_rows = None, None, []
    per_seq = parts * piece
    for c, sources in enumerate(uses):
        share = vec_ref[2 + c : 3 + c]
        mixed = (normed + delta * share).astype(BF16)
        grad = None
        for source, start, size in sources:
            part = dot(source, weight[:, start : start + size], NT)
            grad = part if grad is None else grad + part
            product = dot(mixed, source, TN).astype(BF16)
            for number in range(product.shape[0] // per_seq):
                for w in range(parts):
                    at = number * per_seq + w * piece
                    wide_ref[w, number, :, start : start + size] = product[at : at + piece]
        vec_rows.append(jnp.sum(grad * delta, 0, keepdims=True))
        moved = grad * share
        kept = grad - moved if kept is None else kept + (grad - moved)
        sent = moved if sent is None else sent + moved
    grad = kept + pltpu.roll(sent * flowing, rows - 1, 0)
    vec_rows = jnp.concatenate(
        [jnp.sum(grad * standard, 0, keepdims=True), jnp.sum(grad, 0, keepdims=True)] + vec_rows, 0
    )
    spare = jnp.concatenate([vec_rows.T, other_ref[...]], 1).astype(BF16)
    for number in range(spare.shape[0] // per_seq):
        for w in range(parts):
            at = number * per_seq + w * piece
            wide_ref[w, number, :, base + RANKS[0] : base + PADDED[0]] = spare[at : at + piece]
    scaled = grad * vec_ref[0:1]
    sums_ref[:, 0:1] += jnp.sum(scaled, 1, keepdims=True)
    sums_ref[:, 1:2] += jnp.sum(scaled * standard, 1, keepdims=True)
    grad_ref[...] = scaled


def mix_specs(rows, width, own_width, parts):
    block = 256 if rows <= 1024 else 128

    def columns(height):
        return pl.BlockSpec((height, block), lambda j: (0, j))

    def whole(shape):
        return pl.BlockSpec(shape, lambda j: (0,) * len(shape))

    def weights(array):
        size = array.shape[1] if rows > 1024 else 3 * own_width + WIDE
        return pl.BlockSpec((block, size), lambda j: (j, 0))

    return block, columns, whole, weights


def run_project(balanced, stats, vec, weights, own_width, parts):
    rows, width = balanced.shape
    block, columns, whole, weight_spec = mix_specs(rows, width, own_width, parts)
    shapes = [(rows, own_width)] * 3 + [(rows, WIDE)] * 2
    return pl.pallas_call(
        functools.partial(project_kernel, own_width),
        grid_spec=pltpu.PrefetchScalarGridSpec(
            num_scalar_prefetch=0,
            grid=(width // block,),
            in_specs=[columns(rows), whole(stats.shape), columns(8), weight_spec(weights)],
            out_specs=[whole(s) for s in shapes],
        ),
        out_shape=[jax.ShapeDtypeStruct(s, d) for s, d in zip(shapes, (F32, F32, F32, F32, BF16))],
        compiler_params=pltpu.CompilerParams(vmem_limit_bytes=60 << 20),
        cost_estimate=kernel_cost(rows, own_width, 60),
        name="mix_project",
    )(balanced, stats, vec, weights)


def run_unproject(balanced, stats, vec, weights, others, lows, ups, hidden, downs, up, parts):
    rows, width = balanced.shape
    own_width = lows[0].shape[1]
    seqs = width // own_width
    piece = own_width // parts
    block, columns, whole, weight_spec = mix_specs(rows, width, own_width, parts)
    taken = block // own_width
    total = 3 * own_width + WIDE
    return pl.pallas_call(
        functools.partial(unproject_kernel, own_width, parts, piece),
        grid_spec=pltpu.PrefetchScalarGridSpec(
            num_scalar_prefetch=0,
            grid=(width // block,),
            in_specs=[
                columns(rows), whole(stats.shape), columns(8), weight_spec(weights),
                pl.BlockSpec((block, others.shape[1]), lambda j: (j, 0)),
            ]
            + [whole(a.shape) for a in (*lows, ups, hidden, downs, up)],
            out_specs=[
                columns(rows), whole((rows, 2)),
                pl.BlockSpec((parts, taken, piece, total), lambda j: (0, j, 0, 0)),
                whole((own_width, WIDE)),
            ],
            scratch_shapes=[pltpu.VMEM((rows, WIDE), BF16)],
        ),
        out_shape=[
            jax.ShapeDtypeStruct((rows, width), F32), jax.ShapeDtypeStruct((rows, 2), F32),
            jax.ShapeDtypeStruct((parts, seqs, piece, total), BF16),
            jax.ShapeDtypeStruct((own_width, WIDE), BF16),
        ],
        compiler_params=pltpu.CompilerParams(vmem_limit_bytes=60 << 20),
        cost_estimate=kernel_cost(rows, own_width, 120),
        name="mix_unproject",
    )(balanced, stats, vec, weights, others, *lows, ups, hidden, downs, up)


def norm_stats(values):
    centered = values - jnp.mean(values, -1, keepdims=True)
    scale = lax.rsqrt(jnp.mean(centered * centered, -1, keepdims=True) + 1e-05)
    return centered * scale, scale


def norm_back(grad, standard, scale, gain):
    scaled = grad * gain
    return scale * (
        scaled
        - jnp.mean(scaled, -1, keepdims=True)
        - standard * jnp.mean(scaled * standard, -1, keepdims=True)
    )


def pad_ranks(matrix):
    pieces, start = [], 0
    for rank, padded in zip(RANKS, PADDED):
        pieces.append(jnp.pad(matrix[:, start : start + rank], ((0, 0), (0, padded - rank))))
        start += rank
    return jnp.concatenate(pieces, 1)


def unpad_ranks(matrix):
    return jnp.concatenate([matrix[..., o : o + r] for o, r in zip(OFFSETS, RANKS)], -1)


MESH_ID = pl.DeviceIdType.MESH


def places():
    s, w = lax.axis_index("seq"), lax.axis_index("wsh")
    side = s % 2
    return s, w, side, s // 2, (s + 1 - 2 * side, w), (s, w + 1 - 2 * (w % 2)), (s, w + 2 - 4 * (w // 2))


def greet(neighbours, number):
    barrier = pltpu.get_barrier_semaphore()
    for there, device in neighbours:
        if there is None:
            pl.semaphore_signal(barrier, inc=1, device_id=device, device_id_type=MESH_ID)
        else:

            @pl.when(there)
            def _(device=device):
                pl.semaphore_signal(barrier, inc=1, device_id=device, device_id_type=MESH_ID)

    pl.semaphore_wait(barrier, number)


def send(source, target, send_sem, recv_sem, device):
    return pltpu.make_async_remote_copy(
        src_ref=source, dst_ref=target, send_sem=send_sem, recv_sem=recv_sem, device_id=device, device_id_type=MESH_ID
    )


def line_ends(z):
    return jnp.where(z > 0, 1, 0) + jnp.where(z < 3, 1, 0)


def gather_kernel(
    own_ref, tail_ref, weight_ref, out_ref, tails_ref, weights_ref,
    copy_sem, right_send, right_recv, left_send, left_recv, x_send, x_recv, c_send, c_recv, y_send, y_recv,
):
    s, w, side, z, x_device, core_device, y_device = places()
    up, down = (s + 2, w), (s - 2, w)
    across = w + 2 - 4 * (w // 2)
    kinds = ((own_ref, out_ref), (tail_ref, tails_ref))
    copies = [pltpu.make_async_copy(own, out.at[s], copy_sem.at[k]) for k, (own, out) in enumerate(kinds)]
    copies.append(pltpu.make_async_copy(weight_ref, weights_ref.at[w], copy_sem.at[2]))
    for copy in copies:
        copy.start()
    greet(((None, x_device), (None, core_device), (None, y_device), (z < 3, up), (z > 0, down)), 3 + line_ends(z))

    weight_y = send(weight_ref, weights_ref.at[w], y_send, y_recv, y_device)
    weight_core = send(weight_ref, weights_ref.at[w], c_send.at[0], c_recv.at[0], core_device)
    weight_on = send(weights_ref.at[across], weights_ref.at[across], c_send.at[1], c_recv.at[1], core_device)
    weight_y.start()
    weight_core.start()

    def to_right(j, k, source, number):
        return send(source, kinds[k][1].at[number], right_send.at[j, k], right_recv.at[j, k], up)

    def to_left(j, k, source, number):
        return send(source, kinds[k][1].at[number], left_send.at[j, k], left_recv.at[j, k], down)

    def to_x(at, k, source, number):
        return send(source, kinds[k][1].at[number], x_send.at[at, k], x_recv.at[at, k], x_device)

    for k, (own, _) in enumerate(kinds):

        @pl.when(z < 3)
        def _(k=k, own=own):
            to_right(0, k, own, s).start()

        @pl.when(z > 0)
        def _(k=k, own=own):
            to_left(0, k, own, s).start()

        to_x(z, k, own, s).start()
    for j in (1, 2, 3):
        lower, upper = s - 2 * j, s + 2 * j
        for k, (_, out) in enumerate(kinds):

            @pl.when(z >= j)
            def _(j=j, k=k, out=out, lower=lower):
                block = out.at[lower]
                to_right(j - 1, k, block, lower).wait_recv()

                @pl.when(z < 3)
                def _():
                    to_right(j, k, block, lower).start()

                to_x(z - j, k, block, lower).start()

            @pl.when(z + j <= 3)
            def _(j=j, k=k, out=out, upper=upper):
                block = out.at[upper]
                to_left(j - 1, k, block, upper).wait_recv()

                @pl.when(z > 0)
                def _():
                    to_left(j, k, block, upper).start()

                to_x(z + j, k, block, upper).start()

    weight_y.wait_recv()
    weight_on.start()
    for k, (own, _) in enumerate(kinds):
        for number in range(4):
            done = to_x(number, k, own, s)
            done.wait_send()
            done.wait_recv()
        for j in range(3):

            @pl.when((z >= j) & (z < 3))
            def _(j=j, k=k, own=own):
                to_right(j, k, own, s).wait_send()

            @pl.when((z + j <= 3) & (z > 0))
            def _(j=j, k=k, own=own):
                to_left(j, k, own, s).wait_send()

    weight_core.wait_recv()
    weight_on.wait_recv()
    for copy in (weight_y, weight_core, weight_on):
        copy.wait_send()
    for copy in copies:
        copy.wait()


def gather_first(own, tail, weight):
    seqs, parts = lax.axis_size("seq"), lax.axis_size("wsh")
    if seqs != 8 or parts != 4:
        return (
            lax.all_gather(own, "seq", axis=0, tiled=False),
            lax.all_gather(tail, "seq", axis=0, tiled=False),
            lax.all_gather(weight, "wsh", axis=0, tiled=False),
        )
    dma = pltpu.SemaphoreType.DMA
    given = ((seqs, own), (seqs, tail), (parts, weight))
    return pl.pallas_call(
        gather_kernel,
        in_specs=[pl.BlockSpec(memory_space=pl.ANY)] * 3,
        out_specs=[pl.BlockSpec(memory_space=pl.ANY)] * 3,
        out_shape=[jax.ShapeDtypeStruct((n,) + x.shape, x.dtype) for n, x in given],
        scratch_shapes=[dma((3,))] + [dma((3, 2))] * 4 + [dma((4, 2))] * 2 + [dma((2,))] * 2 + [dma] * 2,
        compiler_params=pltpu.CompilerParams(collective_id=1, has_side_effects=True),
        cost_estimate=pl.CostEstimate(flops=0, bytes_accessed=100 << 20, transcendentals=0),
        name="gather_first",
    )(own, tail, weight)


def reduce_kernel(
    splits, x_ref, out_ref, x_buf, right_buf, left_buf, right_out, left_out,
    x_send, x_recv, right_send, right_recv, left_send, left_recv,
):
    s, w, side, z, x_device, _, _ = places()
    up, down = (s + 2, w), (s - 2, w)
    size = x_ref.shape[2] // splits
    columns = [slice(c * size, (c + 1) * size) for c in range(splits)]
    greet(((None, x_device), (z < 3, up), (z > 0, down)), 1 + line_ends(z))

    def to_x(target, c):
        return send(
            x_ref.at[target * 2 + 1 - side, :, columns[c]], x_buf.at[target, :, columns[c]],
            x_send.at[target, c], x_recv.at[target, c], x_device,
        )

    def start_x(target):
        for c in range(splits):
            to_x(target, c).start()

    def to_right(k, c):
        return send(
            right_out.at[k - 1, :, columns[c]], right_buf.at[k - 1, :, columns[c]],
            right_send.at[k - 1, c], right_recv.at[k - 1, c], up,
        )

    def to_left(k, c):
        return send(
            left_out.at[k - 1, :, columns[c]], left_buf.at[k - 1, :, columns[c]],
            left_send.at[k - 1, c], left_recv.at[k - 1, c], down,
        )

    def pair(target, c):
        to_x(target, c).wait_recv()
        return x_ref[target * 2 + side, :, columns[c]].astype(F32) + x_buf[target, :, columns[c]].astype(F32)

    for k in (3, 2, 1):

        @pl.when(z + k <= 3)
        def _(k=k):
            start_x(z + k)

        @pl.when(z >= k)
        def _(k=k):
            start_x(z - k)

    start_x(z)
    for k in (3, 2, 1):
        for c in range(splits):

            @pl.when(z + k <= 3)
            def _(k=k, c=c):
                right_out[k - 1, :, columns[c]] = pair(z + k, c).astype(BF16)
                if k < 3:

                    @pl.when(z > 0)
                    def _():
                        to_right(k + 1, c).wait_recv()
                        right_out[k - 1, :, columns[c]] = (
                            right_out[k - 1, :, columns[c]].astype(F32) + right_buf[k, :, columns[c]].astype(F32)
                        ).astype(BF16)

                to_right(k, c).start()

            @pl.when(z >= k)
            def _(k=k, c=c):
                left_out[k - 1, :, columns[c]] = pair(z - k, c).astype(BF16)
                if k < 3:

                    @pl.when(z < 3)
                    def _():
                        to_left(k + 1, c).wait_recv()
                        left_out[k - 1, :, columns[c]] = (
                            left_out[k - 1, :, columns[c]].astype(F32) + left_buf[k, :, columns[c]].astype(F32)
                        ).astype(BF16)

                to_left(k, c).start()

    for c in range(splits):
        out_ref[:, columns[c]] = pair(z, c)

        @pl.when(z > 0)
        def _(c=c):
            to_right(1, c).wait_recv()
            out_ref[:, columns[c]] += right_buf[0, :, columns[c]].astype(F32)

        @pl.when(z < 3)
        def _(c=c):
            to_left(1, c).wait_recv()
            out_ref[:, columns[c]] += left_buf[0, :, columns[c]].astype(F32)

    for c in range(splits):
        for target in range(4):
            to_x(target, c).wait_send()
        for k in (3, 2, 1):

            @pl.when(z + k <= 3)
            def _(k=k, c=c):
                to_right(k, c).wait_send()

            @pl.when(z >= k)
            def _(k=k, c=c):
                to_left(k, c).wait_send()


def reduce_seq(x):
    seqs, rows, width = x.shape
    if seqs != 8 or lax.axis_size("wsh") != 4:
        return jnp.sum(exchange(x, "seq").astype(F32), 0)
    splits = 2
    return pl.pallas_call(
        functools.partial(reduce_kernel, splits),
        in_specs=[pl.BlockSpec(memory_space=pltpu.VMEM)],
        out_specs=pl.BlockSpec(memory_space=pltpu.VMEM),
        out_shape=jax.ShapeDtypeStruct((rows, width), F32),
        scratch_shapes=[pltpu.VMEM((4, rows, width), BF16)]
        + [pltpu.VMEM((3, rows, width), BF16)] * 4
        + [pltpu.SemaphoreType.DMA((4, splits))] * 2
        + [pltpu.SemaphoreType.DMA((3, splits))] * 4,
        compiler_params=pltpu.CompilerParams(collective_id=2, has_side_effects=True, vmem_limit_bytes=40 << 20),
        cost_estimate=pl.CostEstimate(flops=0, bytes_accessed=1 << 20, transcendentals=0),
        name="reduce_seq",
    )(x)


def channel_kernel(
    forward, x_ref, first_hbm, second_hbm, active_hbm,
    sum_ref, all_hbm, mine_hbm, other_hbm, extra_hbm,
    first, second, rows_all, middle, active, part, core_buf, far_out, far_buf,
    load_sem, store_sem, core_send, core_recv, y_send, y_recv, x_send, x_recv, r_send, r_recv, f_send, f_recv,
):
    s, w, side, z, x_device, core_device, y_device = places()
    rows, width = x_ref.shape
    units = first.shape[0]
    half = units // 2
    loads = [
        pltpu.make_async_copy(first_hbm, first, load_sem.at[0]),
        pltpu.make_async_copy(second_hbm, second, load_sem.at[1]),
    ]
    if not forward:
        loads.append(pltpu.make_async_copy(active_hbm, active, load_sem.at[2]))
    for load in loads:
        load.start()
    rows_all[0:rows] = x_ref[...]
    greet(((None, x_device), (None, core_device), (None, y_device)), 3)

    def block(number):
        return rows_all.at[pl.ds(number * rows, rows)]

    to_core = [
        send(block(0), block(1), core_send.at[0], core_recv.at[0], core_device),
        send(block(2), block(3), core_send.at[1], core_recv.at[1], core_device),
    ]
    to_y = send(block(0), block(2), y_send, y_recv, y_device)
    if forward:
        to_x = [
            send(
                middle.at[1 - side, pl.ds(2 * n * rows, 2 * rows)], other_hbm.at[pl.ds(2 * n * rows, 2 * rows)],
                x_send.at[n], x_recv.at[n], x_device,
            )
            for n in range(2)
        ]
    else:
        to_x = [
            send(block(n), other_hbm.at[pl.ds(n * rows, rows)], x_send.at[n], x_recv.at[n], x_device) for n in range(4)
        ]
    sums_core = [
        send(part.at[pl.ds((2 * n + 1) * rows, rows)], core_buf.at[n], r_send.at[n], r_recv.at[n], core_device)
        for n in range(2)
    ]
    far = send(far_out, far_buf, f_send, f_recv, y_device)
    stores = [
        pltpu.make_async_copy(rows_all, all_hbm, store_sem.at[0]),
        pltpu.make_async_copy(middle.at[side], mine_hbm, store_sem.at[1]),
        pltpu.make_async_copy(active if forward else middle.at[1 - side], extra_hbm, store_sem.at[2]),
    ]

    def pass_on(number):
        if not forward:
            to_x[number].start()

    to_y.start()
    to_core[0].start()
    pass_on(0)
    tile = min(512, half)

    def multiply(number):
        two = pl.ds(2 * number * rows, 2 * rows)

        def up(t, carry):
            for side_units in range(2):
                at = pl.multiple_of(t * tile, tile)
                unit = pl.multiple_of(side_units * half + at, tile)
                raw = dot(rows_all[two, :], first[pl.ds(unit, tile), :], NT)
                if forward:
                    raw = jnp.maximum(raw, 0.0)
                    active[two, pl.ds(unit, tile)] = raw
                    mid = raw * raw
                else:
                    mid = raw * 2.0 * active[two, pl.ds(unit, tile)]
                middle[side_units, two, pl.ds(at, tile)] = mid.astype(BF16)
            return carry

        lax.fori_loop(0, half // tile, up, 0)
        if forward:
            to_x[number].start()
        if number == 0:
            loads[1].wait()

        def down(t, carry):
            at = pl.multiple_of(t * tile, tile)
            part[two, pl.ds(at, tile)] = dot(middle[0, two, :], second[0:half, pl.ds(at, tile)]) + dot(
                middle[1, two, :], second[half:units, pl.ds(at, tile)]
            )
            return carry

        lax.fori_loop(0, width // tile, down, 0)
        sums_core[number].start()

    loads[0].wait()
    if not forward:
        loads[2].wait()
    to_core[0].wait_recv()
    pass_on(1)
    multiply(0)
    to_y.wait_recv()
    to_core[1].start()
    pass_on(2)
    to_core[1].wait_recv()
    pass_on(3)
    stores[0].start()
    multiply(1)
    for store in stores[1:]:
        store.start()
    sums_core[1].wait_recv()
    far_out[...] = (part[2 * rows : 3 * rows] + core_buf[1]).astype(BF16)
    far.start()
    sums_core[0].wait_recv()
    sum_ref[...] = part[0:rows] + core_buf[0]
    far.wait_recv()
    sum_ref[...] += far_buf[...].astype(F32)
    for copy in to_x:
        copy.wait_recv()
    for copy in to_x + to_core + sums_core + [to_y, far]:
        copy.wait_send()
    for store in stores:
        store.wait()


def channel_stage(x, first, second, active):
    rows, width = x.shape
    units = first.shape[0]
    forward = active is None
    given = (x, first, second) if forward else (x, first, second, active)
    everything = pl.BlockSpec(memory_space=pl.ANY)
    shapes = [
        ((rows, width), F32), ((4 * rows, width), BF16), ((4 * rows, units // 2), BF16),
        ((4 * rows, units // 2 if forward else width), BF16),
        ((4 * rows, units), F32) if forward else ((4 * rows, units // 2), BF16),
    ]

    def body(*refs):
        refs = list(refs)
        if forward:
            refs.insert(3, None)
        channel_kernel(forward, *refs)

    dma = pltpu.SemaphoreType.DMA
    return pl.pallas_call(
        body,
        in_specs=[pl.BlockSpec(memory_space=pltpu.VMEM)] + [everything] * (len(given) - 1),
        out_specs=[pl.BlockSpec(memory_space=pltpu.VMEM)] + [everything] * (len(shapes) - 1),
        out_shape=[jax.ShapeDtypeStruct(s, d) for s, d in shapes],
        scratch_shapes=[
            pltpu.VMEM((units, width), BF16), pltpu.VMEM((units, width), BF16), pltpu.VMEM((4 * rows, width), BF16),
            pltpu.VMEM((2, 4 * rows, units // 2), BF16), pltpu.VMEM((4 * rows, units), F32),
            pltpu.VMEM((4 * rows, width), F32), pltpu.VMEM((2, rows, width), F32),
            pltpu.VMEM((rows, width), BF16), pltpu.VMEM((rows, width), BF16),
            dma((3,)), dma((3,)), dma((2,)), dma((2,)), dma, dma, dma((4,)), dma((4,)), dma((2,)), dma((2,)),
            dma, dma,
        ],
        compiler_params=pltpu.CompilerParams(
            collective_id=3 if forward else 4, has_side_effects=True, vmem_limit_bytes=60 << 20
        ),
        cost_estimate=pl.CostEstimate(flops=0, bytes_accessed=100 << 20, transcendentals=0),
        name="channel_forward" if forward else "channel_backward",
    )(*given)


def from_behind(x, axis, by):
    size = lax.axis_size(axis)
    pairs = [(i, i + by) for i in range(size) if 0 <= i + by < size]
    return lax.ppermute(x, axis, pairs)


def exchange(x, axis):
    return lax.all_to_all(x, axis, split_axis=0, concat_axis=0, tiled=True)


def swap(x, by):
    size = lax.axis_size("wsh")
    return lax.ppermute(x, "wsh", [(i, i ^ by) for i in range(size)])


def gather_near(x):
    if lax.axis_size("wsh") != 4:
        return lax.all_gather(x, "wsh", axis=0, tiled=True)
    return gathered_near(x, swap(x, 1), swap(x, 2))


def gathered_near(x, beside, across):
    return jnp.concatenate([x, beside, across, swap(across, 1)], 0)


def beside(x):
    return lax.ppermute(x, "seq", [(i, i ^ 1) for i in range(lax.axis_size("seq"))])


def scalar_sum(x):
    if lax.axis_size("wsh") != 4:
        return jnp.sum(lax.all_gather(x.reshape(1), "wsh", axis=0, tiled=True))
    x = jnp.full((8, 128), x)
    x = x + swap(x, 1)
    return (x + swap(x, 2))[0, 0]


def near_sum(x):
    if lax.axis_size("wsh") != 4:
        return lax.psum_scatter(x, "wsh", scatter_dimension=0, tiled=True)
    rows = x.shape[0] // 4
    beside = swap(jnp.concatenate([x[rows : 2 * rows], x[3 * rows :]], 0), 1)
    far = x[2 * rows : 3 * rows] + beside[rows:]
    return x[:rows] + beside[:rows] + swap(far.astype(BF16), 2).astype(F32)


def block_sum(x):
    if lax.axis_size("wsh") != 4:
        return lax.psum_scatter(x, "wsh", scatter_dimension=0, tiled=False).astype(F32)
    kept, far = block_halves(x)
    return kept + swap(far, 2).astype(F32)


def block_halves(x):
    number = lax.axis_index("wsh")

    def block(by):
        return lax.dynamic_index_in_dim(x, number ^ by, 0, keepdims=False)

    beside = swap(jnp.stack([block(1), block(3)]), 1).astype(F32)
    return block(0).astype(F32) + beside[0], (block(2).astype(F32) + beside[1]).astype(BF16)


def local(
    tokens, first_layer_values, teacher, valid, destination, lengths,
    receptance_matrix, key_matrix, value_matrix, output_matrix,
    lowrank_down_weight, lowrank_up_weight, channel_key_weight, channel_value_weight, vectors,
):
    rows, width = tokens.shape
    seqs, parts = lax.axis_size("seq"), lax.axis_size("wsh")
    me = lax.axis_index("seq")
    group = rows * seqs
    own_width = width // seqs
    shard = width // parts
    piece = shard // seqs
    column = me * own_width

    def own_columns(matrix):
        return lax.dynamic_slice_in_dim(matrix, column, own_width, 1)

    near = parts == 4
    up_piece = lax.dynamic_slice_in_dim(lowrank_up_weight, column % shard, own_width, 0)
    total = 3 * own_width + WIDE
    own_weights = jnp.concatenate(
        [
            own_columns(receptance_matrix), own_columns(key_matrix), own_columns(value_matrix),
            pad_ranks(lowrank_down_weight), up_piece.reshape(shard, -1),
        ],
        1,
    )

    dest_seq = destination // rows // parts
    position = dest_seq * rows + destination % rows
    digits = jnp.stack([position // DIGIT, position % DIGIT, valid], 1).astype(BF16)
    tail = jnp.pad(digits, ((0, 0), (0, EXTRA - 3)))
    given, tails, weights = gather_first(tokens, tail, own_weights)
    given, tails, weights = given.reshape(group, width), tails.reshape(group, EXTRA), weights.reshape(width, -1)
    info = tails[:, :3].astype(F32)
    places = (info[:, 0] * DIGIT + info[:, 1]).astype(jnp.int32)
    numbers = jnp.arange(group, dtype=jnp.int32)
    permute = (numbers[:, None] == places[None, :]).astype(BF16)
    total_valid = scalar_sum(jnp.sum(info[:, 2]))

    index = jnp.arange(rows, dtype=jnp.int32)
    same_dest = (dest_seq[:, None] == dest_seq[None, :]) & (index[None, :] < index[:, None])
    slot = dest_seq * (rows // seqs) + jnp.sum(same_dest.astype(jnp.int32), 1)
    arrange = (index[:, None] == slot[None, :]).astype(BF16)
    mine = (places // rows) == me
    arrival = jnp.cumsum(mine.astype(jnp.int32)) - 1
    own_rows = ((index[:, None] + me * rows) == places[None, :]).astype(BF16)
    settle = dot(own_rows, (mine[:, None] & (arrival[:, None] == index[None, :])).astype(BF16)).astype(BF16)

    offsets = jnp.cumsum(lengths[0]) - lengths[0]
    starts = jnp.any(numbers[:, None] == offsets[None, :], 1).astype(F32)
    segment_ids = jnp.cumsum(starts).reshape(-1, BLOCK)
    before = segment_ids[:, :1] - starts.reshape(-1, BLOCK)[:, :1]
    segments = jnp.stack(
        [segment_ids, jnp.broadcast_to(before, segment_ids.shape), jnp.broadcast_to(segment_ids[:, -1:], segment_ids.shape)]
        + [jnp.zeros_like(segment_ids)] * 5,
        1,
    ).reshape(-1, BLOCK)
    flowing = (1.0 - starts)[:, None]

    up = pad_ranks(
        lax.dynamic_slice(
            weights, (column // shard * shard, total), (shard, weights.shape[1] - total)
        ).reshape(own_width, -1)
    ).T
    vec = lax.dynamic_slice_in_dim(vectors, column, own_width, 0)[:, 8:16].T

    output_late, given = lax.optimization_barrier((output_matrix, given))
    w_out = lax.all_gather(output_late, "wsh", axis=0, tiled=True)
    balanced = dot(permute, given).astype(BF16)
    wide_rows = balanced.astype(F32)
    mean = jnp.mean(wide_rows, -1, keepdims=True)
    scale_one = lax.rsqrt(jnp.mean(jnp.square(wide_rows - mean), -1, keepdims=True) + 1e-05)
    stats = jnp.concatenate([mean, scale_one, flowing, flowing], 1)
    mix_vec = vectors[:, :8].T
    first_values, stats = lax.optimization_barrier((first_layer_values, stats))
    first_given = exchange(
        first_values.reshape(rows, seqs, own_width).transpose(1, 0, 2), "seq"
    ).reshape(group, own_width)
    recept, keys, values, downs, hidden = run_project(balanced, stats, mix_vec, weights, own_width, parts)
    teacher_late, recept, first_given = lax.optimization_barrier((teacher, recept, first_given))
    first = dot(permute, first_given).astype(BF16)
    teacher_rows = exchange(dot(arrange, teacher_late).astype(BF16).reshape(seqs, rows // seqs, width), "seq")
    inputs = (recept, keys, values, hidden, first, up, vec, segments)
    mixed_out, *saved = run_forward(*inputs)
    teacher_rows, mixed_out = lax.optimization_barrier((teacher_rows, mixed_out))
    target = dot(settle, teacher_rows.reshape(rows, width))

    mixed_rows = exchange(mixed_out.reshape(seqs, rows, own_width), "seq").transpose(1, 0, 2).reshape(rows, width)
    own = lax.dynamic_slice_in_dim(balanced, me * rows, rows, 0).astype(F32)
    own_starts = lax.dynamic_slice_in_dim(starts, me * rows, rows, 0)
    own_flowing = (1.0 - own_starts)[:, None]
    own_valid = dot(own_rows, tails)[:, 2]
    residual = own + dot(mixed_rows, w_out)
    standard_two, scale_two = norm_stats(residual)
    normed_two = standard_two * vectors[:, 16] + vectors[:, 17]
    carried_two = from_behind(normed_two[-1:], "seq", 1)
    delta_two = jnp.concatenate([carried_two, normed_two[:-1]], 0) * own_flowing - normed_two
    channel_in = (normed_two + delta_two * vectors[:, 18]).astype(BF16)
    paired = near and seqs == 8
    if paired:
        summed, channel, hidden_mine, hidden_other, active = channel_stage(
            channel_in, channel_key_weight, channel_value_weight, None
        )
    else:
        channel = gather_near(channel_in)
        active = jax.nn.relu(dot(channel, channel_key_weight, NT))
        hidden_rows = jnp.square(active).astype(BF16)
        summed = near_sum(dot(hidden_rows, channel_value_weight))
    result = residual + summed
    total_tokens = group * parts
    cotangent = (result - target) * (own_valid * (total_tokens / total_valid))[:, None]
    cot_low = cotangent.astype(BF16)

    if paired:
        grad_channel, cot, pre_mine, cot_other, pre_spare = channel_stage(
            cot_low, channel_value_weight, channel_key_weight, active
        )
        channel_other, pre_other = beside(channel), beside(pre_spare)
    else:
        cot = gather_near(cot_low)
        grad_pre = (dot(cot, channel_value_weight, NT) * 2.0 * active).astype(BF16)
        grad_channel = near_sum(dot(grad_pre, channel_key_weight))
    grad_vec_mix_two = jnp.sum(grad_channel * delta_two, 0)
    shifted = grad_channel * vectors[:, 18] * own_flowing
    behind = from_behind(shifted[:1], "seq", -1)
    grad_normed_two = grad_channel * (1.0 - vectors[:, 18]) + jnp.concatenate([shifted[1:], behind], 0)
    grad_residual = cotangent + norm_back(grad_normed_two, standard_two, scale_two, vectors[:, 16])
    grad_low = grad_residual.astype(BF16)

    grad_posted = dot(grad_low, w_out, NT).astype(BF16)
    if paired:
        hidden_mine, grad_posted = lax.optimization_barrier((hidden_mine, grad_posted))
        value_part = (dot(hidden_mine, cot, TN) + dot(hidden_other, cot_other, TN)).astype(BF16)
    else:
        value_part = dot(hidden_rows, cot, TN).astype(BF16)
    grad_heads = exchange(grad_posted.reshape(rows, seqs, own_width).transpose(1, 0, 2), "seq").reshape(group, own_width)
    grad_heads, value_part, mixed_late = lax.optimization_barrier((grad_heads, value_part, mixed_rows))
    lefts = exchange(mixed_late.reshape(rows, seqs, parts, piece).transpose(2, 0, 1, 3), "wsh")
    near_grad = (swap(grad_low, 1), swap(grad_low, 2)) if near else gather_near(grad_low)
    recept_low, keys_low, values_low, ups_low, grad_first, grad_vec_heads = run_backward(grad_heads, *inputs, saved)
    if paired:
        channel_other, pre_other, lefts, near_grad, recept_low = lax.optimization_barrier(
            (channel_other, pre_other, lefts, near_grad, recept_low)
        )
        key_part = (dot(pre_mine, channel, TN) + dot(pre_other, channel_other, TN)).astype(BF16)
    else:
        lefts, near_grad, recept_low = lax.optimization_barrier((lefts, near_grad, recept_low))
        key_part = dot(grad_pre, channel, TN).astype(BF16)
    if near:
        near_grad = gathered_near(grad_low, *near_grad)
        lefts = jnp.stack([lax.dynamic_index_in_dim(lefts, lax.axis_index("wsh") ^ k, 0, keepdims=False) for k in range(4)])
    out_part = dot(lefts.reshape(rows * parts, -1), near_grad, TN).astype(BF16)

    result_back = dot(settle, result.astype(BF16), TN).astype(BF16).reshape(seqs, rows // seqs, width)
    first_back = dot(permute, grad_first, TN).astype(BF16).reshape(seqs, rows // seqs, width)
    moved = exchange(jnp.concatenate([result_back, first_back], 1), "seq")
    recept_low, key_part, out_part = lax.optimization_barrier((recept_low, key_part, out_part))
    if paired:
        lines = [[0, 2, 4, 6], [1, 3, 5, 7]]
        turned = [
            ((z * 2 + x) * 4 + w, (w * 2 + x) * 4 + z) for z in range(4) for x in range(2) for w in range(4)
        ]

        def along(part):
            return lax.psum_scatter(part, "seq", scatter_dimension=0, tiled=True, axis_index_groups=lines)

        def turn(part):
            return lax.ppermute(part, ("seq", "wsh"), turned)

        halves_out = out_part.reshape(seqs // 2, 2, piece, width)
        x_side = me % 2
        out_mine = lax.dynamic_index_in_dim(halves_out, x_side, 1, keepdims=False).astype(F32)
        out_other = beside(lax.dynamic_index_in_dim(halves_out, 1 - x_side, 1, keepdims=False))
        value_turned, key_sum = turn(along(value_part)), along(key_part)
    else:
        moves = [(s * parts + w, w * seqs + s) for s in range(seqs) for w in range(parts)]

        def ffn_grad(part):
            part = lax.psum_scatter(part, "seq", scatter_dimension=0, tiled=True)
            return lax.ppermute(part, ("seq", "wsh"), moves).astype(F32)

        grad_ffn_value, grad_ffn_key = ffn_grad(value_part), ffn_grad(key_part)
        grad_out = lax.psum_scatter(out_part, "seq", scatter_dimension=0, tiled=True)

    heads_part = lax.dynamic_update_slice_in_dim(jnp.zeros((width, 8), F32), grad_vec_heads.T, column, 0)
    vec_two = jnp.stack(
        [jnp.sum(grad_normed_two * standard_two, 0), jnp.sum(grad_normed_two, 0), grad_vec_mix_two], 1
    )
    others = jnp.concatenate([heads_part, jnp.pad(vec_two, ((0, 0), (0, 13)))], 1)
    scaled_grad, sums, wide, up_grad = run_unproject(
        balanced, stats, mix_vec, weights, others, (recept_low, keys_low, values_low), ups_low, hidden, downs, up, parts
    )
    if paired:
        moved, value_turned, out_other, scaled_grad, sums, wide, up_grad = lax.optimization_barrier(
            (moved, value_turned, out_other, scaled_grad, sums, wide, up_grad)
        )
        out_half = (out_mine + out_other.astype(F32)).astype(BF16).reshape(-1, width)
        out_half, sums = lax.optimization_barrier((out_half, sums))
        grad_out = along(out_half)
        grad_ffn_value, grad_ffn_key = value_turned.astype(F32), turn(key_sum).astype(F32)
    else:
        moved, scaled_grad, sums, wide = lax.optimization_barrier((moved, scaled_grad, sums, wide))
    output = dot(arrange, moved[:, : rows // seqs].reshape(rows, width), TN).astype(BF16)
    grad_first_rows = moved[:, rows // seqs :].reshape(seqs, rows, own_width).transpose(1, 0, 2).reshape(rows, width)

    standard = (balanced.astype(F32) - mean) * scale_one
    grad_balanced = scale_one * (scaled_grad - sums[:, :1] * (1.0 / width) - standard * (sums[:, 1:] * (1.0 / width)))
    mine_rows = lax.dynamic_slice_in_dim(grad_balanced, me * rows, rows, 0) + grad_residual
    grad_balanced = lax.dynamic_update_slice_in_dim(grad_balanced, mine_rows, me * rows, 0)
    grad_given = dot(permute, grad_balanced.astype(BF16), TN).astype(BF16).reshape(seqs, rows, width)
    if near:
        kept_part, far = block_halves(wide)
        grad_given, far = lax.optimization_barrier((grad_given, far))
        wide_part = kept_part + swap(far, 2).astype(F32)
    else:
        wide_part = block_sum(wide)
    grad_tokens = reduce_seq(grad_given).astype(BF16)
    wide_part, grad_tokens, grad_out = lax.optimization_barrier((wide_part, grad_tokens, grad_out))
    wide_all = exchange(wide_part.astype(BF16), "seq").astype(F32)

    def square(at):
        taken = wide_all[:, :, at * own_width : (at + 1) * own_width]
        return taken.transpose(1, 0, 2).reshape(piece, width)

    narrow = jnp.sum(wide_all[:, :, 3 * own_width :], 0)
    grad_down = unpad_ranks(narrow)
    grad_vectors = narrow[:, RANKS[0] : RANKS[0] + vectors.shape[1]]
    up_part = unpad_ranks(block_sum(up_grad.reshape(parts, piece, WIDE)))

    return (
        output, grad_tokens, grad_first_rows,
        square(0), square(1), square(2),
        grad_out.astype(F32), grad_down, up_part,
        grad_ffn_key, grad_ffn_value, grad_vectors,
    )


def solution(mesh):
    both, shard = P(("seq", "wsh"), None), P("wsh", None)
    flat = P(("seq", "wsh"))
    return jax.shard_map(
        local,
        mesh=mesh,
        in_specs=(both, both, both, flat, flat) + (shard,) * 9 + (P(),),
        out_specs=(both,) * 12,
        check_vma=False,
    )
```

```python
import functools

import jax
import jax.numpy as jnp
from jax import lax
from jax.experimental import pallas as pl
from jax.experimental.pallas import tpu as pltpu
from jax.sharding import PartitionSpec as P

HEAD = 64
BLOCK = 64
RANKS = (96, 96, 64, 256)
PADDED = (128, 128, 128, 256)
OFFSETS = (0, 128, 256, 384)
WIDE = 640
EXTRA = 128
DIGIT = 64

F32 = jnp.float32
BF16 = jnp.bfloat16

NN = (((1,), (0,)), ((), ()))
NT = (((1,), (1,)), ((), ()))
TN = (((0,), (0,)), ((), ()))


def dot(a, b, dims=NN):
    return lax.dot_general(a, b, dims, preferred_element_type=F32)


def halves(x):
    high = x.astype(BF16)
    return high, (x - high.astype(F32)).astype(BF16)


def dot3(a, b, dims=NN):
    a_high, a_low = halves(a)
    b_high, b_low = halves(b)
    return dot(a_high, b_high, dims) + (dot(a_high, b_low, dims) + dot(a_low, b_high, dims))


def sum_left(mask, x):
    high, low = halves(x)
    low_two = (x - high.astype(F32) - low.astype(F32)).astype(BF16)
    return dot(mask, high) + (dot(mask, low) + dot(mask, low_two))


def head_sum(x, ones):
    high, low = halves(x)
    return dot(high, ones) + dot(low, ones)


def low(x):
    return x.astype(BF16).astype(F32)


def iotas(rows, columns):
    return (
        lax.broadcasted_iota(jnp.int32, (rows, columns), 0),
        lax.broadcasted_iota(jnp.int32, (rows, columns), 1),
    )


def head_ones(width):
    i, j = iotas(width, width)
    return jnp.where((i >> 6) == (j >> 6), 1.0, 0.0).astype(BF16)


def front(keys, values, hidden, up, first, vec, ones):
    z = vec[0:1] + dot(hidden[:, 0:128], up[0:128])
    decay_log = -(jnp.maximum(-z, 0.0) + jnp.log1p(jnp.exp(-jnp.abs(z)))) - 0.5
    rate = jax.nn.sigmoid(vec[1:2] + dot(hidden[:, 128:256], up[128:256]))
    blend = jax.nn.sigmoid(vec[2:3] + dot(hidden[:, 256:384], up[256:384]))
    gate = dot(hidden[:, 384:640], up[384:640])
    mixed_value = values + (first - values) * blend
    scaled = keys * vec[3:4]
    scale = lax.rsqrt(head_sum(scaled * scaled, ones) + 1e-06)
    key_dir = scaled * scale
    key_mod = keys * (1.0 + (rate - 1.0) * vec[4:5])
    return z, decay_log, rate, blend, gate, mixed_value, scale, key_dir, key_mod


def block_masks(segments):
    i, j = iotas(BLOCK, BLOCK)
    across = jnp.broadcast_to(segments[0:1], (BLOCK, BLOCK))
    down = across.T
    before = jnp.broadcast_to(segments[1:2], (BLOCK, BLOCK))
    last = jnp.broadcast_to(segments[2:3], (BLOCK, BLOCK))
    same = across == down
    strict = jnp.where(same & (i > j), 1.0, 0.0)
    closed = jnp.where(same & (i >= j), 1.0, 0.0)
    carry = jnp.where(down == before, 1.0, 0.0)
    tail = jnp.where(down == last, 1.0, 0.0)
    keep = jnp.where(segments[2:3] == segments[1:2], 1.0, 0.0)
    quad = jnp.concatenate(
        [jnp.concatenate([strict, strict], 1), jnp.concatenate([closed, closed], 1)], 0
    )
    return quad, carry, tail, keep


def tile_heads(x, heads):
    return jnp.concatenate([x] * heads, 1) if heads > 1 else x


def join(pieces, axis):
    return jnp.concatenate(pieces, axis) if len(pieces) > 1 else pieces[0]


def decayed(decay_low, key_low, dir_low, rate_low, recept_low, carry, tail):
    i, j = iotas(BLOCK, BLOCK)
    lower = jnp.where(i >= j, 1.0, 0.0).astype(BF16)
    log_step = -jnp.exp(decay_low)
    total = sum_left(lower, log_step)
    before = jnp.exp(total - log_step)
    grown = jnp.exp(total)
    shrunk = jnp.exp(-total)
    end = total[BLOCK - 1 : BLOCK]
    tail_decay = jnp.exp(end - total) * tail
    alpha = -dir_low * before
    beta_plain = dir_low * rate_low
    beta = beta_plain * shrunk
    key = key_low * shrunk
    recept = recept_low * grown
    return dict(
        log_step=log_step, before=before, grown=grown, shrunk=shrunk, end=jnp.exp(end), tail=tail_decay,
        alpha=alpha, beta_plain=beta_plain, beta=beta, key=key, recept=recept,
        beta_end=beta_plain * tail_decay, key_end=key_low * tail_decay,
        alpha_in=alpha * carry, recept_in=recept * carry,
    )


def unit_inverses(lowers):
    i, j = iotas(BLOCK, BLOCK)
    eye = jnp.where(i == j, 1.0, 0.0)

    def within(size):
        return (i // size) == (j // size)

    smalls = [jnp.where(within(4), x, 0.0) for x in lowers]
    low_smalls = [x.astype(BF16) for x in smalls]
    twos = [dot(x, x) for x in low_smalls]
    inverses = [eye + x for x in smalls]
    inverses = [x + dot(x.astype(BF16), y.astype(BF16)) for x, y in zip(inverses, twos)]
    for size in (8, 16, 32, 64):
        mask = within(size) & ~within(size // 2)
        offs = [jnp.where(mask, x, 0.0).astype(BF16) for x in lowers]
        lows = [x.astype(BF16) for x in inverses]
        inner = [dot(x, y).astype(BF16) for x, y in zip(offs, lows)]
        inverses = [x + dot(y, z) for x, y, z in zip(inverses, lows, inner)]
    errors = [eye - x + dot3(y, x) for x, y in zip(inverses, lowers)]
    return [x + dot(x.astype(BF16), y.astype(BF16)) for x, y in zip(inverses, errors)]


def post_norm(head_low, ones):
    centered = head_low - head_sum(head_low, ones) * (1.0 / HEAD)
    spread = lax.rsqrt(head_sum(centered * centered, ones) * (1.0 / HEAD) + HEAD * 1e-05)
    return centered * spread, spread


def forward_kernel(
    count, recept_ref, keys_ref, values_ref, hidden_ref, first_ref, up_ref, vec_ref, segment_ref,
    mixed_ref, head_ref, state_ref, inverse_ref, removed_ref, state,
):
    width = recept_ref.shape[1]
    heads = width // HEAD

    @pl.when(pl.program_id(0) == 0)
    def _():
        state[...] = jnp.zeros_like(state)

    ones = head_ones(width)
    vec = vec_ref[...]
    up = up_ref[...]
    columns = [slice(head * HEAD, (head + 1) * HEAD) for head in range(heads)]
    done = []
    for block in range(count):
        rows = slice(block * BLOCK, (block + 1) * BLOCK)
        recept, keys, values = recept_ref[rows], keys_ref[rows], values_ref[rows]
        _, decay_log, rate, _, gate, mixed_value, _, key_dir, key_mod = front(
            keys, values, hidden_ref[rows], up, first_ref[rows].astype(F32), vec, ones
        )
        quad, carry, tail, keep = block_masks(segment_ref[block * 8 : block * 8 + 8])
        parts = decayed(
            low(decay_log), low(key_mod), low(key_dir), low(rate), low(recept),
            tile_heads(carry, heads), tile_heads(tail, heads),
        )
        lefts = [jnp.concatenate([parts["alpha"][:, c], parts["recept"][:, c]], 0) for c in columns]
        rights = [jnp.concatenate([parts["beta"][:, c], parts["key"][:, c]], 0) for c in columns]
        pairs = [quad * dot3(x, y, NT) for x, y in zip(lefts, rights)]
        done.append((rows, recept, key_mod, gate, mixed_value, keep, parts, pairs))
    inverses = unit_inverses([x[:BLOCK, :BLOCK] for item in done for x in item[-1]])
    for block, (rows, recept, key_mod, gate, mixed_value, keep, parts, pairs) in enumerate(done):
        mine = inverses[block * heads : (block + 1) * heads]
        value_low = low(mixed_value)
        owns = [value_low[:, c] for c in columns]
        by_values = [dot3(x[:, BLOCK:], y) for x, y in zip(pairs, owns)]
        ends = [jnp.concatenate([parts["beta_end"][:, c], parts["key_end"][:, c]], 0) for c in columns]
        inners = [jnp.concatenate([parts["alpha_in"][:, c], parts["recept_in"][:, c]], 0) for c in columns]
        entering = state[...]
        state_ref[rows] = entering
        nows = [entering[:, c] for c in columns]
        inwards = [dot3(x, y, NT) for x, y in zip(inners, nows)]
        removals = [dot3(x, y[:BLOCK] + z[:BLOCK]) for x, y, z in zip(mine, inwards, by_values)]
        outs = [
            y[BLOCK:] + z[BLOCK:] + dot3(x[BLOCK:, :BLOCK], r)
            for x, y, z, r in zip(pairs, inwards, by_values, removals)
        ]
        leaving = [
            x * (parts["end"][:, c] * keep) + dot3(jnp.concatenate([r, v], 0), e, TN)
            for x, c, r, v, e in zip(nows, columns, removals, owns, ends)
        ]
        state[...] = join(leaving, 1)
        inverse_ref[rows] = join(mine, 1)
        removed_ref[rows] = join(removals, 1)
        head_low = join(outs, 1).astype(BF16)
        head_ref[rows] = head_low
        normed, _ = post_norm(head_low.astype(F32), ones)
        bonus = head_sum(recept * key_mod * vec[5:6], ones) * mixed_value
        mixed_ref[rows] = ((normed * vec[6:7] + vec[7:8] + bonus) * gate).astype(BF16)


def backward_kernel(
    count, grad_ref, recept_ref, keys_ref, values_ref, hidden_ref, first_ref, up_ref, vec_ref, segment_ref,
    head_ref, state_ref, inverse_ref, removed_ref,
    recept_out, keys_out, values_out, ups_out, first_out, vec_out, state,
):
    width = recept_ref.shape[1]
    heads = width // HEAD

    @pl.when(pl.program_id(0) == 0)
    def _():
        state[...] = jnp.zeros_like(state)
        vec_out[...] = jnp.zeros_like(vec_out)

    ones = head_ones(width)
    vec = vec_ref[...]
    up = up_ref[...]
    i, j = iotas(BLOCK, BLOCK)
    upper = jnp.where(i <= j, 1.0, 0.0).astype(BF16)
    columns = [slice(head * HEAD, (head + 1) * HEAD) for head in range(heads)]
    order = range(count - 1, -1, -1)
    kept = {}
    for block in order:
        rows = slice(block * BLOCK, (block + 1) * BLOCK)
        recept, keys, values = recept_ref[rows], keys_ref[rows], values_ref[rows]
        first = first_ref[rows].astype(F32)
        z, decay_log, rate, blend, gate, mixed_value, scale, key_dir, key_mod = front(
            keys, values, hidden_ref[rows], up, first, vec, ones
        )
        quad, carry, tail, keep = block_masks(segment_ref[block * 8 : block * 8 + 8])
        rate_low, dir_low = low(rate), low(key_dir)
        parts = decayed(
            low(decay_log), low(key_mod), dir_low, rate_low, low(recept),
            tile_heads(carry, heads), tile_heads(tail, heads),
        )
        value_low = low(mixed_value)

        grad = grad_ref[rows].astype(F32)
        normed, spread = post_norm(head_ref[rows].astype(F32), ones)
        product = recept * key_mod
        coefficient = head_sum(product * vec[5:6], ones)
        grad_gate = grad * (normed * vec[6:7] + vec[7:8] + coefficient * mixed_value)
        opened = grad * gate
        grad_normed = opened * vec[6:7]
        grad_head = spread * (
            grad_normed
            - head_sum(grad_normed, ones) * (1.0 / HEAD)
            - normed * (head_sum(grad_normed * normed, ones) * (1.0 / HEAD))
        )
        grad_coefficient = head_sum(opened * mixed_value, ones)
        weighted = grad_coefficient * vec[5:6]
        head_grad = low(grad_head)

        lefts = [jnp.concatenate([parts["alpha"][:, c], parts["recept"][:, c]], 0) for c in columns]
        rights = [jnp.concatenate([parts["beta"][:, c], parts["key"][:, c]], 0) for c in columns]
        ends = [jnp.concatenate([parts["beta_end"][:, c], parts["key_end"][:, c]], 0) for c in columns]
        inners = [jnp.concatenate([parts["alpha_in"][:, c], parts["recept_in"][:, c]], 0) for c in columns]
        pairs = [quad * dot3(x, y, NT) for x, y in zip(lefts, rights)]
        out_grads = [head_grad[:, c] for c in columns]
        through = [dot3(x[BLOCK:, :BLOCK], y, TN) for x, y in zip(pairs, out_grads)]
        kept[block] = dict(
            rows=rows, recept=recept, keys=keys, values=values, first=first, z=z, rate=rate, blend=blend,
            mixed_value=mixed_value, scale=scale, key_dir=key_dir, key_mod=key_mod, quad=quad, carry=carry, keep=keep,
            rate_low=rate_low, dir_low=dir_low, parts=parts, value_low=value_low, normed=normed, product=product,
            grad_gate=grad_gate, opened=opened, grad_coefficient=grad_coefficient,
            grad_mixed_value=opened * coefficient, grad_recept=weighted * key_mod, grad_key_mod=weighted * recept,
            lefts=lefts, rights=rights, ends=ends, inners=inners, pairs=pairs, out_grads=out_grads, through=through,
        )
    for block in order:
        k = kept[block]
        after, entering, inverse_all = state[...], state_ref[k["rows"]], inverse_ref[k["rows"]]
        laters, nows = [after[:, c] for c in columns], [entering[:, c] for c in columns]
        from_ends = [dot3(x, y, NT) for x, y in zip(k["ends"], laters)]
        inner_grads = [
            dot3(inverse_all[:, c], x + y[:BLOCK], TN) for c, x, y in zip(columns, k["through"], from_ends)
        ]
        boths = [jnp.concatenate([x, y], 0) for x, y in zip(inner_grads, k["out_grads"])]
        stays = [x * (k["parts"]["end"][:, c] * k["keep"]) for x, c in zip(laters, columns)]
        state[...] = join([x + dot3(y, z, TN) for x, y, z in zip(stays, boths, k["inners"])], 1)
        k.update(
            laters=laters, nows=nows, from_ends=from_ends, boths=boths,
            end_sum=join([jnp.sum(x * y, 0, keepdims=True) for x, y in zip(nows, stays)], 1),
        )
    vec_total = jnp.zeros_like(vec)
    for block in order:
        k = kept[block]
        rows, parts, quad = k["rows"], k["parts"], k["quad"]
        removed_all = removed_ref[rows]
        carry_two = jnp.concatenate([k["carry"], k["carry"]], 0)
        sources = [jnp.concatenate([removed_all[:, c], k["value_low"][:, c]], 0) for c in columns]
        grad_pairs = [quad * dot3(x, y, NT) for x, y in zip(k["boths"], sources)]
        grad_values = [
            dot3(x[:, BLOCK:], y, TN) + z[BLOCK:] for x, y, z in zip(k["pairs"], k["boths"], k["from_ends"])
        ]
        grad_ends = [dot3(x, y) for x, y in zip(sources, k["laters"])]
        to_state = [carry_two * dot3(x, y) for x, y in zip(k["boths"], k["nows"])]
        grad_lefts = [dot3(x, y) + z for x, y, z in zip(grad_pairs, k["rights"], to_state)]
        grad_rights = [dot3(x, y, TN) for x, y in zip(grad_pairs, k["lefts"])]
        d_alpha, d_recept = join([x[:BLOCK] for x in grad_lefts], 1), join([x[BLOCK:] for x in grad_lefts], 1)
        d_beta, d_key = join([x[:BLOCK] for x in grad_rights], 1), join([x[BLOCK:] for x in grad_rights], 1)
        d_beta_end, d_key_end = join([x[:BLOCK] for x in grad_ends], 1), join([x[BLOCK:] for x in grad_ends], 1)
        ended = parts["beta_end"] * d_beta_end + parts["key_end"] * d_key_end
        alphas = parts["alpha"] * d_alpha
        d_total = parts["recept"] * d_recept - parts["beta"] * d_beta - parts["key"] * d_key - ended + alphas
        d_step = sum_left(upper, d_total) + (jnp.sum(ended, 0, keepdims=True) + k["end_sum"]) - alphas
        d_beta_plain = d_beta * parts["shrunk"] + d_beta_end * parts["tail"]
        copy_decay = low(d_step * parts["log_step"])
        copy_dir = low(d_beta_plain * k["rate_low"] - d_alpha * parts["before"])
        copy_rate = low(d_beta_plain * k["dir_low"])

        keys, values, rate, blend = k["keys"], k["values"], k["rate"], k["blend"]
        grad_recept = k["grad_recept"] + low(d_recept * parts["grown"])
        grad_key_mod = k["grad_key_mod"] + low(d_key * parts["shrunk"] + d_key_end * parts["tail"])
        grad_mixed_value = k["grad_mixed_value"] + low(join(grad_values, 1))
        grad_z = copy_decay * jax.nn.sigmoid(-k["z"])
        factor = 1.0 + (rate - 1.0) * vec[4:5]
        keyed = grad_key_mod * keys
        grad_rate = copy_rate + keyed * vec[4:5]
        grad_scaled = k["scale"] * (copy_dir - k["key_dir"] * head_sum(copy_dir * k["key_dir"], ones))
        grad_keys = grad_key_mod * factor + grad_scaled * vec[3:4]
        grad_rate_up = grad_rate * rate * (1.0 - rate)
        grad_value_up = grad_mixed_value * (k["first"] - values) * blend * (1.0 - blend)
        recept_out[rows] = grad_recept.astype(BF16)
        keys_out[rows] = grad_keys.astype(BF16)
        values_out[rows] = (grad_mixed_value * (1.0 - blend)).astype(BF16)
        first_out[rows] = (grad_mixed_value * blend).astype(BF16)
        ups_out[0, rows] = grad_z.astype(BF16)
        ups_out[1, rows] = grad_rate_up.astype(BF16)
        ups_out[2, rows] = grad_value_up.astype(BF16)
        ups_out[3, rows] = k["grad_gate"].astype(BF16)

        def total(x):
            return jnp.sum(x, 0, keepdims=True)

        vec_total = vec_total + jnp.concatenate(
            [
                total(grad_z), total(grad_rate_up), total(grad_value_up), total(grad_scaled * keys),
                total(keyed * (rate - 1.0)), total(k["grad_coefficient"] * k["product"]),
                total(k["opened"] * k["normed"]), total(k["opened"]),
            ],
            0,
        )
    vec_out[...] += vec_total


def kernel_cost(rows, width, passes):
    return pl.CostEstimate(flops=2 * rows * width * width, bytes_accessed=4 * rows * width * passes, transcendentals=0)


def per_step(rows, most):
    return most if (rows // BLOCK) % most == 0 else 1


def run_forward(recept, keys, values, hidden, first, up, vec, segments):
    rows, width = recept.shape
    count = per_step(rows, 4)
    step = count * BLOCK

    def spec(columns):
        return pl.BlockSpec((step, columns), lambda i: (i, 0))

    def whole(array):
        return pl.BlockSpec(array.shape, lambda i: (0, 0))

    return pl.pallas_call(
        functools.partial(forward_kernel, count),
        grid=(rows // step,),
        in_specs=[
            spec(width), spec(width), spec(width), spec(WIDE), spec(width), whole(up), whole(vec),
            pl.BlockSpec((count * 8, BLOCK), lambda i: (i, 0)),
        ],
        out_specs=[spec(width)] * 5,
        out_shape=[jax.ShapeDtypeStruct((rows, width), d) for d in (BF16, BF16, F32, F32, F32)],
        scratch_shapes=[pltpu.VMEM((BLOCK, width), F32)],
        compiler_params=pltpu.CompilerParams(vmem_limit_bytes=48 << 20),
        cost_estimate=kernel_cost(rows, width, 110),
        name="mix_forward",
    )(recept, keys, values, hidden, first, up, vec, segments)


def run_backward(grad, recept, keys, values, hidden, first, up, vec, segments, saved):
    rows, width = recept.shape
    count = per_step(rows, 2)
    step = count * BLOCK
    last = rows // step - 1

    def spec(columns):
        return pl.BlockSpec((step, columns), lambda i: (last - i, 0))

    def whole(array):
        return pl.BlockSpec(array.shape, lambda i: (0, 0))

    return pl.pallas_call(
        functools.partial(backward_kernel, count),
        grid=(rows // step,),
        in_specs=[
            spec(width), spec(width), spec(width), spec(width), spec(WIDE), spec(width), whole(up), whole(vec),
            pl.BlockSpec((count * 8, BLOCK), lambda i: (last - i, 0)),
            spec(width), spec(width), spec(width), spec(width),
        ],
        out_specs=[
            spec(width), spec(width), spec(width),
            pl.BlockSpec((4, step, width), lambda i: (0, last - i, 0)),
            spec(width), pl.BlockSpec((8, width), lambda i: (0, 0)),
        ],
        out_shape=[
            jax.ShapeDtypeStruct((rows, width), BF16), jax.ShapeDtypeStruct((rows, width), BF16),
            jax.ShapeDtypeStruct((rows, width), BF16), jax.ShapeDtypeStruct((4, rows, width), BF16),
            jax.ShapeDtypeStruct((rows, width), BF16), jax.ShapeDtypeStruct((8, width), F32),
        ],
        scratch_shapes=[pltpu.VMEM((BLOCK, width), F32)],
        compiler_params=pltpu.CompilerParams(vmem_limit_bytes=48 << 20),
        cost_estimate=kernel_cost(rows, width, 150),
        name="mix_backward",
    )(grad, recept, keys, values, hidden, first, up, vec, segments, *saved)


def mix_norm(block_ref, stats_ref, vec_ref):
    stats = stats_ref[...]
    flowing = stats[:, 2:3]
    standard = (block_ref[...].astype(F32) - stats[:, 0:1]) * stats[:, 1:2]
    normed = standard * vec_ref[0:1] + vec_ref[1:2]
    delta = pltpu.roll(normed, 1, 0) * flowing - normed
    return standard, normed, delta, flowing


def project_kernel(
    width, block_ref, stats_ref, vec_ref, weight_ref,
    recept_ref, keys_ref, values_ref, downs_ref, hidden_ref,
):
    base = 3 * width
    _, normed, delta, _ = mix_norm(block_ref, stats_ref, vec_ref)
    weight = weight_ref[...]
    uses = (
        ((recept_ref, 0, width, 0),),
        ((downs_ref, base + OFFSETS[0], PADDED[0], OFFSETS[0]),),
        ((keys_ref, width, width, 0),),
        ((values_ref, 2 * width, width, 0), (downs_ref, base + OFFSETS[2], PADDED[2], OFFSETS[2])),
        ((downs_ref, base + OFFSETS[1], PADDED[1], OFFSETS[1]),),
        ((downs_ref, base + OFFSETS[3], PADDED[3], OFFSETS[3]),),
    )

    @pl.when(pl.program_id(0) == 0)
    def _():
        for ref in (recept_ref, keys_ref, values_ref, downs_ref):
            ref[...] = jnp.zeros_like(ref)

    for c, targets in enumerate(uses):
        mixed = (normed + delta * vec_ref[2 + c : 3 + c]).astype(BF16)
        for ref, start, size, at in targets:
            ref[:, at : at + size] += dot(mixed, weight[:, start : start + size])

    @pl.when(pl.program_id(0) == pl.num_programs(0) - 1)
    def _():
        hidden_ref[:, 0:128] = jnp.tanh(downs_ref[:, 0:128]).astype(BF16)
        hidden_ref[:, 128:384] = downs_ref[:, 128:384].astype(BF16)
        hidden_ref[:, 384:640] = jax.nn.sigmoid(downs_ref[:, 384:640]).astype(BF16)


def unproject_kernel(
    width, parts, piece, block_ref, stats_ref, vec_ref, weight_ref,
    other_ref, recept_ref, keys_ref, values_ref, ups_ref, hidden_ref, downs_ref, up_ref,
    grad_ref, sums_ref, wide_ref, up_out, down_lows,
):
    rows = block_ref.shape[0]
    base = 3 * width

    @pl.when(pl.program_id(0) == 0)
    def _():
        sums_ref[...] = jnp.zeros_like(sums_ref)
        for k, (at, size) in enumerate(zip(OFFSETS, PADDED)):
            cols = slice(at, at + size)
            grad = dot(ups_ref[k], up_ref[cols], NT)
            if k == 0:
                grad = grad * (1.0 - jnp.square(jnp.tanh(downs_ref[:, cols])))
            if k == 3:
                opening = jax.nn.sigmoid(downs_ref[:, cols])
                grad = grad * opening * (1.0 - opening)
            down_lows[:, cols] = grad.astype(BF16)
            up_out[:, cols] = dot(ups_ref[k], hidden_ref[:, cols], TN).astype(BF16)

    standard, normed, delta, flowing = mix_norm(block_ref, stats_ref, vec_ref)
    weight = weight_ref[...]

    def down(k):
        return (down_lows[:, OFFSETS[k] : OFFSETS[k] + PADDED[k]], base + OFFSETS[k], PADDED[k])

    uses = (
        ((recept_ref[...], 0, width),),
        (down(0),),
        ((keys_ref[...], width, width),),
        ((values_ref[...], 2 * width, width), down(2)),
        (down(1),),
        (down(3),),
    )
    kept, sent, vec_rows = None, None, []
    per_seq = parts * piece
    for c, sources in enumerate(uses):
        share = vec_ref[2 + c : 3 + c]
        mixed = (normed + delta * share).astype(BF16)
        grad = None
        for source, start, size in sources:
            part = dot(source, weight[:, start : start + size], NT)
            grad = part if grad is None else grad + part
            product = dot(mixed, source, TN).astype(BF16)
            for number in range(product.shape[0] // per_seq):
                for w in range(parts):
                    at = number * per_seq + w * piece
                    wide_ref[w, number, :, start : start + size] = product[at : at + piece]
        vec_rows.append(jnp.sum(grad * delta, 0, keepdims=True))
        moved = grad * share
        kept = grad - moved if kept is None else kept + (grad - moved)
        sent = moved if sent is None else sent + moved
    grad = kept + pltpu.roll(sent * flowing, rows - 1, 0)
    vec_rows = jnp.concatenate(
        [jnp.sum(grad * standard, 0, keepdims=True), jnp.sum(grad, 0, keepdims=True)] + vec_rows, 0
    )
    spare = jnp.concatenate([vec_rows.T, other_ref[...]], 1).astype(BF16)
    for number in range(spare.shape[0] // per_seq):
        for w in range(parts):
            at = number * per_seq + w * piece
            wide_ref[w, number, :, base + RANKS[0] : base + PADDED[0]] = spare[at : at + piece]
    scaled = grad * vec_ref[0:1]
    sums_ref[:, 0:1] += jnp.sum(scaled, 1, keepdims=True)
    sums_ref[:, 1:2] += jnp.sum(scaled * standard, 1, keepdims=True)
    grad_ref[...] = scaled


def mix_specs(rows, width, own_width, parts):
    block = 256 if rows <= 1024 else 128

    def columns(height):
        return pl.BlockSpec((height, block), lambda j: (0, j))

    def whole(shape):
        return pl.BlockSpec(shape, lambda j: (0,) * len(shape))

    def weights(array):
        size = array.shape[1] if rows > 1024 else 3 * own_width + WIDE
        return pl.BlockSpec((block, size), lambda j: (j, 0))

    return block, columns, whole, weights


def run_project(balanced, stats, vec, weights, own_width, parts):
    rows, width = balanced.shape
    block, columns, whole, weight_spec = mix_specs(rows, width, own_width, parts)
    shapes = [(rows, own_width)] * 3 + [(rows, WIDE)] * 2
    return pl.pallas_call(
        functools.partial(project_kernel, own_width),
        grid_spec=pltpu.PrefetchScalarGridSpec(
            num_scalar_prefetch=0,
            grid=(width // block,),
            in_specs=[columns(rows), whole(stats.shape), columns(8), weight_spec(weights)],
            out_specs=[whole(s) for s in shapes],
        ),
        out_shape=[jax.ShapeDtypeStruct(s, d) for s, d in zip(shapes, (F32, F32, F32, F32, BF16))],
        compiler_params=pltpu.CompilerParams(vmem_limit_bytes=60 << 20),
        cost_estimate=kernel_cost(rows, own_width, 60),
        name="mix_project",
    )(balanced, stats, vec, weights)


def run_unproject(balanced, stats, vec, weights, others, lows, ups, hidden, downs, up, parts):
    rows, width = balanced.shape
    own_width = lows[0].shape[1]
    seqs = width // own_width
    piece = own_width // parts
    block, columns, whole, weight_spec = mix_specs(rows, width, own_width, parts)
    taken = block // own_width
    total = 3 * own_width + WIDE
    return pl.pallas_call(
        functools.partial(unproject_kernel, own_width, parts, piece),
        grid_spec=pltpu.PrefetchScalarGridSpec(
            num_scalar_prefetch=0,
            grid=(width // block,),
            in_specs=[
                columns(rows), whole(stats.shape), columns(8), weight_spec(weights),
                pl.BlockSpec((block, others.shape[1]), lambda j: (j, 0)),
            ]
            + [whole(a.shape) for a in (*lows, ups, hidden, downs, up)],
            out_specs=[
                columns(rows), whole((rows, 2)),
                pl.BlockSpec((parts, taken, piece, total), lambda j: (0, j, 0, 0)),
                whole((own_width, WIDE)),
            ],
            scratch_shapes=[pltpu.VMEM((rows, WIDE), BF16)],
        ),
        out_shape=[
            jax.ShapeDtypeStruct((rows, width), F32), jax.ShapeDtypeStruct((rows, 2), F32),
            jax.ShapeDtypeStruct((parts, seqs, piece, total), BF16),
            jax.ShapeDtypeStruct((own_width, WIDE), BF16),
        ],
        compiler_params=pltpu.CompilerParams(vmem_limit_bytes=60 << 20),
        cost_estimate=kernel_cost(rows, own_width, 120),
        name="mix_unproject",
    )(balanced, stats, vec, weights, others, *lows, ups, hidden, downs, up)


def norm_stats(values):
    centered = values - jnp.mean(values, -1, keepdims=True)
    scale = lax.rsqrt(jnp.mean(centered * centered, -1, keepdims=True) + 1e-05)
    return centered * scale, scale


def norm_back(grad, standard, scale, gain):
    scaled = grad * gain
    return scale * (
        scaled
        - jnp.mean(scaled, -1, keepdims=True)
        - standard * jnp.mean(scaled * standard, -1, keepdims=True)
    )


def pad_ranks(matrix):
    pieces, start = [], 0
    for rank, padded in zip(RANKS, PADDED):
        pieces.append(jnp.pad(matrix[:, start : start + rank], ((0, 0), (0, padded - rank))))
        start += rank
    return jnp.concatenate(pieces, 1)


def unpad_ranks(matrix):
    return jnp.concatenate([matrix[..., o : o + r] for o, r in zip(OFFSETS, RANKS)], -1)


MESH_ID = pl.DeviceIdType.MESH


def places():
    s, w = lax.axis_index("seq"), lax.axis_index("wsh")
    side = s % 2
    return s, w, side, s // 2, (s + 1 - 2 * side, w), (s, w + 1 - 2 * (w % 2)), (s, w + 2 - 4 * (w // 2))


def greet(neighbours, number):
    barrier = pltpu.get_barrier_semaphore()
    for there, device in neighbours:
        if there is None:
            pl.semaphore_signal(barrier, inc=1, device_id=device, device_id_type=MESH_ID)
        else:

            @pl.when(there)
            def _(device=device):
                pl.semaphore_signal(barrier, inc=1, device_id=device, device_id_type=MESH_ID)

    pl.semaphore_wait(barrier, number)


def send(source, target, send_sem, recv_sem, device):
    return pltpu.make_async_remote_copy(
        src_ref=source, dst_ref=target, send_sem=send_sem, recv_sem=recv_sem, device_id=device, device_id_type=MESH_ID
    )


def line_ends(z):
    return jnp.where(z > 0, 1, 0) + jnp.where(z < 3, 1, 0)


def gather_kernel(
    own_ref, tail_ref, weight_ref, out_ref, tails_ref, weights_ref,
    copy_sem, right_send, right_recv, left_send, left_recv, x_send, x_recv, c_send, c_recv, y_send, y_recv,
):
    s, w, side, z, x_device, core_device, y_device = places()
    up, down = (s + 2, w), (s - 2, w)
    across = w + 2 - 4 * (w // 2)
    kinds = ((own_ref, out_ref), (tail_ref, tails_ref))
    copies = [pltpu.make_async_copy(own, out.at[s], copy_sem.at[k]) for k, (own, out) in enumerate(kinds)]
    copies.append(pltpu.make_async_copy(weight_ref, weights_ref.at[w], copy_sem.at[2]))
    for copy in copies:
        copy.start()
    greet(((None, x_device), (None, core_device), (None, y_device), (z < 3, up), (z > 0, down)), 3 + line_ends(z))

    weight_y = send(weight_ref, weights_ref.at[w], y_send, y_recv, y_device)
    weight_core = send(weight_ref, weights_ref.at[w], c_send.at[0], c_recv.at[0], core_device)
    weight_on = send(weights_ref.at[across], weights_ref.at[across], c_send.at[1], c_recv.at[1], core_device)
    weight_y.start()
    weight_core.start()

    def to_right(j, k, source, number):
        return send(source, kinds[k][1].at[number], right_send.at[j, k], right_recv.at[j, k], up)

    def to_left(j, k, source, number):
        return send(source, kinds[k][1].at[number], left_send.at[j, k], left_recv.at[j, k], down)

    def to_x(at, k, source, number):
        return send(source, kinds[k][1].at[number], x_send.at[at, k], x_recv.at[at, k], x_device)

    for k, (own, _) in enumerate(kinds):

        @pl.when(z < 3)
        def _(k=k, own=own):
            to_right(0, k, own, s).start()

        @pl.when(z > 0)
        def _(k=k, own=own):
            to_left(0, k, own, s).start()

        to_x(z, k, own, s).start()
    for j in (1, 2, 3):
        lower, upper = s - 2 * j, s + 2 * j
        for k, (_, out) in enumerate(kinds):

            @pl.when(z >= j)
            def _(j=j, k=k, out=out, lower=lower):
                block = out.at[lower]
                to_right(j - 1, k, block, lower).wait_recv()

                @pl.when(z < 3)
                def _():
                    to_right(j, k, block, lower).start()

                to_x(z - j, k, block, lower).start()

            @pl.when(z + j <= 3)
            def _(j=j, k=k, out=out, upper=upper):
                block = out.at[upper]
                to_left(j - 1, k, block, upper).wait_recv()

                @pl.when(z > 0)
                def _():
                    to_left(j, k, block, upper).start()

                to_x(z + j, k, block, upper).start()

    weight_y.wait_recv()
    weight_on.start()
    for k, (own, _) in enumerate(kinds):
        for number in range(4):
            done = to_x(number, k, own, s)
            done.wait_send()
            done.wait_recv()
        for j in range(3):

            @pl.when((z >= j) & (z < 3))
            def _(j=j, k=k, own=own):
                to_right(j, k, own, s).wait_send()

            @pl.when((z + j <= 3) & (z > 0))
            def _(j=j, k=k, own=own):
                to_left(j, k, own, s).wait_send()

    weight_core.wait_recv()
    weight_on.wait_recv()
    for copy in (weight_y, weight_core, weight_on):
        copy.wait_send()
    for copy in copies:
        copy.wait()


def gather_first(own, tail, weight):
    seqs, parts = lax.axis_size("seq"), lax.axis_size("wsh")
    if seqs != 8 or parts != 4:
        return (
            lax.all_gather(own, "seq", axis=0, tiled=False),
            lax.all_gather(tail, "seq", axis=0, tiled=False),
            lax.all_gather(weight, "wsh", axis=0, tiled=False),
        )
    dma = pltpu.SemaphoreType.DMA
    given = ((seqs, own), (seqs, tail), (parts, weight))
    return pl.pallas_call(
        gather_kernel,
        in_specs=[pl.BlockSpec(memory_space=pltpu.VMEM)] * 3,
        out_specs=[pl.BlockSpec(memory_space=pl.ANY)] * 3,
        out_shape=[jax.ShapeDtypeStruct((n,) + x.shape, x.dtype) for n, x in given],
        scratch_shapes=[dma((3,))] + [dma((3, 2))] * 4 + [dma((4, 2))] * 2 + [dma((2,))] * 2 + [dma] * 2,
        compiler_params=pltpu.CompilerParams(collective_id=1, has_side_effects=True),
        cost_estimate=pl.CostEstimate(flops=0, bytes_accessed=100 << 20, transcendentals=0),
        name="gather_first",
    )(own, tail, weight)


def reduce_kernel(
    splits, x_ref, out_ref, x_buf, right_buf, left_buf, right_out, left_out,
    x_send, x_recv, right_send, right_recv, left_send, left_recv,
):
    s, w, side, z, x_device, _, _ = places()
    up, down = (s + 2, w), (s - 2, w)
    size = x_ref.shape[2] // splits
    columns = [slice(c * size, (c + 1) * size) for c in range(splits)]
    greet(((None, x_device), (z < 3, up), (z > 0, down)), 1 + line_ends(z))

    def to_x(target, c):
        return send(
            x_ref.at[target * 2 + 1 - side, :, columns[c]], x_buf.at[target, :, columns[c]],
            x_send.at[target, c], x_recv.at[target, c], x_device,
        )

    def start_x(target):
        for c in range(splits):
            to_x(target, c).start()

    def to_right(k, c):
        return send(
            right_out.at[k - 1, :, columns[c]], right_buf.at[k - 1, :, columns[c]],
            right_send.at[k - 1, c], right_recv.at[k - 1, c], up,
        )

    def to_left(k, c):
        return send(
            left_out.at[k - 1, :, columns[c]], left_buf.at[k - 1, :, columns[c]],
            left_send.at[k - 1, c], left_recv.at[k - 1, c], down,
        )

    def pair(target, c):
        to_x(target, c).wait_recv()
        return x_ref[target * 2 + side, :, columns[c]].astype(F32) + x_buf[target, :, columns[c]].astype(F32)

    for k in (3, 2, 1):

        @pl.when(z + k <= 3)
        def _(k=k):
            start_x(z + k)

        @pl.when(z >= k)
        def _(k=k):
            start_x(z - k)

    start_x(z)
    for k in (3, 2, 1):
        for c in range(splits):

            @pl.when(z + k <= 3)
            def _(k=k, c=c):
                right_out[k - 1, :, columns[c]] = pair(z + k, c).astype(BF16)
                if k < 3:

                    @pl.when(z > 0)
                    def _():
                        to_right(k + 1, c).wait_recv()
                        right_out[k - 1, :, columns[c]] = (
                            right_out[k - 1, :, columns[c]].astype(F32) + right_buf[k, :, columns[c]].astype(F32)
                        ).astype(BF16)

                to_right(k, c).start()

            @pl.when(z >= k)
            def _(k=k, c=c):
                left_out[k - 1, :, columns[c]] = pair(z - k, c).astype(BF16)
                if k < 3:

                    @pl.when(z < 3)
                    def _():
                        to_left(k + 1, c).wait_recv()
                        left_out[k - 1, :, columns[c]] = (
                            left_out[k - 1, :, columns[c]].astype(F32) + left_buf[k, :, columns[c]].astype(F32)
                        ).astype(BF16)

                to_left(k, c).start()

    for c in range(splits):
        out_ref[:, columns[c]] = pair(z, c)

        @pl.when(z > 0)
        def _(c=c):
            to_right(1, c).wait_recv()
            out_ref[:, columns[c]] += right_buf[0, :, columns[c]].astype(F32)

        @pl.when(z < 3)
        def _(c=c):
            to_left(1, c).wait_recv()
            out_ref[:, columns[c]] += left_buf[0, :, columns[c]].astype(F32)

    for c in range(splits):
        for target in range(4):
            to_x(target, c).wait_send()
        for k in (3, 2, 1):

            @pl.when(z + k <= 3)
            def _(k=k, c=c):
                to_right(k, c).wait_send()

            @pl.when(z >= k)
            def _(k=k, c=c):
                to_left(k, c).wait_send()


def reduce_seq(x):
    seqs, rows, width = x.shape
    if seqs != 8 or lax.axis_size("wsh") != 4:
        return jnp.sum(exchange(x, "seq").astype(F32), 0)
    splits = 2
    return pl.pallas_call(
        functools.partial(reduce_kernel, splits),
        in_specs=[pl.BlockSpec(memory_space=pltpu.VMEM)],
        out_specs=pl.BlockSpec(memory_space=pltpu.VMEM),
        out_shape=jax.ShapeDtypeStruct((rows, width), F32),
        scratch_shapes=[pltpu.VMEM((4, rows, width), BF16)]
        + [pltpu.VMEM((3, rows, width), BF16)] * 4
        + [pltpu.SemaphoreType.DMA((4, splits))] * 2
        + [pltpu.SemaphoreType.DMA((3, splits))] * 4,
        compiler_params=pltpu.CompilerParams(collective_id=2, has_side_effects=True, vmem_limit_bytes=40 << 20),
        cost_estimate=pl.CostEstimate(flops=0, bytes_accessed=1 << 20, transcendentals=0),
        name="reduce_seq",
    )(x)


def channel_kernel(
    forward, x_ref, first_hbm, second_hbm, active_hbm,
    sum_ref, all_hbm, mine_hbm, other_hbm, extra_hbm,
    first, second, rows_all, middle, active, part, core_buf, far_out, far_buf,
    load_sem, store_sem, core_send, core_recv, y_send, y_recv, x_send, x_recv, r_send, r_recv, f_send, f_recv,
):
    s, w, side, z, x_device, core_device, y_device = places()
    rows, width = x_ref.shape
    units = first.shape[0]
    half = units // 2
    loads = [
        pltpu.make_async_copy(first_hbm, first, load_sem.at[0]),
        pltpu.make_async_copy(second_hbm, second, load_sem.at[1]),
    ]
    if not forward:
        loads.append(pltpu.make_async_copy(active_hbm, active, load_sem.at[2]))
    for load in loads:
        load.start()
    rows_all[0:rows] = x_ref[...]
    greet(((None, x_device), (None, core_device), (None, y_device)), 3)

    def block(number):
        return rows_all.at[pl.ds(number * rows, rows)]

    to_core = [
        send(block(0), block(1), core_send.at[0], core_recv.at[0], core_device),
        send(block(2), block(3), core_send.at[1], core_recv.at[1], core_device),
    ]
    to_y = send(block(0), block(2), y_send, y_recv, y_device)
    if forward:
        to_x = [
            send(
                middle.at[1 - side, pl.ds(2 * n * rows, 2 * rows)], other_hbm.at[pl.ds(2 * n * rows, 2 * rows)],
                x_send.at[n], x_recv.at[n], x_device,
            )
            for n in range(2)
        ]
    else:
        to_x = [
            send(block(n), other_hbm.at[pl.ds(n * rows, rows)], x_send.at[n], x_recv.at[n], x_device) for n in range(4)
        ]
    sums_core = [
        send(part.at[pl.ds((2 * n + 1) * rows, rows)], core_buf.at[n], r_send.at[n], r_recv.at[n], core_device)
        for n in range(2)
    ]
    far = send(far_out, far_buf, f_send, f_recv, y_device)
    stores = [
        pltpu.make_async_copy(rows_all, all_hbm, store_sem.at[0]),
        pltpu.make_async_copy(middle.at[side], mine_hbm, store_sem.at[1]),
        pltpu.make_async_copy(active if forward else middle.at[1 - side], extra_hbm, store_sem.at[2]),
    ]

    def pass_on(number):
        if not forward:
            to_x[number].start()

    to_y.start()
    to_core[0].start()
    pass_on(0)
    tile = min(512, half)

    def multiply(number):
        two = pl.ds(2 * number * rows, 2 * rows)

        def up(t, carry):
            for side_units in range(2):
                at = pl.multiple_of(t * tile, tile)
                unit = pl.multiple_of(side_units * half + at, tile)
                raw = dot(rows_all[two, :], first[pl.ds(unit, tile), :], NT)
                if forward:
                    raw = jnp.maximum(raw, 0.0)
                    active[two, pl.ds(unit, tile)] = raw
                    mid = raw * raw
                else:
                    mid = raw * 2.0 * active[two, pl.ds(unit, tile)]
                middle[side_units, two, pl.ds(at, tile)] = mid.astype(BF16)
            return carry

        lax.fori_loop(0, half // tile, up, 0)
        if forward:
            to_x[number].start()
        if number == 0:
            loads[1].wait()

        def down(t, carry):
            at = pl.multiple_of(t * tile, tile)
            part[two, pl.ds(at, tile)] = dot(middle[0, two, :], second[0:half, pl.ds(at, tile)]) + dot(
                middle[1, two, :], second[half:units, pl.ds(at, tile)]
            )
            return carry

        lax.fori_loop(0, width // tile, down, 0)
        sums_core[number].start()

    loads[0].wait()
    if not forward:
        loads[2].wait()
    to_core[0].wait_recv()
    pass_on(1)
    multiply(0)
    to_y.wait_recv()
    to_core[1].start()
    pass_on(2)
    to_core[1].wait_recv()
    pass_on(3)
    stores[0].start()
    multiply(1)
    for store in stores[1:]:
        store.start()
    sums_core[1].wait_recv()
    far_out[...] = (part[2 * rows : 3 * rows] + core_buf[1]).astype(BF16)
    far.start()
    sums_core[0].wait_recv()
    sum_ref[...] = part[0:rows] + core_buf[0]
    far.wait_recv()
    sum_ref[...] += far_buf[...].astype(F32)
    for copy in to_x:
        copy.wait_recv()
    for copy in to_x + to_core + sums_core + [to_y, far]:
        copy.wait_send()
    for store in stores:
        store.wait()


def channel_stage(x, first, second, active):
    rows, width = x.shape
    units = first.shape[0]
    forward = active is None
    given = (x, first, second) if forward else (x, first, second, active)
    everything = pl.BlockSpec(memory_space=pl.ANY)
    shapes = [
        ((rows, width), F32), ((4 * rows, width), BF16), ((4 * rows, units // 2), BF16),
        ((4 * rows, units // 2 if forward else width), BF16),
        ((4 * rows, units), F32) if forward else ((4 * rows, units // 2), BF16),
    ]

    def body(*refs):
        refs = list(refs)
        if forward:
            refs.insert(3, None)
        channel_kernel(forward, *refs)

    dma = pltpu.SemaphoreType.DMA
    return pl.pallas_call(
        body,
        in_specs=[pl.BlockSpec(memory_space=pltpu.VMEM)] + [everything] * (len(given) - 1),
        out_specs=[pl.BlockSpec(memory_space=pltpu.VMEM)] + [everything] * (len(shapes) - 1),
        out_shape=[jax.ShapeDtypeStruct(s, d) for s, d in shapes],
        scratch_shapes=[
            pltpu.VMEM((units, width), BF16), pltpu.VMEM((units, width), BF16), pltpu.VMEM((4 * rows, width), BF16),
            pltpu.VMEM((2, 4 * rows, units // 2), BF16), pltpu.VMEM((4 * rows, units), F32),
            pltpu.VMEM((4 * rows, width), F32), pltpu.VMEM((2, rows, width), F32),
            pltpu.VMEM((rows, width), BF16), pltpu.VMEM((rows, width), BF16),
            dma((3,)), dma((3,)), dma((2,)), dma((2,)), dma, dma, dma((4,)), dma((4,)), dma((2,)), dma((2,)),
            dma, dma,
        ],
        compiler_params=pltpu.CompilerParams(
            collective_id=3 if forward else 4, has_side_effects=True, vmem_limit_bytes=60 << 20
        ),
        cost_estimate=pl.CostEstimate(flops=0, bytes_accessed=100 << 20, transcendentals=0),
        name="channel_forward" if forward else "channel_backward",
    )(*given)


def from_behind(x, axis, by):
    size = lax.axis_size(axis)
    pairs = [(i, i + by) for i in range(size) if 0 <= i + by < size]
    return lax.ppermute(x, axis, pairs)


def exchange(x, axis):
    return lax.all_to_all(x, axis, split_axis=0, concat_axis=0, tiled=True)


def swap(x, by):
    size = lax.axis_size("wsh")
    return lax.ppermute(x, "wsh", [(i, i ^ by) for i in range(size)])


def gather_near(x):
    if lax.axis_size("wsh") != 4:
        return lax.all_gather(x, "wsh", axis=0, tiled=True)
    return gathered_near(x, swap(x, 1), swap(x, 2))


def gathered_near(x, beside, across):
    return jnp.concatenate([x, beside, across, swap(across, 1)], 0)


def beside(x):
    return lax.ppermute(x, "seq", [(i, i ^ 1) for i in range(lax.axis_size("seq"))])


def scalar_sum(x):
    if lax.axis_size("wsh") != 4:
        return jnp.sum(lax.all_gather(x.reshape(1), "wsh", axis=0, tiled=True))
    x = jnp.full((8, 128), x)
    x = x + swap(x, 1)
    return (x + swap(x, 2))[0, 0]


def near_sum(x):
    if lax.axis_size("wsh") != 4:
        return lax.psum_scatter(x, "wsh", scatter_dimension=0, tiled=True)
    rows = x.shape[0] // 4
    beside = swap(jnp.concatenate([x[rows : 2 * rows], x[3 * rows :]], 0), 1)
    far = x[2 * rows : 3 * rows] + beside[rows:]
    return x[:rows] + beside[:rows] + swap(far.astype(BF16), 2).astype(F32)


def block_sum(x):
    if lax.axis_size("wsh") != 4:
        return lax.psum_scatter(x, "wsh", scatter_dimension=0, tiled=False).astype(F32)
    kept, far = block_halves(x)
    return kept + swap(far, 2).astype(F32)


def block_halves(x):
    number = lax.axis_index("wsh")

    def block(by):
        return lax.dynamic_index_in_dim(x, number ^ by, 0, keepdims=False)

    beside = swap(jnp.stack([block(1), block(3)]), 1).astype(F32)
    return block(0).astype(F32) + beside[0], (block(2).astype(F32) + beside[1]).astype(BF16)


def local(
    tokens, first_layer_values, teacher, valid, destination, lengths,
    receptance_matrix, key_matrix, value_matrix, output_matrix,
    lowrank_down_weight, lowrank_up_weight, channel_key_weight, channel_value_weight, vectors,
):
    rows, width = tokens.shape
    seqs, parts = lax.axis_size("seq"), lax.axis_size("wsh")
    me = lax.axis_index("seq")
    group = rows * seqs
    own_width = width // seqs
    shard = width // parts
    piece = shard // seqs
    column = me * own_width

    def own_columns(matrix):
        return lax.dynamic_slice_in_dim(matrix, column, own_width, 1)

    near = parts == 4
    up_piece = lax.dynamic_slice_in_dim(lowrank_up_weight, column % shard, own_width, 0)
    total = 3 * own_width + WIDE
    own_weights = jnp.concatenate(
        [
            own_columns(receptance_matrix), own_columns(key_matrix), own_columns(value_matrix),
            pad_ranks(lowrank_down_weight), up_piece.reshape(shard, -1),
        ],
        1,
    )

    dest_seq = destination // rows // parts
    position = dest_seq * rows + destination % rows
    digits = jnp.stack([position // DIGIT, position % DIGIT, valid], 1).astype(BF16)
    tail = jnp.pad(digits, ((0, 0), (0, EXTRA - 3)))
    given, tails, weights = gather_first(tokens, tail, own_weights)
    given, tails, weights = given.reshape(group, width), tails.reshape(group, EXTRA), weights.reshape(width, -1)
    info = tails[:, :3].astype(F32)
    places = (info[:, 0] * DIGIT + info[:, 1]).astype(jnp.int32)
    numbers = jnp.arange(group, dtype=jnp.int32)
    permute = (numbers[:, None] == places[None, :]).astype(BF16)
    total_valid = scalar_sum(jnp.sum(info[:, 2]))

    index = jnp.arange(rows, dtype=jnp.int32)
    same_dest = (dest_seq[:, None] == dest_seq[None, :]) & (index[None, :] < index[:, None])
    slot = dest_seq * (rows // seqs) + jnp.sum(same_dest.astype(jnp.int32), 1)
    arrange = (index[:, None] == slot[None, :]).astype(BF16)
    mine = (places // rows) == me
    arrival = jnp.cumsum(mine.astype(jnp.int32)) - 1
    own_rows = ((index[:, None] + me * rows) == places[None, :]).astype(BF16)
    settle = dot(own_rows, (mine[:, None] & (arrival[:, None] == index[None, :])).astype(BF16)).astype(BF16)

    offsets = jnp.cumsum(lengths[0]) - lengths[0]
    starts = jnp.any(numbers[:, None] == offsets[None, :], 1).astype(F32)
    segment_ids = jnp.cumsum(starts).reshape(-1, BLOCK)
    before = segment_ids[:, :1] - starts.reshape(-1, BLOCK)[:, :1]
    segments = jnp.stack(
        [segment_ids, jnp.broadcast_to(before, segment_ids.shape), jnp.broadcast_to(segment_ids[:, -1:], segment_ids.shape)]
        + [jnp.zeros_like(segment_ids)] * 5,
        1,
    ).reshape(-1, BLOCK)
    flowing = (1.0 - starts)[:, None]

    up = pad_ranks(
        lax.dynamic_slice(
            weights, (column // shard * shard, total), (shard, weights.shape[1] - total)
        ).reshape(own_width, -1)
    ).T
    vec = lax.dynamic_slice_in_dim(vectors, column, own_width, 0)[:, 8:16].T

    output_late, given = lax.optimization_barrier((output_matrix, given))
    w_out = lax.all_gather(output_late, "wsh", axis=0, tiled=True)
    balanced = dot(permute, given).astype(BF16)
    wide_rows = balanced.astype(F32)
    mean = jnp.mean(wide_rows, -1, keepdims=True)
    scale_one = lax.rsqrt(jnp.mean(jnp.square(wide_rows - mean), -1, keepdims=True) + 1e-05)
    stats = jnp.concatenate([mean, scale_one, flowing, flowing], 1)
    mix_vec = vectors[:, :8].T
    first_values, stats = lax.optimization_barrier((first_layer_values, stats))
    first_given = exchange(
        first_values.reshape(rows, seqs, own_width).transpose(1, 0, 2), "seq"
    ).reshape(group, own_width)
    recept, keys, values, downs, hidden = run_project(balanced, stats, mix_vec, weights, own_width, parts)
    teacher_late, recept, first_given = lax.optimization_barrier((teacher, recept, first_given))
    first = dot(permute, first_given).astype(BF16)
    teacher_rows = exchange(dot(arrange, teacher_late).astype(BF16).reshape(seqs, rows // seqs, width), "seq")
    inputs = (recept, keys, values, hidden, first, up, vec, segments)
    mixed_out, *saved = run_forward(*inputs)
    teacher_rows, mixed_out = lax.optimization_barrier((teacher_rows, mixed_out))
    target = dot(settle, teacher_rows.reshape(rows, width))

    mixed_rows = exchange(mixed_out.reshape(seqs, rows, own_width), "seq").transpose(1, 0, 2).reshape(rows, width)
    own = lax.dynamic_slice_in_dim(balanced, me * rows, rows, 0).astype(F32)
    own_starts = lax.dynamic_slice_in_dim(starts, me * rows, rows, 0)
    own_flowing = (1.0 - own_starts)[:, None]
    own_valid = dot(own_rows, tails)[:, 2]
    residual = own + dot(mixed_rows, w_out)
    standard_two, scale_two = norm_stats(residual)
    normed_two = standard_two * vectors[:, 16] + vectors[:, 17]
    carried_two = from_behind(normed_two[-1:], "seq", 1)
    delta_two = jnp.concatenate([carried_two, normed_two[:-1]], 0) * own_flowing - normed_two
    channel_in = (normed_two + delta_two * vectors[:, 18]).astype(BF16)
    paired = near and seqs == 8
    if paired:
        summed, channel, hidden_mine, hidden_other, active = channel_stage(
            channel_in, channel_key_weight, channel_value_weight, None
        )
    else:
        channel = gather_near(channel_in)
        active = jax.nn.relu(dot(channel, channel_key_weight, NT))
        hidden_rows = jnp.square(active).astype(BF16)
        summed = near_sum(dot(hidden_rows, channel_value_weight))
    result = residual + summed
    total_tokens = group * parts
    cotangent = (result - target) * (own_valid * (total_tokens / total_valid))[:, None]
    cot_low = cotangent.astype(BF16)

    if paired:
        grad_channel, cot, pre_mine, cot_other, pre_spare = channel_stage(
            cot_low, channel_value_weight, channel_key_weight, active
        )
        channel_other, pre_other = beside(channel), beside(pre_spare)
    else:
        cot = gather_near(cot_low)
        grad_pre = (dot(cot, channel_value_weight, NT) * 2.0 * active).astype(BF16)
        grad_channel = near_sum(dot(grad_pre, channel_key_weight))
    grad_vec_mix_two = jnp.sum(grad_channel * delta_two, 0)
    shifted = grad_channel * vectors[:, 18] * own_flowing
    behind = from_behind(shifted[:1], "seq", -1)
    grad_normed_two = grad_channel * (1.0 - vectors[:, 18]) + jnp.concatenate([shifted[1:], behind], 0)
    grad_residual = cotangent + norm_back(grad_normed_two, standard_two, scale_two, vectors[:, 16])
    grad_low = grad_residual.astype(BF16)

    grad_posted = dot(grad_low, w_out, NT).astype(BF16)
    if paired:
        hidden_mine, grad_posted = lax.optimization_barrier((hidden_mine, grad_posted))
        value_part = (dot(hidden_mine, cot, TN) + dot(hidden_other, cot_other, TN)).astype(BF16)
    else:
        value_part = dot(hidden_rows, cot, TN).astype(BF16)
    grad_heads = exchange(grad_posted.reshape(rows, seqs, own_width).transpose(1, 0, 2), "seq").reshape(group, own_width)
    grad_heads, value_part, mixed_late = lax.optimization_barrier((grad_heads, value_part, mixed_rows))
    lefts = exchange(mixed_late.reshape(rows, seqs, parts, piece).transpose(2, 0, 1, 3), "wsh")
    near_grad = (swap(grad_low, 1), swap(grad_low, 2)) if near else gather_near(grad_low)
    recept_low, keys_low, values_low, ups_low, grad_first, grad_vec_heads = run_backward(grad_heads, *inputs, saved)
    if paired:
        channel_other, pre_other, lefts, near_grad, recept_low = lax.optimization_barrier(
            (channel_other, pre_other, lefts, near_grad, recept_low)
        )
        key_part = (dot(pre_mine, channel, TN) + dot(pre_other, channel_other, TN)).astype(BF16)
    else:
        lefts, near_grad, recept_low = lax.optimization_barrier((lefts, near_grad, recept_low))
        key_part = dot(grad_pre, channel, TN).astype(BF16)
    if near:
        near_grad = gathered_near(grad_low, *near_grad)
        lefts = jnp.stack([lax.dynamic_index_in_dim(lefts, lax.axis_index("wsh") ^ k, 0, keepdims=False) for k in range(4)])
    out_part = dot(lefts.reshape(rows * parts, -1), near_grad, TN).astype(BF16)

    result_back = dot(settle, result.astype(BF16), TN).astype(BF16).reshape(seqs, rows // seqs, width)
    first_back = dot(permute, grad_first, TN).astype(BF16).reshape(seqs, rows // seqs, width)
    moved = exchange(jnp.concatenate([result_back, first_back], 1), "seq")
    recept_low, key_part, out_part = lax.optimization_barrier((recept_low, key_part, out_part))
    if paired:
        lines = [[0, 2, 4, 6], [1, 3, 5, 7]]
        turned = [
            ((z * 2 + x) * 4 + w, (w * 2 + x) * 4 + z) for z in range(4) for x in range(2) for w in range(4)
        ]

        def along(part):
            return lax.psum_scatter(part, "seq", scatter_dimension=0, tiled=True, axis_index_groups=lines)

        def turn(part):
            return lax.ppermute(part, ("seq", "wsh"), turned)

        halves_out = out_part.reshape(seqs // 2, 2, piece, width)
        x_side = me % 2
        out_mine = lax.dynamic_index_in_dim(halves_out, x_side, 1, keepdims=False).astype(F32)
        out_other = beside(lax.dynamic_index_in_dim(halves_out, 1 - x_side, 1, keepdims=False))
        value_turned, key_sum = turn(along(value_part)), along(key_part)
    else:
        moves = [(s * parts + w, w * seqs + s) for s in range(seqs) for w in range(parts)]

        def ffn_grad(part):
            part = lax.psum_scatter(part, "seq", scatter_dimension=0, tiled=True)
            return lax.ppermute(part, ("seq", "wsh"), moves).astype(F32)

        grad_ffn_value, grad_ffn_key = ffn_grad(value_part), ffn_grad(key_part)
        grad_out = lax.psum_scatter(out_part, "seq", scatter_dimension=0, tiled=True)

    heads_part = lax.dynamic_update_slice_in_dim(jnp.zeros((width, 8), F32), grad_vec_heads.T, column, 0)
    vec_two = jnp.stack(
        [jnp.sum(grad_normed_two * standard_two, 0), jnp.sum(grad_normed_two, 0), grad_vec_mix_two], 1
    )
    others = jnp.concatenate([heads_part, jnp.pad(vec_two, ((0, 0), (0, 13)))], 1)
    scaled_grad, sums, wide, up_grad = run_unproject(
        balanced, stats, mix_vec, weights, others, (recept_low, keys_low, values_low), ups_low, hidden, downs, up, parts
    )
    if paired:
        moved, value_turned, out_other, scaled_grad, sums, wide, up_grad = lax.optimization_barrier(
            (moved, value_turned, out_other, scaled_grad, sums, wide, up_grad)
        )
        out_half = (out_mine + out_other.astype(F32)).astype(BF16).reshape(-1, width)
        out_half, sums = lax.optimization_barrier((out_half, sums))
        grad_out = along(out_half)
        grad_ffn_value = value_turned.astype(F32)
    else:
        moved, scaled_grad, sums, wide = lax.optimization_barrier((moved, scaled_grad, sums, wide))
    output = dot(arrange, moved[:, : rows // seqs].reshape(rows, width), TN).astype(BF16)
    grad_first_rows = moved[:, rows // seqs :].reshape(seqs, rows, own_width).transpose(1, 0, 2).reshape(rows, width)

    standard = (balanced.astype(F32) - mean) * scale_one
    grad_balanced = scale_one * (scaled_grad - sums[:, :1] * (1.0 / width) - standard * (sums[:, 1:] * (1.0 / width)))
    mine_rows = lax.dynamic_slice_in_dim(grad_balanced, me * rows, rows, 0) + grad_residual
    grad_balanced = lax.dynamic_update_slice_in_dim(grad_balanced, mine_rows, me * rows, 0)
    grad_given = dot(permute, grad_balanced.astype(BF16), TN).astype(BF16).reshape(seqs, rows, width)
    if near:
        kept_part, far = block_halves(wide)
        grad_given, far = lax.optimization_barrier((grad_given, far))
        wide_part = kept_part + swap(far, 2).astype(F32)
    else:
        wide_part = block_sum(wide)
    grad_tokens = reduce_seq(grad_given).astype(BF16)
    if paired:
        wide_part, grad_tokens, grad_out, key_sum = lax.optimization_barrier((wide_part, grad_tokens, grad_out, key_sum))
        grad_ffn_key = turn(key_sum).astype(F32)
    wide_all = exchange(wide_part.astype(BF16), "seq").astype(F32)

    def square(at):
        taken = wide_all[:, :, at * own_width : (at + 1) * own_width]
        return taken.transpose(1, 0, 2).reshape(piece, width)

    narrow = jnp.sum(wide_all[:, :, 3 * own_width :], 0)
    grad_down = unpad_ranks(narrow)
    grad_vectors = narrow[:, RANKS[0] : RANKS[0] + vectors.shape[1]]
    up_part = unpad_ranks(block_sum(up_grad.reshape(parts, piece, WIDE)))

    return (
        output, grad_tokens, grad_first_rows,
        square(0), square(1), square(2),
        grad_out.astype(F32), grad_down, up_part,
        grad_ffn_key, grad_ffn_value, grad_vectors,
    )


def solution(mesh):
    both, shard = P(("seq", "wsh"), None), P("wsh", None)
    flat = P(("seq", "wsh"))
    return jax.shard_map(
        local,
        mesh=mesh,
        in_specs=(both, both, both, flat, flat) + (shard,) * 9 + (P(),),
        out_specs=(both,) * 12,
        check_vma=False,
    )
```

```python
import functools

import jax
import jax.numpy as jnp
from jax import lax
from jax.experimental import pallas as pl
from jax.experimental.pallas import tpu as pltpu
from jax.sharding import PartitionSpec as P

HEAD = 64
BLOCK = 64
RANKS = (96, 96, 64, 256)
PADDED = (128, 128, 128, 256)
OFFSETS = (0, 128, 256, 384)
WIDE = 640
EXTRA = 128
DIGIT = 64

F32 = jnp.float32
BF16 = jnp.bfloat16

NN = (((1,), (0,)), ((), ()))
NT = (((1,), (1,)), ((), ()))
TN = (((0,), (0,)), ((), ()))


def dot(a, b, dims=NN):
    return lax.dot_general(a, b, dims, preferred_element_type=F32)


def halves(x):
    high = x.astype(BF16)
    return high, (x - high.astype(F32)).astype(BF16)


def dot3(a, b, dims=NN):
    a_high, a_low = halves(a)
    b_high, b_low = halves(b)
    return dot(a_high, b_high, dims) + (dot(a_high, b_low, dims) + dot(a_low, b_high, dims))


def sum_left(mask, x):
    high, low = halves(x)
    low_two = (x - high.astype(F32) - low.astype(F32)).astype(BF16)
    return dot(mask, high) + (dot(mask, low) + dot(mask, low_two))


def head_sum(x, ones):
    high, low = halves(x)
    return dot(high, ones) + dot(low, ones)


def low(x):
    return x.astype(BF16).astype(F32)


def iotas(rows, columns):
    return (
        lax.broadcasted_iota(jnp.int32, (rows, columns), 0),
        lax.broadcasted_iota(jnp.int32, (rows, columns), 1),
    )


def head_ones(width):
    i, j = iotas(width, width)
    return jnp.where((i >> 6) == (j >> 6), 1.0, 0.0).astype(BF16)


def front(keys, values, hidden, up, first, vec, ones):
    z = vec[0:1] + dot(hidden[:, 0:128], up[0:128])
    decay_log = -(jnp.maximum(-z, 0.0) + jnp.log1p(jnp.exp(-jnp.abs(z)))) - 0.5
    rate = jax.nn.sigmoid(vec[1:2] + dot(hidden[:, 128:256], up[128:256]))
    blend = jax.nn.sigmoid(vec[2:3] + dot(hidden[:, 256:384], up[256:384]))
    gate = dot(hidden[:, 384:640], up[384:640])
    mixed_value = values + (first - values) * blend
    scaled = keys * vec[3:4]
    scale = lax.rsqrt(head_sum(scaled * scaled, ones) + 1e-06)
    key_dir = scaled * scale
    key_mod = keys * (1.0 + (rate - 1.0) * vec[4:5])
    return z, decay_log, rate, blend, gate, mixed_value, scale, key_dir, key_mod


def block_masks(segments):
    i, j = iotas(BLOCK, BLOCK)
    across = jnp.broadcast_to(segments[0:1], (BLOCK, BLOCK))
    down = across.T
    before = jnp.broadcast_to(segments[1:2], (BLOCK, BLOCK))
    last = jnp.broadcast_to(segments[2:3], (BLOCK, BLOCK))
    same = across == down
    strict = jnp.where(same & (i > j), 1.0, 0.0)
    closed = jnp.where(same & (i >= j), 1.0, 0.0)
    carry = jnp.where(down == before, 1.0, 0.0)
    tail = jnp.where(down == last, 1.0, 0.0)
    keep = jnp.where(segments[2:3] == segments[1:2], 1.0, 0.0)
    quad = jnp.concatenate(
        [jnp.concatenate([strict, strict], 1), jnp.concatenate([closed, closed], 1)], 0
    )
    return quad, carry, tail, keep


def tile_heads(x, heads):
    return jnp.concatenate([x] * heads, 1) if heads > 1 else x


def join(pieces, axis):
    return jnp.concatenate(pieces, axis) if len(pieces) > 1 else pieces[0]


def decayed(decay_low, key_low, dir_low, rate_low, recept_low, carry, tail):
    i, j = iotas(BLOCK, BLOCK)
    lower = jnp.where(i >= j, 1.0, 0.0).astype(BF16)
    log_step = -jnp.exp(decay_low)
    total = sum_left(lower, log_step)
    before = jnp.exp(total - log_step)
    grown = jnp.exp(total)
    shrunk = jnp.exp(-total)
    end = total[BLOCK - 1 : BLOCK]
    tail_decay = jnp.exp(end - total) * tail
    alpha = -dir_low * before
    beta_plain = dir_low * rate_low
    beta = beta_plain * shrunk
    key = key_low * shrunk
    recept = recept_low * grown
    return dict(
        log_step=log_step, before=before, grown=grown, shrunk=shrunk, end=jnp.exp(end), tail=tail_decay,
        alpha=alpha, beta_plain=beta_plain, beta=beta, key=key, recept=recept,
        beta_end=beta_plain * tail_decay, key_end=key_low * tail_decay,
        alpha_in=alpha * carry, recept_in=recept * carry,
    )


def unit_inverses(lowers):
    i, j = iotas(BLOCK, BLOCK)
    eye = jnp.where(i == j, 1.0, 0.0)

    def within(size):
        return (i // size) == (j // size)

    smalls = [jnp.where(within(4), x, 0.0) for x in lowers]
    low_smalls = [x.astype(BF16) for x in smalls]
    twos = [dot(x, x) for x in low_smalls]
    inverses = [eye + x for x in smalls]
    inverses = [x + dot(x.astype(BF16), y.astype(BF16)) for x, y in zip(inverses, twos)]
    for size in (8, 16, 32, 64):
        mask = within(size) & ~within(size // 2)
        offs = [jnp.where(mask, x, 0.0).astype(BF16) for x in lowers]
        lows = [x.astype(BF16) for x in inverses]
        inner = [dot(x, y).astype(BF16) for x, y in zip(offs, lows)]
        inverses = [x + dot(y, z) for x, y, z in zip(inverses, lows, inner)]
    errors = [eye - x + dot3(y, x) for x, y in zip(inverses, lowers)]
    return [x + dot(x.astype(BF16), y.astype(BF16)) for x, y in zip(inverses, errors)]


def post_norm(head_low, ones):
    centered = head_low - head_sum(head_low, ones) * (1.0 / HEAD)
    spread = lax.rsqrt(head_sum(centered * centered, ones) * (1.0 / HEAD) + HEAD * 1e-05)
    return centered * spread, spread


def forward_kernel(
    count, recept_ref, keys_ref, values_ref, hidden_ref, first_ref, up_ref, vec_ref, segment_ref,
    mixed_ref, head_ref, state_ref, inverse_ref, removed_ref, state,
):
    width = recept_ref.shape[1]
    heads = width // HEAD

    @pl.when(pl.program_id(0) == 0)
    def _():
        state[...] = jnp.zeros_like(state)

    ones = head_ones(width)
    vec = vec_ref[...]
    up = up_ref[...]
    columns = [slice(head * HEAD, (head + 1) * HEAD) for head in range(heads)]
    done = []
    for block in range(count):
        rows = slice(block * BLOCK, (block + 1) * BLOCK)
        recept, keys, values = recept_ref[rows], keys_ref[rows], values_ref[rows]
        _, decay_log, rate, _, gate, mixed_value, _, key_dir, key_mod = front(
            keys, values, hidden_ref[rows], up, first_ref[rows].astype(F32), vec, ones
        )
        quad, carry, tail, keep = block_masks(segment_ref[block * 8 : block * 8 + 8])
        parts = decayed(
            low(decay_log), low(key_mod), low(key_dir), low(rate), low(recept),
            tile_heads(carry, heads), tile_heads(tail, heads),
        )
        lefts = [jnp.concatenate([parts["alpha"][:, c], parts["recept"][:, c]], 0) for c in columns]
        rights = [jnp.concatenate([parts["beta"][:, c], parts["key"][:, c]], 0) for c in columns]
        pairs = [quad * dot3(x, y, NT) for x, y in zip(lefts, rights)]
        done.append((rows, recept, key_mod, gate, mixed_value, keep, parts, pairs))
    inverses = unit_inverses([x[:BLOCK, :BLOCK] for item in done for x in item[-1]])
    for block, (rows, recept, key_mod, gate, mixed_value, keep, parts, pairs) in enumerate(done):
        mine = inverses[block * heads : (block + 1) * heads]
        value_low = low(mixed_value)
        owns = [value_low[:, c] for c in columns]
        by_values = [dot3(x[:, BLOCK:], y) for x, y in zip(pairs, owns)]
        ends = [jnp.concatenate([parts["beta_end"][:, c], parts["key_end"][:, c]], 0) for c in columns]
        inners = [jnp.concatenate([parts["alpha_in"][:, c], parts["recept_in"][:, c]], 0) for c in columns]
        entering = state[...]
        state_ref[rows] = entering
        nows = [entering[:, c] for c in columns]
        inwards = [dot3(x, y, NT) for x, y in zip(inners, nows)]
        removals = [dot3(x, y[:BLOCK] + z[:BLOCK]) for x, y, z in zip(mine, inwards, by_values)]
        outs = [
            y[BLOCK:] + z[BLOCK:] + dot3(x[BLOCK:, :BLOCK], r)
            for x, y, z, r in zip(pairs, inwards, by_values, removals)
        ]
        leaving = [
            x * (parts["end"][:, c] * keep) + dot3(jnp.concatenate([r, v], 0), e, TN)
            for x, c, r, v, e in zip(nows, columns, removals, owns, ends)
        ]
        state[...] = join(leaving, 1)
        inverse_ref[rows] = join(mine, 1)
        removed_ref[rows] = join(removals, 1)
        head_low = join(outs, 1).astype(BF16)
        head_ref[rows] = head_low
        normed, _ = post_norm(head_low.astype(F32), ones)
        bonus = head_sum(recept * key_mod * vec[5:6], ones) * mixed_value
        mixed_ref[rows] = ((normed * vec[6:7] + vec[7:8] + bonus) * gate).astype(BF16)


def backward_kernel(
    count, grad_ref, recept_ref, keys_ref, values_ref, hidden_ref, first_ref, up_ref, vec_ref, segment_ref,
    head_ref, state_ref, inverse_ref, removed_ref,
    recept_out, keys_out, values_out, ups_out, first_out, vec_out, state,
):
    width = recept_ref.shape[1]
    heads = width // HEAD

    @pl.when(pl.program_id(0) == 0)
    def _():
        state[...] = jnp.zeros_like(state)
        vec_out[...] = jnp.zeros_like(vec_out)

    ones = head_ones(width)
    vec = vec_ref[...]
    up = up_ref[...]
    i, j = iotas(BLOCK, BLOCK)
    upper = jnp.where(i <= j, 1.0, 0.0).astype(BF16)
    columns = [slice(head * HEAD, (head + 1) * HEAD) for head in range(heads)]
    order = range(count - 1, -1, -1)
    kept = {}
    for block in order:
        rows = slice(block * BLOCK, (block + 1) * BLOCK)
        recept, keys, values = recept_ref[rows], keys_ref[rows], values_ref[rows]
        first = first_ref[rows].astype(F32)
        z, decay_log, rate, blend, gate, mixed_value, scale, key_dir, key_mod = front(
            keys, values, hidden_ref[rows], up, first, vec, ones
        )
        quad, carry, tail, keep = block_masks(segment_ref[block * 8 : block * 8 + 8])
        rate_low, dir_low = low(rate), low(key_dir)
        parts = decayed(
            low(decay_log), low(key_mod), dir_low, rate_low, low(recept),
            tile_heads(carry, heads), tile_heads(tail, heads),
        )
        value_low = low(mixed_value)

        grad = grad_ref[rows].astype(F32)
        normed, spread = post_norm(head_ref[rows].astype(F32), ones)
        product = recept * key_mod
        coefficient = head_sum(product * vec[5:6], ones)
        grad_gate = grad * (normed * vec[6:7] + vec[7:8] + coefficient * mixed_value)
        opened = grad * gate
        grad_normed = opened * vec[6:7]
        grad_head = spread * (
            grad_normed
            - head_sum(grad_normed, ones) * (1.0 / HEAD)
            - normed * (head_sum(grad_normed * normed, ones) * (1.0 / HEAD))
        )
        grad_coefficient = head_sum(opened * mixed_value, ones)
        weighted = grad_coefficient * vec[5:6]
        head_grad = low(grad_head)

        lefts = [jnp.concatenate([parts["alpha"][:, c], parts["recept"][:, c]], 0) for c in columns]
        rights = [jnp.concatenate([parts["beta"][:, c], parts["key"][:, c]], 0) for c in columns]
        ends = [jnp.concatenate([parts["beta_end"][:, c], parts["key_end"][:, c]], 0) for c in columns]
        inners = [jnp.concatenate([parts["alpha_in"][:, c], parts["recept_in"][:, c]], 0) for c in columns]
        pairs = [quad * dot3(x, y, NT) for x, y in zip(lefts, rights)]
        out_grads = [head_grad[:, c] for c in columns]
        through = [dot3(x[BLOCK:, :BLOCK], y, TN) for x, y in zip(pairs, out_grads)]
        kept[block] = dict(
            rows=rows, recept=recept, keys=keys, values=values, first=first, z=z, rate=rate, blend=blend,
            mixed_value=mixed_value, scale=scale, key_dir=key_dir, key_mod=key_mod, quad=quad, carry=carry, keep=keep,
            rate_low=rate_low, dir_low=dir_low, parts=parts, value_low=value_low, normed=normed, product=product,
            grad_gate=grad_gate, opened=opened, grad_coefficient=grad_coefficient,
            grad_mixed_value=opened * coefficient, grad_recept=weighted * key_mod, grad_key_mod=weighted * recept,
            lefts=lefts, rights=rights, ends=ends, inners=inners, pairs=pairs, out_grads=out_grads, through=through,
        )
    for block in order:
        k = kept[block]
        after, entering, inverse_all = state[...], state_ref[k["rows"]], inverse_ref[k["rows"]]
        laters, nows = [after[:, c] for c in columns], [entering[:, c] for c in columns]
        from_ends = [dot3(x, y, NT) for x, y in zip(k["ends"], laters)]
        inner_grads = [
            dot3(inverse_all[:, c], x + y[:BLOCK], TN) for c, x, y in zip(columns, k["through"], from_ends)
        ]
        boths = [jnp.concatenate([x, y], 0) for x, y in zip(inner_grads, k["out_grads"])]
        stays = [x * (k["parts"]["end"][:, c] * k["keep"]) for x, c in zip(laters, columns)]
        state[...] = join([x + dot3(y, z, TN) for x, y, z in zip(stays, boths, k["inners"])], 1)
        k.update(
            laters=laters, nows=nows, from_ends=from_ends, boths=boths,
            end_sum=join([jnp.sum(x * y, 0, keepdims=True) for x, y in zip(nows, stays)], 1),
        )
    vec_total = jnp.zeros_like(vec)
    for block in order:
        k = kept[block]
        rows, parts, quad = k["rows"], k["parts"], k["quad"]
        removed_all = removed_ref[rows]
        carry_two = jnp.concatenate([k["carry"], k["carry"]], 0)
        sources = [jnp.concatenate([removed_all[:, c], k["value_low"][:, c]], 0) for c in columns]
        grad_pairs = [quad * dot3(x, y, NT) for x, y in zip(k["boths"], sources)]
        grad_values = [
            dot3(x[:, BLOCK:], y, TN) + z[BLOCK:] for x, y, z in zip(k["pairs"], k["boths"], k["from_ends"])
        ]
        grad_ends = [dot3(x, y) for x, y in zip(sources, k["laters"])]
        to_state = [carry_two * dot3(x, y) for x, y in zip(k["boths"], k["nows"])]
        grad_lefts = [dot3(x, y) + z for x, y, z in zip(grad_pairs, k["rights"], to_state)]
        grad_rights = [dot3(x, y, TN) for x, y in zip(grad_pairs, k["lefts"])]
        d_alpha, d_recept = join([x[:BLOCK] for x in grad_lefts], 1), join([x[BLOCK:] for x in grad_lefts], 1)
        d_beta, d_key = join([x[:BLOCK] for x in grad_rights], 1), join([x[BLOCK:] for x in grad_rights], 1)
        d_beta_end, d_key_end = join([x[:BLOCK] for x in grad_ends], 1), join([x[BLOCK:] for x in grad_ends], 1)
        ended = parts["beta_end"] * d_beta_end + parts["key_end"] * d_key_end
        alphas = parts["alpha"] * d_alpha
        d_total = parts["recept"] * d_recept - parts["beta"] * d_beta - parts["key"] * d_key - ended + alphas
        d_step = sum_left(upper, d_total) + (jnp.sum(ended, 0, keepdims=True) + k["end_sum"]) - alphas
        d_beta_plain = d_beta * parts["shrunk"] + d_beta_end * parts["tail"]
        copy_decay = low(d_step * parts["log_step"])
        copy_dir = low(d_beta_plain * k["rate_low"] - d_alpha * parts["before"])
        copy_rate = low(d_beta_plain * k["dir_low"])

        keys, values, rate, blend = k["keys"], k["values"], k["rate"], k["blend"]
        grad_recept = k["grad_recept"] + low(d_recept * parts["grown"])
        grad_key_mod = k["grad_key_mod"] + low(d_key * parts["shrunk"] + d_key_end * parts["tail"])
        grad_mixed_value = k["grad_mixed_value"] + low(join(grad_values, 1))
        grad_z = copy_decay * jax.nn.sigmoid(-k["z"])
        factor = 1.0 + (rate - 1.0) * vec[4:5]
        keyed = grad_key_mod * keys
        grad_rate = copy_rate + keyed * vec[4:5]
        grad_scaled = k["scale"] * (copy_dir - k["key_dir"] * head_sum(copy_dir * k["key_dir"], ones))
        grad_keys = grad_key_mod * factor + grad_scaled * vec[3:4]
        grad_rate_up = grad_rate * rate * (1.0 - rate)
        grad_value_up = grad_mixed_value * (k["first"] - values) * blend * (1.0 - blend)
        recept_out[rows] = grad_recept.astype(BF16)
        keys_out[rows] = grad_keys.astype(BF16)
        values_out[rows] = (grad_mixed_value * (1.0 - blend)).astype(BF16)
        first_out[rows] = (grad_mixed_value * blend).astype(BF16)
        ups_out[0, rows] = grad_z.astype(BF16)
        ups_out[1, rows] = grad_rate_up.astype(BF16)
        ups_out[2, rows] = grad_value_up.astype(BF16)
        ups_out[3, rows] = k["grad_gate"].astype(BF16)

        def total(x):
            return jnp.sum(x, 0, keepdims=True)

        vec_total = vec_total + jnp.concatenate(
            [
                total(grad_z), total(grad_rate_up), total(grad_value_up), total(grad_scaled * keys),
                total(keyed * (rate - 1.0)), total(k["grad_coefficient"] * k["product"]),
                total(k["opened"] * k["normed"]), total(k["opened"]),
            ],
            0,
        )
    vec_out[...] += vec_total


def kernel_cost(rows, width, passes):
    return pl.CostEstimate(flops=2 * rows * width * width, bytes_accessed=4 * rows * width * passes, transcendentals=0)


def per_step(rows, most):
    return most if (rows // BLOCK) % most == 0 else 1


def run_forward(recept, keys, values, hidden, first, up, vec, segments):
    rows, width = recept.shape
    count = per_step(rows, 4)
    step = count * BLOCK

    def spec(columns):
        return pl.BlockSpec((step, columns), lambda i: (i, 0))

    def whole(array):
        return pl.BlockSpec(array.shape, lambda i: (0, 0))

    return pl.pallas_call(
        functools.partial(forward_kernel, count),
        grid=(rows // step,),
        in_specs=[
            spec(width), spec(width), spec(width), spec(WIDE), spec(width), whole(up), whole(vec),
            pl.BlockSpec((count * 8, BLOCK), lambda i: (i, 0)),
        ],
        out_specs=[spec(width)] * 5,
        out_shape=[jax.ShapeDtypeStruct((rows, width), d) for d in (BF16, BF16, F32, F32, F32)],
        scratch_shapes=[pltpu.VMEM((BLOCK, width), F32)],
        compiler_params=pltpu.CompilerParams(vmem_limit_bytes=48 << 20),
        cost_estimate=kernel_cost(rows, width, 110),
        name="mix_forward",
    )(recept, keys, values, hidden, first, up, vec, segments)


def run_backward(grad, recept, keys, values, hidden, first, up, vec, segments, saved):
    rows, width = recept.shape
    count = per_step(rows, 2)
    step = count * BLOCK
    last = rows // step - 1

    def spec(columns):
        return pl.BlockSpec((step, columns), lambda i: (last - i, 0))

    def whole(array):
        return pl.BlockSpec(array.shape, lambda i: (0, 0))

    return pl.pallas_call(
        functools.partial(backward_kernel, count),
        grid=(rows // step,),
        in_specs=[
            spec(width), spec(width), spec(width), spec(width), spec(WIDE), spec(width), whole(up), whole(vec),
            pl.BlockSpec((count * 8, BLOCK), lambda i: (last - i, 0)),
            spec(width), spec(width), spec(width), spec(width),
        ],
        out_specs=[
            spec(width), spec(width), spec(width),
            pl.BlockSpec((4, step, width), lambda i: (0, last - i, 0)),
            spec(width), pl.BlockSpec((8, width), lambda i: (0, 0)),
        ],
        out_shape=[
            jax.ShapeDtypeStruct((rows, width), BF16), jax.ShapeDtypeStruct((rows, width), BF16),
            jax.ShapeDtypeStruct((rows, width), BF16), jax.ShapeDtypeStruct((4, rows, width), BF16),
            jax.ShapeDtypeStruct((rows, width), BF16), jax.ShapeDtypeStruct((8, width), F32),
        ],
        scratch_shapes=[pltpu.VMEM((BLOCK, width), F32)],
        compiler_params=pltpu.CompilerParams(vmem_limit_bytes=48 << 20),
        cost_estimate=kernel_cost(rows, width, 150),
        name="mix_backward",
    )(grad, recept, keys, values, hidden, first, up, vec, segments, *saved)


def mix_norm(block_ref, stats_ref, vec_ref):
    stats = stats_ref[...]
    flowing = stats[:, 2:3]
    standard = (block_ref[...].astype(F32) - stats[:, 0:1]) * stats[:, 1:2]
    normed = standard * vec_ref[0:1] + vec_ref[1:2]
    delta = pltpu.roll(normed, 1, 0) * flowing - normed
    return standard, normed, delta, flowing


def project_kernel(
    width, block_ref, stats_ref, vec_ref, weight_ref,
    recept_ref, keys_ref, values_ref, downs_ref, hidden_ref,
):
    base = 3 * width
    _, normed, delta, _ = mix_norm(block_ref, stats_ref, vec_ref)
    weight = weight_ref[...]
    uses = (
        ((recept_ref, 0, width, 0),),
        ((downs_ref, base + OFFSETS[0], PADDED[0], OFFSETS[0]),),
        ((keys_ref, width, width, 0),),
        ((values_ref, 2 * width, width, 0), (downs_ref, base + OFFSETS[2], PADDED[2], OFFSETS[2])),
        ((downs_ref, base + OFFSETS[1], PADDED[1], OFFSETS[1]),),
        ((downs_ref, base + OFFSETS[3], PADDED[3], OFFSETS[3]),),
    )

    @pl.when(pl.program_id(0) == 0)
    def _():
        for ref in (recept_ref, keys_ref, values_ref, downs_ref):
            ref[...] = jnp.zeros_like(ref)

    for c, targets in enumerate(uses):
        mixed = (normed + delta * vec_ref[2 + c : 3 + c]).astype(BF16)
        for ref, start, size, at in targets:
            ref[:, at : at + size] += dot(mixed, weight[:, start : start + size])

    @pl.when(pl.program_id(0) == pl.num_programs(0) - 1)
    def _():
        hidden_ref[:, 0:128] = jnp.tanh(downs_ref[:, 0:128]).astype(BF16)
        hidden_ref[:, 128:384] = downs_ref[:, 128:384].astype(BF16)
        hidden_ref[:, 384:640] = jax.nn.sigmoid(downs_ref[:, 384:640]).astype(BF16)


def unproject_kernel(
    width, parts, piece, block_ref, stats_ref, vec_ref, weight_ref,
    other_ref, recept_ref, keys_ref, values_ref, ups_ref, hidden_ref, downs_ref, up_ref,
    grad_ref, sums_ref, wide_ref, up_out, down_lows,
):
    rows = block_ref.shape[0]
    base = 3 * width

    @pl.when(pl.program_id(0) == 0)
    def _():
        sums_ref[...] = jnp.zeros_like(sums_ref)
        for k, (at, size) in enumerate(zip(OFFSETS, PADDED)):
            cols = slice(at, at + size)
            grad = dot(ups_ref[k], up_ref[cols], NT)
            if k == 0:
                grad = grad * (1.0 - jnp.square(jnp.tanh(downs_ref[:, cols])))
            if k == 3:
                opening = jax.nn.sigmoid(downs_ref[:, cols])
                grad = grad * opening * (1.0 - opening)
            down_lows[:, cols] = grad.astype(BF16)
            up_out[:, cols] = dot(ups_ref[k], hidden_ref[:, cols], TN).astype(BF16)

    standard, normed, delta, flowing = mix_norm(block_ref, stats_ref, vec_ref)
    weight = weight_ref[...]

    def down(k):
        return (down_lows[:, OFFSETS[k] : OFFSETS[k] + PADDED[k]], base + OFFSETS[k], PADDED[k])

    uses = (
        ((recept_ref[...], 0, width),),
        (down(0),),
        ((keys_ref[...], width, width),),
        ((values_ref[...], 2 * width, width), down(2)),
        (down(1),),
        (down(3),),
    )
    kept, sent, vec_rows = None, None, []
    per_seq = parts * piece
    for c, sources in enumerate(uses):
        share = vec_ref[2 + c : 3 + c]
        mixed = (normed + delta * share).astype(BF16)
        grad = None
        for source, start, size in sources:
            part = dot(source, weight[:, start : start + size], NT)
            grad = part if grad is None else grad + part
            product = dot(mixed, source, TN).astype(BF16)
            for number in range(product.shape[0] // per_seq):
                for w in range(parts):
                    at = number * per_seq + w * piece
                    wide_ref[w, number, :, start : start + size] = product[at : at + piece]
        vec_rows.append(jnp.sum(grad * delta, 0, keepdims=True))
        moved = grad * share
        kept = grad - moved if kept is None else kept + (grad - moved)
        sent = moved if sent is None else sent + moved
    grad = kept + pltpu.roll(sent * flowing, rows - 1, 0)
    vec_rows = jnp.concatenate(
        [jnp.sum(grad * standard, 0, keepdims=True), jnp.sum(grad, 0, keepdims=True)] + vec_rows, 0
    )
    spare = jnp.concatenate([vec_rows.T, other_ref[...]], 1).astype(BF16)
    for number in range(spare.shape[0] // per_seq):
        for w in range(parts):
            at = number * per_seq + w * piece
            wide_ref[w, number, :, base + RANKS[0] : base + PADDED[0]] = spare[at : at + piece]
    scaled = grad * vec_ref[0:1]
    sums_ref[:, 0:1] += jnp.sum(scaled, 1, keepdims=True)
    sums_ref[:, 1:2] += jnp.sum(scaled * standard, 1, keepdims=True)
    grad_ref[...] = scaled


def mix_specs(rows, width, own_width, parts):
    block = 256 if rows <= 1024 else 128

    def columns(height):
        return pl.BlockSpec((height, block), lambda j: (0, j))

    def whole(shape):
        return pl.BlockSpec(shape, lambda j: (0,) * len(shape))

    def weights(array):
        size = array.shape[1] if rows > 1024 else 3 * own_width + WIDE
        return pl.BlockSpec((block, size), lambda j: (j, 0))

    return block, columns, whole, weights


def run_project(balanced, stats, vec, weights, own_width, parts):
    rows, width = balanced.shape
    block, columns, whole, weight_spec = mix_specs(rows, width, own_width, parts)
    shapes = [(rows, own_width)] * 3 + [(rows, WIDE)] * 2
    return pl.pallas_call(
        functools.partial(project_kernel, own_width),
        grid_spec=pltpu.PrefetchScalarGridSpec(
            num_scalar_prefetch=0,
            grid=(width // block,),
            in_specs=[columns(rows), whole(stats.shape), columns(8), weight_spec(weights)],
            out_specs=[whole(s) for s in shapes],
        ),
        out_shape=[jax.ShapeDtypeStruct(s, d) for s, d in zip(shapes, (F32, F32, F32, F32, BF16))],
        compiler_params=pltpu.CompilerParams(vmem_limit_bytes=60 << 20),
        cost_estimate=kernel_cost(rows, own_width, 60),
        name="mix_project",
    )(balanced, stats, vec, weights)


def run_unproject(balanced, stats, vec, weights, others, lows, ups, hidden, downs, up, parts):
    rows, width = balanced.shape
    own_width = lows[0].shape[1]
    seqs = width // own_width
    piece = own_width // parts
    block, columns, whole, weight_spec = mix_specs(rows, width, own_width, parts)
    taken = block // own_width
    total = 3 * own_width + WIDE
    return pl.pallas_call(
        functools.partial(unproject_kernel, own_width, parts, piece),
        grid_spec=pltpu.PrefetchScalarGridSpec(
            num_scalar_prefetch=0,
            grid=(width // block,),
            in_specs=[
                columns(rows), whole(stats.shape), columns(8), weight_spec(weights),
                pl.BlockSpec((block, others.shape[1]), lambda j: (j, 0)),
            ]
            + [whole(a.shape) for a in (*lows, ups, hidden, downs, up)],
            out_specs=[
                columns(rows), whole((rows, 2)),
                pl.BlockSpec((parts, taken, piece, total), lambda j: (0, j, 0, 0)),
                whole((own_width, WIDE)),
            ],
            scratch_shapes=[pltpu.VMEM((rows, WIDE), BF16)],
        ),
        out_shape=[
            jax.ShapeDtypeStruct((rows, width), F32), jax.ShapeDtypeStruct((rows, 2), F32),
            jax.ShapeDtypeStruct((parts, seqs, piece, total), BF16),
            jax.ShapeDtypeStruct((own_width, WIDE), BF16),
        ],
        compiler_params=pltpu.CompilerParams(vmem_limit_bytes=60 << 20),
        cost_estimate=kernel_cost(rows, own_width, 120),
        name="mix_unproject",
    )(balanced, stats, vec, weights, others, *lows, ups, hidden, downs, up)


def norm_stats(values):
    centered = values - jnp.mean(values, -1, keepdims=True)
    scale = lax.rsqrt(jnp.mean(centered * centered, -1, keepdims=True) + 1e-05)
    return centered * scale, scale


def norm_back(grad, standard, scale, gain):
    scaled = grad * gain
    return scale * (
        scaled
        - jnp.mean(scaled, -1, keepdims=True)
        - standard * jnp.mean(scaled * standard, -1, keepdims=True)
    )


def pad_ranks(matrix):
    pieces, start = [], 0
    for rank, padded in zip(RANKS, PADDED):
        pieces.append(jnp.pad(matrix[:, start : start + rank], ((0, 0), (0, padded - rank))))
        start += rank
    return jnp.concatenate(pieces, 1)


def unpad_ranks(matrix):
    return jnp.concatenate([matrix[..., o : o + r] for o, r in zip(OFFSETS, RANKS)], -1)


MESH_ID = pl.DeviceIdType.MESH


def places():
    s, w = lax.axis_index("seq"), lax.axis_index("wsh")
    side = s % 2
    return s, w, side, s // 2, (s + 1 - 2 * side, w), (s, w + 1 - 2 * (w % 2)), (s, w + 2 - 4 * (w // 2))


def greet(neighbours, number):
    barrier = pltpu.get_barrier_semaphore()
    for there, device in neighbours:
        if there is None:
            pl.semaphore_signal(barrier, inc=1, device_id=device, device_id_type=MESH_ID)
        else:

            @pl.when(there)
            def _(device=device):
                pl.semaphore_signal(barrier, inc=1, device_id=device, device_id_type=MESH_ID)

    pl.semaphore_wait(barrier, number)


def send(source, target, send_sem, recv_sem, device):
    return pltpu.make_async_remote_copy(
        src_ref=source, dst_ref=target, send_sem=send_sem, recv_sem=recv_sem, device_id=device, device_id_type=MESH_ID
    )


def line_ends(z):
    return jnp.where(z > 0, 1, 0) + jnp.where(z < 3, 1, 0)


def gather_kernel(
    own_ref, tail_ref, weight_ref, out_ref, tails_ref, weights_ref,
    copy_sem, right_send, right_recv, left_send, left_recv, x_send, x_recv, c_send, c_recv, y_send, y_recv,
):
    s, w, side, z, x_device, core_device, y_device = places()
    up, down = (s + 2, w), (s - 2, w)
    across = w + 2 - 4 * (w // 2)
    kinds = ((own_ref, out_ref), (tail_ref, tails_ref))
    copies = [pltpu.make_async_copy(own, out.at[s], copy_sem.at[k]) for k, (own, out) in enumerate(kinds)]
    copies.append(pltpu.make_async_copy(weight_ref, weights_ref.at[w], copy_sem.at[2]))
    for copy in copies:
        copy.start()
    greet(((None, x_device), (None, core_device), (None, y_device), (z < 3, up), (z > 0, down)), 3 + line_ends(z))

    weight_y = send(weight_ref, weights_ref.at[w], y_send, y_recv, y_device)
    weight_core = send(weight_ref, weights_ref.at[w], c_send.at[0], c_recv.at[0], core_device)
    weight_on = send(weights_ref.at[across], weights_ref.at[across], c_send.at[1], c_recv.at[1], core_device)
    weight_y.start()
    weight_core.start()

    def to_right(j, k, source, number):
        return send(source, kinds[k][1].at[number], right_send.at[j, k], right_recv.at[j, k], up)

    def to_left(j, k, source, number):
        return send(source, kinds[k][1].at[number], left_send.at[j, k], left_recv.at[j, k], down)

    def to_x(at, k, source, number):
        return send(source, kinds[k][1].at[number], x_send.at[at, k], x_recv.at[at, k], x_device)

    for k, (own, _) in enumerate(kinds):

        @pl.when(z < 3)
        def _(k=k, own=own):
            to_right(0, k, own, s).start()

        @pl.when(z > 0)
        def _(k=k, own=own):
            to_left(0, k, own, s).start()

        to_x(z, k, own, s).start()
    for j in (1, 2, 3):
        lower, upper = s - 2 * j, s + 2 * j
        for k, (_, out) in enumerate(kinds):

            @pl.when(z >= j)
            def _(j=j, k=k, out=out, lower=lower):
                block = out.at[lower]
                to_right(j - 1, k, block, lower).wait_recv()

                @pl.when(z < 3)
                def _():
                    to_right(j, k, block, lower).start()

                to_x(z - j, k, block, lower).start()

            @pl.when(z + j <= 3)
            def _(j=j, k=k, out=out, upper=upper):
                block = out.at[upper]
                to_left(j - 1, k, block, upper).wait_recv()

                @pl.when(z > 0)
                def _():
                    to_left(j, k, block, upper).start()

                to_x(z + j, k, block, upper).start()

    weight_y.wait_recv()
    weight_on.start()
    for k, (own, _) in enumerate(kinds):
        for number in range(4):
            done = to_x(number, k, own, s)
            done.wait_send()
            done.wait_recv()
        for j in range(3):

            @pl.when((z >= j) & (z < 3))
            def _(j=j, k=k, own=own):
                to_right(j, k, own, s).wait_send()

            @pl.when((z + j <= 3) & (z > 0))
            def _(j=j, k=k, own=own):
                to_left(j, k, own, s).wait_send()

    weight_core.wait_recv()
    weight_on.wait_recv()
    for copy in (weight_y, weight_core, weight_on):
        copy.wait_send()
    for copy in copies:
        copy.wait()


def gather_first(own, tail, weight):
    seqs, parts = lax.axis_size("seq"), lax.axis_size("wsh")
    if seqs != 8 or parts != 4:
        return (
            lax.all_gather(own, "seq", axis=0, tiled=False),
            lax.all_gather(tail, "seq", axis=0, tiled=False),
            lax.all_gather(weight, "wsh", axis=0, tiled=False),
        )
    dma = pltpu.SemaphoreType.DMA
    given = ((seqs, own), (seqs, tail), (parts, weight))
    return pl.pallas_call(
        gather_kernel,
        in_specs=[pl.BlockSpec(memory_space=pltpu.VMEM)] * 3,
        out_specs=[pl.BlockSpec(memory_space=pl.ANY)] * 3,
        out_shape=[jax.ShapeDtypeStruct((n,) + x.shape, x.dtype) for n, x in given],
        scratch_shapes=[dma((3,))] + [dma((3, 2))] * 4 + [dma((4, 2))] * 2 + [dma((2,))] * 2 + [dma] * 2,
        compiler_params=pltpu.CompilerParams(collective_id=1, has_side_effects=True),
        cost_estimate=pl.CostEstimate(flops=0, bytes_accessed=100 << 20, transcendentals=0),
        name="gather_first",
    )(own, tail, weight)


def reduce_kernel(
    splits, x_ref, out_ref, x_buf, right_buf, left_buf, right_out, left_out,
    x_send, x_recv, right_send, right_recv, left_send, left_recv,
):
    s, w, side, z, x_device, _, _ = places()
    up, down = (s + 2, w), (s - 2, w)
    size = x_ref.shape[2] // splits
    columns = [slice(c * size, (c + 1) * size) for c in range(splits)]
    greet(((None, x_device), (z < 3, up), (z > 0, down)), 1 + line_ends(z))

    def to_x(target, c):
        return send(
            x_ref.at[target * 2 + 1 - side, :, columns[c]], x_buf.at[target, :, columns[c]],
            x_send.at[target, c], x_recv.at[target, c], x_device,
        )

    def start_x(target):
        for c in range(splits):
            to_x(target, c).start()

    def to_right(k, c):
        return send(
            right_out.at[k - 1, :, columns[c]], right_buf.at[k - 1, :, columns[c]],
            right_send.at[k - 1, c], right_recv.at[k - 1, c], up,
        )

    def to_left(k, c):
        return send(
            left_out.at[k - 1, :, columns[c]], left_buf.at[k - 1, :, columns[c]],
            left_send.at[k - 1, c], left_recv.at[k - 1, c], down,
        )

    def pair(target, c):
        to_x(target, c).wait_recv()
        return x_ref[target * 2 + side, :, columns[c]].astype(F32) + x_buf[target, :, columns[c]].astype(F32)

    for k in (3, 2, 1):

        @pl.when(z + k <= 3)
        def _(k=k):
            start_x(z + k)

        @pl.when(z >= k)
        def _(k=k):
            start_x(z - k)

    start_x(z)
    for k in (3, 2, 1):
        for c in range(splits):

            @pl.when(z + k <= 3)
            def _(k=k, c=c):
                right_out[k - 1, :, columns[c]] = pair(z + k, c).astype(BF16)
                if k < 3:

                    @pl.when(z > 0)
                    def _():
                        to_right(k + 1, c).wait_recv()
                        right_out[k - 1, :, columns[c]] = (
                            right_out[k - 1, :, columns[c]].astype(F32) + right_buf[k, :, columns[c]].astype(F32)
                        ).astype(BF16)

                to_right(k, c).start()

            @pl.when(z >= k)
            def _(k=k, c=c):
                left_out[k - 1, :, columns[c]] = pair(z - k, c).astype(BF16)
                if k < 3:

                    @pl.when(z < 3)
                    def _():
                        to_left(k + 1, c).wait_recv()
                        left_out[k - 1, :, columns[c]] = (
                            left_out[k - 1, :, columns[c]].astype(F32) + left_buf[k, :, columns[c]].astype(F32)
                        ).astype(BF16)

                to_left(k, c).start()

    for c in range(splits):
        out_ref[:, columns[c]] = pair(z, c)

        @pl.when(z > 0)
        def _(c=c):
            to_right(1, c).wait_recv()
            out_ref[:, columns[c]] += right_buf[0, :, columns[c]].astype(F32)

        @pl.when(z < 3)
        def _(c=c):
            to_left(1, c).wait_recv()
            out_ref[:, columns[c]] += left_buf[0, :, columns[c]].astype(F32)

    for c in range(splits):
        for target in range(4):
            to_x(target, c).wait_send()
        for k in (3, 2, 1):

            @pl.when(z + k <= 3)
            def _(k=k, c=c):
                to_right(k, c).wait_send()

            @pl.when(z >= k)
            def _(k=k, c=c):
                to_left(k, c).wait_send()


def reduce_seq(x):
    seqs, rows, width = x.shape
    if seqs != 8 or lax.axis_size("wsh") != 4:
        return jnp.sum(exchange(x, "seq").astype(F32), 0)
    splits = 2
    return pl.pallas_call(
        functools.partial(reduce_kernel, splits),
        in_specs=[pl.BlockSpec(memory_space=pltpu.VMEM)],
        out_specs=pl.BlockSpec(memory_space=pltpu.VMEM),
        out_shape=jax.ShapeDtypeStruct((rows, width), F32),
        scratch_shapes=[pltpu.VMEM((4, rows, width), BF16)]
        + [pltpu.VMEM((3, rows, width), BF16)] * 4
        + [pltpu.SemaphoreType.DMA((4, splits))] * 2
        + [pltpu.SemaphoreType.DMA((3, splits))] * 4,
        compiler_params=pltpu.CompilerParams(collective_id=2, has_side_effects=True, vmem_limit_bytes=40 << 20),
        cost_estimate=pl.CostEstimate(flops=0, bytes_accessed=1 << 20, transcendentals=0),
        name="reduce_seq",
    )(x)


def channel_kernel(
    forward, x_ref, first_hbm, second_hbm, active_hbm,
    sum_ref, all_hbm, mine_hbm, other_hbm, extra_hbm,
    first, second, rows_all, middle, active, part, core_buf, far_out, far_buf,
    load_sem, store_sem, core_send, core_recv, y_send, y_recv, x_send, x_recv, r_send, r_recv, f_send, f_recv,
):
    s, w, side, z, x_device, core_device, y_device = places()
    rows, width = x_ref.shape
    units = first.shape[0]
    half = units // 2
    loads = [
        pltpu.make_async_copy(first_hbm, first, load_sem.at[0]),
        pltpu.make_async_copy(second_hbm, second, load_sem.at[1]),
    ]
    if not forward:
        loads.append(pltpu.make_async_copy(active_hbm, active, load_sem.at[2]))
    for load in loads:
        load.start()
    rows_all[0:rows] = x_ref[...]
    greet(((None, x_device), (None, core_device), (None, y_device)), 3)

    def block(number):
        return rows_all.at[pl.ds(number * rows, rows)]

    to_core = [
        send(block(0), block(1), core_send.at[0], core_recv.at[0], core_device),
        send(block(2), block(3), core_send.at[1], core_recv.at[1], core_device),
    ]
    to_y = send(block(0), block(2), y_send, y_recv, y_device)
    if forward:
        to_x = [
            send(
                middle.at[1 - side, pl.ds(2 * n * rows, 2 * rows)], other_hbm.at[pl.ds(2 * n * rows, 2 * rows)],
                x_send.at[n], x_recv.at[n], x_device,
            )
            for n in range(2)
        ]
    else:
        to_x = [
            send(block(n), other_hbm.at[pl.ds(n * rows, rows)], x_send.at[n], x_recv.at[n], x_device) for n in range(4)
        ]
    sums_core = [
        send(part.at[pl.ds((2 * n + 1) * rows, rows)], core_buf.at[n], r_send.at[n], r_recv.at[n], core_device)
        for n in range(2)
    ]
    far = send(far_out, far_buf, f_send, f_recv, y_device)
    stores = [
        pltpu.make_async_copy(rows_all, all_hbm, store_sem.at[0]),
        pltpu.make_async_copy(middle.at[side], mine_hbm, store_sem.at[1]),
        pltpu.make_async_copy(active if forward else middle.at[1 - side], extra_hbm, store_sem.at[2]),
    ]

    def pass_on(number):
        if not forward:
            to_x[number].start()

    to_y.start()
    to_core[0].start()
    pass_on(0)
    tile = min(512, half)

    def multiply(number):
        two = pl.ds(2 * number * rows, 2 * rows)

        def up(t, carry):
            for side_units in range(2):
                at = pl.multiple_of(t * tile, tile)
                unit = pl.multiple_of(side_units * half + at, tile)
                raw = dot(rows_all[two, :], first[pl.ds(unit, tile), :], NT)
                if forward:
                    raw = jnp.maximum(raw, 0.0)
                    active[two, pl.ds(unit, tile)] = raw
                    mid = raw * raw
                else:
                    mid = raw * 2.0 * active[two, pl.ds(unit, tile)]
                middle[side_units, two, pl.ds(at, tile)] = mid.astype(BF16)
            return carry

        lax.fori_loop(0, half // tile, up, 0)
        if forward:
            to_x[number].start()
        if number == 0:
            loads[1].wait()

        def down(t, carry):
            at = pl.multiple_of(t * tile, tile)
            part[two, pl.ds(at, tile)] = dot(middle[0, two, :], second[0:half, pl.ds(at, tile)]) + dot(
                middle[1, two, :], second[half:units, pl.ds(at, tile)]
            )
            return carry

        lax.fori_loop(0, width // tile, down, 0)
        sums_core[number].start()

    loads[0].wait()
    if not forward:
        loads[2].wait()
    to_core[0].wait_recv()
    pass_on(1)
    multiply(0)
    to_y.wait_recv()
    to_core[1].start()
    pass_on(2)
    to_core[1].wait_recv()
    pass_on(3)
    stores[0].start()
    multiply(1)
    for store in stores[1:]:
        store.start()
    sums_core[1].wait_recv()
    far_out[...] = (part[2 * rows : 3 * rows] + core_buf[1]).astype(BF16)
    far.start()
    sums_core[0].wait_recv()
    sum_ref[...] = part[0:rows] + core_buf[0]
    far.wait_recv()
    sum_ref[...] += far_buf[...].astype(F32)
    for copy in to_x:
        copy.wait_recv()
    for copy in to_x + to_core + sums_core + [to_y, far]:
        copy.wait_send()
    for store in stores:
        store.wait()


def channel_stage(x, first, second, active):
    rows, width = x.shape
    units = first.shape[0]
    forward = active is None
    given = (x, first, second) if forward else (x, first, second, active)
    everything = pl.BlockSpec(memory_space=pl.ANY)
    shapes = [
        ((rows, width), F32), ((4 * rows, width), BF16), ((4 * rows, units // 2), BF16),
        ((4 * rows, units // 2 if forward else width), BF16),
        ((4 * rows, units), F32) if forward else ((4 * rows, units // 2), BF16),
    ]

    def body(*refs):
        refs = list(refs)
        if forward:
            refs.insert(3, None)
        channel_kernel(forward, *refs)

    dma = pltpu.SemaphoreType.DMA
    return pl.pallas_call(
        body,
        in_specs=[pl.BlockSpec(memory_space=pltpu.VMEM)] + [everything] * (len(given) - 1),
        out_specs=[pl.BlockSpec(memory_space=pltpu.VMEM)] + [everything] * (len(shapes) - 1),
        out_shape=[jax.ShapeDtypeStruct(s, d) for s, d in shapes],
        scratch_shapes=[
            pltpu.VMEM((units, width), BF16), pltpu.VMEM((units, width), BF16), pltpu.VMEM((4 * rows, width), BF16),
            pltpu.VMEM((2, 4 * rows, units // 2), BF16), pltpu.VMEM((4 * rows, units), F32),
            pltpu.VMEM((4 * rows, width), F32), pltpu.VMEM((2, rows, width), F32),
            pltpu.VMEM((rows, width), BF16), pltpu.VMEM((rows, width), BF16),
            dma((3,)), dma((3,)), dma((2,)), dma((2,)), dma, dma, dma((4,)), dma((4,)), dma((2,)), dma((2,)),
            dma, dma,
        ],
        compiler_params=pltpu.CompilerParams(
            collective_id=3 if forward else 4, has_side_effects=True, vmem_limit_bytes=60 << 20
        ),
        cost_estimate=pl.CostEstimate(flops=0, bytes_accessed=100 << 20, transcendentals=0),
        name="channel_forward" if forward else "channel_backward",
    )(*given)


def from_behind(x, axis, by):
    size = lax.axis_size(axis)
    pairs = [(i, i + by) for i in range(size) if 0 <= i + by < size]
    return lax.ppermute(x, axis, pairs)


def exchange(x, axis):
    return lax.all_to_all(x, axis, split_axis=0, concat_axis=0, tiled=True)


def swap(x, by):
    size = lax.axis_size("wsh")
    return lax.ppermute(x, "wsh", [(i, i ^ by) for i in range(size)])


def gather_near(x):
    if lax.axis_size("wsh") != 4:
        return lax.all_gather(x, "wsh", axis=0, tiled=True)
    return gathered_near(x, swap(x, 1), swap(x, 2))


def gathered_near(x, beside, across):
    return jnp.concatenate([x, beside, across, swap(across, 1)], 0)


def beside(x):
    return lax.ppermute(x, "seq", [(i, i ^ 1) for i in range(lax.axis_size("seq"))])


def scalar_sum(x):
    if lax.axis_size("wsh") != 4:
        return jnp.sum(lax.all_gather(x.reshape(1), "wsh", axis=0, tiled=True))
    x = jnp.full((8, 128), x)
    x = x + swap(x, 1)
    return (x + swap(x, 2))[0, 0]


def near_sum(x):
    if lax.axis_size("wsh") != 4:
        return lax.psum_scatter(x, "wsh", scatter_dimension=0, tiled=True)
    rows = x.shape[0] // 4
    beside = swap(jnp.concatenate([x[rows : 2 * rows], x[3 * rows :]], 0), 1)
    far = x[2 * rows : 3 * rows] + beside[rows:]
    return x[:rows] + beside[:rows] + swap(far.astype(BF16), 2).astype(F32)


def block_sum(x):
    if lax.axis_size("wsh") != 4:
        return lax.psum_scatter(x, "wsh", scatter_dimension=0, tiled=False).astype(F32)
    kept, far = block_halves(x)
    return kept + swap(far, 2).astype(F32)


def block_halves(x):
    number = lax.axis_index("wsh")

    def block(by):
        return lax.dynamic_index_in_dim(x, number ^ by, 0, keepdims=False)

    beside = swap(jnp.stack([block(1), block(3)]), 1).astype(F32)
    return block(0).astype(F32) + beside[0], (block(2).astype(F32) + beside[1]).astype(BF16)


def local(
    tokens, first_layer_values, teacher, valid, destination, lengths,
    receptance_matrix, key_matrix, value_matrix, output_matrix,
    lowrank_down_weight, lowrank_up_weight, channel_key_weight, channel_value_weight, vectors,
):
    rows, width = tokens.shape
    seqs, parts = lax.axis_size("seq"), lax.axis_size("wsh")
    me = lax.axis_index("seq")
    group = rows * seqs
    own_width = width // seqs
    shard = width // parts
    piece = shard // seqs
    column = me * own_width

    def own_columns(matrix):
        return lax.dynamic_slice_in_dim(matrix, column, own_width, 1)

    near = parts == 4
    up_piece = lax.dynamic_slice_in_dim(lowrank_up_weight, column % shard, own_width, 0)
    total = 3 * own_width + WIDE
    own_weights = jnp.concatenate(
        [
            own_columns(receptance_matrix), own_columns(key_matrix), own_columns(value_matrix),
            pad_ranks(lowrank_down_weight), up_piece.reshape(shard, -1),
        ],
        1,
    )

    dest_seq = destination // rows // parts
    position = dest_seq * rows + destination % rows
    digits = jnp.stack([position // DIGIT, position % DIGIT, valid], 1).astype(BF16)
    tail = jnp.pad(digits, ((0, 0), (0, EXTRA - 3)))
    given, tails, weights = gather_first(tokens, tail, own_weights)
    given, tails, weights = given.reshape(group, width), tails.reshape(group, EXTRA), weights.reshape(width, -1)
    info = tails[:, :3].astype(F32)
    places = (info[:, 0] * DIGIT + info[:, 1]).astype(jnp.int32)
    numbers = jnp.arange(group, dtype=jnp.int32)
    permute = (numbers[:, None] == places[None, :]).astype(BF16)
    total_valid = scalar_sum(jnp.sum(info[:, 2]))

    index = jnp.arange(rows, dtype=jnp.int32)
    same_dest = (dest_seq[:, None] == dest_seq[None, :]) & (index[None, :] < index[:, None])
    slot = dest_seq * (rows // seqs) + jnp.sum(same_dest.astype(jnp.int32), 1)
    arrange = (index[:, None] == slot[None, :]).astype(BF16)
    mine = (places // rows) == me
    arrival = jnp.cumsum(mine.astype(jnp.int32)) - 1
    own_rows = ((index[:, None] + me * rows) == places[None, :]).astype(BF16)
    settle = dot(own_rows, (mine[:, None] & (arrival[:, None] == index[None, :])).astype(BF16)).astype(BF16)

    offsets = jnp.cumsum(lengths[0]) - lengths[0]
    starts = jnp.any(numbers[:, None] == offsets[None, :], 1).astype(F32)
    segment_ids = jnp.cumsum(starts).reshape(-1, BLOCK)
    before = segment_ids[:, :1] - starts.reshape(-1, BLOCK)[:, :1]
    segments = jnp.stack(
        [segment_ids, jnp.broadcast_to(before, segment_ids.shape), jnp.broadcast_to(segment_ids[:, -1:], segment_ids.shape)]
        + [jnp.zeros_like(segment_ids)] * 5,
        1,
    ).reshape(-1, BLOCK)
    flowing = (1.0 - starts)[:, None]

    up = pad_ranks(
        lax.dynamic_slice(
            weights, (column // shard * shard, total), (shard, weights.shape[1] - total)
        ).reshape(own_width, -1)
    ).T
    vec = lax.dynamic_slice_in_dim(vectors, column, own_width, 0)[:, 8:16].T

    output_late, given = lax.optimization_barrier((output_matrix, given))
    w_out = lax.all_gather(output_late, "wsh", axis=0, tiled=True)
    balanced = dot(permute, given).astype(BF16)
    wide_rows = balanced.astype(F32)
    mean = jnp.mean(wide_rows, -1, keepdims=True)
    scale_one = lax.rsqrt(jnp.mean(jnp.square(wide_rows - mean), -1, keepdims=True) + 1e-05)
    stats = jnp.concatenate([mean, scale_one, flowing, flowing], 1)
    mix_vec = vectors[:, :8].T
    first_values, stats = lax.optimization_barrier((first_layer_values, stats))
    first_given = exchange(
        first_values.reshape(rows, seqs, own_width).transpose(1, 0, 2), "seq"
    ).reshape(group, own_width)
    recept, keys, values, downs, hidden = run_project(balanced, stats, mix_vec, weights, own_width, parts)
    teacher_late, recept, first_given = lax.optimization_barrier((teacher, recept, first_given))
    first = dot(permute, first_given).astype(BF16)
    teacher_rows = exchange(dot(arrange, teacher_late).astype(BF16).reshape(seqs, rows // seqs, width), "seq")
    inputs = (recept, keys, values, hidden, first, up, vec, segments)
    mixed_out, *saved = run_forward(*inputs)
    teacher_rows, mixed_out = lax.optimization_barrier((teacher_rows, mixed_out))
    target = dot(settle, teacher_rows.reshape(rows, width))

    mixed_rows = exchange(mixed_out.reshape(seqs, rows, own_width), "seq").transpose(1, 0, 2).reshape(rows, width)
    own = lax.dynamic_slice_in_dim(balanced, me * rows, rows, 0).astype(F32)
    own_starts = lax.dynamic_slice_in_dim(starts, me * rows, rows, 0)
    own_flowing = (1.0 - own_starts)[:, None]
    own_valid = dot(own_rows, tails)[:, 2]
    residual = own + dot(mixed_rows, w_out)
    standard_two, scale_two = norm_stats(residual)
    normed_two = standard_two * vectors[:, 16] + vectors[:, 17]
    carried_two = from_behind(normed_two[-1:], "seq", 1)
    delta_two = jnp.concatenate([carried_two, normed_two[:-1]], 0) * own_flowing - normed_two
    channel_in = (normed_two + delta_two * vectors[:, 18]).astype(BF16)
    paired = near and seqs == 8
    if paired:
        summed, channel, hidden_mine, hidden_other, active = channel_stage(
            channel_in, channel_key_weight, channel_value_weight, None
        )
    else:
        channel = gather_near(channel_in)
        active = jax.nn.relu(dot(channel, channel_key_weight, NT))
        hidden_rows = jnp.square(active).astype(BF16)
        summed = near_sum(dot(hidden_rows, channel_value_weight))
    result = residual + summed
    total_tokens = group * parts
    cotangent = (result - target) * (own_valid * (total_tokens / total_valid))[:, None]
    cot_low = cotangent.astype(BF16)

    result_back = exchange(dot(settle, result.astype(BF16), TN).astype(BF16).reshape(seqs, rows // seqs, width), "seq")
    if paired:
        grad_channel, cot, pre_mine, cot_other, pre_spare = channel_stage(
            cot_low, channel_value_weight, channel_key_weight, active
        )
        channel_other, pre_other = beside(channel), beside(pre_spare)
    else:
        cot = gather_near(cot_low)
        grad_pre = (dot(cot, channel_value_weight, NT) * 2.0 * active).astype(BF16)
        grad_channel = near_sum(dot(grad_pre, channel_key_weight))
    result_back, grad_channel = lax.optimization_barrier((result_back, grad_channel))
    output = dot(arrange, result_back.reshape(rows, width), TN).astype(BF16)
    grad_vec_mix_two = jnp.sum(grad_channel * delta_two, 0)
    shifted = grad_channel * vectors[:, 18] * own_flowing
    behind = from_behind(shifted[:1], "seq", -1)
    grad_normed_two = grad_channel * (1.0 - vectors[:, 18]) + jnp.concatenate([shifted[1:], behind], 0)
    grad_residual = cotangent + norm_back(grad_normed_two, standard_two, scale_two, vectors[:, 16])
    grad_low = grad_residual.astype(BF16)

    grad_posted = dot(grad_low, w_out, NT).astype(BF16)
    if paired:
        hidden_mine, grad_posted = lax.optimization_barrier((hidden_mine, grad_posted))
        value_part = (dot(hidden_mine, cot, TN) + dot(hidden_other, cot_other, TN)).astype(BF16)
    else:
        value_part = dot(hidden_rows, cot, TN).astype(BF16)
    grad_heads = exchange(grad_posted.reshape(rows, seqs, own_width).transpose(1, 0, 2), "seq").reshape(group, own_width)
    grad_heads, value_part, mixed_late = lax.optimization_barrier((grad_heads, value_part, mixed_rows))
    lefts = exchange(mixed_late.reshape(rows, seqs, parts, piece).transpose(2, 0, 1, 3), "wsh")
    near_grad = (swap(grad_low, 1), swap(grad_low, 2)) if near else gather_near(grad_low)
    recept_low, keys_low, values_low, ups_low, grad_first, grad_vec_heads = run_backward(grad_heads, *inputs, saved)
    if paired:
        channel_other, pre_other, lefts, near_grad, recept_low = lax.optimization_barrier(
            (channel_other, pre_other, lefts, near_grad, recept_low)
        )
        key_part = (dot(pre_mine, channel, TN) + dot(pre_other, channel_other, TN)).astype(BF16)
    else:
        lefts, near_grad, recept_low = lax.optimization_barrier((lefts, near_grad, recept_low))
        key_part = dot(grad_pre, channel, TN).astype(BF16)
    if near:
        near_grad = gathered_near(grad_low, *near_grad)
        lefts = jnp.stack([lax.dynamic_index_in_dim(lefts, lax.axis_index("wsh") ^ k, 0, keepdims=False) for k in range(4)])
    out_part = dot(lefts.reshape(rows * parts, -1), near_grad, TN).astype(BF16)

    moved = exchange(dot(permute, grad_first, TN).astype(BF16).reshape(seqs, rows, own_width), "seq")
    recept_low, key_part, out_part = lax.optimization_barrier((recept_low, key_part, out_part))
    if paired:
        lines = [[0, 2, 4, 6], [1, 3, 5, 7]]
        turned = [
            ((z * 2 + x) * 4 + w, (w * 2 + x) * 4 + z) for z in range(4) for x in range(2) for w in range(4)
        ]

        def along(part):
            return lax.psum_scatter(part, "seq", scatter_dimension=0, tiled=True, axis_index_groups=lines)

        def turn(part):
            return lax.ppermute(part, ("seq", "wsh"), turned)

        halves_out = out_part.reshape(seqs // 2, 2, piece, width)
        x_side = me % 2
        out_mine = lax.dynamic_index_in_dim(halves_out, x_side, 1, keepdims=False).astype(F32)
        out_other = beside(lax.dynamic_index_in_dim(halves_out, 1 - x_side, 1, keepdims=False))
        value_sum, key_sum = along(value_part), along(key_part)
    else:
        moves = [(s * parts + w, w * seqs + s) for s in range(seqs) for w in range(parts)]

        def ffn_grad(part):
            part = lax.psum_scatter(part, "seq", scatter_dimension=0, tiled=True)
            return lax.ppermute(part, ("seq", "wsh"), moves).astype(F32)

        grad_ffn_value, grad_ffn_key = ffn_grad(value_part), ffn_grad(key_part)
        grad_out = lax.psum_scatter(out_part, "seq", scatter_dimension=0, tiled=True)

    heads_part = lax.dynamic_update_slice_in_dim(jnp.zeros((width, 8), F32), grad_vec_heads.T, column, 0)
    vec_two = jnp.stack(
        [jnp.sum(grad_normed_two * standard_two, 0), jnp.sum(grad_normed_two, 0), grad_vec_mix_two], 1
    )
    others = jnp.concatenate([heads_part, jnp.pad(vec_two, ((0, 0), (0, 13)))], 1)
    scaled_grad, sums, wide, up_grad = run_unproject(
        balanced, stats, mix_vec, weights, others, (recept_low, keys_low, values_low), ups_low, hidden, downs, up, parts
    )
    if paired:
        moved, value_sum, out_other, scaled_grad, sums, wide, up_grad = lax.optimization_barrier(
            (moved, value_sum, out_other, scaled_grad, sums, wide, up_grad)
        )
        out_half = (out_mine + out_other.astype(F32)).astype(BF16).reshape(-1, width)
        out_half, sums = lax.optimization_barrier((out_half, sums))
        grad_out = along(out_half)
        grad_ffn_value = turn(value_sum).astype(F32)
    else:
        moved, scaled_grad, sums, wide = lax.optimization_barrier((moved, scaled_grad, sums, wide))
    grad_first_rows = moved.transpose(1, 0, 2).reshape(rows, width)

    standard = (balanced.astype(F32) - mean) * scale_one
    grad_balanced = scale_one * (scaled_grad - sums[:, :1] * (1.0 / width) - standard * (sums[:, 1:] * (1.0 / width)))
    mine_rows = lax.dynamic_slice_in_dim(grad_balanced, me * rows, rows, 0) + grad_residual
    grad_balanced = lax.dynamic_update_slice_in_dim(grad_balanced, mine_rows, me * rows, 0)
    grad_given = dot(permute, grad_balanced.astype(BF16), TN).astype(BF16).reshape(seqs, rows, width)
    if near:
        kept_part, far = block_halves(wide)
        grad_given, far = lax.optimization_barrier((grad_given, far))
        wide_part = kept_part + swap(far, 2).astype(F32)
    else:
        wide_part = block_sum(wide)
    grad_tokens = reduce_seq(grad_given).astype(BF16)
    if paired:
        wide_part, grad_tokens, grad_out, key_sum = lax.optimization_barrier((wide_part, grad_tokens, grad_out, key_sum))
        grad_ffn_key = turn(key_sum).astype(F32)
    wide_all = exchange(wide_part.astype(BF16), "seq").astype(F32)

    def square(at):
        taken = wide_all[:, :, at * own_width : (at + 1) * own_width]
        return taken.transpose(1, 0, 2).reshape(piece, width)

    narrow = jnp.sum(wide_all[:, :, 3 * own_width :], 0)
    grad_down = unpad_ranks(narrow)
    grad_vectors = narrow[:, RANKS[0] : RANKS[0] + vectors.shape[1]]
    up_part = unpad_ranks(block_sum(up_grad.reshape(parts, piece, WIDE)))

    return (
        output, grad_tokens, grad_first_rows,
        square(0), square(1), square(2),
        grad_out.astype(F32), grad_down, up_part,
        grad_ffn_key, grad_ffn_value, grad_vectors,
    )


def solution(mesh):
    both, shard = P(("seq", "wsh"), None), P("wsh", None)
    flat = P(("seq", "wsh"))
    return jax.shard_map(
        local,
        mesh=mesh,
        in_specs=(both, both, both, flat, flat) + (shard,) * 9 + (P(),),
        out_specs=(both,) * 12,
        check_vma=False,
    )
```

```python
import functools

import jax
import jax.numpy as jnp
from jax import lax
from jax.experimental import pallas as pl
from jax.experimental.pallas import tpu as pltpu
from jax.sharding import PartitionSpec as P

HEAD = 64
BLOCK = 64
RANKS = (96, 96, 64, 256)
PADDED = (128, 128, 128, 256)
OFFSETS = (0, 128, 256, 384)
WIDE = 640
EXTRA = 128
DIGIT = 64

F32 = jnp.float32
BF16 = jnp.bfloat16

NN = (((1,), (0,)), ((), ()))
NT = (((1,), (1,)), ((), ()))
TN = (((0,), (0,)), ((), ()))


def dot(a, b, dims=NN):
    return lax.dot_general(a, b, dims, preferred_element_type=F32)


def halves(x):
    high = x.astype(BF16)
    return high, (x - high.astype(F32)).astype(BF16)


def dot3(a, b, dims=NN):
    a_high, a_low = halves(a)
    b_high, b_low = halves(b)
    return dot(a_high, b_high, dims) + (dot(a_high, b_low, dims) + dot(a_low, b_high, dims))


def sum_left(mask, x):
    high, low = halves(x)
    low_two = (x - high.astype(F32) - low.astype(F32)).astype(BF16)
    return dot(mask, high) + (dot(mask, low) + dot(mask, low_two))


def head_sum(x, ones):
    high, low = halves(x)
    return dot(high, ones) + dot(low, ones)


def low(x):
    return x.astype(BF16).astype(F32)


def iotas(rows, columns):
    return (
        lax.broadcasted_iota(jnp.int32, (rows, columns), 0),
        lax.broadcasted_iota(jnp.int32, (rows, columns), 1),
    )


def head_ones(width):
    i, j = iotas(width, width)
    return jnp.where((i >> 6) == (j >> 6), 1.0, 0.0).astype(BF16)


def front(keys, values, hidden, up, first, vec, ones):
    z = vec[0:1] + dot(hidden[:, 0:128], up[0:128])
    decay_log = -(jnp.maximum(-z, 0.0) + jnp.log1p(jnp.exp(-jnp.abs(z)))) - 0.5
    rate = jax.nn.sigmoid(vec[1:2] + dot(hidden[:, 128:256], up[128:256]))
    blend = jax.nn.sigmoid(vec[2:3] + dot(hidden[:, 256:384], up[256:384]))
    gate = dot(hidden[:, 384:640], up[384:640])
    mixed_value = values + (first - values) * blend
    scaled = keys * vec[3:4]
    scale = lax.rsqrt(head_sum(scaled * scaled, ones) + 1e-06)
    key_dir = scaled * scale
    key_mod = keys * (1.0 + (rate - 1.0) * vec[4:5])
    return z, decay_log, rate, blend, gate, mixed_value, scale, key_dir, key_mod


def block_masks(segments):
    i, j = iotas(BLOCK, BLOCK)
    across = jnp.broadcast_to(segments[0:1], (BLOCK, BLOCK))
    down = across.T
    before = jnp.broadcast_to(segments[1:2], (BLOCK, BLOCK))
    last = jnp.broadcast_to(segments[2:3], (BLOCK, BLOCK))
    same = across == down
    strict = jnp.where(same & (i > j), 1.0, 0.0)
    closed = jnp.where(same & (i >= j), 1.0, 0.0)
    carry = jnp.where(down == before, 1.0, 0.0)
    tail = jnp.where(down == last, 1.0, 0.0)
    keep = jnp.where(segments[2:3] == segments[1:2], 1.0, 0.0)
    quad = jnp.concatenate(
        [jnp.concatenate([strict, strict], 1), jnp.concatenate([closed, closed], 1)], 0
    )
    return quad, carry, tail, keep


def tile_heads(x, heads):
    return jnp.concatenate([x] * heads, 1) if heads > 1 else x


def join(pieces, axis):
    return jnp.concatenate(pieces, axis) if len(pieces) > 1 else pieces[0]


def decayed(decay_low, key_low, dir_low, rate_low, recept_low, carry, tail):
    i, j = iotas(BLOCK, BLOCK)
    lower = jnp.where(i >= j, 1.0, 0.0).astype(BF16)
    log_step = -jnp.exp(decay_low)
    total = sum_left(lower, log_step)
    before = jnp.exp(total - log_step)
    grown = jnp.exp(total)
    shrunk = jnp.exp(-total)
    end = total[BLOCK - 1 : BLOCK]
    tail_decay = jnp.exp(end - total) * tail
    alpha = -dir_low * before
    beta_plain = dir_low * rate_low
    beta = beta_plain * shrunk
    key = key_low * shrunk
    recept = recept_low * grown
    return dict(
        log_step=log_step, before=before, grown=grown, shrunk=shrunk, end=jnp.exp(end), tail=tail_decay,
        alpha=alpha, beta_plain=beta_plain, beta=beta, key=key, recept=recept,
        beta_end=beta_plain * tail_decay, key_end=key_low * tail_decay,
        alpha_in=alpha * carry, recept_in=recept * carry,
    )


def unit_inverses(lowers):
    i, j = iotas(BLOCK, BLOCK)
    eye = jnp.where(i == j, 1.0, 0.0)

    def within(size):
        return (i // size) == (j // size)

    smalls = [jnp.where(within(4), x, 0.0) for x in lowers]
    low_smalls = [x.astype(BF16) for x in smalls]
    twos = [dot(x, x) for x in low_smalls]
    inverses = [eye + x for x in smalls]
    inverses = [x + dot(x.astype(BF16), y.astype(BF16)) for x, y in zip(inverses, twos)]
    for size in (8, 16, 32, 64):
        mask = within(size) & ~within(size // 2)
        offs = [jnp.where(mask, x, 0.0).astype(BF16) for x in lowers]
        lows = [x.astype(BF16) for x in inverses]
        inner = [dot(x, y).astype(BF16) for x, y in zip(offs, lows)]
        inverses = [x + dot(y, z) for x, y, z in zip(inverses, lows, inner)]
    errors = [eye - x + dot3(y, x) for x, y in zip(inverses, lowers)]
    return [x + dot(x.astype(BF16), y.astype(BF16)) for x, y in zip(inverses, errors)]


def post_norm(head_low, ones):
    centered = head_low - head_sum(head_low, ones) * (1.0 / HEAD)
    spread = lax.rsqrt(head_sum(centered * centered, ones) * (1.0 / HEAD) + HEAD * 1e-05)
    return centered * spread, spread


def forward_kernel(
    count, recept_ref, keys_ref, values_ref, hidden_ref, first_ref, up_ref, vec_ref, segment_ref,
    mixed_ref, head_ref, state_ref, inverse_ref, removed_ref, state,
):
    width = recept_ref.shape[1]
    heads = width // HEAD

    @pl.when(pl.program_id(0) == 0)
    def _():
        state[...] = jnp.zeros_like(state)

    ones = head_ones(width)
    vec = vec_ref[...]
    up = up_ref[...]
    columns = [slice(head * HEAD, (head + 1) * HEAD) for head in range(heads)]
    done = []
    for block in range(count):
        rows = slice(block * BLOCK, (block + 1) * BLOCK)
        recept, keys, values = recept_ref[rows], keys_ref[rows], values_ref[rows]
        _, decay_log, rate, _, gate, mixed_value, _, key_dir, key_mod = front(
            keys, values, hidden_ref[rows], up, first_ref[rows].astype(F32), vec, ones
        )
        quad, carry, tail, keep = block_masks(segment_ref[block * 8 : block * 8 + 8])
        parts = decayed(
            low(decay_log), low(key_mod), low(key_dir), low(rate), low(recept),
            tile_heads(carry, heads), tile_heads(tail, heads),
        )
        lefts = [jnp.concatenate([parts["alpha"][:, c], parts["recept"][:, c]], 0) for c in columns]
        rights = [jnp.concatenate([parts["beta"][:, c], parts["key"][:, c]], 0) for c in columns]
        pairs = [quad * dot3(x, y, NT) for x, y in zip(lefts, rights)]
        done.append((rows, recept, key_mod, gate, mixed_value, keep, parts, pairs))
    inverses = unit_inverses([x[:BLOCK, :BLOCK] for item in done for x in item[-1]])
    for block, (rows, recept, key_mod, gate, mixed_value, keep, parts, pairs) in enumerate(done):
        mine = inverses[block * heads : (block + 1) * heads]
        value_low = low(mixed_value)
        owns = [value_low[:, c] for c in columns]
        by_values = [dot3(x[:, BLOCK:], y) for x, y in zip(pairs, owns)]
        ends = [jnp.concatenate([parts["beta_end"][:, c], parts["key_end"][:, c]], 0) for c in columns]
        inners = [jnp.concatenate([parts["alpha_in"][:, c], parts["recept_in"][:, c]], 0) for c in columns]
        entering = state[...]
        state_ref[rows] = entering
        nows = [entering[:, c] for c in columns]
        inwards = [dot3(x, y, NT) for x, y in zip(inners, nows)]
        removals = [dot3(x, y[:BLOCK] + z[:BLOCK]) for x, y, z in zip(mine, inwards, by_values)]
        outs = [
            y[BLOCK:] + z[BLOCK:] + dot3(x[BLOCK:, :BLOCK], r)
            for x, y, z, r in zip(pairs, inwards, by_values, removals)
        ]
        leaving = [
            x * (parts["end"][:, c] * keep) + dot3(jnp.concatenate([r, v], 0), e, TN)
            for x, c, r, v, e in zip(nows, columns, removals, owns, ends)
        ]
        state[...] = join(leaving, 1)
        inverse_ref[rows] = join(mine, 1)
        removed_ref[rows] = join(removals, 1)
        head_low = join(outs, 1).astype(BF16)
        head_ref[rows] = head_low
        normed, _ = post_norm(head_low.astype(F32), ones)
        bonus = head_sum(recept * key_mod * vec[5:6], ones) * mixed_value
        mixed_ref[rows] = ((normed * vec[6:7] + vec[7:8] + bonus) * gate).astype(BF16)


def backward_kernel(
    count, grad_ref, recept_ref, keys_ref, values_ref, hidden_ref, first_ref, up_ref, vec_ref, segment_ref,
    head_ref, state_ref, inverse_ref, removed_ref,
    recept_out, keys_out, values_out, ups_out, first_out, vec_out, state,
):
    width = recept_ref.shape[1]
    heads = width // HEAD

    @pl.when(pl.program_id(0) == 0)
    def _():
        state[...] = jnp.zeros_like(state)
        vec_out[...] = jnp.zeros_like(vec_out)

    ones = head_ones(width)
    vec = vec_ref[...]
    up = up_ref[...]
    i, j = iotas(BLOCK, BLOCK)
    upper = jnp.where(i <= j, 1.0, 0.0).astype(BF16)
    columns = [slice(head * HEAD, (head + 1) * HEAD) for head in range(heads)]
    order = range(count - 1, -1, -1)
    kept = {}
    for block in order:
        rows = slice(block * BLOCK, (block + 1) * BLOCK)
        recept, keys, values = recept_ref[rows], keys_ref[rows], values_ref[rows]
        first = first_ref[rows].astype(F32)
        z, decay_log, rate, blend, gate, mixed_value, scale, key_dir, key_mod = front(
            keys, values, hidden_ref[rows], up, first, vec, ones
        )
        quad, carry, tail, keep = block_masks(segment_ref[block * 8 : block * 8 + 8])
        rate_low, dir_low = low(rate), low(key_dir)
        parts = decayed(
            low(decay_log), low(key_mod), dir_low, rate_low, low(recept),
            tile_heads(carry, heads), tile_heads(tail, heads),
        )
        value_low = low(mixed_value)

        grad = grad_ref[rows].astype(F32)
        normed, spread = post_norm(head_ref[rows].astype(F32), ones)
        product = recept * key_mod
        coefficient = head_sum(product * vec[5:6], ones)
        grad_gate = grad * (normed * vec[6:7] + vec[7:8] + coefficient * mixed_value)
        opened = grad * gate
        grad_normed = opened * vec[6:7]
        grad_head = spread * (
            grad_normed
            - head_sum(grad_normed, ones) * (1.0 / HEAD)
            - normed * (head_sum(grad_normed * normed, ones) * (1.0 / HEAD))
        )
        grad_coefficient = head_sum(opened * mixed_value, ones)
        weighted = grad_coefficient * vec[5:6]
        head_grad = low(grad_head)

        lefts = [jnp.concatenate([parts["alpha"][:, c], parts["recept"][:, c]], 0) for c in columns]
        rights = [jnp.concatenate([parts["beta"][:, c], parts["key"][:, c]], 0) for c in columns]
        ends = [jnp.concatenate([parts["beta_end"][:, c], parts["key_end"][:, c]], 0) for c in columns]
        inners = [jnp.concatenate([parts["alpha_in"][:, c], parts["recept_in"][:, c]], 0) for c in columns]
        pairs = [quad * dot3(x, y, NT) for x, y in zip(lefts, rights)]
        out_grads = [head_grad[:, c] for c in columns]
        through = [dot3(x[BLOCK:, :BLOCK], y, TN) for x, y in zip(pairs, out_grads)]
        kept[block] = dict(
            rows=rows, recept=recept, keys=keys, values=values, first=first, z=z, rate=rate, blend=blend,
            mixed_value=mixed_value, scale=scale, key_dir=key_dir, key_mod=key_mod, quad=quad, carry=carry, keep=keep,
            rate_low=rate_low, dir_low=dir_low, parts=parts, value_low=value_low, normed=normed, product=product,
            grad_gate=grad_gate, opened=opened, grad_coefficient=grad_coefficient,
            grad_mixed_value=opened * coefficient, grad_recept=weighted * key_mod, grad_key_mod=weighted * recept,
            lefts=lefts, rights=rights, ends=ends, inners=inners, pairs=pairs, out_grads=out_grads, through=through,
        )
    for block in order:
        k = kept[block]
        after, entering, inverse_all = state[...], state_ref[k["rows"]], inverse_ref[k["rows"]]
        laters, nows = [after[:, c] for c in columns], [entering[:, c] for c in columns]
        from_ends = [dot3(x, y, NT) for x, y in zip(k["ends"], laters)]
        inner_grads = [
            dot3(inverse_all[:, c], x + y[:BLOCK], TN) for c, x, y in zip(columns, k["through"], from_ends)
        ]
        boths = [jnp.concatenate([x, y], 0) for x, y in zip(inner_grads, k["out_grads"])]
        stays = [x * (k["parts"]["end"][:, c] * k["keep"]) for x, c in zip(laters, columns)]
        state[...] = join([x + dot3(y, z, TN) for x, y, z in zip(stays, boths, k["inners"])], 1)
        k.update(
            laters=laters, nows=nows, from_ends=from_ends, boths=boths,
            end_sum=join([jnp.sum(x * y, 0, keepdims=True) for x, y in zip(nows, stays)], 1),
        )
    vec_total = jnp.zeros_like(vec)
    for block in order:
        k = kept[block]
        rows, parts, quad = k["rows"], k["parts"], k["quad"]
        removed_all = removed_ref[rows]
        carry_two = jnp.concatenate([k["carry"], k["carry"]], 0)
        sources = [jnp.concatenate([removed_all[:, c], k["value_low"][:, c]], 0) for c in columns]
        grad_pairs = [quad * dot3(x, y, NT) for x, y in zip(k["boths"], sources)]
        grad_values = [
            dot3(x[:, BLOCK:], y, TN) + z[BLOCK:] for x, y, z in zip(k["pairs"], k["boths"], k["from_ends"])
        ]
        grad_ends = [dot3(x, y) for x, y in zip(sources, k["laters"])]
        to_state = [carry_two * dot3(x, y) for x, y in zip(k["boths"], k["nows"])]
        grad_lefts = [dot3(x, y) + z for x, y, z in zip(grad_pairs, k["rights"], to_state)]
        grad_rights = [dot3(x, y, TN) for x, y in zip(grad_pairs, k["lefts"])]
        d_alpha, d_recept = join([x[:BLOCK] for x in grad_lefts], 1), join([x[BLOCK:] for x in grad_lefts], 1)
        d_beta, d_key = join([x[:BLOCK] for x in grad_rights], 1), join([x[BLOCK:] for x in grad_rights], 1)
        d_beta_end, d_key_end = join([x[:BLOCK] for x in grad_ends], 1), join([x[BLOCK:] for x in grad_ends], 1)
        ended = parts["beta_end"] * d_beta_end + parts["key_end"] * d_key_end
        alphas = parts["alpha"] * d_alpha
        d_total = parts["recept"] * d_recept - parts["beta"] * d_beta - parts["key"] * d_key - ended + alphas
        d_step = sum_left(upper, d_total) + (jnp.sum(ended, 0, keepdims=True) + k["end_sum"]) - alphas
        d_beta_plain = d_beta * parts["shrunk"] + d_beta_end * parts["tail"]
        copy_decay = low(d_step * parts["log_step"])
        copy_dir = low(d_beta_plain * k["rate_low"] - d_alpha * parts["before"])
        copy_rate = low(d_beta_plain * k["dir_low"])

        keys, values, rate, blend = k["keys"], k["values"], k["rate"], k["blend"]
        grad_recept = k["grad_recept"] + low(d_recept * parts["grown"])
        grad_key_mod = k["grad_key_mod"] + low(d_key * parts["shrunk"] + d_key_end * parts["tail"])
        grad_mixed_value = k["grad_mixed_value"] + low(join(grad_values, 1))
        grad_z = copy_decay * jax.nn.sigmoid(-k["z"])
        factor = 1.0 + (rate - 1.0) * vec[4:5]
        keyed = grad_key_mod * keys
        grad_rate = copy_rate + keyed * vec[4:5]
        grad_scaled = k["scale"] * (copy_dir - k["key_dir"] * head_sum(copy_dir * k["key_dir"], ones))
        grad_keys = grad_key_mod * factor + grad_scaled * vec[3:4]
        grad_rate_up = grad_rate * rate * (1.0 - rate)
        grad_value_up = grad_mixed_value * (k["first"] - values) * blend * (1.0 - blend)
        recept_out[rows] = grad_recept.astype(BF16)
        keys_out[rows] = grad_keys.astype(BF16)
        values_out[rows] = (grad_mixed_value * (1.0 - blend)).astype(BF16)
        first_out[rows] = (grad_mixed_value * blend).astype(BF16)
        ups_out[0, rows] = grad_z.astype(BF16)
        ups_out[1, rows] = grad_rate_up.astype(BF16)
        ups_out[2, rows] = grad_value_up.astype(BF16)
        ups_out[3, rows] = k["grad_gate"].astype(BF16)

        def total(x):
            return jnp.sum(x, 0, keepdims=True)

        vec_total = vec_total + jnp.concatenate(
            [
                total(grad_z), total(grad_rate_up), total(grad_value_up), total(grad_scaled * keys),
                total(keyed * (rate - 1.0)), total(k["grad_coefficient"] * k["product"]),
                total(k["opened"] * k["normed"]), total(k["opened"]),
            ],
            0,
        )
    vec_out[...] += vec_total


def kernel_cost(rows, width, passes):
    return pl.CostEstimate(flops=2 * rows * width * width, bytes_accessed=4 * rows * width * passes, transcendentals=0)


def per_step(rows, most):
    return most if (rows // BLOCK) % most == 0 else 1


def run_forward(recept, keys, values, hidden, first, up, vec, segments):
    rows, width = recept.shape
    count = per_step(rows, 4)
    step = count * BLOCK

    def spec(columns):
        return pl.BlockSpec((step, columns), lambda i: (i, 0))

    def whole(array):
        return pl.BlockSpec(array.shape, lambda i: (0, 0))

    return pl.pallas_call(
        functools.partial(forward_kernel, count),
        grid=(rows // step,),
        in_specs=[
            spec(width), spec(width), spec(width), spec(WIDE), spec(width), whole(up), whole(vec),
            pl.BlockSpec((count * 8, BLOCK), lambda i: (i, 0)),
        ],
        out_specs=[spec(width)] * 5,
        out_shape=[jax.ShapeDtypeStruct((rows, width), d) for d in (BF16, BF16, F32, F32, F32)],
        scratch_shapes=[pltpu.VMEM((BLOCK, width), F32)],
        compiler_params=pltpu.CompilerParams(vmem_limit_bytes=48 << 20),
        cost_estimate=kernel_cost(rows, width, 110),
        name="mix_forward",
    )(recept, keys, values, hidden, first, up, vec, segments)


def run_backward(grad, recept, keys, values, hidden, first, up, vec, segments, saved):
    rows, width = recept.shape
    count = per_step(rows, 2)
    step = count * BLOCK
    last = rows // step - 1

    def spec(columns):
        return pl.BlockSpec((step, columns), lambda i: (last - i, 0))

    def whole(array):
        return pl.BlockSpec(array.shape, lambda i: (0, 0))

    return pl.pallas_call(
        functools.partial(backward_kernel, count),
        grid=(rows // step,),
        in_specs=[
            spec(width), spec(width), spec(width), spec(width), spec(WIDE), spec(width), whole(up), whole(vec),
            pl.BlockSpec((count * 8, BLOCK), lambda i: (last - i, 0)),
            spec(width), spec(width), spec(width), spec(width),
        ],
        out_specs=[
            spec(width), spec(width), spec(width),
            pl.BlockSpec((4, step, width), lambda i: (0, last - i, 0)),
            spec(width), pl.BlockSpec((8, width), lambda i: (0, 0)),
        ],
        out_shape=[
            jax.ShapeDtypeStruct((rows, width), BF16), jax.ShapeDtypeStruct((rows, width), BF16),
            jax.ShapeDtypeStruct((rows, width), BF16), jax.ShapeDtypeStruct((4, rows, width), BF16),
            jax.ShapeDtypeStruct((rows, width), BF16), jax.ShapeDtypeStruct((8, width), F32),
        ],
        scratch_shapes=[pltpu.VMEM((BLOCK, width), F32)],
        compiler_params=pltpu.CompilerParams(vmem_limit_bytes=48 << 20),
        cost_estimate=kernel_cost(rows, width, 150),
        name="mix_backward",
    )(grad, recept, keys, values, hidden, first, up, vec, segments, *saved)


def mix_norm(block_ref, stats_ref, vec_ref):
    stats = stats_ref[...]
    flowing = stats[:, 2:3]
    standard = (block_ref[...].astype(F32) - stats[:, 0:1]) * stats[:, 1:2]
    normed = standard * vec_ref[0:1] + vec_ref[1:2]
    delta = pltpu.roll(normed, 1, 0) * flowing - normed
    return standard, normed, delta, flowing


def project_kernel(
    width, block_ref, stats_ref, vec_ref, weight_ref,
    recept_ref, keys_ref, values_ref, downs_ref, hidden_ref,
):
    base = 3 * width
    _, normed, delta, _ = mix_norm(block_ref, stats_ref, vec_ref)
    weight = weight_ref[...]
    uses = (
        ((recept_ref, 0, width, 0),),
        ((downs_ref, base + OFFSETS[0], PADDED[0], OFFSETS[0]),),
        ((keys_ref, width, width, 0),),
        ((values_ref, 2 * width, width, 0), (downs_ref, base + OFFSETS[2], PADDED[2], OFFSETS[2])),
        ((downs_ref, base + OFFSETS[1], PADDED[1], OFFSETS[1]),),
        ((downs_ref, base + OFFSETS[3], PADDED[3], OFFSETS[3]),),
    )

    @pl.when(pl.program_id(0) == 0)
    def _():
        for ref in (recept_ref, keys_ref, values_ref, downs_ref):
            ref[...] = jnp.zeros_like(ref)

    for c, targets in enumerate(uses):
        mixed = (normed + delta * vec_ref[2 + c : 3 + c]).astype(BF16)
        for ref, start, size, at in targets:
            ref[:, at : at + size] += dot(mixed, weight[:, start : start + size])

    @pl.when(pl.program_id(0) == pl.num_programs(0) - 1)
    def _():
        hidden_ref[:, 0:128] = jnp.tanh(downs_ref[:, 0:128]).astype(BF16)
        hidden_ref[:, 128:384] = downs_ref[:, 128:384].astype(BF16)
        hidden_ref[:, 384:640] = jax.nn.sigmoid(downs_ref[:, 384:640]).astype(BF16)


def unproject_kernel(
    width, parts, piece, block_ref, stats_ref, vec_ref, weight_ref,
    other_ref, recept_ref, keys_ref, values_ref, ups_ref, hidden_ref, downs_ref, up_ref,
    grad_ref, sums_ref, wide_ref, up_out, down_lows,
):
    rows = block_ref.shape[0]
    base = 3 * width

    @pl.when(pl.program_id(0) == 0)
    def _():
        sums_ref[...] = jnp.zeros_like(sums_ref)
        for k, (at, size) in enumerate(zip(OFFSETS, PADDED)):
            cols = slice(at, at + size)
            grad = dot(ups_ref[k], up_ref[cols], NT)
            if k == 0:
                grad = grad * (1.0 - jnp.square(jnp.tanh(downs_ref[:, cols])))
            if k == 3:
                opening = jax.nn.sigmoid(downs_ref[:, cols])
                grad = grad * opening * (1.0 - opening)
            down_lows[:, cols] = grad.astype(BF16)
            up_out[:, cols] = dot(ups_ref[k], hidden_ref[:, cols], TN).astype(BF16)

    standard, normed, delta, flowing = mix_norm(block_ref, stats_ref, vec_ref)
    weight = weight_ref[...]

    def down(k):
        return (down_lows[:, OFFSETS[k] : OFFSETS[k] + PADDED[k]], base + OFFSETS[k], PADDED[k])

    uses = (
        ((recept_ref[...], 0, width),),
        (down(0),),
        ((keys_ref[...], width, width),),
        ((values_ref[...], 2 * width, width), down(2)),
        (down(1),),
        (down(3),),
    )
    kept, sent, vec_rows = None, None, []
    per_seq = parts * piece
    for c, sources in enumerate(uses):
        share = vec_ref[2 + c : 3 + c]
        mixed = (normed + delta * share).astype(BF16)
        grad = None
        for source, start, size in sources:
            part = dot(source, weight[:, start : start + size], NT)
            grad = part if grad is None else grad + part
            product = dot(mixed, source, TN).astype(BF16)
            for number in range(product.shape[0] // per_seq):
                for w in range(parts):
                    at = number * per_seq + w * piece
                    wide_ref[w, number, :, start : start + size] = product[at : at + piece]
        vec_rows.append(jnp.sum(grad * delta, 0, keepdims=True))
        moved = grad * share
        kept = grad - moved if kept is None else kept + (grad - moved)
        sent = moved if sent is None else sent + moved
    grad = kept + pltpu.roll(sent * flowing, rows - 1, 0)
    vec_rows = jnp.concatenate(
        [jnp.sum(grad * standard, 0, keepdims=True), jnp.sum(grad, 0, keepdims=True)] + vec_rows, 0
    )
    spare = jnp.concatenate([vec_rows.T, other_ref[...]], 1).astype(BF16)
    for number in range(spare.shape[0] // per_seq):
        for w in range(parts):
            at = number * per_seq + w * piece
            wide_ref[w, number, :, base + RANKS[0] : base + PADDED[0]] = spare[at : at + piece]
    scaled = grad * vec_ref[0:1]
    sums_ref[:, 0:1] += jnp.sum(scaled, 1, keepdims=True)
    sums_ref[:, 1:2] += jnp.sum(scaled * standard, 1, keepdims=True)
    grad_ref[...] = scaled


def mix_specs(rows, width, own_width, parts):
    block = 256 if rows <= 1024 else 128

    def columns(height):
        return pl.BlockSpec((height, block), lambda j: (0, j))

    def whole(shape):
        return pl.BlockSpec(shape, lambda j: (0,) * len(shape))

    def weights(array):
        size = array.shape[1] if rows > 1024 else 3 * own_width + WIDE
        return pl.BlockSpec((block, size), lambda j: (j, 0))

    return block, columns, whole, weights


def run_project(balanced, stats, vec, weights, own_width, parts):
    rows, width = balanced.shape
    block, columns, whole, weight_spec = mix_specs(rows, width, own_width, parts)
    shapes = [(rows, own_width)] * 3 + [(rows, WIDE)] * 2
    return pl.pallas_call(
        functools.partial(project_kernel, own_width),
        grid_spec=pltpu.PrefetchScalarGridSpec(
            num_scalar_prefetch=0,
            grid=(width // block,),
            in_specs=[columns(rows), whole(stats.shape), columns(8), weight_spec(weights)],
            out_specs=[whole(s) for s in shapes],
        ),
        out_shape=[jax.ShapeDtypeStruct(s, d) for s, d in zip(shapes, (F32, F32, F32, F32, BF16))],
        compiler_params=pltpu.CompilerParams(vmem_limit_bytes=60 << 20),
        cost_estimate=kernel_cost(rows, own_width, 60),
        name="mix_project",
    )(balanced, stats, vec, weights)


def run_unproject(balanced, stats, vec, weights, others, lows, ups, hidden, downs, up, parts):
    rows, width = balanced.shape
    own_width = lows[0].shape[1]
    seqs = width // own_width
    piece = own_width // parts
    block, columns, whole, weight_spec = mix_specs(rows, width, own_width, parts)
    taken = block // own_width
    total = 3 * own_width + WIDE
    return pl.pallas_call(
        functools.partial(unproject_kernel, own_width, parts, piece),
        grid_spec=pltpu.PrefetchScalarGridSpec(
            num_scalar_prefetch=0,
            grid=(width // block,),
            in_specs=[
                columns(rows), whole(stats.shape), columns(8), weight_spec(weights),
                pl.BlockSpec((block, others.shape[1]), lambda j: (j, 0)),
            ]
            + [whole(a.shape) for a in (*lows, ups, hidden, downs, up)],
            out_specs=[
                columns(rows), whole((rows, 2)),
                pl.BlockSpec((parts, taken, piece, total), lambda j: (0, j, 0, 0)),
                whole((own_width, WIDE)),
            ],
            scratch_shapes=[pltpu.VMEM((rows, WIDE), BF16)],
        ),
        out_shape=[
            jax.ShapeDtypeStruct((rows, width), F32), jax.ShapeDtypeStruct((rows, 2), F32),
            jax.ShapeDtypeStruct((parts, seqs, piece, total), BF16),
            jax.ShapeDtypeStruct((own_width, WIDE), BF16),
        ],
        compiler_params=pltpu.CompilerParams(vmem_limit_bytes=60 << 20),
        cost_estimate=kernel_cost(rows, own_width, 120),
        name="mix_unproject",
    )(balanced, stats, vec, weights, others, *lows, ups, hidden, downs, up)


def norm_stats(values):
    centered = values - jnp.mean(values, -1, keepdims=True)
    scale = lax.rsqrt(jnp.mean(centered * centered, -1, keepdims=True) + 1e-05)
    return centered * scale, scale


def norm_back(grad, standard, scale, gain):
    scaled = grad * gain
    return scale * (
        scaled
        - jnp.mean(scaled, -1, keepdims=True)
        - standard * jnp.mean(scaled * standard, -1, keepdims=True)
    )


def pad_ranks(matrix):
    pieces, start = [], 0
    for rank, padded in zip(RANKS, PADDED):
        pieces.append(jnp.pad(matrix[:, start : start + rank], ((0, 0), (0, padded - rank))))
        start += rank
    return jnp.concatenate(pieces, 1)


def unpad_ranks(matrix):
    return jnp.concatenate([matrix[..., o : o + r] for o, r in zip(OFFSETS, RANKS)], -1)


MESH_ID = pl.DeviceIdType.MESH


def places():
    s, w = lax.axis_index("seq"), lax.axis_index("wsh")
    side = s % 2
    return s, w, side, s // 2, (s + 1 - 2 * side, w), (s, w + 1 - 2 * (w % 2)), (s, w + 2 - 4 * (w // 2))


def greet(neighbours, number):
    barrier = pltpu.get_barrier_semaphore()
    for there, device in neighbours:
        if there is None:
            pl.semaphore_signal(barrier, inc=1, device_id=device, device_id_type=MESH_ID)
        else:

            @pl.when(there)
            def _(device=device):
                pl.semaphore_signal(barrier, inc=1, device_id=device, device_id_type=MESH_ID)

    pl.semaphore_wait(barrier, number)


def send(source, target, send_sem, recv_sem, device):
    return pltpu.make_async_remote_copy(
        src_ref=source, dst_ref=target, send_sem=send_sem, recv_sem=recv_sem, device_id=device, device_id_type=MESH_ID
    )


def line_ends(z):
    return jnp.where(z > 0, 1, 0) + jnp.where(z < 3, 1, 0)


def gather_kernel(
    own_ref, tail_ref, weight_ref, out_ref, tails_ref, weights_ref,
    copy_sem, right_send, right_recv, left_send, left_recv, x_send, x_recv, c_send, c_recv, y_send, y_recv,
):
    s, w, side, z, x_device, core_device, y_device = places()
    up, down = (s + 2, w), (s - 2, w)
    across = w + 2 - 4 * (w // 2)
    kinds = ((own_ref, out_ref), (tail_ref, tails_ref))
    copies = [pltpu.make_async_copy(own, out.at[s], copy_sem.at[k]) for k, (own, out) in enumerate(kinds)]
    copies.append(pltpu.make_async_copy(weight_ref, weights_ref.at[w], copy_sem.at[2]))
    for copy in copies:
        copy.start()
    greet(((None, x_device), (None, core_device), (None, y_device), (z < 3, up), (z > 0, down)), 3 + line_ends(z))

    weight_y = send(weight_ref, weights_ref.at[w], y_send, y_recv, y_device)
    weight_core = send(weight_ref, weights_ref.at[w], c_send.at[0], c_recv.at[0], core_device)
    weight_on = send(weights_ref.at[across], weights_ref.at[across], c_send.at[1], c_recv.at[1], core_device)
    weight_y.start()
    weight_core.start()

    def to_right(j, k, source, number):
        return send(source, kinds[k][1].at[number], right_send.at[j, k], right_recv.at[j, k], up)

    def to_left(j, k, source, number):
        return send(source, kinds[k][1].at[number], left_send.at[j, k], left_recv.at[j, k], down)

    def to_x(at, k, source, number):
        return send(source, kinds[k][1].at[number], x_send.at[at, k], x_recv.at[at, k], x_device)

    for k, (own, _) in enumerate(kinds):

        @pl.when(z < 3)
        def _(k=k, own=own):
            to_right(0, k, own, s).start()

        @pl.when(z > 0)
        def _(k=k, own=own):
            to_left(0, k, own, s).start()

        to_x(z, k, own, s).start()
    for j in (1, 2, 3):
        lower, upper = s - 2 * j, s + 2 * j
        for k, (_, out) in enumerate(kinds):

            @pl.when(z >= j)
            def _(j=j, k=k, out=out, lower=lower):
                block = out.at[lower]
                to_right(j - 1, k, block, lower).wait_recv()

                @pl.when(z < 3)
                def _():
                    to_right(j, k, block, lower).start()

                to_x(z - j, k, block, lower).start()

            @pl.when(z + j <= 3)
            def _(j=j, k=k, out=out, upper=upper):
                block = out.at[upper]
                to_left(j - 1, k, block, upper).wait_recv()

                @pl.when(z > 0)
                def _():
                    to_left(j, k, block, upper).start()

                to_x(z + j, k, block, upper).start()

    weight_y.wait_recv()
    weight_on.start()
    for k, (own, _) in enumerate(kinds):
        for number in range(4):
            done = to_x(number, k, own, s)
            done.wait_send()
            done.wait_recv()
        for j in range(3):

            @pl.when((z >= j) & (z < 3))
            def _(j=j, k=k, own=own):
                to_right(j, k, own, s).wait_send()

            @pl.when((z + j <= 3) & (z > 0))
            def _(j=j, k=k, own=own):
                to_left(j, k, own, s).wait_send()

    weight_core.wait_recv()
    weight_on.wait_recv()
    for copy in (weight_y, weight_core, weight_on):
        copy.wait_send()
    for copy in copies:
        copy.wait()


def gather_first(own, tail, weight):
    seqs, parts = lax.axis_size("seq"), lax.axis_size("wsh")
    if seqs != 8 or parts != 4:
        return (
            lax.all_gather(own, "seq", axis=0, tiled=False),
            lax.all_gather(tail, "seq", axis=0, tiled=False),
            lax.all_gather(weight, "wsh", axis=0, tiled=False),
        )
    dma = pltpu.SemaphoreType.DMA
    given = ((seqs, own), (seqs, tail), (parts, weight))
    return pl.pallas_call(
        gather_kernel,
        in_specs=[pl.BlockSpec(memory_space=pltpu.VMEM)] * 3,
        out_specs=[pl.BlockSpec(memory_space=pl.ANY)] * 3,
        out_shape=[jax.ShapeDtypeStruct((n,) + x.shape, x.dtype) for n, x in given],
        scratch_shapes=[dma((3,))] + [dma((3, 2))] * 4 + [dma((4, 2))] * 2 + [dma((2,))] * 2 + [dma] * 2,
        compiler_params=pltpu.CompilerParams(collective_id=1, has_side_effects=True),
        cost_estimate=pl.CostEstimate(flops=0, bytes_accessed=100 << 20, transcendentals=0),
        name="gather_first",
    )(own, tail, weight)


def turning(x_ref, out_ref, send_sem, recv_sem):
    s, w, side, z, _, _, _ = places()
    home = z == w
    greetings = tuple(((source != z) | (z != w), (source * 2 + side, z)) for source in range(4))

    def copy(j):
        piece = (z + j) % 4
        return send(x_ref.at[piece], out_ref.at[z], send_sem.at[j], recv_sem.at[j], (w * 2 + side, piece))

    def start():
        for j in (3, 2, 1):
            copy(j).start()

        @pl.when(jnp.logical_not(home))
        def _():
            copy(0).start()

        @pl.when(home)
        def _():
            out_ref[z] = x_ref[z]

    def end():
        for j in range(1, 4):
            copy(j).wait_recv()
            copy(j).wait_send()

        @pl.when(jnp.logical_not(home))
        def _():
            copy(0).wait_recv()
            copy(0).wait_send()

    return greetings, jnp.where(home, 3, 4), start, end


def reduce_kernel(
    splits, x_ref, turn_ref, out_ref, turn_out, x_buf, right_buf, left_buf, right_out, left_out,
    x_send, x_recv, right_send, right_recv, left_send, left_recv, turn_send, turn_recv,
):
    s, w, side, z, x_device, _, _ = places()
    up, down = (s + 2, w), (s - 2, w)
    size = x_ref.shape[2] // splits
    columns = [slice(c * size, (c + 1) * size) for c in range(splits)]
    greetings, number, start_turn, end_turn = turning(turn_ref, turn_out, turn_send, turn_recv)
    greet(((None, x_device), (z < 3, up), (z > 0, down)) + greetings, 1 + line_ends(z) + number)

    def to_x(target, c):
        return send(
            x_ref.at[target * 2 + 1 - side, :, columns[c]], x_buf.at[target, :, columns[c]],
            x_send.at[target, c], x_recv.at[target, c], x_device,
        )

    def start_x(target):
        for c in range(splits):
            to_x(target, c).start()

    def to_right(k, c):
        return send(
            right_out.at[k - 1, :, columns[c]], right_buf.at[k - 1, :, columns[c]],
            right_send.at[k - 1, c], right_recv.at[k - 1, c], up,
        )

    def to_left(k, c):
        return send(
            left_out.at[k - 1, :, columns[c]], left_buf.at[k - 1, :, columns[c]],
            left_send.at[k - 1, c], left_recv.at[k - 1, c], down,
        )

    def pair(target, c):
        to_x(target, c).wait_recv()
        return x_ref[target * 2 + side, :, columns[c]].astype(F32) + x_buf[target, :, columns[c]].astype(F32)

    for k in (3, 2, 1):

        @pl.when(z + k <= 3)
        def _(k=k):
            start_x(z + k)

        @pl.when(z >= k)
        def _(k=k):
            start_x(z - k)

    start_x(z)
    start_turn()
    for k in (3, 2, 1):
        for c in range(splits):

            @pl.when(z + k <= 3)
            def _(k=k, c=c):
                right_out[k - 1, :, columns[c]] = pair(z + k, c).astype(BF16)
                if k < 3:

                    @pl.when(z > 0)
                    def _():
                        to_right(k + 1, c).wait_recv()
                        right_out[k - 1, :, columns[c]] = (
                            right_out[k - 1, :, columns[c]].astype(F32) + right_buf[k, :, columns[c]].astype(F32)
                        ).astype(BF16)

                to_right(k, c).start()

            @pl.when(z >= k)
            def _(k=k, c=c):
                left_out[k - 1, :, columns[c]] = pair(z - k, c).astype(BF16)
                if k < 3:

                    @pl.when(z < 3)
                    def _():
                        to_left(k + 1, c).wait_recv()
                        left_out[k - 1, :, columns[c]] = (
                            left_out[k - 1, :, columns[c]].astype(F32) + left_buf[k, :, columns[c]].astype(F32)
                        ).astype(BF16)

                to_left(k, c).start()

    for c in range(splits):
        out_ref[:, columns[c]] = pair(z, c)

        @pl.when(z > 0)
        def _(c=c):
            to_right(1, c).wait_recv()
            out_ref[:, columns[c]] += right_buf[0, :, columns[c]].astype(F32)

        @pl.when(z < 3)
        def _(c=c):
            to_left(1, c).wait_recv()
            out_ref[:, columns[c]] += left_buf[0, :, columns[c]].astype(F32)

    for c in range(splits):
        for target in range(4):
            to_x(target, c).wait_send()
        for k in (3, 2, 1):

            @pl.when(z + k <= 3)
            def _(k=k, c=c):
                to_right(k, c).wait_send()

            @pl.when(z >= k)
            def _(k=k, c=c):
                to_left(k, c).wait_send()

    end_turn()


def reduce_seq(x, turned):
    seqs, rows, width = x.shape
    splits = 2
    vmem = pl.BlockSpec(memory_space=pltpu.VMEM)
    dma = pltpu.SemaphoreType.DMA
    return pl.pallas_call(
        functools.partial(reduce_kernel, splits),
        in_specs=[vmem] * 2,
        out_specs=[vmem] * 2,
        out_shape=[jax.ShapeDtypeStruct((rows, width), F32), jax.ShapeDtypeStruct(turned.shape, turned.dtype)],
        scratch_shapes=[pltpu.VMEM((4, rows, width), BF16)]
        + [pltpu.VMEM((3, rows, width), BF16)] * 4
        + [dma((4, splits))] * 2 + [dma((3, splits))] * 4 + [dma((4,))] * 2,
        compiler_params=pltpu.CompilerParams(collective_id=2, has_side_effects=True, vmem_limit_bytes=40 << 20),
        cost_estimate=pl.CostEstimate(flops=0, bytes_accessed=1 << 20, transcendentals=0),
        name="reduce_seq",
    )(x, turned)


def finish_kernel(wide_ref, key_ref, wide_out, key_out, wide_send, wide_recv, key_send, key_recv):
    s, w, _, _, _, _, _ = places()
    greetings, number, start_turn, end_turn = turning(key_ref, key_out, key_send, key_recv)
    greet(tuple((None, ((s + d) % 8, w)) for d in range(1, 8)) + greetings, 7 + number)

    def wide(d):
        target = (s + d) % 8
        return send(wide_ref.at[target], wide_out.at[s], wide_send.at[d - 1], wide_recv.at[d - 1], (target, w))

    for d in (4, 3, 5, 2, 6, 1, 7):
        wide(d).start()
    start_turn()
    wide_out[s] = wide_ref[s]
    for d in range(1, 8):
        wide(d).wait_recv()
        wide(d).wait_send()
    end_turn()


def finish(wide, key):
    vmem = pl.BlockSpec(memory_space=pltpu.VMEM)
    dma = pltpu.SemaphoreType.DMA
    return pl.pallas_call(
        finish_kernel,
        in_specs=[vmem] * 2,
        out_specs=[vmem] * 2,
        out_shape=[jax.ShapeDtypeStruct(x.shape, x.dtype) for x in (wide, key)],
        scratch_shapes=[dma((7,)), dma((7,)), dma((4,)), dma((4,))],
        compiler_params=pltpu.CompilerParams(collective_id=5, has_side_effects=True, vmem_limit_bytes=24 << 20),
        cost_estimate=pl.CostEstimate(flops=0, bytes_accessed=100 << 20, transcendentals=0),
        name="finish",
    )(wide, key)


def channel_kernel(
    forward, x_ref, first_hbm, second_hbm, active_hbm,
    sum_ref, all_hbm, mine_hbm, other_hbm, extra_hbm,
    first, second, rows_all, middle, active, part, core_buf, far_out, far_buf,
    load_sem, store_sem, core_send, core_recv, y_send, y_recv, x_send, x_recv, r_send, r_recv, f_send, f_recv,
):
    s, w, side, z, x_device, core_device, y_device = places()
    rows, width = x_ref.shape
    units = first.shape[0]
    half = units // 2
    loads = [
        pltpu.make_async_copy(first_hbm, first, load_sem.at[0]),
        pltpu.make_async_copy(second_hbm, second, load_sem.at[1]),
    ]
    if not forward:
        loads.append(pltpu.make_async_copy(active_hbm, active, load_sem.at[2]))
    for load in loads:
        load.start()
    rows_all[0:rows] = x_ref[...]
    greet(((None, x_device), (None, core_device), (None, y_device)), 3)

    def block(number):
        return rows_all.at[pl.ds(number * rows, rows)]

    to_core = [
        send(block(0), block(1), core_send.at[0], core_recv.at[0], core_device),
        send(block(2), block(3), core_send.at[1], core_recv.at[1], core_device),
    ]
    to_y = send(block(0), block(2), y_send, y_recv, y_device)
    if forward:
        to_x = [
            send(
                middle.at[1 - side, pl.ds(2 * n * rows, 2 * rows)], other_hbm.at[pl.ds(2 * n * rows, 2 * rows)],
                x_send.at[n], x_recv.at[n], x_device,
            )
            for n in range(2)
        ]
    else:
        to_x = [
            send(block(n), other_hbm.at[pl.ds(n * rows, rows)], x_send.at[n], x_recv.at[n], x_device) for n in range(4)
        ]
    sums_core = [
        send(part.at[pl.ds((2 * n + 1) * rows, rows)], core_buf.at[n], r_send.at[n], r_recv.at[n], core_device)
        for n in range(2)
    ]
    far = send(far_out, far_buf, f_send, f_recv, y_device)
    stores = [
        pltpu.make_async_copy(rows_all, all_hbm, store_sem.at[0]),
        pltpu.make_async_copy(middle.at[side], mine_hbm, store_sem.at[1]),
        pltpu.make_async_copy(active if forward else middle.at[1 - side], extra_hbm, store_sem.at[2]),
    ]

    def pass_on(number):
        if not forward:
            to_x[number].start()

    to_y.start()
    to_core[0].start()
    pass_on(0)
    tile = min(512, half)

    def multiply(number):
        two = pl.ds(2 * number * rows, 2 * rows)

        def up(t, carry):
            for side_units in range(2):
                at = pl.multiple_of(t * tile, tile)
                unit = pl.multiple_of(side_units * half + at, tile)
                raw = dot(rows_all[two, :], first[pl.ds(unit, tile), :], NT)
                if forward:
                    raw = jnp.maximum(raw, 0.0)
                    active[two, pl.ds(unit, tile)] = raw
                    mid = raw * raw
                else:
                    mid = raw * 2.0 * active[two, pl.ds(unit, tile)]
                middle[side_units, two, pl.ds(at, tile)] = mid.astype(BF16)
            return carry

        lax.fori_loop(0, half // tile, up, 0)
        if forward:
            to_x[number].start()
        if number == 0:
            loads[1].wait()

        def down(t, carry):
            at = pl.multiple_of(t * tile, tile)
            part[two, pl.ds(at, tile)] = dot(middle[0, two, :], second[0:half, pl.ds(at, tile)]) + dot(
                middle[1, two, :], second[half:units, pl.ds(at, tile)]
            )
            return carry

        lax.fori_loop(0, width // tile, down, 0)
        sums_core[number].start()

    loads[0].wait()
    if not forward:
        loads[2].wait()
    to_core[0].wait_recv()
    pass_on(1)
    multiply(0)
    to_y.wait_recv()
    to_core[1].start()
    pass_on(2)
    to_core[1].wait_recv()
    pass_on(3)
    stores[0].start()
    multiply(1)
    for store in stores[1:]:
        store.start()
    sums_core[1].wait_recv()
    far_out[...] = (part[2 * rows : 3 * rows] + core_buf[1]).astype(BF16)
    far.start()
    sums_core[0].wait_recv()
    sum_ref[...] = part[0:rows] + core_buf[0]
    far.wait_recv()
    sum_ref[...] += far_buf[...].astype(F32)
    for copy in to_x:
        copy.wait_recv()
    for copy in to_x + to_core + sums_core + [to_y, far]:
        copy.wait_send()
    for store in stores:
        store.wait()


def channel_stage(x, first, second, active):
    rows, width = x.shape
    units = first.shape[0]
    forward = active is None
    given = (x, first, second) if forward else (x, first, second, active)
    everything = pl.BlockSpec(memory_space=pl.ANY)
    shapes = [
        ((rows, width), F32), ((4 * rows, width), BF16), ((4 * rows, units // 2), BF16),
        ((4 * rows, units // 2 if forward else width), BF16),
        ((4 * rows, units), F32) if forward else ((4 * rows, units // 2), BF16),
    ]

    def body(*refs):
        refs = list(refs)
        if forward:
            refs.insert(3, None)
        channel_kernel(forward, *refs)

    dma = pltpu.SemaphoreType.DMA
    return pl.pallas_call(
        body,
        in_specs=[pl.BlockSpec(memory_space=pltpu.VMEM)] + [everything] * (len(given) - 1),
        out_specs=[pl.BlockSpec(memory_space=pltpu.VMEM)] + [everything] * (len(shapes) - 1),
        out_shape=[jax.ShapeDtypeStruct(s, d) for s, d in shapes],
        scratch_shapes=[
            pltpu.VMEM((units, width), BF16), pltpu.VMEM((units, width), BF16), pltpu.VMEM((4 * rows, width), BF16),
            pltpu.VMEM((2, 4 * rows, units // 2), BF16), pltpu.VMEM((4 * rows, units), F32),
            pltpu.VMEM((4 * rows, width), F32), pltpu.VMEM((2, rows, width), F32),
            pltpu.VMEM((rows, width), BF16), pltpu.VMEM((rows, width), BF16),
            dma((3,)), dma((3,)), dma((2,)), dma((2,)), dma, dma, dma((4,)), dma((4,)), dma((2,)), dma((2,)),
            dma, dma,
        ],
        compiler_params=pltpu.CompilerParams(
            collective_id=3 if forward else 4, has_side_effects=True, vmem_limit_bytes=60 << 20
        ),
        cost_estimate=pl.CostEstimate(flops=0, bytes_accessed=100 << 20, transcendentals=0),
        name="channel_forward" if forward else "channel_backward",
    )(*given)


def from_behind(x, axis, by):
    size = lax.axis_size(axis)
    pairs = [(i, i + by) for i in range(size) if 0 <= i + by < size]
    return lax.ppermute(x, axis, pairs)


def exchange(x, axis):
    return lax.all_to_all(x, axis, split_axis=0, concat_axis=0, tiled=True)


def swap(x, by):
    size = lax.axis_size("wsh")
    return lax.ppermute(x, "wsh", [(i, i ^ by) for i in range(size)])


def gather_near(x):
    if lax.axis_size("wsh") != 4:
        return lax.all_gather(x, "wsh", axis=0, tiled=True)
    return gathered_near(x, swap(x, 1), swap(x, 2))


def gathered_near(x, beside, across):
    return jnp.concatenate([x, beside, across, swap(across, 1)], 0)


def beside(x):
    return lax.ppermute(x, "seq", [(i, i ^ 1) for i in range(lax.axis_size("seq"))])


def quartered(x):
    rows, columns = x.shape
    return x.reshape(rows, 4, 4, columns // 16).transpose(0, 2, 1, 3).reshape(rows, columns)


def scalar_sum(x):
    if lax.axis_size("wsh") != 4:
        return jnp.sum(lax.all_gather(x.reshape(1), "wsh", axis=0, tiled=True))
    x = jnp.full((8, 128), x)
    x = x + swap(x, 1)
    return (x + swap(x, 2))[0, 0]


def near_sum(x):
    if lax.axis_size("wsh") != 4:
        return lax.psum_scatter(x, "wsh", scatter_dimension=0, tiled=True)
    rows = x.shape[0] // 4
    beside = swap(jnp.concatenate([x[rows : 2 * rows], x[3 * rows :]], 0), 1)
    far = x[2 * rows : 3 * rows] + beside[rows:]
    return x[:rows] + beside[:rows] + swap(far.astype(BF16), 2).astype(F32)


def block_sum(x):
    if lax.axis_size("wsh") != 4:
        return lax.psum_scatter(x, "wsh", scatter_dimension=0, tiled=False).astype(F32)
    kept, far = block_halves(x)
    return kept + swap(far, 2).astype(F32)


def block_halves(x):
    number = lax.axis_index("wsh")

    def block(by):
        return lax.dynamic_index_in_dim(x, number ^ by, 0, keepdims=False)

    beside = swap(jnp.stack([block(1), block(3)]), 1).astype(F32)
    return block(0).astype(F32) + beside[0], (block(2).astype(F32) + beside[1]).astype(BF16)


def local(
    tokens, first_layer_values, teacher, valid, destination, lengths,
    receptance_matrix, key_matrix, value_matrix, output_matrix,
    lowrank_down_weight, lowrank_up_weight, channel_key_weight, channel_value_weight, vectors,
):
    rows, width = tokens.shape
    seqs, parts = lax.axis_size("seq"), lax.axis_size("wsh")
    me = lax.axis_index("seq")
    group = rows * seqs
    own_width = width // seqs
    shard = width // parts
    piece = shard // seqs
    column = me * own_width

    def own_columns(matrix):
        return lax.dynamic_slice_in_dim(matrix, column, own_width, 1)

    near = parts == 4
    up_piece = lax.dynamic_slice_in_dim(lowrank_up_weight, column % shard, own_width, 0)
    total = 3 * own_width + WIDE
    own_weights = jnp.concatenate(
        [
            own_columns(receptance_matrix), own_columns(key_matrix), own_columns(value_matrix),
            pad_ranks(lowrank_down_weight), up_piece.reshape(shard, -1),
        ],
        1,
    )

    dest_seq = destination // rows // parts
    position = dest_seq * rows + destination % rows
    digits = jnp.stack([position // DIGIT, position % DIGIT, valid], 1).astype(BF16)
    tail = jnp.pad(digits, ((0, 0), (0, EXTRA - 3)))
    given, tails, weights = gather_first(tokens, tail, own_weights)
    given, tails, weights = given.reshape(group, width), tails.reshape(group, EXTRA), weights.reshape(width, -1)
    info = tails[:, :3].astype(F32)
    places = (info[:, 0] * DIGIT + info[:, 1]).astype(jnp.int32)
    numbers = jnp.arange(group, dtype=jnp.int32)
    permute = (numbers[:, None] == places[None, :]).astype(BF16)
    total_valid = scalar_sum(jnp.sum(info[:, 2]))

    index = jnp.arange(rows, dtype=jnp.int32)
    same_dest = (dest_seq[:, None] == dest_seq[None, :]) & (index[None, :] < index[:, None])
    slot = dest_seq * (rows // seqs) + jnp.sum(same_dest.astype(jnp.int32), 1)
    arrange = (index[:, None] == slot[None, :]).astype(BF16)
    mine = (places // rows) == me
    arrival = jnp.cumsum(mine.astype(jnp.int32)) - 1
    own_rows = ((index[:, None] + me * rows) == places[None, :]).astype(BF16)
    settle = dot(own_rows, (mine[:, None] & (arrival[:, None] == index[None, :])).astype(BF16)).astype(BF16)

    offsets = jnp.cumsum(lengths[0]) - lengths[0]
    starts = jnp.any(numbers[:, None] == offsets[None, :], 1).astype(F32)
    segment_ids = jnp.cumsum(starts).reshape(-1, BLOCK)
    before = segment_ids[:, :1] - starts.reshape(-1, BLOCK)[:, :1]
    segments = jnp.stack(
        [segment_ids, jnp.broadcast_to(before, segment_ids.shape), jnp.broadcast_to(segment_ids[:, -1:], segment_ids.shape)]
        + [jnp.zeros_like(segment_ids)] * 5,
        1,
    ).reshape(-1, BLOCK)
    flowing = (1.0 - starts)[:, None]

    up = pad_ranks(
        lax.dynamic_slice(
            weights, (column // shard * shard, total), (shard, weights.shape[1] - total)
        ).reshape(own_width, -1)
    ).T
    vec = lax.dynamic_slice_in_dim(vectors, column, own_width, 0)[:, 8:16].T

    output_late, given = lax.optimization_barrier((output_matrix, given))
    w_out = lax.all_gather(output_late, "wsh", axis=0, tiled=True)
    balanced = dot(permute, given).astype(BF16)
    wide_rows = balanced.astype(F32)
    mean = jnp.mean(wide_rows, -1, keepdims=True)
    scale_one = lax.rsqrt(jnp.mean(jnp.square(wide_rows - mean), -1, keepdims=True) + 1e-05)
    stats = jnp.concatenate([mean, scale_one, flowing, flowing], 1)
    mix_vec = vectors[:, :8].T
    first_values, stats = lax.optimization_barrier((first_layer_values, stats))
    first_given = exchange(
        first_values.reshape(rows, seqs, own_width).transpose(1, 0, 2), "seq"
    ).reshape(group, own_width)
    recept, keys, values, downs, hidden = run_project(balanced, stats, mix_vec, weights, own_width, parts)
    teacher_late, recept, first_given = lax.optimization_barrier((teacher, recept, first_given))
    first = dot(permute, first_given).astype(BF16)
    teacher_rows = exchange(dot(arrange, teacher_late).astype(BF16).reshape(seqs, rows // seqs, width), "seq")
    inputs = (recept, keys, values, hidden, first, up, vec, segments)
    mixed_out, *saved = run_forward(*inputs)
    teacher_rows, mixed_out, total_valid = lax.optimization_barrier((teacher_rows, mixed_out, total_valid))
    target = dot(settle, teacher_rows.reshape(rows, width))

    mixed_rows = exchange(mixed_out.reshape(seqs, rows, own_width), "seq").transpose(1, 0, 2).reshape(rows, width)
    own = lax.dynamic_slice_in_dim(balanced, me * rows, rows, 0).astype(F32)
    own_starts = lax.dynamic_slice_in_dim(starts, me * rows, rows, 0)
    own_flowing = (1.0 - own_starts)[:, None]
    own_valid = dot(own_rows, tails)[:, 2]
    residual = own + dot(mixed_rows, w_out)
    standard_two, scale_two = norm_stats(residual)
    normed_two = standard_two * vectors[:, 16] + vectors[:, 17]
    carried_two = from_behind(normed_two[-1:], "seq", 1)
    delta_two = jnp.concatenate([carried_two, normed_two[:-1]], 0) * own_flowing - normed_two
    channel_in = (normed_two + delta_two * vectors[:, 18]).astype(BF16)
    paired = near and seqs == 8
    if paired:
        summed, channel, hidden_mine, hidden_other, active = channel_stage(
            channel_in, channel_key_weight, channel_value_weight, None
        )
    else:
        channel = gather_near(channel_in)
        active = jax.nn.relu(dot(channel, channel_key_weight, NT))
        hidden_rows = jnp.square(active).astype(BF16)
        summed = near_sum(dot(hidden_rows, channel_value_weight))
    result = residual + summed
    total_tokens = group * parts
    cotangent = (result - target) * (own_valid * (total_tokens / total_valid))[:, None]
    cot_low = cotangent.astype(BF16)

    result_back = exchange(dot(settle, result.astype(BF16), TN).astype(BF16).reshape(seqs, rows // seqs, width), "seq")
    if paired:
        grad_channel, cot, pre_mine, cot_other, pre_spare = channel_stage(
            cot_low, channel_value_weight, channel_key_weight, active
        )
        channel_other, pre_other = beside(channel), beside(pre_spare)
    else:
        cot = gather_near(cot_low)
        grad_pre = (dot(cot, channel_value_weight, NT) * 2.0 * active).astype(BF16)
        grad_channel = near_sum(dot(grad_pre, channel_key_weight))
    result_back, grad_channel = lax.optimization_barrier((result_back, grad_channel))
    output = dot(arrange, result_back.reshape(rows, width), TN).astype(BF16)
    grad_vec_mix_two = jnp.sum(grad_channel * delta_two, 0)
    shifted = grad_channel * vectors[:, 18] * own_flowing
    behind = from_behind(shifted[:1], "seq", -1)
    grad_normed_two = grad_channel * (1.0 - vectors[:, 18]) + jnp.concatenate([shifted[1:], behind], 0)
    grad_residual = cotangent + norm_back(grad_normed_two, standard_two, scale_two, vectors[:, 16])
    grad_low = grad_residual.astype(BF16)

    grad_posted = dot(grad_low, w_out, NT).astype(BF16)
    if paired:
        hidden_mine, grad_posted = lax.optimization_barrier((hidden_mine, grad_posted))
        value_part = (
            dot(quartered(hidden_mine), cot, TN) + dot(quartered(hidden_other), cot_other, TN)
        ).astype(BF16)
    else:
        value_part = dot(hidden_rows, cot, TN).astype(BF16)
    grad_heads = exchange(grad_posted.reshape(rows, seqs, own_width).transpose(1, 0, 2), "seq").reshape(group, own_width)
    grad_heads, value_part, mixed_late = lax.optimization_barrier((grad_heads, value_part, mixed_rows))
    lefts = exchange(mixed_late.reshape(rows, seqs, parts, piece).transpose(2, 0, 1, 3), "wsh")
    near_grad = (swap(grad_low, 1), swap(grad_low, 2)) if near else gather_near(grad_low)
    recept_low, keys_low, values_low, ups_low, grad_first, grad_vec_heads = run_backward(grad_heads, *inputs, saved)
    if paired:
        channel_other, pre_other, lefts, near_grad, recept_low = lax.optimization_barrier(
            (channel_other, pre_other, lefts, near_grad, recept_low)
        )
        key_part = (
            dot(quartered(pre_mine), channel, TN) + dot(quartered(pre_other), channel_other, TN)
        ).astype(BF16)
    else:
        lefts, near_grad, recept_low = lax.optimization_barrier((lefts, near_grad, recept_low))
        key_part = dot(grad_pre, channel, TN).astype(BF16)
    if near:
        near_grad = gathered_near(grad_low, *near_grad)
        lefts = jnp.stack([lax.dynamic_index_in_dim(lefts, lax.axis_index("wsh") ^ k, 0, keepdims=False) for k in range(4)])
    out_part = dot(lefts.reshape(rows * parts, -1), near_grad, TN).astype(BF16)

    moved = exchange(dot(permute, grad_first, TN).astype(BF16).reshape(seqs, rows, own_width), "seq")
    recept_low, key_part, out_part = lax.optimization_barrier((recept_low, key_part, out_part))
    if paired:
        lines = [[0, 2, 4, 6], [1, 3, 5, 7]]
        def along(part):
            return lax.psum_scatter(part, "seq", scatter_dimension=0, tiled=True, axis_index_groups=lines)

        halves_out = out_part.reshape(seqs // 2, 2, piece, width)
        x_side = me % 2
        out_mine = lax.dynamic_index_in_dim(halves_out, x_side, 1, keepdims=False).astype(F32)
        out_other = beside(lax.dynamic_index_in_dim(halves_out, 1 - x_side, 1, keepdims=False))
        value_sum, key_sum = along(value_part), along(key_part)
    else:
        moves = [(s * parts + w, w * seqs + s) for s in range(seqs) for w in range(parts)]

        def ffn_grad(part):
            part = lax.psum_scatter(part, "seq", scatter_dimension=0, tiled=True)
            return lax.ppermute(part, ("seq", "wsh"), moves).astype(F32)

        grad_ffn_value, grad_ffn_key = ffn_grad(value_part), ffn_grad(key_part)
        grad_out = lax.psum_scatter(out_part, "seq", scatter_dimension=0, tiled=True)

    heads_part = lax.dynamic_update_slice_in_dim(jnp.zeros((width, 8), F32), grad_vec_heads.T, column, 0)
    vec_two = jnp.stack(
        [jnp.sum(grad_normed_two * standard_two, 0), jnp.sum(grad_normed_two, 0), grad_vec_mix_two], 1
    )
    others = jnp.concatenate([heads_part, jnp.pad(vec_two, ((0, 0), (0, 13)))], 1)
    scaled_grad, sums, wide, up_grad = run_unproject(
        balanced, stats, mix_vec, weights, others, (recept_low, keys_low, values_low), ups_low, hidden, downs, up, parts
    )
    if paired:
        moved, value_sum, out_other, scaled_grad, sums, wide, up_grad = lax.optimization_barrier(
            (moved, value_sum, out_other, scaled_grad, sums, wide, up_grad)
        )
        out_half = (out_mine + out_other.astype(F32)).astype(BF16).reshape(-1, width)
        out_half, sums = lax.optimization_barrier((out_half, sums))
        grad_out = along(out_half)
    else:
        moved, scaled_grad, sums, wide = lax.optimization_barrier((moved, scaled_grad, sums, wide))
    grad_first_rows = moved.transpose(1, 0, 2).reshape(rows, width)

    standard = (balanced.astype(F32) - mean) * scale_one
    grad_balanced = scale_one * (scaled_grad - sums[:, :1] * (1.0 / width) - standard * (sums[:, 1:] * (1.0 / width)))
    mine_rows = lax.dynamic_slice_in_dim(grad_balanced, me * rows, rows, 0) + grad_residual
    grad_balanced = lax.dynamic_update_slice_in_dim(grad_balanced, mine_rows, me * rows, 0)
    grad_given = dot(permute, grad_balanced.astype(BF16), TN).astype(BF16).reshape(seqs, rows, width)
    if near:
        kept_part, far = block_halves(wide)
        grad_given, far = lax.optimization_barrier((grad_given, far))
        wide_part = kept_part + swap(far, 2).astype(F32)
    else:
        wide_part = block_sum(wide)
    if paired:
        grad_tokens, value_all = reduce_seq(grad_given, value_sum.reshape(4, -1, width))
        wide_part, grad_tokens, grad_out, key_sum = lax.optimization_barrier((wide_part, grad_tokens, grad_out, key_sum))
        wide_all, key_all = finish(wide_part.astype(BF16), key_sum.reshape(4, -1, width))
        wide_all = wide_all.astype(F32)
        grad_ffn_key, grad_ffn_value = [x.reshape(-1, width).astype(F32) for x in (key_all, value_all)]
    else:
        grad_tokens = jnp.sum(exchange(grad_given, "seq").astype(F32), 0)
        wide_all = exchange(wide_part.astype(BF16), "seq").astype(F32)

    def square(at):
        taken = wide_all[:, :, at * own_width : (at + 1) * own_width]
        return taken.transpose(1, 0, 2).reshape(piece, width)

    narrow = jnp.sum(wide_all[:, :, 3 * own_width :], 0)
    grad_down = unpad_ranks(narrow)
    grad_vectors = narrow[:, RANKS[0] : RANKS[0] + vectors.shape[1]]
    up_part = unpad_ranks(block_sum(up_grad.reshape(parts, piece, WIDE)))

    return (
        output, grad_tokens.astype(BF16), grad_first_rows,
        square(0), square(1), square(2),
        grad_out.astype(F32), grad_down, up_part,
        grad_ffn_key, grad_ffn_value, grad_vectors,
    )


def solution(mesh):
    both, shard = P(("seq", "wsh"), None), P("wsh", None)
    flat = P(("seq", "wsh"))
    return jax.shard_map(
        local,
        mesh=mesh,
        in_specs=(both, both, both, flat, flat) + (shard,) * 9 + (P(),),
        out_specs=(both,) * 12,
        check_vma=False,
    )
```

```python
import functools

import jax
import jax.numpy as jnp
from jax import lax
from jax.experimental import pallas as pl
from jax.experimental.pallas import tpu as pltpu
from jax.sharding import PartitionSpec as P

HEAD = 64
BLOCK = 64
RANKS = (96, 96, 64, 256)
PADDED = (128, 128, 128, 256)
OFFSETS = (0, 128, 256, 384)
WIDE = 640
EXTRA = 128
DIGIT = 64

F32 = jnp.float32
BF16 = jnp.bfloat16

NN = (((1,), (0,)), ((), ()))
NT = (((1,), (1,)), ((), ()))
TN = (((0,), (0,)), ((), ()))


def dot(a, b, dims=NN):
    return lax.dot_general(a, b, dims, preferred_element_type=F32)


def halves(x):
    high = x.astype(BF16)
    return high, (x - high.astype(F32)).astype(BF16)


def dot3(a, b, dims=NN):
    a_high, a_low = halves(a)
    b_high, b_low = halves(b)
    return dot(a_high, b_high, dims) + (dot(a_high, b_low, dims) + dot(a_low, b_high, dims))


def sum_left(mask, x):
    high, low = halves(x)
    low_two = (x - high.astype(F32) - low.astype(F32)).astype(BF16)
    return dot(mask, high) + (dot(mask, low) + dot(mask, low_two))


def head_sum(x, ones):
    high, low = halves(x)
    return dot(high, ones) + dot(low, ones)


def low(x):
    return x.astype(BF16).astype(F32)


def iotas(rows, columns):
    return (
        lax.broadcasted_iota(jnp.int32, (rows, columns), 0),
        lax.broadcasted_iota(jnp.int32, (rows, columns), 1),
    )


def head_ones(width):
    i, j = iotas(width, width)
    return jnp.where((i >> 6) == (j >> 6), 1.0, 0.0).astype(BF16)


def front(keys, values, hidden, up, first, vec, ones):
    z = vec[0:1] + dot(hidden[:, 0:128], up[0:128])
    decay_log = -(jnp.maximum(-z, 0.0) + jnp.log1p(jnp.exp(-jnp.abs(z)))) - 0.5
    rate = jax.nn.sigmoid(vec[1:2] + dot(hidden[:, 128:256], up[128:256]))
    blend = jax.nn.sigmoid(vec[2:3] + dot(hidden[:, 256:384], up[256:384]))
    gate = dot(hidden[:, 384:640], up[384:640])
    mixed_value = values + (first - values) * blend
    scaled = keys * vec[3:4]
    scale = lax.rsqrt(head_sum(scaled * scaled, ones) + 1e-06)
    key_dir = scaled * scale
    key_mod = keys * (1.0 + (rate - 1.0) * vec[4:5])
    return z, decay_log, rate, blend, gate, mixed_value, scale, key_dir, key_mod


def block_masks(segments):
    i, j = iotas(BLOCK, BLOCK)
    across = jnp.broadcast_to(segments[0:1], (BLOCK, BLOCK))
    down = across.T
    before = jnp.broadcast_to(segments[1:2], (BLOCK, BLOCK))
    last = jnp.broadcast_to(segments[2:3], (BLOCK, BLOCK))
    same = across == down
    strict = jnp.where(same & (i > j), 1.0, 0.0)
    closed = jnp.where(same & (i >= j), 1.0, 0.0)
    carry = jnp.where(down == before, 1.0, 0.0)
    tail = jnp.where(down == last, 1.0, 0.0)
    keep = jnp.where(segments[2:3] == segments[1:2], 1.0, 0.0)
    quad = jnp.concatenate(
        [jnp.concatenate([strict, strict], 1), jnp.concatenate([closed, closed], 1)], 0
    )
    return quad, carry, tail, keep


def tile_heads(x, heads):
    return jnp.concatenate([x] * heads, 1) if heads > 1 else x


def join(pieces, axis):
    return jnp.concatenate(pieces, axis) if len(pieces) > 1 else pieces[0]


def decayed(decay_low, key_low, dir_low, rate_low, recept_low, carry, tail):
    i, j = iotas(BLOCK, BLOCK)
    lower = jnp.where(i >= j, 1.0, 0.0).astype(BF16)
    log_step = -jnp.exp(decay_low)
    total = sum_left(lower, log_step)
    before = jnp.exp(total - log_step)
    grown = jnp.exp(total)
    shrunk = jnp.exp(-total)
    end = total[BLOCK - 1 : BLOCK]
    tail_decay = jnp.exp(end - total) * tail
    alpha = -dir_low * before
    beta_plain = dir_low * rate_low
    beta = beta_plain * shrunk
    key = key_low * shrunk
    recept = recept_low * grown
    return dict(
        log_step=log_step, before=before, grown=grown, shrunk=shrunk, end=jnp.exp(end), tail=tail_decay,
        alpha=alpha, beta_plain=beta_plain, beta=beta, key=key, recept=recept,
        beta_end=beta_plain * tail_decay, key_end=key_low * tail_decay,
        alpha_in=alpha * carry, recept_in=recept * carry,
    )


def unit_inverses(lowers):
    i, j = iotas(BLOCK, BLOCK)
    eye = jnp.where(i == j, 1.0, 0.0)

    def within(size):
        return (i // size) == (j // size)

    smalls = [jnp.where(within(4), x, 0.0) for x in lowers]
    low_smalls = [x.astype(BF16) for x in smalls]
    twos = [dot(x, x) for x in low_smalls]
    inverses = [eye + x for x in smalls]
    inverses = [x + dot(x.astype(BF16), y.astype(BF16)) for x, y in zip(inverses, twos)]
    for size in (8, 16, 32, 64):
        mask = within(size) & ~within(size // 2)
        offs = [jnp.where(mask, x, 0.0).astype(BF16) for x in lowers]
        lows = [x.astype(BF16) for x in inverses]
        inner = [dot(x, y).astype(BF16) for x, y in zip(offs, lows)]
        inverses = [x + dot(y, z) for x, y, z in zip(inverses, lows, inner)]
    errors = [eye - x + dot3(y, x) for x, y in zip(inverses, lowers)]
    return [x + dot(x.astype(BF16), y.astype(BF16)) for x, y in zip(inverses, errors)]


def post_norm(head_low, ones):
    centered = head_low - head_sum(head_low, ones) * (1.0 / HEAD)
    spread = lax.rsqrt(head_sum(centered * centered, ones) * (1.0 / HEAD) + HEAD * 1e-05)
    return centered * spread, spread


def forward_kernel(
    count, recept_ref, keys_ref, values_ref, hidden_ref, first_ref, up_ref, vec_ref, segment_ref,
    mixed_ref, head_ref, state_ref, inverse_ref, removed_ref, state,
):
    width = recept_ref.shape[1]
    heads = width // HEAD

    @pl.when(pl.program_id(0) == 0)
    def _():
        state[...] = jnp.zeros_like(state)

    ones = head_ones(width)
    vec = vec_ref[...]
    up = up_ref[...]
    columns = [slice(head * HEAD, (head + 1) * HEAD) for head in range(heads)]
    done = []
    for block in range(count):
        rows = slice(block * BLOCK, (block + 1) * BLOCK)
        recept, keys, values = recept_ref[rows], keys_ref[rows], values_ref[rows]
        _, decay_log, rate, _, gate, mixed_value, _, key_dir, key_mod = front(
            keys, values, hidden_ref[rows], up, first_ref[rows].astype(F32), vec, ones
        )
        quad, carry, tail, keep = block_masks(segment_ref[block * 8 : block * 8 + 8])
        parts = decayed(
            low(decay_log), low(key_mod), low(key_dir), low(rate), low(recept),
            tile_heads(carry, heads), tile_heads(tail, heads),
        )
        lefts = [jnp.concatenate([parts["alpha"][:, c], parts["recept"][:, c]], 0) for c in columns]
        rights = [jnp.concatenate([parts["beta"][:, c], parts["key"][:, c]], 0) for c in columns]
        pairs = [quad * dot3(x, y, NT) for x, y in zip(lefts, rights)]
        done.append((rows, recept, key_mod, gate, mixed_value, keep, parts, pairs))
    inverses = unit_inverses([x[:BLOCK, :BLOCK] for item in done for x in item[-1]])
    for block, (rows, recept, key_mod, gate, mixed_value, keep, parts, pairs) in enumerate(done):
        mine = inverses[block * heads : (block + 1) * heads]
        value_low = low(mixed_value)
        owns = [value_low[:, c] for c in columns]
        by_values = [dot3(x[:, BLOCK:], y) for x, y in zip(pairs, owns)]
        ends = [jnp.concatenate([parts["beta_end"][:, c], parts["key_end"][:, c]], 0) for c in columns]
        inners = [jnp.concatenate([parts["alpha_in"][:, c], parts["recept_in"][:, c]], 0) for c in columns]
        entering = state[...]
        state_ref[rows] = entering
        nows = [entering[:, c] for c in columns]
        inwards = [dot3(x, y, NT) for x, y in zip(inners, nows)]
        removals = [dot3(x, y[:BLOCK] + z[:BLOCK]) for x, y, z in zip(mine, inwards, by_values)]
        outs = [
            y[BLOCK:] + z[BLOCK:] + dot3(x[BLOCK:, :BLOCK], r)
            for x, y, z, r in zip(pairs, inwards, by_values, removals)
        ]
        leaving = [
            x * (parts["end"][:, c] * keep) + dot3(jnp.concatenate([r, v], 0), e, TN)
            for x, c, r, v, e in zip(nows, columns, removals, owns, ends)
        ]
        state[...] = join(leaving, 1)
        inverse_ref[rows] = join(mine, 1)
        removed_ref[rows] = join(removals, 1)
        head_low = join(outs, 1).astype(BF16)
        head_ref[rows] = head_low
        normed, _ = post_norm(head_low.astype(F32), ones)
        bonus = head_sum(recept * key_mod * vec[5:6], ones) * mixed_value
        mixed_ref[rows] = ((normed * vec[6:7] + vec[7:8] + bonus) * gate).astype(BF16)


def backward_kernel(
    count, grad_ref, recept_ref, keys_ref, values_ref, hidden_ref, first_ref, up_ref, vec_ref, segment_ref,
    head_ref, state_ref, inverse_ref, removed_ref,
    recept_out, keys_out, values_out, ups_out, first_out, vec_out, state,
):
    width = recept_ref.shape[1]
    heads = width // HEAD

    @pl.when(pl.program_id(0) == 0)
    def _():
        state[...] = jnp.zeros_like(state)
        vec_out[...] = jnp.zeros_like(vec_out)

    ones = head_ones(width)
    vec = vec_ref[...]
    up = up_ref[...]
    i, j = iotas(BLOCK, BLOCK)
    upper = jnp.where(i <= j, 1.0, 0.0).astype(BF16)
    columns = [slice(head * HEAD, (head + 1) * HEAD) for head in range(heads)]
    order = range(count - 1, -1, -1)
    kept = {}
    for block in order:
        rows = slice(block * BLOCK, (block + 1) * BLOCK)
        recept, keys, values = recept_ref[rows], keys_ref[rows], values_ref[rows]
        first = first_ref[rows].astype(F32)
        z, decay_log, rate, blend, gate, mixed_value, scale, key_dir, key_mod = front(
            keys, values, hidden_ref[rows], up, first, vec, ones
        )
        quad, carry, tail, keep = block_masks(segment_ref[block * 8 : block * 8 + 8])
        rate_low, dir_low = low(rate), low(key_dir)
        parts = decayed(
            low(decay_log), low(key_mod), dir_low, rate_low, low(recept),
            tile_heads(carry, heads), tile_heads(tail, heads),
        )
        value_low = low(mixed_value)

        grad = grad_ref[rows].astype(F32)
        normed, spread = post_norm(head_ref[rows].astype(F32), ones)
        product = recept * key_mod
        coefficient = head_sum(product * vec[5:6], ones)
        grad_gate = grad * (normed * vec[6:7] + vec[7:8] + coefficient * mixed_value)
        opened = grad * gate
        grad_normed = opened * vec[6:7]
        grad_head = spread * (
            grad_normed
            - head_sum(grad_normed, ones) * (1.0 / HEAD)
            - normed * (head_sum(grad_normed * normed, ones) * (1.0 / HEAD))
        )
        grad_coefficient = head_sum(opened * mixed_value, ones)
        weighted = grad_coefficient * vec[5:6]
        head_grad = low(grad_head)

        lefts = [jnp.concatenate([parts["alpha"][:, c], parts["recept"][:, c]], 0) for c in columns]
        rights = [jnp.concatenate([parts["beta"][:, c], parts["key"][:, c]], 0) for c in columns]
        ends = [jnp.concatenate([parts["beta_end"][:, c], parts["key_end"][:, c]], 0) for c in columns]
        inners = [jnp.concatenate([parts["alpha_in"][:, c], parts["recept_in"][:, c]], 0) for c in columns]
        pairs = [quad * dot3(x, y, NT) for x, y in zip(lefts, rights)]
        out_grads = [head_grad[:, c] for c in columns]
        through = [dot3(x[BLOCK:, :BLOCK], y, TN) for x, y in zip(pairs, out_grads)]
        kept[block] = dict(
            rows=rows, recept=recept, keys=keys, values=values, first=first, z=z, rate=rate, blend=blend,
            mixed_value=mixed_value, scale=scale, key_dir=key_dir, key_mod=key_mod, quad=quad, carry=carry, keep=keep,
            rate_low=rate_low, dir_low=dir_low, parts=parts, value_low=value_low, normed=normed, product=product,
            grad_gate=grad_gate, opened=opened, grad_coefficient=grad_coefficient,
            grad_mixed_value=opened * coefficient, grad_recept=weighted * key_mod, grad_key_mod=weighted * recept,
            lefts=lefts, rights=rights, ends=ends, inners=inners, pairs=pairs, out_grads=out_grads, through=through,
        )
    for block in order:
        k = kept[block]
        after, entering, inverse_all = state[...], state_ref[k["rows"]], inverse_ref[k["rows"]]
        laters, nows = [after[:, c] for c in columns], [entering[:, c] for c in columns]
        from_ends = [dot3(x, y, NT) for x, y in zip(k["ends"], laters)]
        inner_grads = [
            dot3(inverse_all[:, c], x + y[:BLOCK], TN) for c, x, y in zip(columns, k["through"], from_ends)
        ]
        boths = [jnp.concatenate([x, y], 0) for x, y in zip(inner_grads, k["out_grads"])]
        stays = [x * (k["parts"]["end"][:, c] * k["keep"]) for x, c in zip(laters, columns)]
        state[...] = join([x + dot3(y, z, TN) for x, y, z in zip(stays, boths, k["inners"])], 1)
        k.update(
            laters=laters, nows=nows, from_ends=from_ends, boths=boths,
            end_sum=join([jnp.sum(x * y, 0, keepdims=True) for x, y in zip(nows, stays)], 1),
        )
    vec_total = jnp.zeros_like(vec)
    for block in order:
        k = kept[block]
        rows, parts, quad = k["rows"], k["parts"], k["quad"]
        removed_all = removed_ref[rows]
        carry_two = jnp.concatenate([k["carry"], k["carry"]], 0)
        sources = [jnp.concatenate([removed_all[:, c], k["value_low"][:, c]], 0) for c in columns]
        grad_pairs = [quad * dot3(x, y, NT) for x, y in zip(k["boths"], sources)]
        grad_values = [
            dot3(x[:, BLOCK:], y, TN) + z[BLOCK:] for x, y, z in zip(k["pairs"], k["boths"], k["from_ends"])
        ]
        grad_ends = [dot3(x, y) for x, y in zip(sources, k["laters"])]
        to_state = [carry_two * dot3(x, y) for x, y in zip(k["boths"], k["nows"])]
        grad_lefts = [dot3(x, y) + z for x, y, z in zip(grad_pairs, k["rights"], to_state)]
        grad_rights = [dot3(x, y, TN) for x, y in zip(grad_pairs, k["lefts"])]
        d_alpha, d_recept = join([x[:BLOCK] for x in grad_lefts], 1), join([x[BLOCK:] for x in grad_lefts], 1)
        d_beta, d_key = join([x[:BLOCK] for x in grad_rights], 1), join([x[BLOCK:] for x in grad_rights], 1)
        d_beta_end, d_key_end = join([x[:BLOCK] for x in grad_ends], 1), join([x[BLOCK:] for x in grad_ends], 1)
        ended = parts["beta_end"] * d_beta_end + parts["key_end"] * d_key_end
        alphas = parts["alpha"] * d_alpha
        d_total = parts["recept"] * d_recept - parts["beta"] * d_beta - parts["key"] * d_key - ended + alphas
        d_step = sum_left(upper, d_total) + (jnp.sum(ended, 0, keepdims=True) + k["end_sum"]) - alphas
        d_beta_plain = d_beta * parts["shrunk"] + d_beta_end * parts["tail"]
        copy_decay = low(d_step * parts["log_step"])
        copy_dir = low(d_beta_plain * k["rate_low"] - d_alpha * parts["before"])
        copy_rate = low(d_beta_plain * k["dir_low"])

        keys, values, rate, blend = k["keys"], k["values"], k["rate"], k["blend"]
        grad_recept = k["grad_recept"] + low(d_recept * parts["grown"])
        grad_key_mod = k["grad_key_mod"] + low(d_key * parts["shrunk"] + d_key_end * parts["tail"])
        grad_mixed_value = k["grad_mixed_value"] + low(join(grad_values, 1))
        grad_z = copy_decay * jax.nn.sigmoid(-k["z"])
        factor = 1.0 + (rate - 1.0) * vec[4:5]
        keyed = grad_key_mod * keys
        grad_rate = copy_rate + keyed * vec[4:5]
        grad_scaled = k["scale"] * (copy_dir - k["key_dir"] * head_sum(copy_dir * k["key_dir"], ones))
        grad_keys = grad_key_mod * factor + grad_scaled * vec[3:4]
        grad_rate_up = grad_rate * rate * (1.0 - rate)
        grad_value_up = grad_mixed_value * (k["first"] - values) * blend * (1.0 - blend)
        recept_out[rows] = grad_recept.astype(BF16)
        keys_out[rows] = grad_keys.astype(BF16)
        values_out[rows] = (grad_mixed_value * (1.0 - blend)).astype(BF16)
        first_out[rows] = (grad_mixed_value * blend).astype(BF16)
        ups_out[0, rows] = grad_z.astype(BF16)
        ups_out[1, rows] = grad_rate_up.astype(BF16)
        ups_out[2, rows] = grad_value_up.astype(BF16)
        ups_out[3, rows] = k["grad_gate"].astype(BF16)

        def total(x):
            return jnp.sum(x, 0, keepdims=True)

        vec_total = vec_total + jnp.concatenate(
            [
                total(grad_z), total(grad_rate_up), total(grad_value_up), total(grad_scaled * keys),
                total(keyed * (rate - 1.0)), total(k["grad_coefficient"] * k["product"]),
                total(k["opened"] * k["normed"]), total(k["opened"]),
            ],
            0,
        )
    vec_out[...] += vec_total


def kernel_cost(rows, width, passes):
    return pl.CostEstimate(flops=2 * rows * width * width, bytes_accessed=4 * rows * width * passes, transcendentals=0)


def per_step(rows, most):
    return most if (rows // BLOCK) % most == 0 else 1


def run_forward(recept, keys, values, hidden, first, up, vec, segments):
    rows, width = recept.shape
    count = per_step(rows, 4)
    step = count * BLOCK

    def spec(columns):
        return pl.BlockSpec((step, columns), lambda i: (i, 0))

    def whole(array):
        return pl.BlockSpec(array.shape, lambda i: (0, 0))

    return pl.pallas_call(
        functools.partial(forward_kernel, count),
        grid=(rows // step,),
        in_specs=[
            spec(width), spec(width), spec(width), spec(WIDE), spec(width), whole(up), whole(vec),
            pl.BlockSpec((count * 8, BLOCK), lambda i: (i, 0)),
        ],
        out_specs=[spec(width)] * 5,
        out_shape=[jax.ShapeDtypeStruct((rows, width), d) for d in (BF16, BF16, F32, F32, F32)],
        scratch_shapes=[pltpu.VMEM((BLOCK, width), F32)],
        compiler_params=pltpu.CompilerParams(vmem_limit_bytes=48 << 20),
        cost_estimate=kernel_cost(rows, width, 110),
        name="mix_forward",
    )(recept, keys, values, hidden, first, up, vec, segments)


def run_backward(grad, recept, keys, values, hidden, first, up, vec, segments, saved):
    rows, width = recept.shape
    count = per_step(rows, 2)
    step = count * BLOCK
    last = rows // step - 1

    def spec(columns):
        return pl.BlockSpec((step, columns), lambda i: (last - i, 0))

    def whole(array):
        return pl.BlockSpec(array.shape, lambda i: (0, 0))

    return pl.pallas_call(
        functools.partial(backward_kernel, count),
        grid=(rows // step,),
        in_specs=[
            spec(width), spec(width), spec(width), spec(width), spec(WIDE), spec(width), whole(up), whole(vec),
            pl.BlockSpec((count * 8, BLOCK), lambda i: (last - i, 0)),
            spec(width), spec(width), spec(width), spec(width),
        ],
        out_specs=[
            spec(width), spec(width), spec(width),
            pl.BlockSpec((4, step, width), lambda i: (0, last - i, 0)),
            spec(width), pl.BlockSpec((8, width), lambda i: (0, 0)),
        ],
        out_shape=[
            jax.ShapeDtypeStruct((rows, width), BF16), jax.ShapeDtypeStruct((rows, width), BF16),
            jax.ShapeDtypeStruct((rows, width), BF16), jax.ShapeDtypeStruct((4, rows, width), BF16),
            jax.ShapeDtypeStruct((rows, width), BF16), jax.ShapeDtypeStruct((8, width), F32),
        ],
        scratch_shapes=[pltpu.VMEM((BLOCK, width), F32)],
        compiler_params=pltpu.CompilerParams(vmem_limit_bytes=48 << 20),
        cost_estimate=kernel_cost(rows, width, 150),
        name="mix_backward",
    )(grad, recept, keys, values, hidden, first, up, vec, segments, *saved)


def mix_norm(block_ref, stats_ref, vec_ref):
    stats = stats_ref[...]
    flowing = stats[:, 2:3]
    standard = (block_ref[...].astype(F32) - stats[:, 0:1]) * stats[:, 1:2]
    normed = standard * vec_ref[0:1] + vec_ref[1:2]
    delta = pltpu.roll(normed, 1, 0) * flowing - normed
    return standard, normed, delta, flowing


def project_kernel(
    width, block_ref, stats_ref, vec_ref, weight_ref,
    recept_ref, keys_ref, values_ref, downs_ref, hidden_ref,
):
    base = 3 * width
    _, normed, delta, _ = mix_norm(block_ref, stats_ref, vec_ref)
    weight = weight_ref[...]
    uses = (
        ((recept_ref, 0, width, 0),),
        ((downs_ref, base + OFFSETS[0], PADDED[0], OFFSETS[0]),),
        ((keys_ref, width, width, 0),),
        ((values_ref, 2 * width, width, 0), (downs_ref, base + OFFSETS[2], PADDED[2], OFFSETS[2])),
        ((downs_ref, base + OFFSETS[1], PADDED[1], OFFSETS[1]),),
        ((downs_ref, base + OFFSETS[3], PADDED[3], OFFSETS[3]),),
    )

    @pl.when(pl.program_id(0) == 0)
    def _():
        for ref in (recept_ref, keys_ref, values_ref, downs_ref):
            ref[...] = jnp.zeros_like(ref)

    for c, targets in enumerate(uses):
        mixed = (normed + delta * vec_ref[2 + c : 3 + c]).astype(BF16)
        for ref, start, size, at in targets:
            ref[:, at : at + size] += dot(mixed, weight[:, start : start + size])

    @pl.when(pl.program_id(0) == pl.num_programs(0) - 1)
    def _():
        hidden_ref[:, 0:128] = jnp.tanh(downs_ref[:, 0:128]).astype(BF16)
        hidden_ref[:, 128:384] = downs_ref[:, 128:384].astype(BF16)
        hidden_ref[:, 384:640] = jax.nn.sigmoid(downs_ref[:, 384:640]).astype(BF16)


def unproject_kernel(
    width, parts, piece, block_ref, stats_ref, vec_ref, weight_ref,
    other_ref, recept_ref, keys_ref, values_ref, ups_ref, hidden_ref, downs_ref, up_ref,
    grad_ref, sums_ref, wide_ref, up_out, down_lows,
):
    rows = block_ref.shape[0]
    base = 3 * width

    @pl.when(pl.program_id(0) == 0)
    def _():
        sums_ref[...] = jnp.zeros_like(sums_ref)
        for k, (at, size) in enumerate(zip(OFFSETS, PADDED)):
            cols = slice(at, at + size)
            grad = dot(ups_ref[k], up_ref[cols], NT)
            if k == 0:
                grad = grad * (1.0 - jnp.square(jnp.tanh(downs_ref[:, cols])))
            if k == 3:
                opening = jax.nn.sigmoid(downs_ref[:, cols])
                grad = grad * opening * (1.0 - opening)
            down_lows[:, cols] = grad.astype(BF16)
            up_out[:, cols] = dot(ups_ref[k], hidden_ref[:, cols], TN).astype(BF16)

    standard, normed, delta, flowing = mix_norm(block_ref, stats_ref, vec_ref)
    weight = weight_ref[...]

    def down(k):
        return (down_lows[:, OFFSETS[k] : OFFSETS[k] + PADDED[k]], base + OFFSETS[k], PADDED[k])

    uses = (
        ((recept_ref[...], 0, width),),
        (down(0),),
        ((keys_ref[...], width, width),),
        ((values_ref[...], 2 * width, width), down(2)),
        (down(1),),
        (down(3),),
    )
    kept, sent, vec_rows = None, None, []
    per_seq = parts * piece
    for c, sources in enumerate(uses):
        share = vec_ref[2 + c : 3 + c]
        mixed = (normed + delta * share).astype(BF16)
        grad = None
        for source, start, size in sources:
            part = dot(source, weight[:, start : start + size], NT)
            grad = part if grad is None else grad + part
            product = dot(mixed, source, TN).astype(BF16)
            for number in range(product.shape[0] // per_seq):
                for w in range(parts):
                    at = number * per_seq + w * piece
                    wide_ref[w, number, :, start : start + size] = product[at : at + piece]
        vec_rows.append(jnp.sum(grad * delta, 0, keepdims=True))
        moved = grad * share
        kept = grad - moved if kept is None else kept + (grad - moved)
        sent = moved if sent is None else sent + moved
    grad = kept + pltpu.roll(sent * flowing, rows - 1, 0)
    vec_rows = jnp.concatenate(
        [jnp.sum(grad * standard, 0, keepdims=True), jnp.sum(grad, 0, keepdims=True)] + vec_rows, 0
    )
    spare = jnp.concatenate([vec_rows.T, other_ref[...]], 1).astype(BF16)
    for number in range(spare.shape[0] // per_seq):
        for w in range(parts):
            at = number * per_seq + w * piece
            wide_ref[w, number, :, base + RANKS[0] : base + PADDED[0]] = spare[at : at + piece]
    scaled = grad * vec_ref[0:1]
    sums_ref[:, 0:1] += jnp.sum(scaled, 1, keepdims=True)
    sums_ref[:, 1:2] += jnp.sum(scaled * standard, 1, keepdims=True)
    grad_ref[...] = scaled


def mix_specs(rows, width, own_width, parts):
    block = 256 if rows <= 1024 else 128

    def columns(height):
        return pl.BlockSpec((height, block), lambda j: (0, j))

    def whole(shape):
        return pl.BlockSpec(shape, lambda j: (0,) * len(shape))

    def weights(array):
        size = array.shape[1] if rows > 1024 else 3 * own_width + WIDE
        return pl.BlockSpec((block, size), lambda j: (j, 0))

    return block, columns, whole, weights


def run_project(balanced, stats, vec, weights, own_width, parts):
    rows, width = balanced.shape
    block, columns, whole, weight_spec = mix_specs(rows, width, own_width, parts)
    shapes = [(rows, own_width)] * 3 + [(rows, WIDE)] * 2
    return pl.pallas_call(
        functools.partial(project_kernel, own_width),
        grid_spec=pltpu.PrefetchScalarGridSpec(
            num_scalar_prefetch=0,
            grid=(width // block,),
            in_specs=[columns(rows), whole(stats.shape), columns(8), weight_spec(weights)],
            out_specs=[whole(s) for s in shapes],
        ),
        out_shape=[jax.ShapeDtypeStruct(s, d) for s, d in zip(shapes, (F32, F32, F32, F32, BF16))],
        compiler_params=pltpu.CompilerParams(vmem_limit_bytes=60 << 20),
        cost_estimate=kernel_cost(rows, own_width, 60),
        name="mix_project",
    )(balanced, stats, vec, weights)


def run_unproject(balanced, stats, vec, weights, others, lows, ups, hidden, downs, up, parts):
    rows, width = balanced.shape
    own_width = lows[0].shape[1]
    seqs = width // own_width
    piece = own_width // parts
    block, columns, whole, weight_spec = mix_specs(rows, width, own_width, parts)
    taken = block // own_width
    total = 3 * own_width + WIDE
    return pl.pallas_call(
        functools.partial(unproject_kernel, own_width, parts, piece),
        grid_spec=pltpu.PrefetchScalarGridSpec(
            num_scalar_prefetch=0,
            grid=(width // block,),
            in_specs=[
                columns(rows), whole(stats.shape), columns(8), weight_spec(weights),
                pl.BlockSpec((block, others.shape[1]), lambda j: (j, 0)),
            ]
            + [whole(a.shape) for a in (*lows, ups, hidden, downs, up)],
            out_specs=[
                columns(rows), whole((rows, 2)),
                pl.BlockSpec((parts, taken, piece, total), lambda j: (0, j, 0, 0)),
                whole((own_width, WIDE)),
            ],
            scratch_shapes=[pltpu.VMEM((rows, WIDE), BF16)],
        ),
        out_shape=[
            jax.ShapeDtypeStruct((rows, width), F32), jax.ShapeDtypeStruct((rows, 2), F32),
            jax.ShapeDtypeStruct((parts, seqs, piece, total), BF16),
            jax.ShapeDtypeStruct((own_width, WIDE), BF16),
        ],
        compiler_params=pltpu.CompilerParams(vmem_limit_bytes=60 << 20),
        cost_estimate=kernel_cost(rows, own_width, 120),
        name="mix_unproject",
    )(balanced, stats, vec, weights, others, *lows, ups, hidden, downs, up)


def norm_stats(values):
    centered = values - jnp.mean(values, -1, keepdims=True)
    scale = lax.rsqrt(jnp.mean(centered * centered, -1, keepdims=True) + 1e-05)
    return centered * scale, scale


def norm_back(grad, standard, scale, gain):
    scaled = grad * gain
    return scale * (
        scaled
        - jnp.mean(scaled, -1, keepdims=True)
        - standard * jnp.mean(scaled * standard, -1, keepdims=True)
    )


def pad_ranks(matrix):
    pieces, start = [], 0
    for rank, padded in zip(RANKS, PADDED):
        pieces.append(jnp.pad(matrix[:, start : start + rank], ((0, 0), (0, padded - rank))))
        start += rank
    return jnp.concatenate(pieces, 1)


def unpad_ranks(matrix):
    return jnp.concatenate([matrix[..., o : o + r] for o, r in zip(OFFSETS, RANKS)], -1)


MESH_ID = pl.DeviceIdType.MESH


def places():
    s, w = lax.axis_index("seq"), lax.axis_index("wsh")
    side = s % 2
    return s, w, side, s // 2, (s + 1 - 2 * side, w), (s, w + 1 - 2 * (w % 2)), (s, w + 2 - 4 * (w // 2))


def greet(neighbours, number):
    barrier = pltpu.get_barrier_semaphore()
    for there, device in neighbours:
        if there is None:
            pl.semaphore_signal(barrier, inc=1, device_id=device, device_id_type=MESH_ID)
        else:

            @pl.when(there)
            def _(device=device):
                pl.semaphore_signal(barrier, inc=1, device_id=device, device_id_type=MESH_ID)

    pl.semaphore_wait(barrier, number)


def send(source, target, send_sem, recv_sem, device):
    return pltpu.make_async_remote_copy(
        src_ref=source, dst_ref=target, send_sem=send_sem, recv_sem=recv_sem, device_id=device, device_id_type=MESH_ID
    )


def line_ends(z):
    return jnp.where(z > 0, 1, 0) + jnp.where(z < 3, 1, 0)


def gather_kernel(
    own_ref, tail_ref, weight_ref, out_ref, tails_ref, weights_ref,
    copy_sem, right_send, right_recv, left_send, left_recv, x_send, x_recv, c_send, c_recv, y_send, y_recv,
):
    s, w, side, z, x_device, core_device, y_device = places()
    up, down = (s + 2, w), (s - 2, w)
    across = w + 2 - 4 * (w // 2)
    kinds = ((own_ref, out_ref), (tail_ref, tails_ref))
    copies = [pltpu.make_async_copy(own, out.at[s], copy_sem.at[k]) for k, (own, out) in enumerate(kinds)]
    copies.append(pltpu.make_async_copy(weight_ref, weights_ref.at[w], copy_sem.at[2]))
    for copy in copies:
        copy.start()
    greet(((None, x_device), (None, core_device), (None, y_device), (z < 3, up), (z > 0, down)), 3 + line_ends(z))

    weight_y = send(weight_ref, weights_ref.at[w], y_send, y_recv, y_device)
    weight_core = send(weight_ref, weights_ref.at[w], c_send.at[0], c_recv.at[0], core_device)
    weight_on = send(weights_ref.at[across], weights_ref.at[across], c_send.at[1], c_recv.at[1], core_device)
    weight_y.start()
    weight_core.start()

    def to_right(j, k, source, number):
        return send(source, kinds[k][1].at[number], right_send.at[j, k], right_recv.at[j, k], up)

    def to_left(j, k, source, number):
        return send(source, kinds[k][1].at[number], left_send.at[j, k], left_recv.at[j, k], down)

    def to_x(at, k, source, number):
        return send(source, kinds[k][1].at[number], x_send.at[at, k], x_recv.at[at, k], x_device)

    for k, (own, _) in enumerate(kinds):

        @pl.when(z < 3)
        def _(k=k, own=own):
            to_right(0, k, own, s).start()

        @pl.when(z > 0)
        def _(k=k, own=own):
            to_left(0, k, own, s).start()

        to_x(z, k, own, s).start()
    for j in (1, 2, 3):
        lower, upper = s - 2 * j, s + 2 * j
        for k, (_, out) in enumerate(kinds):

            @pl.when(z >= j)
            def _(j=j, k=k, out=out, lower=lower):
                block = out.at[lower]
                to_right(j - 1, k, block, lower).wait_recv()

                @pl.when(z < 3)
                def _():
                    to_right(j, k, block, lower).start()

                to_x(z - j, k, block, lower).start()

            @pl.when(z + j <= 3)
            def _(j=j, k=k, out=out, upper=upper):
                block = out.at[upper]
                to_left(j - 1, k, block, upper).wait_recv()

                @pl.when(z > 0)
                def _():
                    to_left(j, k, block, upper).start()

                to_x(z + j, k, block, upper).start()

    weight_y.wait_recv()
    weight_on.start()
    for k, (own, _) in enumerate(kinds):
        for number in range(4):
            done = to_x(number, k, own, s)
            done.wait_send()
            done.wait_recv()
        for j in range(3):

            @pl.when((z >= j) & (z < 3))
            def _(j=j, k=k, own=own):
                to_right(j, k, own, s).wait_send()

            @pl.when((z + j <= 3) & (z > 0))
            def _(j=j, k=k, own=own):
                to_left(j, k, own, s).wait_send()

    weight_core.wait_recv()
    weight_on.wait_recv()
    for copy in (weight_y, weight_core, weight_on):
        copy.wait_send()
    for copy in copies:
        copy.wait()


def gather_first(own, tail, weight):
    seqs, parts = lax.axis_size("seq"), lax.axis_size("wsh")
    if seqs != 8 or parts != 4:
        return (
            lax.all_gather(own, "seq", axis=0, tiled=False),
            lax.all_gather(tail, "seq", axis=0, tiled=False),
            lax.all_gather(weight, "wsh", axis=0, tiled=False),
        )
    dma = pltpu.SemaphoreType.DMA
    given = ((seqs, own), (seqs, tail), (parts, weight))
    return pl.pallas_call(
        gather_kernel,
        in_specs=[pl.BlockSpec(memory_space=pltpu.VMEM)] * 3,
        out_specs=[pl.BlockSpec(memory_space=pl.ANY)] * 3,
        out_shape=[jax.ShapeDtypeStruct((n,) + x.shape, x.dtype) for n, x in given],
        scratch_shapes=[dma((3,))] + [dma((3, 2))] * 4 + [dma((4, 2))] * 2 + [dma((2,))] * 2 + [dma] * 2,
        compiler_params=pltpu.CompilerParams(collective_id=1, has_side_effects=True),
        cost_estimate=pl.CostEstimate(flops=0, bytes_accessed=100 << 20, transcendentals=0),
        name="gather_first",
    )(own, tail, weight)


def turning(x_ref, out_ref, send_sem, recv_sem):
    s, w, side, z, _, _, _ = places()
    home = z == w
    greetings = tuple(((source != z) | (z != w), (source * 2 + side, z)) for source in range(4))

    def copy(j):
        piece = (z + j) % 4
        return send(x_ref.at[piece], out_ref.at[z], send_sem.at[j], recv_sem.at[j], (w * 2 + side, piece))

    def start():
        for j in (3, 2, 1):
            copy(j).start()

        @pl.when(jnp.logical_not(home))
        def _():
            copy(0).start()

        @pl.when(home)
        def _():
            out_ref[z] = x_ref[z]

    def end():
        for j in range(1, 4):
            copy(j).wait_recv()
            copy(j).wait_send()

        @pl.when(jnp.logical_not(home))
        def _():
            copy(0).wait_recv()
            copy(0).wait_send()

    return greetings, jnp.where(home, 3, 4), start, end


def reduce_kernel(
    splits, x_ref, turn_ref, out_ref, turn_out, x_buf, right_buf, left_buf, right_out, left_out,
    x_send, x_recv, right_send, right_recv, left_send, left_recv, turn_send, turn_recv,
):
    s, w, side, z, x_device, _, _ = places()
    up, down = (s + 2, w), (s - 2, w)
    size = x_ref.shape[2] // splits
    columns = [slice(c * size, (c + 1) * size) for c in range(splits)]
    greetings, number, start_turn, end_turn = turning(turn_ref, turn_out, turn_send, turn_recv)
    greet(((None, x_device), (z < 3, up), (z > 0, down)) + greetings, 1 + line_ends(z) + number)

    def to_x(target, c):
        return send(
            x_ref.at[target * 2 + 1 - side, :, columns[c]], x_buf.at[target, :, columns[c]],
            x_send.at[target, c], x_recv.at[target, c], x_device,
        )

    def start_x(target):
        for c in range(splits):
            to_x(target, c).start()

    def to_right(k, c):
        return send(
            right_out.at[k - 1, :, columns[c]], right_buf.at[k - 1, :, columns[c]],
            right_send.at[k - 1, c], right_recv.at[k - 1, c], up,
        )

    def to_left(k, c):
        return send(
            left_out.at[k - 1, :, columns[c]], left_buf.at[k - 1, :, columns[c]],
            left_send.at[k - 1, c], left_recv.at[k - 1, c], down,
        )

    def pair(target, c):
        to_x(target, c).wait_recv()
        return x_ref[target * 2 + side, :, columns[c]].astype(F32) + x_buf[target, :, columns[c]].astype(F32)

    for k in (3, 2, 1):

        @pl.when(z + k <= 3)
        def _(k=k):
            start_x(z + k)

        @pl.when(z >= k)
        def _(k=k):
            start_x(z - k)

    start_x(z)
    start_turn()
    for k in (3, 2, 1):
        for c in range(splits):

            @pl.when(z + k <= 3)
            def _(k=k, c=c):
                right_out[k - 1, :, columns[c]] = pair(z + k, c).astype(BF16)
                if k < 3:

                    @pl.when(z > 0)
                    def _():
                        to_right(k + 1, c).wait_recv()
                        right_out[k - 1, :, columns[c]] = (
                            right_out[k - 1, :, columns[c]].astype(F32) + right_buf[k, :, columns[c]].astype(F32)
                        ).astype(BF16)

                to_right(k, c).start()

            @pl.when(z >= k)
            def _(k=k, c=c):
                left_out[k - 1, :, columns[c]] = pair(z - k, c).astype(BF16)
                if k < 3:

                    @pl.when(z < 3)
                    def _():
                        to_left(k + 1, c).wait_recv()
                        left_out[k - 1, :, columns[c]] = (
                            left_out[k - 1, :, columns[c]].astype(F32) + left_buf[k, :, columns[c]].astype(F32)
                        ).astype(BF16)

                to_left(k, c).start()

    for c in range(splits):
        out_ref[:, columns[c]] = pair(z, c)

        @pl.when(z > 0)
        def _(c=c):
            to_right(1, c).wait_recv()
            out_ref[:, columns[c]] += right_buf[0, :, columns[c]].astype(F32)

        @pl.when(z < 3)
        def _(c=c):
            to_left(1, c).wait_recv()
            out_ref[:, columns[c]] += left_buf[0, :, columns[c]].astype(F32)

    for c in range(splits):
        for target in range(4):
            to_x(target, c).wait_send()
        for k in (3, 2, 1):

            @pl.when(z + k <= 3)
            def _(k=k, c=c):
                to_right(k, c).wait_send()

            @pl.when(z >= k)
            def _(k=k, c=c):
                to_left(k, c).wait_send()

    end_turn()


def reduce_seq(x, turned):
    seqs, rows, width = x.shape
    splits = 2
    vmem = pl.BlockSpec(memory_space=pltpu.VMEM)
    dma = pltpu.SemaphoreType.DMA
    return pl.pallas_call(
        functools.partial(reduce_kernel, splits),
        in_specs=[vmem] * 2,
        out_specs=[vmem] * 2,
        out_shape=[jax.ShapeDtypeStruct((rows, width), F32), jax.ShapeDtypeStruct(turned.shape, turned.dtype)],
        scratch_shapes=[pltpu.VMEM((4, rows, width), BF16)]
        + [pltpu.VMEM((3, rows, width), BF16)] * 4
        + [dma((4, splits))] * 2 + [dma((3, splits))] * 4 + [dma((4,))] * 2,
        compiler_params=pltpu.CompilerParams(collective_id=2, has_side_effects=True, vmem_limit_bytes=40 << 20),
        cost_estimate=pl.CostEstimate(flops=0, bytes_accessed=1 << 20, transcendentals=0),
        name="reduce_seq",
    )(x, turned)


def finish_kernel(wide_ref, key_ref, wide_out, key_out, wide_send, wide_recv, key_send, key_recv):
    s, w, _, _, _, _, _ = places()
    greetings, number, start_turn, end_turn = turning(key_ref, key_out, key_send, key_recv)
    greet(tuple((None, ((s + d) % 8, w)) for d in range(1, 8)) + greetings, 7 + number)

    def wide(d):
        target = (s + d) % 8
        return send(wide_ref.at[target], wide_out.at[s], wide_send.at[d - 1], wide_recv.at[d - 1], (target, w))

    for d in (4, 3, 5, 2, 6, 1, 7):
        wide(d).start()
    start_turn()
    wide_out[s] = wide_ref[s]
    for d in range(1, 8):
        wide(d).wait_recv()
        wide(d).wait_send()
    end_turn()


def finish(wide, key):
    vmem = pl.BlockSpec(memory_space=pltpu.VMEM)
    dma = pltpu.SemaphoreType.DMA
    return pl.pallas_call(
        finish_kernel,
        in_specs=[vmem] * 2,
        out_specs=[vmem] * 2,
        out_shape=[jax.ShapeDtypeStruct(x.shape, x.dtype) for x in (wide, key)],
        scratch_shapes=[dma((7,)), dma((7,)), dma((4,)), dma((4,))],
        compiler_params=pltpu.CompilerParams(collective_id=5, has_side_effects=True, vmem_limit_bytes=24 << 20),
        cost_estimate=pl.CostEstimate(flops=0, bytes_accessed=100 << 20, transcendentals=0),
        name="finish",
    )(wide, key)


def deal_kernel(to_heads, x_ref, out_ref, send_sem, recv_sem):
    s, w, _, _, _, _, _ = places()
    tall, thin = (out_ref, x_ref) if to_heads else (x_ref, out_ref)
    columns, rows = tall.shape[1], thin.shape[0]

    def column(number):
        return pl.ds(pl.multiple_of(number * columns, columns), columns)

    def row(number):
        return pl.ds(pl.multiple_of(number * rows, rows), rows)

    greet(tuple((None, ((s + d) % 8, w)) for d in range(1, 8)), 7)

    def copy(d):
        target = (s + d) % 8
        if to_heads:
            source, goal = x_ref.at[:, column(target)], out_ref.at[row(s)]
        else:
            source, goal = x_ref.at[row(target)], out_ref.at[:, column(s)]
        return send(source, goal, send_sem.at[d - 1], recv_sem.at[d - 1], (target, w))

    for d in (4, 3, 5, 2, 6, 1, 7):
        copy(d).start()
    if to_heads:
        out_ref[row(s), :] = x_ref[:, column(s)]
    else:
        out_ref[:, column(s)] = x_ref[row(s), :]
    for d in range(1, 8):
        copy(d).wait_recv()
        copy(d).wait_send()


def deal(x, to_heads):
    seqs = lax.axis_size("seq")
    if seqs != 8 or lax.axis_size("wsh") != 4:
        if to_heads:
            split = x.reshape(x.shape[0], seqs, -1).transpose(1, 0, 2)
            return exchange(split, "seq").reshape(x.shape[0] * seqs, -1)
        moved = exchange(x.reshape(seqs, x.shape[0] // seqs, -1), "seq")
        return moved.transpose(1, 0, 2).reshape(x.shape[0] // seqs, -1)
    shape = (x.shape[0] * seqs, x.shape[1] // seqs) if to_heads else (x.shape[0] // seqs, x.shape[1] * seqs)
    vmem, dma = pl.BlockSpec(memory_space=pltpu.VMEM), pltpu.SemaphoreType.DMA
    return pl.pallas_call(
        functools.partial(deal_kernel, to_heads),
        in_specs=[vmem],
        out_specs=vmem,
        out_shape=jax.ShapeDtypeStruct(shape, x.dtype),
        scratch_shapes=[dma((7,)), dma((7,))],
        compiler_params=pltpu.CompilerParams(collective_id=6 if to_heads else 7, has_side_effects=True),
        cost_estimate=pl.CostEstimate(flops=0, bytes_accessed=60 << 20, transcendentals=0),
        name="deal_heads" if to_heads else "deal_rows",
    )(x)


def channel_kernel(
    forward, x_ref, first_hbm, second_hbm, active_hbm,
    sum_ref, all_hbm, mine_hbm, other_hbm, extra_hbm,
    first, second, rows_all, middle, active, part, core_buf, far_out, far_buf,
    load_sem, store_sem, core_send, core_recv, y_send, y_recv, x_send, x_recv, r_send, r_recv, f_send, f_recv,
):
    s, w, side, z, x_device, core_device, y_device = places()
    rows, width = x_ref.shape
    units = first.shape[0]
    half = units // 2
    loads = [
        pltpu.make_async_copy(first_hbm, first, load_sem.at[0]),
        pltpu.make_async_copy(second_hbm, second, load_sem.at[1]),
    ]
    if not forward:
        loads.append(pltpu.make_async_copy(active_hbm, active, load_sem.at[2]))
    for load in loads:
        load.start()
    rows_all[0:rows] = x_ref[...]
    greet(((None, x_device), (None, core_device), (None, y_device)), 3)

    def block(number):
        return rows_all.at[pl.ds(number * rows, rows)]

    to_core = [
        send(block(0), block(1), core_send.at[0], core_recv.at[0], core_device),
        send(block(2), block(3), core_send.at[1], core_recv.at[1], core_device),
    ]
    to_y = send(block(0), block(2), y_send, y_recv, y_device)
    if forward:
        to_x = [
            send(
                middle.at[1 - side, pl.ds(2 * n * rows, 2 * rows)], other_hbm.at[pl.ds(2 * n * rows, 2 * rows)],
                x_send.at[n], x_recv.at[n], x_device,
            )
            for n in range(2)
        ]
    else:
        to_x = [
            send(block(n), other_hbm.at[pl.ds(n * rows, rows)], x_send.at[n], x_recv.at[n], x_device) for n in range(4)
        ]
    sums_core = [
        send(part.at[pl.ds((2 * n + 1) * rows, rows)], core_buf.at[n], r_send.at[n], r_recv.at[n], core_device)
        for n in range(2)
    ]
    far = send(far_out, far_buf, f_send, f_recv, y_device)
    stores = [
        pltpu.make_async_copy(rows_all, all_hbm, store_sem.at[0]),
        pltpu.make_async_copy(middle.at[side], mine_hbm, store_sem.at[1]),
        pltpu.make_async_copy(active if forward else middle.at[1 - side], extra_hbm, store_sem.at[2]),
    ]

    def pass_on(number):
        if not forward:
            to_x[number].start()

    to_y.start()
    to_core[0].start()
    pass_on(0)
    tile = min(512, half)

    def multiply(number):
        two = pl.ds(2 * number * rows, 2 * rows)

        def up(t, carry):
            for side_units in range(2):
                at = pl.multiple_of(t * tile, tile)
                unit = pl.multiple_of(side_units * half + at, tile)
                raw = dot(rows_all[two, :], first[pl.ds(unit, tile), :], NT)
                if forward:
                    raw = jnp.maximum(raw, 0.0)
                    active[two, pl.ds(unit, tile)] = raw
                    mid = raw * raw
                else:
                    mid = raw * 2.0 * active[two, pl.ds(unit, tile)]
                middle[side_units, two, pl.ds(at, tile)] = mid.astype(BF16)
            return carry

        lax.fori_loop(0, half // tile, up, 0)
        if forward:
            to_x[number].start()
        if number == 0:
            loads[1].wait()

        def down(t, carry):
            at = pl.multiple_of(t * tile, tile)
            part[two, pl.ds(at, tile)] = dot(middle[0, two, :], second[0:half, pl.ds(at, tile)]) + dot(
                middle[1, two, :], second[half:units, pl.ds(at, tile)]
            )
            return carry

        lax.fori_loop(0, width // tile, down, 0)
        sums_core[number].start()

    loads[0].wait()
    if not forward:
        loads[2].wait()
    to_core[0].wait_recv()
    pass_on(1)
    multiply(0)
    to_y.wait_recv()
    to_core[1].start()
    pass_on(2)
    to_core[1].wait_recv()
    pass_on(3)
    stores[0].start()
    multiply(1)
    for store in stores[1:]:
        store.start()
    sums_core[1].wait_recv()
    far_out[...] = (part[2 * rows : 3 * rows] + core_buf[1]).astype(BF16)
    far.start()
    sums_core[0].wait_recv()
    sum_ref[...] = part[0:rows] + core_buf[0]
    far.wait_recv()
    sum_ref[...] += far_buf[...].astype(F32)
    for copy in to_x:
        copy.wait_recv()
    for copy in to_x + to_core + sums_core + [to_y, far]:
        copy.wait_send()
    for store in stores:
        store.wait()


def channel_stage(x, first, second, active):
    rows, width = x.shape
    units = first.shape[0]
    forward = active is None
    given = (x, first, second) if forward else (x, first, second, active)
    everything = pl.BlockSpec(memory_space=pl.ANY)
    shapes = [
        ((rows, width), F32), ((4 * rows, width), BF16), ((4 * rows, units // 2), BF16),
        ((4 * rows, units // 2 if forward else width), BF16),
        ((4 * rows, units), F32) if forward else ((4 * rows, units // 2), BF16),
    ]

    def body(*refs):
        refs = list(refs)
        if forward:
            refs.insert(3, None)
        channel_kernel(forward, *refs)

    dma = pltpu.SemaphoreType.DMA
    return pl.pallas_call(
        body,
        in_specs=[pl.BlockSpec(memory_space=pltpu.VMEM)] + [everything] * (len(given) - 1),
        out_specs=[pl.BlockSpec(memory_space=pltpu.VMEM)] + [everything] * (len(shapes) - 1),
        out_shape=[jax.ShapeDtypeStruct(s, d) for s, d in shapes],
        scratch_shapes=[
            pltpu.VMEM((units, width), BF16), pltpu.VMEM((units, width), BF16), pltpu.VMEM((4 * rows, width), BF16),
            pltpu.VMEM((2, 4 * rows, units // 2), BF16), pltpu.VMEM((4 * rows, units), F32),
            pltpu.VMEM((4 * rows, width), F32), pltpu.VMEM((2, rows, width), F32),
            pltpu.VMEM((rows, width), BF16), pltpu.VMEM((rows, width), BF16),
            dma((3,)), dma((3,)), dma((2,)), dma((2,)), dma, dma, dma((4,)), dma((4,)), dma((2,)), dma((2,)),
            dma, dma,
        ],
        compiler_params=pltpu.CompilerParams(
            collective_id=3 if forward else 4, has_side_effects=True, vmem_limit_bytes=60 << 20
        ),
        cost_estimate=pl.CostEstimate(flops=0, bytes_accessed=100 << 20, transcendentals=0),
        name="channel_forward" if forward else "channel_backward",
    )(*given)


def from_behind(x, axis, by):
    size = lax.axis_size(axis)
    pairs = [(i, i + by) for i in range(size) if 0 <= i + by < size]
    return lax.ppermute(x, axis, pairs)


def exchange(x, axis):
    return lax.all_to_all(x, axis, split_axis=0, concat_axis=0, tiled=True)


def swap(x, by):
    size = lax.axis_size("wsh")
    return lax.ppermute(x, "wsh", [(i, i ^ by) for i in range(size)])


def gather_near(x):
    if lax.axis_size("wsh") != 4:
        return lax.all_gather(x, "wsh", axis=0, tiled=True)
    return gathered_near(x, swap(x, 1), swap(x, 2))


def gathered_near(x, beside, across):
    return jnp.concatenate([x, beside, across, swap(across, 1)], 0)


def beside(x):
    return lax.ppermute(x, "seq", [(i, i ^ 1) for i in range(lax.axis_size("seq"))])


def quartered(x):
    rows, columns = x.shape
    return x.reshape(rows, 4, 4, columns // 16).transpose(0, 2, 1, 3).reshape(rows, columns)


def scalar_sum(x):
    if lax.axis_size("wsh") != 4:
        return jnp.sum(lax.all_gather(x.reshape(1), "wsh", axis=0, tiled=True))
    x = jnp.full((8, 128), x)
    x = x + swap(x, 1)
    return (x + swap(x, 2))[0, 0]


def near_sum(x):
    if lax.axis_size("wsh") != 4:
        return lax.psum_scatter(x, "wsh", scatter_dimension=0, tiled=True)
    rows = x.shape[0] // 4
    beside = swap(jnp.concatenate([x[rows : 2 * rows], x[3 * rows :]], 0), 1)
    far = x[2 * rows : 3 * rows] + beside[rows:]
    return x[:rows] + beside[:rows] + swap(far.astype(BF16), 2).astype(F32)


def block_sum(x):
    if lax.axis_size("wsh") != 4:
        return lax.psum_scatter(x, "wsh", scatter_dimension=0, tiled=False).astype(F32)
    kept, far = block_halves(x)
    return kept + swap(far, 2).astype(F32)


def block_halves(x):
    number = lax.axis_index("wsh")

    def block(by):
        return lax.dynamic_index_in_dim(x, number ^ by, 0, keepdims=False)

    beside = swap(jnp.stack([block(1), block(3)]), 1).astype(F32)
    return block(0).astype(F32) + beside[0], (block(2).astype(F32) + beside[1]).astype(BF16)


def local(
    tokens, first_layer_values, teacher, valid, destination, lengths,
    receptance_matrix, key_matrix, value_matrix, output_matrix,
    lowrank_down_weight, lowrank_up_weight, channel_key_weight, channel_value_weight, vectors,
):
    rows, width = tokens.shape
    seqs, parts = lax.axis_size("seq"), lax.axis_size("wsh")
    me = lax.axis_index("seq")
    group = rows * seqs
    own_width = width // seqs
    shard = width // parts
    piece = shard // seqs
    column = me * own_width

    def own_columns(matrix):
        return lax.dynamic_slice_in_dim(matrix, column, own_width, 1)

    near = parts == 4
    up_piece = lax.dynamic_slice_in_dim(lowrank_up_weight, column % shard, own_width, 0)
    total = 3 * own_width + WIDE
    own_weights = jnp.concatenate(
        [
            own_columns(receptance_matrix), own_columns(key_matrix), own_columns(value_matrix),
            pad_ranks(lowrank_down_weight), up_piece.reshape(shard, -1),
        ],
        1,
    )

    dest_seq = destination // rows // parts
    position = dest_seq * rows + destination % rows
    digits = jnp.stack([position // DIGIT, position % DIGIT, valid], 1).astype(BF16)
    tail = jnp.pad(digits, ((0, 0), (0, EXTRA - 3)))
    given, tails, weights = gather_first(tokens, tail, own_weights)
    given, tails, weights = given.reshape(group, width), tails.reshape(group, EXTRA), weights.reshape(width, -1)
    info = tails[:, :3].astype(F32)
    places = (info[:, 0] * DIGIT + info[:, 1]).astype(jnp.int32)
    numbers = jnp.arange(group, dtype=jnp.int32)
    permute = (numbers[:, None] == places[None, :]).astype(BF16)
    total_valid = scalar_sum(jnp.sum(info[:, 2]))

    index = jnp.arange(rows, dtype=jnp.int32)
    same_dest = (dest_seq[:, None] == dest_seq[None, :]) & (index[None, :] < index[:, None])
    slot = dest_seq * (rows // seqs) + jnp.sum(same_dest.astype(jnp.int32), 1)
    arrange = (index[:, None] == slot[None, :]).astype(BF16)
    mine = (places // rows) == me
    arrival = jnp.cumsum(mine.astype(jnp.int32)) - 1
    own_rows = ((index[:, None] + me * rows) == places[None, :]).astype(BF16)
    settle = dot(own_rows, (mine[:, None] & (arrival[:, None] == index[None, :])).astype(BF16)).astype(BF16)

    offsets = jnp.cumsum(lengths[0]) - lengths[0]
    starts = jnp.any(numbers[:, None] == offsets[None, :], 1).astype(F32)
    segment_ids = jnp.cumsum(starts).reshape(-1, BLOCK)
    before = segment_ids[:, :1] - starts.reshape(-1, BLOCK)[:, :1]
    segments = jnp.stack(
        [segment_ids, jnp.broadcast_to(before, segment_ids.shape), jnp.broadcast_to(segment_ids[:, -1:], segment_ids.shape)]
        + [jnp.zeros_like(segment_ids)] * 5,
        1,
    ).reshape(-1, BLOCK)
    flowing = (1.0 - starts)[:, None]

    up = pad_ranks(
        lax.dynamic_slice(
            weights, (column // shard * shard, total), (shard, weights.shape[1] - total)
        ).reshape(own_width, -1)
    ).T
    vec = lax.dynamic_slice_in_dim(vectors, column, own_width, 0)[:, 8:16].T

    output_late, given = lax.optimization_barrier((output_matrix, given))
    w_out = lax.all_gather(output_late, "wsh", axis=0, tiled=True)
    balanced = dot(permute, given).astype(BF16)
    wide_rows = balanced.astype(F32)
    mean = jnp.mean(wide_rows, -1, keepdims=True)
    scale_one = lax.rsqrt(jnp.mean(jnp.square(wide_rows - mean), -1, keepdims=True) + 1e-05)
    stats = jnp.concatenate([mean, scale_one, flowing, flowing], 1)
    mix_vec = vectors[:, :8].T
    first_values, stats = lax.optimization_barrier((first_layer_values, stats))
    first_given = exchange(
        first_values.reshape(rows, seqs, own_width).transpose(1, 0, 2), "seq"
    ).reshape(group, own_width)
    recept, keys, values, downs, hidden = run_project(balanced, stats, mix_vec, weights, own_width, parts)
    teacher_late, recept, first_given = lax.optimization_barrier((teacher, recept, first_given))
    first = dot(permute, first_given).astype(BF16)
    teacher_rows = exchange(dot(arrange, teacher_late).astype(BF16).reshape(seqs, rows // seqs, width), "seq")
    inputs = (recept, keys, values, hidden, first, up, vec, segments)
    mixed_out, *saved = run_forward(*inputs)
    teacher_rows, mixed_out, total_valid = lax.optimization_barrier((teacher_rows, mixed_out, total_valid))
    target = dot(settle, teacher_rows.reshape(rows, width))

    mixed_rows = deal(mixed_out, False)
    own = lax.dynamic_slice_in_dim(balanced, me * rows, rows, 0).astype(F32)
    own_starts = lax.dynamic_slice_in_dim(starts, me * rows, rows, 0)
    own_flowing = (1.0 - own_starts)[:, None]
    own_valid = dot(own_rows, tails)[:, 2]
    residual = own + dot(mixed_rows, w_out)
    standard_two, scale_two = norm_stats(residual)
    normed_two = standard_two * vectors[:, 16] + vectors[:, 17]
    carried_two = from_behind(normed_two[-1:], "seq", 1)
    delta_two = jnp.concatenate([carried_two, normed_two[:-1]], 0) * own_flowing - normed_two
    channel_in = (normed_two + delta_two * vectors[:, 18]).astype(BF16)
    paired = near and seqs == 8
    if paired:
        summed, channel, hidden_mine, hidden_other, active = channel_stage(
            channel_in, channel_key_weight, channel_value_weight, None
        )
    else:
        channel = gather_near(channel_in)
        active = jax.nn.relu(dot(channel, channel_key_weight, NT))
        hidden_rows = jnp.square(active).astype(BF16)
        summed = near_sum(dot(hidden_rows, channel_value_weight))
    result = residual + summed
    total_tokens = group * parts
    cotangent = (result - target) * (own_valid * (total_tokens / total_valid))[:, None]
    cot_low = cotangent.astype(BF16)

    result_back = exchange(dot(settle, result.astype(BF16), TN).astype(BF16).reshape(seqs, rows // seqs, width), "seq")
    if paired:
        grad_channel, cot, pre_mine, cot_other, pre_spare = channel_stage(
            cot_low, channel_value_weight, channel_key_weight, active
        )
        channel_other, pre_other = beside(channel), beside(pre_spare)
    else:
        cot = gather_near(cot_low)
        grad_pre = (dot(cot, channel_value_weight, NT) * 2.0 * active).astype(BF16)
        grad_channel = near_sum(dot(grad_pre, channel_key_weight))
    if paired:
        value_part = (
            dot(quartered(hidden_mine), cot, TN) + dot(quartered(hidden_other), cot_other, TN)
        ).astype(BF16)
    else:
        value_part = dot(hidden_rows, cot, TN).astype(BF16)
    result_back, grad_channel, value_part = lax.optimization_barrier((result_back, grad_channel, value_part))
    output = dot(arrange, result_back.reshape(rows, width), TN).astype(BF16)
    grad_vec_mix_two = jnp.sum(grad_channel * delta_two, 0)
    shifted = grad_channel * vectors[:, 18] * own_flowing
    behind = from_behind(shifted[:1], "seq", -1)
    grad_normed_two = grad_channel * (1.0 - vectors[:, 18]) + jnp.concatenate([shifted[1:], behind], 0)
    grad_residual = cotangent + norm_back(grad_normed_two, standard_two, scale_two, vectors[:, 16])
    grad_low = grad_residual.astype(BF16)

    grad_posted = dot(grad_low, w_out, NT).astype(BF16)
    grad_heads = deal(grad_posted, True)
    grad_heads, mixed_late = lax.optimization_barrier((grad_heads, mixed_rows))
    lefts = exchange(mixed_late.reshape(rows, seqs, parts, piece).transpose(2, 0, 1, 3), "wsh")
    near_grad = (swap(grad_low, 1), swap(grad_low, 2)) if near else gather_near(grad_low)
    recept_low, keys_low, values_low, ups_low, grad_first, grad_vec_heads = run_backward(grad_heads, *inputs, saved)
    if paired:
        channel_other, pre_mine, pre_other, lefts, near_grad, recept_low = lax.optimization_barrier(
            (channel_other, pre_mine, pre_other, lefts, near_grad, recept_low)
        )
        key_part = (
            dot(quartered(pre_mine), channel, TN) + dot(quartered(pre_other), channel_other, TN)
        ).astype(BF16)
    else:
        lefts, near_grad, recept_low = lax.optimization_barrier((lefts, near_grad, recept_low))
        key_part = dot(grad_pre, channel, TN).astype(BF16)
    if near:
        near_grad = gathered_near(grad_low, *near_grad)
        lefts = jnp.stack([lax.dynamic_index_in_dim(lefts, lax.axis_index("wsh") ^ k, 0, keepdims=False) for k in range(4)])
    out_part = dot(lefts.reshape(rows * parts, -1), near_grad, TN).astype(BF16)

    moved = exchange(dot(permute, grad_first, TN).astype(BF16).reshape(seqs, rows, own_width), "seq")
    recept_low, key_part, out_part = lax.optimization_barrier((recept_low, key_part, out_part))
    if paired:
        lines = [[0, 2, 4, 6], [1, 3, 5, 7]]
        def along(part):
            return lax.psum_scatter(part, "seq", scatter_dimension=0, tiled=True, axis_index_groups=lines)

        halves_out = out_part.reshape(seqs // 2, 2, piece, width)
        x_side = me % 2
        out_mine = lax.dynamic_index_in_dim(halves_out, x_side, 1, keepdims=False).astype(F32)
        out_other = beside(lax.dynamic_index_in_dim(halves_out, 1 - x_side, 1, keepdims=False))
        value_sum, key_sum = along(value_part), along(key_part)
    else:
        moves = [(s * parts + w, w * seqs + s) for s in range(seqs) for w in range(parts)]

        def ffn_grad(part):
            part = lax.psum_scatter(part, "seq", scatter_dimension=0, tiled=True)
            return lax.ppermute(part, ("seq", "wsh"), moves).astype(F32)

        grad_ffn_value, grad_ffn_key = ffn_grad(value_part), ffn_grad(key_part)
        grad_out = lax.psum_scatter(out_part, "seq", scatter_dimension=0, tiled=True)

    heads_part = lax.dynamic_update_slice_in_dim(jnp.zeros((width, 8), F32), grad_vec_heads.T, column, 0)
    vec_two = jnp.stack(
        [jnp.sum(grad_normed_two * standard_two, 0), jnp.sum(grad_normed_two, 0), grad_vec_mix_two], 1
    )
    others = jnp.concatenate([heads_part, jnp.pad(vec_two, ((0, 0), (0, 13)))], 1)
    scaled_grad, sums, wide, up_grad = run_unproject(
        balanced, stats, mix_vec, weights, others, (recept_low, keys_low, values_low), ups_low, hidden, downs, up, parts
    )
    if paired:
        moved, value_sum, out_other, scaled_grad, sums, wide, up_grad = lax.optimization_barrier(
            (moved, value_sum, out_other, scaled_grad, sums, wide, up_grad)
        )
        out_half = (out_mine + out_other.astype(F32)).astype(BF16).reshape(-1, width)
        out_half, sums = lax.optimization_barrier((out_half, sums))
        grad_out = along(out_half)
    else:
        moved, scaled_grad, sums, wide = lax.optimization_barrier((moved, scaled_grad, sums, wide))
    grad_first_rows = moved.transpose(1, 0, 2).reshape(rows, width)

    standard = (balanced.astype(F32) - mean) * scale_one
    grad_balanced = scale_one * (scaled_grad - sums[:, :1] * (1.0 / width) - standard * (sums[:, 1:] * (1.0 / width)))
    mine_rows = lax.dynamic_slice_in_dim(grad_balanced, me * rows, rows, 0) + grad_residual
    grad_balanced = lax.dynamic_update_slice_in_dim(grad_balanced, mine_rows, me * rows, 0)
    grad_given = dot(permute, grad_balanced.astype(BF16), TN).astype(BF16).reshape(seqs, rows, width)
    if near:
        kept_part, far = block_halves(wide)
        kept_up, far_up = block_halves(up_grad.reshape(parts, piece, WIDE))
        grad_given, far, far_up = lax.optimization_barrier((grad_given, far, far_up))
        wide_part, across_up = kept_part + swap(far, 2).astype(F32), swap(far_up, 2)
    else:
        wide_part = block_sum(wide)
    if paired:
        grad_tokens, value_all = reduce_seq(grad_given, value_sum.reshape(4, -1, width))
        wide_part, grad_tokens, grad_out, key_sum, across_up = lax.optimization_barrier(
            (wide_part, grad_tokens, grad_out, key_sum, across_up)
        )
        wide_all, key_all = finish(wide_part.astype(BF16), key_sum.reshape(4, -1, width))
        wide_all = wide_all.astype(F32)
        grad_ffn_key, grad_ffn_value = [x.reshape(-1, width).astype(F32) for x in (key_all, value_all)]
    else:
        grad_tokens = jnp.sum(exchange(grad_given, "seq").astype(F32), 0)
        wide_all = exchange(wide_part.astype(BF16), "seq").astype(F32)

    def square(at):
        taken = wide_all[:, :, at * own_width : (at + 1) * own_width]
        return taken.transpose(1, 0, 2).reshape(piece, width)

    narrow = jnp.sum(wide_all[:, :, 3 * own_width :], 0)
    grad_down = unpad_ranks(narrow)
    grad_vectors = narrow[:, RANKS[0] : RANKS[0] + vectors.shape[1]]
    up_part = unpad_ranks(kept_up + across_up.astype(F32) if near else block_sum(up_grad.reshape(parts, piece, WIDE)))

    return (
        output, grad_tokens.astype(BF16), grad_first_rows,
        square(0), square(1), square(2),
        grad_out.astype(F32), grad_down, up_part,
        grad_ffn_key, grad_ffn_value, grad_vectors,
    )


def solution(mesh):
    both, shard = P(("seq", "wsh"), None), P("wsh", None)
    flat = P(("seq", "wsh"))
    return jax.shard_map(
        local,
        mesh=mesh,
        in_specs=(both, both, both, flat, flat) + (shard,) * 9 + (P(),),
        out_specs=(both,) * 12,
        check_vma=False,
    )
```

```python
import functools

import jax
import jax.numpy as jnp
from jax import lax
from jax.experimental import pallas as pl
from jax.experimental.pallas import tpu as pltpu
from jax.sharding import PartitionSpec as P

HEAD = 64
BLOCK = 64
RANKS = (96, 96, 64, 256)
PADDED = (128, 128, 128, 256)
OFFSETS = (0, 128, 256, 384)
WIDE = 640
EXTRA = 128
DIGIT = 64

F32 = jnp.float32
BF16 = jnp.bfloat16

NN = (((1,), (0,)), ((), ()))
NT = (((1,), (1,)), ((), ()))
TN = (((0,), (0,)), ((), ()))


def dot(a, b, dims=NN):
    return lax.dot_general(a, b, dims, preferred_element_type=F32)


def halves(x):
    high = x.astype(BF16)
    return high, (x - high.astype(F32)).astype(BF16)


def dot3(a, b, dims=NN):
    a_high, a_low = halves(a)
    b_high, b_low = halves(b)
    return dot(a_high, b_high, dims) + (dot(a_high, b_low, dims) + dot(a_low, b_high, dims))


def sum_left(mask, x):
    high, low = halves(x)
    low_two = (x - high.astype(F32) - low.astype(F32)).astype(BF16)
    return dot(mask, high) + (dot(mask, low) + dot(mask, low_two))


def head_sum(x, ones):
    high, low = halves(x)
    return dot(high, ones) + dot(low, ones)


def low(x):
    return x.astype(BF16).astype(F32)


def iotas(rows, columns):
    return (
        lax.broadcasted_iota(jnp.int32, (rows, columns), 0),
        lax.broadcasted_iota(jnp.int32, (rows, columns), 1),
    )


def head_ones(width):
    i, j = iotas(width, width)
    return jnp.where((i >> 6) == (j >> 6), 1.0, 0.0).astype(BF16)


def front(keys, values, hidden, up, first, vec, ones):
    z = vec[0:1] + dot(hidden[:, 0:128], up[0:128])
    decay_log = -(jnp.maximum(-z, 0.0) + jnp.log1p(jnp.exp(-jnp.abs(z)))) - 0.5
    rate = jax.nn.sigmoid(vec[1:2] + dot(hidden[:, 128:256], up[128:256]))
    blend = jax.nn.sigmoid(vec[2:3] + dot(hidden[:, 256:384], up[256:384]))
    gate = dot(hidden[:, 384:640], up[384:640])
    mixed_value = values + (first - values) * blend
    scaled = keys * vec[3:4]
    scale = lax.rsqrt(head_sum(scaled * scaled, ones) + 1e-06)
    key_dir = scaled * scale
    key_mod = keys * (1.0 + (rate - 1.0) * vec[4:5])
    return z, decay_log, rate, blend, gate, mixed_value, scale, key_dir, key_mod


def block_masks(segments):
    i, j = iotas(BLOCK, BLOCK)
    across = jnp.broadcast_to(segments[0:1], (BLOCK, BLOCK))
    down = across.T
    before = jnp.broadcast_to(segments[1:2], (BLOCK, BLOCK))
    last = jnp.broadcast_to(segments[2:3], (BLOCK, BLOCK))
    same = across == down
    strict = jnp.where(same & (i > j), 1.0, 0.0)
    closed = jnp.where(same & (i >= j), 1.0, 0.0)
    carry = jnp.where(down == before, 1.0, 0.0)
    tail = jnp.where(down == last, 1.0, 0.0)
    keep = jnp.where(segments[2:3] == segments[1:2], 1.0, 0.0)
    quad = jnp.concatenate(
        [jnp.concatenate([strict, strict], 1), jnp.concatenate([closed, closed], 1)], 0
    )
    return quad, carry, tail, keep


def tile_heads(x, heads):
    return jnp.concatenate([x] * heads, 1) if heads > 1 else x


def join(pieces, axis):
    return jnp.concatenate(pieces, axis) if len(pieces) > 1 else pieces[0]


def decayed(decay_low, key_low, dir_low, rate_low, recept_low, carry, tail):
    i, j = iotas(BLOCK, BLOCK)
    lower = jnp.where(i >= j, 1.0, 0.0).astype(BF16)
    log_step = -jnp.exp(decay_low)
    total = sum_left(lower, log_step)
    before = jnp.exp(total - log_step)
    grown = jnp.exp(total)
    shrunk = jnp.exp(-total)
    end = total[BLOCK - 1 : BLOCK]
    tail_decay = jnp.exp(end - total) * tail
    alpha = -dir_low * before
    beta_plain = dir_low * rate_low
    beta = beta_plain * shrunk
    key = key_low * shrunk
    recept = recept_low * grown
    return dict(
        log_step=log_step, before=before, grown=grown, shrunk=shrunk, end=jnp.exp(end), tail=tail_decay,
        alpha=alpha, beta_plain=beta_plain, beta=beta, key=key, recept=recept,
        beta_end=beta_plain * tail_decay, key_end=key_low * tail_decay,
        alpha_in=alpha * carry, recept_in=recept * carry,
    )


def unit_inverses(lowers):
    i, j = iotas(BLOCK, BLOCK)
    eye = jnp.where(i == j, 1.0, 0.0)

    def within(size):
        return (i // size) == (j // size)

    smalls = [jnp.where(within(4), x, 0.0) for x in lowers]
    low_smalls = [x.astype(BF16) for x in smalls]
    twos = [dot(x, x) for x in low_smalls]
    inverses = [eye + x for x in smalls]
    inverses = [x + dot(x.astype(BF16), y.astype(BF16)) for x, y in zip(inverses, twos)]
    for size in (8, 16, 32, 64):
        mask = within(size) & ~within(size // 2)
        offs = [jnp.where(mask, x, 0.0).astype(BF16) for x in lowers]
        lows = [x.astype(BF16) for x in inverses]
        inner = [dot(x, y).astype(BF16) for x, y in zip(offs, lows)]
        inverses = [x + dot(y, z) for x, y, z in zip(inverses, lows, inner)]
    errors = [eye - x + dot3(y, x) for x, y in zip(inverses, lowers)]
    return [x + dot(x.astype(BF16), y.astype(BF16)) for x, y in zip(inverses, errors)]


def post_norm(head_low, ones):
    centered = head_low - head_sum(head_low, ones) * (1.0 / HEAD)
    spread = lax.rsqrt(head_sum(centered * centered, ones) * (1.0 / HEAD) + HEAD * 1e-05)
    return centered * spread, spread


def forward_kernel(
    count, recept_ref, keys_ref, values_ref, hidden_ref, first_ref, up_ref, vec_ref, segment_ref,
    mixed_ref, head_ref, state_ref, inverse_ref, removed_ref, state,
):
    width = recept_ref.shape[1]
    heads = width // HEAD

    @pl.when(pl.program_id(0) == 0)
    def _():
        state[...] = jnp.zeros_like(state)

    ones = head_ones(width)
    vec = vec_ref[...]
    up = up_ref[...]
    columns = [slice(head * HEAD, (head + 1) * HEAD) for head in range(heads)]
    done = []
    for block in range(count):
        rows = slice(block * BLOCK, (block + 1) * BLOCK)
        recept, keys, values = recept_ref[rows], keys_ref[rows], values_ref[rows]
        _, decay_log, rate, _, gate, mixed_value, _, key_dir, key_mod = front(
            keys, values, hidden_ref[rows], up, first_ref[rows].astype(F32), vec, ones
        )
        quad, carry, tail, keep = block_masks(segment_ref[block * 8 : block * 8 + 8])
        parts = decayed(
            low(decay_log), low(key_mod), low(key_dir), low(rate), low(recept),
            tile_heads(carry, heads), tile_heads(tail, heads),
        )
        lefts = [jnp.concatenate([parts["alpha"][:, c], parts["recept"][:, c]], 0) for c in columns]
        rights = [jnp.concatenate([parts["beta"][:, c], parts["key"][:, c]], 0) for c in columns]
        pairs = [quad * dot3(x, y, NT) for x, y in zip(lefts, rights)]
        done.append((rows, recept, key_mod, gate, mixed_value, keep, parts, pairs))
    inverses = unit_inverses([x[:BLOCK, :BLOCK] for item in done for x in item[-1]])
    for block, (rows, recept, key_mod, gate, mixed_value, keep, parts, pairs) in enumerate(done):
        mine = inverses[block * heads : (block + 1) * heads]
        value_low = low(mixed_value)
        owns = [value_low[:, c] for c in columns]
        by_values = [dot3(x[:, BLOCK:], y) for x, y in zip(pairs, owns)]
        ends = [jnp.concatenate([parts["beta_end"][:, c], parts["key_end"][:, c]], 0) for c in columns]
        inners = [jnp.concatenate([parts["alpha_in"][:, c], parts["recept_in"][:, c]], 0) for c in columns]
        entering = state[...]
        state_ref[rows] = entering
        nows = [entering[:, c] for c in columns]
        inwards = [dot3(x, y, NT) for x, y in zip(inners, nows)]
        removals = [dot3(x, y[:BLOCK] + z[:BLOCK]) for x, y, z in zip(mine, inwards, by_values)]
        outs = [
            y[BLOCK:] + z[BLOCK:] + dot3(x[BLOCK:, :BLOCK], r)
            for x, y, z, r in zip(pairs, inwards, by_values, removals)
        ]
        leaving = [
            x * (parts["end"][:, c] * keep) + dot3(jnp.concatenate([r, v], 0), e, TN)
            for x, c, r, v, e in zip(nows, columns, removals, owns, ends)
        ]
        state[...] = join(leaving, 1)
        inverse_ref[rows] = join(mine, 1)
        removed_ref[rows] = join(removals, 1)
        head_low = join(outs, 1).astype(BF16)
        head_ref[rows] = head_low
        normed, _ = post_norm(head_low.astype(F32), ones)
        bonus = head_sum(recept * key_mod * vec[5:6], ones) * mixed_value
        mixed_ref[rows] = ((normed * vec[6:7] + vec[7:8] + bonus) * gate).astype(BF16)


def backward_kernel(
    count, grad_ref, recept_ref, keys_ref, values_ref, hidden_ref, first_ref, up_ref, vec_ref, segment_ref,
    head_ref, state_ref, inverse_ref, removed_ref,
    recept_out, keys_out, values_out, ups_out, first_out, vec_out, state,
):
    width = recept_ref.shape[1]
    heads = width // HEAD

    @pl.when(pl.program_id(0) == 0)
    def _():
        state[...] = jnp.zeros_like(state)
        vec_out[...] = jnp.zeros_like(vec_out)

    ones = head_ones(width)
    vec = vec_ref[...]
    up = up_ref[...]
    i, j = iotas(BLOCK, BLOCK)
    upper = jnp.where(i <= j, 1.0, 0.0).astype(BF16)
    columns = [slice(head * HEAD, (head + 1) * HEAD) for head in range(heads)]
    order = range(count - 1, -1, -1)
    kept = {}
    for block in order:
        rows = slice(block * BLOCK, (block + 1) * BLOCK)
        recept, keys, values = recept_ref[rows], keys_ref[rows], values_ref[rows]
        first = first_ref[rows].astype(F32)
        z, decay_log, rate, blend, gate, mixed_value, scale, key_dir, key_mod = front(
            keys, values, hidden_ref[rows], up, first, vec, ones
        )
        quad, carry, tail, keep = block_masks(segment_ref[block * 8 : block * 8 + 8])
        rate_low, dir_low = low(rate), low(key_dir)
        parts = decayed(
            low(decay_log), low(key_mod), dir_low, rate_low, low(recept),
            tile_heads(carry, heads), tile_heads(tail, heads),
        )
        value_low = low(mixed_value)

        grad = grad_ref[rows].astype(F32)
        normed, spread = post_norm(head_ref[rows].astype(F32), ones)
        product = recept * key_mod
        coefficient = head_sum(product * vec[5:6], ones)
        grad_gate = grad * (normed * vec[6:7] + vec[7:8] + coefficient * mixed_value)
        opened = grad * gate
        grad_normed = opened * vec[6:7]
        grad_head = spread * (
            grad_normed
            - head_sum(grad_normed, ones) * (1.0 / HEAD)
            - normed * (head_sum(grad_normed * normed, ones) * (1.0 / HEAD))
        )
        grad_coefficient = head_sum(opened * mixed_value, ones)
        weighted = grad_coefficient * vec[5:6]
        head_grad = low(grad_head)

        lefts = [jnp.concatenate([parts["alpha"][:, c], parts["recept"][:, c]], 0) for c in columns]
        rights = [jnp.concatenate([parts["beta"][:, c], parts["key"][:, c]], 0) for c in columns]
        ends = [jnp.concatenate([parts["beta_end"][:, c], parts["key_end"][:, c]], 0) for c in columns]
        inners = [jnp.concatenate([parts["alpha_in"][:, c], parts["recept_in"][:, c]], 0) for c in columns]
        pairs = [quad * dot3(x, y, NT) for x, y in zip(lefts, rights)]
        out_grads = [head_grad[:, c] for c in columns]
        through = [dot3(x[BLOCK:, :BLOCK], y, TN) for x, y in zip(pairs, out_grads)]
        kept[block] = dict(
            rows=rows, recept=recept, keys=keys, values=values, first=first, z=z, rate=rate, blend=blend,
            mixed_value=mixed_value, scale=scale, key_dir=key_dir, key_mod=key_mod, quad=quad, carry=carry, keep=keep,
            rate_low=rate_low, dir_low=dir_low, parts=parts, value_low=value_low, normed=normed, product=product,
            grad_gate=grad_gate, opened=opened, grad_coefficient=grad_coefficient,
            grad_mixed_value=opened * coefficient, grad_recept=weighted * key_mod, grad_key_mod=weighted * recept,
            lefts=lefts, rights=rights, ends=ends, inners=inners, pairs=pairs, out_grads=out_grads, through=through,
        )
    for block in order:
        k = kept[block]
        after, entering, inverse_all = state[...], state_ref[k["rows"]], inverse_ref[k["rows"]]
        laters, nows = [after[:, c] for c in columns], [entering[:, c] for c in columns]
        from_ends = [dot3(x, y, NT) for x, y in zip(k["ends"], laters)]
        inner_grads = [
            dot3(inverse_all[:, c], x + y[:BLOCK], TN) for c, x, y in zip(columns, k["through"], from_ends)
        ]
        boths = [jnp.concatenate([x, y], 0) for x, y in zip(inner_grads, k["out_grads"])]
        stays = [x * (k["parts"]["end"][:, c] * k["keep"]) for x, c in zip(laters, columns)]
        state[...] = join([x + dot3(y, z, TN) for x, y, z in zip(stays, boths, k["inners"])], 1)
        k.update(
            laters=laters, nows=nows, from_ends=from_ends, boths=boths,
            end_sum=join([jnp.sum(x * y, 0, keepdims=True) for x, y in zip(nows, stays)], 1),
        )
    vec_total = jnp.zeros_like(vec)
    for block in order:
        k = kept[block]
        rows, parts, quad = k["rows"], k["parts"], k["quad"]
        removed_all = removed_ref[rows]
        carry_two = jnp.concatenate([k["carry"], k["carry"]], 0)
        sources = [jnp.concatenate([removed_all[:, c], k["value_low"][:, c]], 0) for c in columns]
        grad_pairs = [quad * dot3(x, y, NT) for x, y in zip(k["boths"], sources)]
        grad_values = [
            dot3(x[:, BLOCK:], y, TN) + z[BLOCK:] for x, y, z in zip(k["pairs"], k["boths"], k["from_ends"])
        ]
        grad_ends = [dot3(x, y) for x, y in zip(sources, k["laters"])]
        to_state = [carry_two * dot3(x, y) for x, y in zip(k["boths"], k["nows"])]
        grad_lefts = [dot3(x, y) + z for x, y, z in zip(grad_pairs, k["rights"], to_state)]
        grad_rights = [dot3(x, y, TN) for x, y in zip(grad_pairs, k["lefts"])]
        d_alpha, d_recept = join([x[:BLOCK] for x in grad_lefts], 1), join([x[BLOCK:] for x in grad_lefts], 1)
        d_beta, d_key = join([x[:BLOCK] for x in grad_rights], 1), join([x[BLOCK:] for x in grad_rights], 1)
        d_beta_end, d_key_end = join([x[:BLOCK] for x in grad_ends], 1), join([x[BLOCK:] for x in grad_ends], 1)
        ended = parts["beta_end"] * d_beta_end + parts["key_end"] * d_key_end
        alphas = parts["alpha"] * d_alpha
        d_total = parts["recept"] * d_recept - parts["beta"] * d_beta - parts["key"] * d_key - ended + alphas
        d_step = sum_left(upper, d_total) + (jnp.sum(ended, 0, keepdims=True) + k["end_sum"]) - alphas
        d_beta_plain = d_beta * parts["shrunk"] + d_beta_end * parts["tail"]
        copy_decay = low(d_step * parts["log_step"])
        copy_dir = low(d_beta_plain * k["rate_low"] - d_alpha * parts["before"])
        copy_rate = low(d_beta_plain * k["dir_low"])

        keys, values, rate, blend = k["keys"], k["values"], k["rate"], k["blend"]
        grad_recept = k["grad_recept"] + low(d_recept * parts["grown"])
        grad_key_mod = k["grad_key_mod"] + low(d_key * parts["shrunk"] + d_key_end * parts["tail"])
        grad_mixed_value = k["grad_mixed_value"] + low(join(grad_values, 1))
        grad_z = copy_decay * jax.nn.sigmoid(-k["z"])
        factor = 1.0 + (rate - 1.0) * vec[4:5]
        keyed = grad_key_mod * keys
        grad_rate = copy_rate + keyed * vec[4:5]
        grad_scaled = k["scale"] * (copy_dir - k["key_dir"] * head_sum(copy_dir * k["key_dir"], ones))
        grad_keys = grad_key_mod * factor + grad_scaled * vec[3:4]
        grad_rate_up = grad_rate * rate * (1.0 - rate)
        grad_value_up = grad_mixed_value * (k["first"] - values) * blend * (1.0 - blend)
        recept_out[rows] = grad_recept.astype(BF16)
        keys_out[rows] = grad_keys.astype(BF16)
        values_out[rows] = (grad_mixed_value * (1.0 - blend)).astype(BF16)
        first_out[rows] = (grad_mixed_value * blend).astype(BF16)
        ups_out[0, rows] = grad_z.astype(BF16)
        ups_out[1, rows] = grad_rate_up.astype(BF16)
        ups_out[2, rows] = grad_value_up.astype(BF16)
        ups_out[3, rows] = k["grad_gate"].astype(BF16)

        def total(x):
            return jnp.sum(x, 0, keepdims=True)

        vec_total = vec_total + jnp.concatenate(
            [
                total(grad_z), total(grad_rate_up), total(grad_value_up), total(grad_scaled * keys),
                total(keyed * (rate - 1.0)), total(k["grad_coefficient"] * k["product"]),
                total(k["opened"] * k["normed"]), total(k["opened"]),
            ],
            0,
        )
    vec_out[...] += vec_total


def kernel_cost(rows, width, passes):
    return pl.CostEstimate(flops=2 * rows * width * width, bytes_accessed=4 * rows * width * passes, transcendentals=0)


def per_step(rows, most):
    return most if (rows // BLOCK) % most == 0 else 1


def run_forward(recept, keys, values, hidden, first, up, vec, segments):
    rows, width = recept.shape
    count = per_step(rows, 4)
    step = count * BLOCK

    def spec(columns):
        return pl.BlockSpec((step, columns), lambda i: (i, 0))

    def whole(array):
        return pl.BlockSpec(array.shape, lambda i: (0, 0))

    return pl.pallas_call(
        functools.partial(forward_kernel, count),
        grid=(rows // step,),
        in_specs=[
            spec(width), spec(width), spec(width), spec(WIDE), spec(width), whole(up), whole(vec),
            pl.BlockSpec((count * 8, BLOCK), lambda i: (i, 0)),
        ],
        out_specs=[spec(width)] * 5,
        out_shape=[jax.ShapeDtypeStruct((rows, width), d) for d in (BF16, BF16, F32, F32, F32)],
        scratch_shapes=[pltpu.VMEM((BLOCK, width), F32)],
        compiler_params=pltpu.CompilerParams(vmem_limit_bytes=48 << 20),
        cost_estimate=kernel_cost(rows, width, 110),
        name="mix_forward",
    )(recept, keys, values, hidden, first, up, vec, segments)


def run_backward(grad, recept, keys, values, hidden, first, up, vec, segments, saved):
    rows, width = recept.shape
    count = per_step(rows, 2)
    step = count * BLOCK
    last = rows // step - 1

    def spec(columns):
        return pl.BlockSpec((step, columns), lambda i: (last - i, 0))

    def whole(array):
        return pl.BlockSpec(array.shape, lambda i: (0, 0))

    return pl.pallas_call(
        functools.partial(backward_kernel, count),
        grid=(rows // step,),
        in_specs=[
            spec(width), spec(width), spec(width), spec(width), spec(WIDE), spec(width), whole(up), whole(vec),
            pl.BlockSpec((count * 8, BLOCK), lambda i: (last - i, 0)),
            spec(width), spec(width), spec(width), spec(width),
        ],
        out_specs=[
            spec(width), spec(width), spec(width),
            pl.BlockSpec((4, step, width), lambda i: (0, last - i, 0)),
            spec(width), pl.BlockSpec((8, width), lambda i: (0, 0)),
        ],
        out_shape=[
            jax.ShapeDtypeStruct((rows, width), BF16), jax.ShapeDtypeStruct((rows, width), BF16),
            jax.ShapeDtypeStruct((rows, width), BF16), jax.ShapeDtypeStruct((4, rows, width), BF16),
            jax.ShapeDtypeStruct((rows, width), BF16), jax.ShapeDtypeStruct((8, width), F32),
        ],
        scratch_shapes=[pltpu.VMEM((BLOCK, width), F32)],
        compiler_params=pltpu.CompilerParams(vmem_limit_bytes=48 << 20),
        cost_estimate=kernel_cost(rows, width, 150),
        name="mix_backward",
    )(grad, recept, keys, values, hidden, first, up, vec, segments, *saved)


def mix_norm(block_ref, stats_ref, vec_ref):
    stats = stats_ref[...]
    flowing = stats[:, 2:3]
    standard = (block_ref[...].astype(F32) - stats[:, 0:1]) * stats[:, 1:2]
    normed = standard * vec_ref[0:1] + vec_ref[1:2]
    delta = pltpu.roll(normed, 1, 0) * flowing - normed
    return standard, normed, delta, flowing


def project_kernel(
    width, block_ref, stats_ref, vec_ref, weight_ref,
    recept_ref, keys_ref, values_ref, downs_ref, hidden_ref,
):
    base = 3 * width
    _, normed, delta, _ = mix_norm(block_ref, stats_ref, vec_ref)
    weight = weight_ref[...]
    uses = (
        ((recept_ref, 0, width, 0),),
        ((downs_ref, base + OFFSETS[0], PADDED[0], OFFSETS[0]),),
        ((keys_ref, width, width, 0),),
        ((values_ref, 2 * width, width, 0), (downs_ref, base + OFFSETS[2], PADDED[2], OFFSETS[2])),
        ((downs_ref, base + OFFSETS[1], PADDED[1], OFFSETS[1]),),
        ((downs_ref, base + OFFSETS[3], PADDED[3], OFFSETS[3]),),
    )

    @pl.when(pl.program_id(0) == 0)
    def _():
        for ref in (recept_ref, keys_ref, values_ref, downs_ref):
            ref[...] = jnp.zeros_like(ref)

    for c, targets in enumerate(uses):
        mixed = (normed + delta * vec_ref[2 + c : 3 + c]).astype(BF16)
        for ref, start, size, at in targets:
            ref[:, at : at + size] += dot(mixed, weight[:, start : start + size])

    @pl.when(pl.program_id(0) == pl.num_programs(0) - 1)
    def _():
        hidden_ref[:, 0:128] = jnp.tanh(downs_ref[:, 0:128]).astype(BF16)
        hidden_ref[:, 128:384] = downs_ref[:, 128:384].astype(BF16)
        hidden_ref[:, 384:640] = jax.nn.sigmoid(downs_ref[:, 384:640]).astype(BF16)


def unproject_kernel(
    width, parts, piece, block_ref, stats_ref, vec_ref, weight_ref,
    other_ref, recept_ref, keys_ref, values_ref, ups_ref, hidden_ref, downs_ref, up_ref,
    grad_ref, sums_ref, wide_ref, up_out, down_lows,
):
    rows = block_ref.shape[0]
    base = 3 * width

    @pl.when(pl.program_id(0) == 0)
    def _():
        sums_ref[...] = jnp.zeros_like(sums_ref)
        for k, (at, size) in enumerate(zip(OFFSETS, PADDED)):
            cols = slice(at, at + size)
            grad = dot(ups_ref[k], up_ref[cols], NT)
            if k == 0:
                grad = grad * (1.0 - jnp.square(jnp.tanh(downs_ref[:, cols])))
            if k == 3:
                opening = jax.nn.sigmoid(downs_ref[:, cols])
                grad = grad * opening * (1.0 - opening)
            down_lows[:, cols] = grad.astype(BF16)
            up_out[:, cols] = dot(ups_ref[k], hidden_ref[:, cols], TN).astype(BF16)

    standard, normed, delta, flowing = mix_norm(block_ref, stats_ref, vec_ref)
    weight = weight_ref[...]

    def down(k):
        return (down_lows[:, OFFSETS[k] : OFFSETS[k] + PADDED[k]], base + OFFSETS[k], PADDED[k])

    uses = (
        ((recept_ref[...], 0, width),),
        (down(0),),
        ((keys_ref[...], width, width),),
        ((values_ref[...], 2 * width, width), down(2)),
        (down(1),),
        (down(3),),
    )
    kept, sent, vec_rows = None, None, []
    per_seq = parts * piece
    for c, sources in enumerate(uses):
        share = vec_ref[2 + c : 3 + c]
        mixed = (normed + delta * share).astype(BF16)
        grad = None
        for source, start, size in sources:
            part = dot(source, weight[:, start : start + size], NT)
            grad = part if grad is None else grad + part
            product = dot(mixed, source, TN).astype(BF16)
            for number in range(product.shape[0] // per_seq):
                for w in range(parts):
                    at = number * per_seq + w * piece
                    wide_ref[w, number, :, start : start + size] = product[at : at + piece]
        vec_rows.append(jnp.sum(grad * delta, 0, keepdims=True))
        moved = grad * share
        kept = grad - moved if kept is None else kept + (grad - moved)
        sent = moved if sent is None else sent + moved
    grad = kept + pltpu.roll(sent * flowing, rows - 1, 0)
    vec_rows = jnp.concatenate(
        [jnp.sum(grad * standard, 0, keepdims=True), jnp.sum(grad, 0, keepdims=True)] + vec_rows, 0
    )
    spare = jnp.concatenate([vec_rows.T, other_ref[...]], 1).astype(BF16)
    for number in range(spare.shape[0] // per_seq):
        for w in range(parts):
            at = number * per_seq + w * piece
            wide_ref[w, number, :, base + RANKS[0] : base + PADDED[0]] = spare[at : at + piece]
    scaled = grad * vec_ref[0:1]
    sums_ref[:, 0:1] += jnp.sum(scaled, 1, keepdims=True)
    sums_ref[:, 1:2] += jnp.sum(scaled * standard, 1, keepdims=True)
    grad_ref[...] = scaled


def mix_specs(rows, width, own_width, parts):
    block = 256 if rows <= 1024 else 128

    def columns(height):
        return pl.BlockSpec((height, block), lambda j: (0, j))

    def whole(shape):
        return pl.BlockSpec(shape, lambda j: (0,) * len(shape))

    def weights(array):
        size = array.shape[1] if rows > 1024 else 3 * own_width + WIDE
        return pl.BlockSpec((block, size), lambda j: (j, 0))

    return block, columns, whole, weights


def run_project(balanced, stats, vec, weights, own_width, parts):
    rows, width = balanced.shape
    block, columns, whole, weight_spec = mix_specs(rows, width, own_width, parts)
    shapes = [(rows, own_width)] * 3 + [(rows, WIDE)] * 2
    return pl.pallas_call(
        functools.partial(project_kernel, own_width),
        grid_spec=pltpu.PrefetchScalarGridSpec(
            num_scalar_prefetch=0,
            grid=(width // block,),
            in_specs=[columns(rows), whole(stats.shape), columns(8), weight_spec(weights)],
            out_specs=[whole(s) for s in shapes],
        ),
        out_shape=[jax.ShapeDtypeStruct(s, d) for s, d in zip(shapes, (F32, F32, F32, F32, BF16))],
        compiler_params=pltpu.CompilerParams(vmem_limit_bytes=60 << 20),
        cost_estimate=kernel_cost(rows, own_width, 60),
        name="mix_project",
    )(balanced, stats, vec, weights)


def run_unproject(balanced, stats, vec, weights, others, lows, ups, hidden, downs, up, parts):
    rows, width = balanced.shape
    own_width = lows[0].shape[1]
    seqs = width // own_width
    piece = own_width // parts
    block, columns, whole, weight_spec = mix_specs(rows, width, own_width, parts)
    taken = block // own_width
    total = 3 * own_width + WIDE
    return pl.pallas_call(
        functools.partial(unproject_kernel, own_width, parts, piece),
        grid_spec=pltpu.PrefetchScalarGridSpec(
            num_scalar_prefetch=0,
            grid=(width // block,),
            in_specs=[
                columns(rows), whole(stats.shape), columns(8), weight_spec(weights),
                pl.BlockSpec((block, others.shape[1]), lambda j: (j, 0)),
            ]
            + [whole(a.shape) for a in (*lows, ups, hidden, downs, up)],
            out_specs=[
                columns(rows), whole((rows, 2)),
                pl.BlockSpec((parts, taken, piece, total), lambda j: (0, j, 0, 0)),
                whole((own_width, WIDE)),
            ],
            scratch_shapes=[pltpu.VMEM((rows, WIDE), BF16)],
        ),
        out_shape=[
            jax.ShapeDtypeStruct((rows, width), F32), jax.ShapeDtypeStruct((rows, 2), F32),
            jax.ShapeDtypeStruct((parts, seqs, piece, total), BF16),
            jax.ShapeDtypeStruct((own_width, WIDE), BF16),
        ],
        compiler_params=pltpu.CompilerParams(vmem_limit_bytes=60 << 20),
        cost_estimate=kernel_cost(rows, own_width, 120),
        name="mix_unproject",
    )(balanced, stats, vec, weights, others, *lows, ups, hidden, downs, up)


def norm_stats(values):
    centered = values - jnp.mean(values, -1, keepdims=True)
    scale = lax.rsqrt(jnp.mean(centered * centered, -1, keepdims=True) + 1e-05)
    return centered * scale, scale


def norm_back(grad, standard, scale, gain):
    scaled = grad * gain
    return scale * (
        scaled
        - jnp.mean(scaled, -1, keepdims=True)
        - standard * jnp.mean(scaled * standard, -1, keepdims=True)
    )


def pad_ranks(matrix):
    pieces, start = [], 0
    for rank, padded in zip(RANKS, PADDED):
        pieces.append(jnp.pad(matrix[:, start : start + rank], ((0, 0), (0, padded - rank))))
        start += rank
    return jnp.concatenate(pieces, 1)


def unpad_ranks(matrix):
    return jnp.concatenate([matrix[..., o : o + r] for o, r in zip(OFFSETS, RANKS)], -1)


MESH_ID = pl.DeviceIdType.MESH


def places():
    s, w = lax.axis_index("seq"), lax.axis_index("wsh")
    side = s % 2
    return s, w, side, s // 2, (s + 1 - 2 * side, w), (s, w + 1 - 2 * (w % 2)), (s, w + 2 - 4 * (w // 2))


def greet(neighbours, number):
    barrier = pltpu.get_barrier_semaphore()
    for there, device in neighbours:
        if there is None:
            pl.semaphore_signal(barrier, inc=1, device_id=device, device_id_type=MESH_ID)
        else:

            @pl.when(there)
            def _(device=device):
                pl.semaphore_signal(barrier, inc=1, device_id=device, device_id_type=MESH_ID)

    pl.semaphore_wait(barrier, number)


def send(source, target, send_sem, recv_sem, device):
    return pltpu.make_async_remote_copy(
        src_ref=source, dst_ref=target, send_sem=send_sem, recv_sem=recv_sem, device_id=device, device_id_type=MESH_ID
    )


def line_ends(z):
    return jnp.where(z > 0, 1, 0) + jnp.where(z < 3, 1, 0)


def gather_kernel(
    own_ref, tail_ref, weight_ref, out_ref, tails_ref, weights_ref,
    copy_sem, right_send, right_recv, left_send, left_recv, x_send, x_recv, c_send, c_recv, y_send, y_recv,
):
    s, w, side, z, x_device, core_device, y_device = places()
    up, down = (s + 2, w), (s - 2, w)
    across = w + 2 - 4 * (w // 2)
    kinds = ((own_ref, out_ref), (tail_ref, tails_ref))
    copies = [pltpu.make_async_copy(own, out.at[s], copy_sem.at[k]) for k, (own, out) in enumerate(kinds)]
    copies.append(pltpu.make_async_copy(weight_ref, weights_ref.at[w], copy_sem.at[2]))
    for copy in copies:
        copy.start()
    greet(((None, x_device), (None, core_device), (None, y_device), (z < 3, up), (z > 0, down)), 3 + line_ends(z))

    weight_y = send(weight_ref, weights_ref.at[w], y_send, y_recv, y_device)
    weight_core = send(weight_ref, weights_ref.at[w], c_send.at[0], c_recv.at[0], core_device)
    weight_on = send(weights_ref.at[across], weights_ref.at[across], c_send.at[1], c_recv.at[1], core_device)
    weight_y.start()
    weight_core.start()

    def to_right(j, k, source, number):
        return send(source, kinds[k][1].at[number], right_send.at[j, k], right_recv.at[j, k], up)

    def to_left(j, k, source, number):
        return send(source, kinds[k][1].at[number], left_send.at[j, k], left_recv.at[j, k], down)

    def to_x(at, k, source, number):
        return send(source, kinds[k][1].at[number], x_send.at[at, k], x_recv.at[at, k], x_device)

    for k, (own, _) in enumerate(kinds):

        @pl.when(z < 3)
        def _(k=k, own=own):
            to_right(0, k, own, s).start()

        @pl.when(z > 0)
        def _(k=k, own=own):
            to_left(0, k, own, s).start()

        to_x(z, k, own, s).start()
    for j in (1, 2, 3):
        lower, upper = s - 2 * j, s + 2 * j
        for k, (_, out) in enumerate(kinds):

            @pl.when(z >= j)
            def _(j=j, k=k, out=out, lower=lower):
                block = out.at[lower]
                to_right(j - 1, k, block, lower).wait_recv()

                @pl.when(z < 3)
                def _():
                    to_right(j, k, block, lower).start()

                to_x(z - j, k, block, lower).start()

            @pl.when(z + j <= 3)
            def _(j=j, k=k, out=out, upper=upper):
                block = out.at[upper]
                to_left(j - 1, k, block, upper).wait_recv()

                @pl.when(z > 0)
                def _():
                    to_left(j, k, block, upper).start()

                to_x(z + j, k, block, upper).start()

    weight_y.wait_recv()
    weight_on.start()
    for k, (own, _) in enumerate(kinds):
        for number in range(4):
            done = to_x(number, k, own, s)
            done.wait_send()
            done.wait_recv()
        for j in range(3):

            @pl.when((z >= j) & (z < 3))
            def _(j=j, k=k, own=own):
                to_right(j, k, own, s).wait_send()

            @pl.when((z + j <= 3) & (z > 0))
            def _(j=j, k=k, own=own):
                to_left(j, k, own, s).wait_send()

    weight_core.wait_recv()
    weight_on.wait_recv()
    for copy in (weight_y, weight_core, weight_on):
        copy.wait_send()
    for copy in copies:
        copy.wait()


def gather_first(own, tail, weight):
    seqs, parts = lax.axis_size("seq"), lax.axis_size("wsh")
    if seqs != 8 or parts != 4:
        return (
            lax.all_gather(own, "seq", axis=0, tiled=False),
            lax.all_gather(tail, "seq", axis=0, tiled=False),
            lax.all_gather(weight, "wsh", axis=0, tiled=False),
        )
    dma = pltpu.SemaphoreType.DMA
    given = ((seqs, own), (seqs, tail), (parts, weight))
    return pl.pallas_call(
        gather_kernel,
        in_specs=[pl.BlockSpec(memory_space=pltpu.VMEM)] * 3,
        out_specs=[pl.BlockSpec(memory_space=pl.ANY)] * 3,
        out_shape=[jax.ShapeDtypeStruct((n,) + x.shape, x.dtype) for n, x in given],
        scratch_shapes=[dma((3,))] + [dma((3, 2))] * 4 + [dma((4, 2))] * 2 + [dma((2,))] * 2 + [dma] * 2,
        compiler_params=pltpu.CompilerParams(collective_id=1, has_side_effects=True),
        cost_estimate=pl.CostEstimate(flops=0, bytes_accessed=100 << 20, transcendentals=0),
        name="gather_first",
    )(own, tail, weight)


def turning(x_ref, out_ref, send_sem, recv_sem):
    s, w, side, z, _, _, _ = places()
    home = z == w
    greetings = tuple(((source != z) | (z != w), (source * 2 + side, z)) for source in range(4))

    def copy(j):
        piece = (z + j) % 4
        return send(x_ref.at[piece], out_ref.at[z], send_sem.at[j], recv_sem.at[j], (w * 2 + side, piece))

    def start():
        for j in (3, 2, 1):
            copy(j).start()

        @pl.when(jnp.logical_not(home))
        def _():
            copy(0).start()

        @pl.when(home)
        def _():
            out_ref[z] = x_ref[z]

    def end():
        for j in range(1, 4):
            copy(j).wait_recv()
            copy(j).wait_send()

        @pl.when(jnp.logical_not(home))
        def _():
            copy(0).wait_recv()
            copy(0).wait_send()

    return greetings, jnp.where(home, 3, 4), start, end


def reduce_kernel(
    splits, x_ref, turn_ref, out_ref, turn_out, x_buf, right_buf, left_buf, right_out, left_out,
    x_send, x_recv, right_send, right_recv, left_send, left_recv, turn_send, turn_recv,
):
    s, w, side, z, x_device, _, _ = places()
    up, down = (s + 2, w), (s - 2, w)
    size = x_ref.shape[2] // splits
    columns = [slice(c * size, (c + 1) * size) for c in range(splits)]
    greetings, number, start_turn, end_turn = turning(turn_ref, turn_out, turn_send, turn_recv)
    greet(((None, x_device), (z < 3, up), (z > 0, down)) + greetings, 1 + line_ends(z) + number)

    def to_x(target, c):
        return send(
            x_ref.at[target * 2 + 1 - side, :, columns[c]], x_buf.at[target, :, columns[c]],
            x_send.at[target, c], x_recv.at[target, c], x_device,
        )

    def start_x(target):
        for c in range(splits):
            to_x(target, c).start()

    def to_right(k, c):
        return send(
            right_out.at[k - 1, :, columns[c]], right_buf.at[k - 1, :, columns[c]],
            right_send.at[k - 1, c], right_recv.at[k - 1, c], up,
        )

    def to_left(k, c):
        return send(
            left_out.at[k - 1, :, columns[c]], left_buf.at[k - 1, :, columns[c]],
            left_send.at[k - 1, c], left_recv.at[k - 1, c], down,
        )

    def pair(target, c):
        to_x(target, c).wait_recv()
        return x_ref[target * 2 + side, :, columns[c]].astype(F32) + x_buf[target, :, columns[c]].astype(F32)

    for k in (3, 2, 1):

        @pl.when(z + k <= 3)
        def _(k=k):
            start_x(z + k)

        @pl.when(z >= k)
        def _(k=k):
            start_x(z - k)

    start_x(z)
    start_turn()
    for k in (3, 2, 1):
        for c in range(splits):

            @pl.when(z + k <= 3)
            def _(k=k, c=c):
                right_out[k - 1, :, columns[c]] = pair(z + k, c).astype(BF16)
                if k < 3:

                    @pl.when(z > 0)
                    def _():
                        to_right(k + 1, c).wait_recv()
                        right_out[k - 1, :, columns[c]] = (
                            right_out[k - 1, :, columns[c]].astype(F32) + right_buf[k, :, columns[c]].astype(F32)
                        ).astype(BF16)

                to_right(k, c).start()

            @pl.when(z >= k)
            def _(k=k, c=c):
                left_out[k - 1, :, columns[c]] = pair(z - k, c).astype(BF16)
                if k < 3:

                    @pl.when(z < 3)
                    def _():
                        to_left(k + 1, c).wait_recv()
                        left_out[k - 1, :, columns[c]] = (
                            left_out[k - 1, :, columns[c]].astype(F32) + left_buf[k, :, columns[c]].astype(F32)
                        ).astype(BF16)

                to_left(k, c).start()

    for c in range(splits):
        out_ref[:, columns[c]] = pair(z, c)

        @pl.when(z > 0)
        def _(c=c):
            to_right(1, c).wait_recv()
            out_ref[:, columns[c]] += right_buf[0, :, columns[c]].astype(F32)

        @pl.when(z < 3)
        def _(c=c):
            to_left(1, c).wait_recv()
            out_ref[:, columns[c]] += left_buf[0, :, columns[c]].astype(F32)

    for c in range(splits):
        for target in range(4):
            to_x(target, c).wait_send()
        for k in (3, 2, 1):

            @pl.when(z + k <= 3)
            def _(k=k, c=c):
                to_right(k, c).wait_send()

            @pl.when(z >= k)
            def _(k=k, c=c):
                to_left(k, c).wait_send()

    end_turn()


def reduce_seq(x, turned):
    seqs, rows, width = x.shape
    splits = 2
    vmem = pl.BlockSpec(memory_space=pltpu.VMEM)
    dma = pltpu.SemaphoreType.DMA
    return pl.pallas_call(
        functools.partial(reduce_kernel, splits),
        in_specs=[vmem] * 2,
        out_specs=[vmem] * 2,
        out_shape=[jax.ShapeDtypeStruct((rows, width), F32), jax.ShapeDtypeStruct(turned.shape, turned.dtype)],
        scratch_shapes=[pltpu.VMEM((4, rows, width), BF16)]
        + [pltpu.VMEM((3, rows, width), BF16)] * 4
        + [dma((4, splits))] * 2 + [dma((3, splits))] * 4 + [dma((4,))] * 2,
        compiler_params=pltpu.CompilerParams(collective_id=2, has_side_effects=True, vmem_limit_bytes=40 << 20),
        cost_estimate=pl.CostEstimate(flops=0, bytes_accessed=1 << 20, transcendentals=0),
        name="reduce_seq",
    )(x, turned)


def finish_kernel(wide_ref, key_ref, wide_out, key_out, wide_send, wide_recv, key_send, key_recv):
    s, w, _, _, _, _, _ = places()
    greetings, number, start_turn, end_turn = turning(key_ref, key_out, key_send, key_recv)
    greet(tuple((None, ((s + d) % 8, w)) for d in range(1, 8)) + greetings, 7 + number)

    def wide(d):
        target = (s + d) % 8
        return send(wide_ref.at[target], wide_out.at[s], wide_send.at[d - 1], wide_recv.at[d - 1], (target, w))

    for d in (4, 3, 5, 2, 6, 1, 7):
        wide(d).start()
    start_turn()
    wide_out[s] = wide_ref[s]
    for d in range(1, 8):
        wide(d).wait_recv()
        wide(d).wait_send()
    end_turn()


def finish(wide, key):
    vmem = pl.BlockSpec(memory_space=pltpu.VMEM)
    dma = pltpu.SemaphoreType.DMA
    return pl.pallas_call(
        finish_kernel,
        in_specs=[vmem] * 2,
        out_specs=[vmem] * 2,
        out_shape=[jax.ShapeDtypeStruct(x.shape, x.dtype) for x in (wide, key)],
        scratch_shapes=[dma((7,)), dma((7,)), dma((4,)), dma((4,))],
        compiler_params=pltpu.CompilerParams(collective_id=5, has_side_effects=True, vmem_limit_bytes=24 << 20),
        cost_estimate=pl.CostEstimate(flops=0, bytes_accessed=100 << 20, transcendentals=0),
        name="finish",
    )(wide, key)


def deal_kernel(to_heads, x_ref, out_ref, send_sem, recv_sem):
    s, w, _, _, _, _, _ = places()
    tall, thin = (out_ref, x_ref) if to_heads else (x_ref, out_ref)
    columns, rows = tall.shape[1], thin.shape[0]

    def column(number):
        return pl.ds(pl.multiple_of(number * columns, columns), columns)

    def row(number):
        return pl.ds(pl.multiple_of(number * rows, rows), rows)

    greet(tuple((None, ((s + d) % 8, w)) for d in range(1, 8)), 7)

    def copy(d):
        target = (s + d) % 8
        if to_heads:
            source, goal = x_ref.at[:, column(target)], out_ref.at[row(s)]
        else:
            source, goal = x_ref.at[row(target)], out_ref.at[:, column(s)]
        return send(source, goal, send_sem.at[d - 1], recv_sem.at[d - 1], (target, w))

    for d in (4, 3, 5, 2, 6, 1, 7):
        copy(d).start()
    if to_heads:
        out_ref[row(s), :] = x_ref[:, column(s)]
    else:
        out_ref[:, column(s)] = x_ref[row(s), :]
    for d in range(1, 8):
        copy(d).wait_recv()
        copy(d).wait_send()


def deal(x, to_heads):
    seqs = lax.axis_size("seq")
    if seqs != 8 or lax.axis_size("wsh") != 4:
        if to_heads:
            split = x.reshape(x.shape[0], seqs, -1).transpose(1, 0, 2)
            return exchange(split, "seq").reshape(x.shape[0] * seqs, -1)
        moved = exchange(x.reshape(seqs, x.shape[0] // seqs, -1), "seq")
        return moved.transpose(1, 0, 2).reshape(x.shape[0] // seqs, -1)
    shape = (x.shape[0] * seqs, x.shape[1] // seqs) if to_heads else (x.shape[0] // seqs, x.shape[1] * seqs)
    vmem, dma = pl.BlockSpec(memory_space=pltpu.VMEM), pltpu.SemaphoreType.DMA
    return pl.pallas_call(
        functools.partial(deal_kernel, to_heads),
        in_specs=[vmem],
        out_specs=vmem,
        out_shape=jax.ShapeDtypeStruct(shape, x.dtype),
        scratch_shapes=[dma((7,)), dma((7,))],
        compiler_params=pltpu.CompilerParams(collective_id=6 if to_heads else 7, has_side_effects=True),
        cost_estimate=pl.CostEstimate(flops=0, bytes_accessed=60 << 20, transcendentals=0),
        name="deal_heads" if to_heads else "deal_rows",
    )(x)


def channel_kernel(
    forward, x_ref, first_hbm, second_hbm, active_hbm,
    sum_ref, all_hbm, mine_hbm, other_hbm, extra_hbm,
    first, second, rows_all, middle, active, part, core_buf, far_out, far_buf,
    load_sem, store_sem, core_send, core_recv, y_send, y_recv, x_send, x_recv, r_send, r_recv, f_send, f_recv,
):
    s, w, side, z, x_device, core_device, y_device = places()
    rows, width = x_ref.shape
    units = first.shape[0]
    half = units // 2
    loads = [
        pltpu.make_async_copy(first_hbm, first, load_sem.at[0]),
        pltpu.make_async_copy(second_hbm, second, load_sem.at[1]),
    ]
    size = units // 32
    for number, (source, target) in enumerate(((first_hbm, first), (second_hbm, second))):
        for at in range(32):
            h, k, q = at // 16, at // 4 % 4, at % 4
            to = (h * 4 + q) * 4 + k
            pltpu.make_async_copy(
                source.at[pl.ds(at * size, size)], target.at[pl.ds(to * size, size)], load_sem.at[number]
            ).start()
    if not forward:
        loads.append(pltpu.make_async_copy(active_hbm, active, load_sem.at[2]))
        loads[2].start()
    rows_all[0:rows] = x_ref[...]
    greet(((None, x_device), (None, core_device), (None, y_device)), 3)

    def block(number):
        return rows_all.at[pl.ds(number * rows, rows)]

    to_core = [
        send(block(0), block(1), core_send.at[0], core_recv.at[0], core_device),
        send(block(2), block(3), core_send.at[1], core_recv.at[1], core_device),
    ]
    to_y = send(block(0), block(2), y_send, y_recv, y_device)
    if forward:
        to_x = [
            send(
                middle.at[1 - side, pl.ds(2 * n * rows, 2 * rows)], other_hbm.at[pl.ds(2 * n * rows, 2 * rows)],
                x_send.at[n], x_recv.at[n], x_device,
            )
            for n in range(2)
        ]
    else:
        to_x = [
            send(block(n), other_hbm.at[pl.ds(n * rows, rows)], x_send.at[n], x_recv.at[n], x_device) for n in range(4)
        ]
    sums_core = [
        send(part.at[pl.ds((2 * n + 1) * rows, rows)], core_buf.at[n], r_send.at[n], r_recv.at[n], core_device)
        for n in range(2)
    ]
    far = send(far_out, far_buf, f_send, f_recv, y_device)
    stores = [
        pltpu.make_async_copy(rows_all, all_hbm, store_sem.at[0]),
        pltpu.make_async_copy(middle.at[side], mine_hbm, store_sem.at[1]),
        pltpu.make_async_copy(active if forward else middle.at[1 - side], extra_hbm, store_sem.at[2]),
    ]

    def pass_on(number):
        if not forward:
            to_x[number].start()

    to_y.start()
    to_core[0].start()
    pass_on(0)
    tile = min(512, half)

    def multiply(number):
        two = pl.ds(2 * number * rows, 2 * rows)

        def up(t, carry):
            for side_units in range(2):
                at = pl.multiple_of(t * tile, tile)
                unit = pl.multiple_of(side_units * half + at, tile)
                raw = dot(rows_all[two, :], first[pl.ds(unit, tile), :], NT)
                if forward:
                    raw = jnp.maximum(raw, 0.0)
                    active[two, pl.ds(unit, tile)] = raw
                    mid = raw * raw
                else:
                    mid = raw * 2.0 * active[two, pl.ds(unit, tile)]
                middle[side_units, two, pl.ds(at, tile)] = mid.astype(BF16)
            return carry

        lax.fori_loop(0, half // tile, up, 0)
        if forward:
            to_x[number].start()
        if number == 0:
            loads[1].wait()

        def down(t, carry):
            at = pl.multiple_of(t * tile, tile)
            part[two, pl.ds(at, tile)] = dot(middle[0, two, :], second[0:half, pl.ds(at, tile)]) + dot(
                middle[1, two, :], second[half:units, pl.ds(at, tile)]
            )
            return carry

        lax.fori_loop(0, width // tile, down, 0)
        sums_core[number].start()

    loads[0].wait()
    if not forward:
        loads[2].wait()
    to_core[0].wait_recv()
    pass_on(1)
    multiply(0)
    to_y.wait_recv()
    to_core[1].start()
    pass_on(2)
    to_core[1].wait_recv()
    pass_on(3)
    stores[0].start()
    multiply(1)
    for store in stores[1:]:
        store.start()
    sums_core[1].wait_recv()
    far_out[...] = (part[2 * rows : 3 * rows] + core_buf[1]).astype(BF16)
    far.start()
    sums_core[0].wait_recv()
    sum_ref[...] = part[0:rows] + core_buf[0]
    far.wait_recv()
    sum_ref[...] += far_buf[...].astype(F32)
    for copy in to_x:
        copy.wait_recv()
    for copy in to_x + to_core + sums_core + [to_y, far]:
        copy.wait_send()
    for store in stores:
        store.wait()


def channel_stage(x, first, second, active):
    rows, width = x.shape
    units = first.shape[0]
    forward = active is None
    given = (x, first, second) if forward else (x, first, second, active)
    everything = pl.BlockSpec(memory_space=pl.ANY)
    shapes = [
        ((rows, width), F32), ((4 * rows, width), BF16), ((4 * rows, units // 2), BF16),
        ((4 * rows, units // 2 if forward else width), BF16),
        ((4 * rows, units), F32) if forward else ((4 * rows, units // 2), BF16),
    ]

    def body(*refs):
        refs = list(refs)
        if forward:
            refs.insert(3, None)
        channel_kernel(forward, *refs)

    dma = pltpu.SemaphoreType.DMA
    return pl.pallas_call(
        body,
        in_specs=[pl.BlockSpec(memory_space=pltpu.VMEM)] + [everything] * (len(given) - 1),
        out_specs=[pl.BlockSpec(memory_space=pltpu.VMEM)] + [everything] * (len(shapes) - 1),
        out_shape=[jax.ShapeDtypeStruct(s, d) for s, d in shapes],
        scratch_shapes=[
            pltpu.VMEM((units, width), BF16), pltpu.VMEM((units, width), BF16), pltpu.VMEM((4 * rows, width), BF16),
            pltpu.VMEM((2, 4 * rows, units // 2), BF16), pltpu.VMEM((4 * rows, units), F32),
            pltpu.VMEM((4 * rows, width), F32), pltpu.VMEM((2, rows, width), F32),
            pltpu.VMEM((rows, width), BF16), pltpu.VMEM((rows, width), BF16),
            dma((3,)), dma((3,)), dma((2,)), dma((2,)), dma, dma, dma((4,)), dma((4,)), dma((2,)), dma((2,)),
            dma, dma,
        ],
        compiler_params=pltpu.CompilerParams(
            collective_id=3 if forward else 4, has_side_effects=True, vmem_limit_bytes=60 << 20
        ),
        cost_estimate=pl.CostEstimate(flops=0, bytes_accessed=100 << 20, transcendentals=0),
        name="channel_forward" if forward else "channel_backward",
    )(*given)


def from_behind(x, axis, by):
    size = lax.axis_size(axis)
    pairs = [(i, i + by) for i in range(size) if 0 <= i + by < size]
    return lax.ppermute(x, axis, pairs)


def exchange(x, axis):
    return lax.all_to_all(x, axis, split_axis=0, concat_axis=0, tiled=True)


def swap(x, by):
    size = lax.axis_size("wsh")
    return lax.ppermute(x, "wsh", [(i, i ^ by) for i in range(size)])


def gather_near(x):
    if lax.axis_size("wsh") != 4:
        return lax.all_gather(x, "wsh", axis=0, tiled=True)
    return gathered_near(x, swap(x, 1), swap(x, 2))


def gathered_near(x, beside, across):
    return jnp.concatenate([x, beside, across, swap(across, 1)], 0)


def beside(x):
    return lax.ppermute(x, "seq", [(i, i ^ 1) for i in range(lax.axis_size("seq"))])


def scalar_sum(x):
    if lax.axis_size("wsh") != 4:
        return jnp.sum(lax.all_gather(x.reshape(1), "wsh", axis=0, tiled=True))
    x = jnp.full((8, 128), x)
    x = x + swap(x, 1)
    return (x + swap(x, 2))[0, 0]


def near_sum(x):
    if lax.axis_size("wsh") != 4:
        return lax.psum_scatter(x, "wsh", scatter_dimension=0, tiled=True)
    rows = x.shape[0] // 4
    beside = swap(jnp.concatenate([x[rows : 2 * rows], x[3 * rows :]], 0), 1)
    far = x[2 * rows : 3 * rows] + beside[rows:]
    return x[:rows] + beside[:rows] + swap(far.astype(BF16), 2).astype(F32)


def block_sum(x):
    if lax.axis_size("wsh") != 4:
        return lax.psum_scatter(x, "wsh", scatter_dimension=0, tiled=False).astype(F32)
    kept, far = block_halves(x)
    return kept + swap(far, 2).astype(F32)


def block_halves(x):
    number = lax.axis_index("wsh")

    def block(by):
        return lax.dynamic_index_in_dim(x, number ^ by, 0, keepdims=False)

    beside = swap(jnp.stack([block(1), block(3)]), 1).astype(F32)
    return block(0).astype(F32) + beside[0], (block(2).astype(F32) + beside[1]).astype(BF16)


def local(
    tokens, first_layer_values, teacher, valid, destination, lengths,
    receptance_matrix, key_matrix, value_matrix, output_matrix,
    lowrank_down_weight, lowrank_up_weight, channel_key_weight, channel_value_weight, vectors,
):
    rows, width = tokens.shape
    seqs, parts = lax.axis_size("seq"), lax.axis_size("wsh")
    me = lax.axis_index("seq")
    group = rows * seqs
    own_width = width // seqs
    shard = width // parts
    piece = shard // seqs
    column = me * own_width

    def own_columns(matrix):
        return lax.dynamic_slice_in_dim(matrix, column, own_width, 1)

    near = parts == 4
    up_piece = lax.dynamic_slice_in_dim(lowrank_up_weight, column % shard, own_width, 0)
    total = 3 * own_width + WIDE
    own_weights = jnp.concatenate(
        [
            own_columns(receptance_matrix), own_columns(key_matrix), own_columns(value_matrix),
            pad_ranks(lowrank_down_weight), up_piece.reshape(shard, -1),
        ],
        1,
    )

    dest_seq = destination // rows // parts
    position = dest_seq * rows + destination % rows
    digits = jnp.stack([position // DIGIT, position % DIGIT, valid], 1).astype(BF16)
    tail = jnp.pad(digits, ((0, 0), (0, EXTRA - 3)))
    given, tails, weights = gather_first(tokens, tail, own_weights)
    given, tails, weights = given.reshape(group, width), tails.reshape(group, EXTRA), weights.reshape(width, -1)
    info = tails[:, :3].astype(F32)
    places = (info[:, 0] * DIGIT + info[:, 1]).astype(jnp.int32)
    numbers = jnp.arange(group, dtype=jnp.int32)
    permute = (numbers[:, None] == places[None, :]).astype(BF16)
    total_valid = scalar_sum(jnp.sum(info[:, 2]))

    index = jnp.arange(rows, dtype=jnp.int32)
    same_dest = (dest_seq[:, None] == dest_seq[None, :]) & (index[None, :] < index[:, None])
    slot = dest_seq * (rows // seqs) + jnp.sum(same_dest.astype(jnp.int32), 1)
    arrange = (index[:, None] == slot[None, :]).astype(BF16)
    mine = (places // rows) == me
    arrival = jnp.cumsum(mine.astype(jnp.int32)) - 1
    own_rows = ((index[:, None] + me * rows) == places[None, :]).astype(BF16)
    settle = dot(own_rows, (mine[:, None] & (arrival[:, None] == index[None, :])).astype(BF16)).astype(BF16)

    offsets = jnp.cumsum(lengths[0]) - lengths[0]
    starts = jnp.any(numbers[:, None] == offsets[None, :], 1).astype(F32)
    segment_ids = jnp.cumsum(starts).reshape(-1, BLOCK)
    before = segment_ids[:, :1] - starts.reshape(-1, BLOCK)[:, :1]
    segments = jnp.stack(
        [segment_ids, jnp.broadcast_to(before, segment_ids.shape), jnp.broadcast_to(segment_ids[:, -1:], segment_ids.shape)]
        + [jnp.zeros_like(segment_ids)] * 5,
        1,
    ).reshape(-1, BLOCK)
    flowing = (1.0 - starts)[:, None]

    up = pad_ranks(
        lax.dynamic_slice(
            weights, (column // shard * shard, total), (shard, weights.shape[1] - total)
        ).reshape(own_width, -1)
    ).T
    vec = lax.dynamic_slice_in_dim(vectors, column, own_width, 0)[:, 8:16].T

    output_late, given = lax.optimization_barrier((output_matrix, given))
    w_out = lax.all_gather(output_late, "wsh", axis=0, tiled=True)
    balanced = dot(permute, given).astype(BF16)
    wide_rows = balanced.astype(F32)
    mean = jnp.mean(wide_rows, -1, keepdims=True)
    scale_one = lax.rsqrt(jnp.mean(jnp.square(wide_rows - mean), -1, keepdims=True) + 1e-05)
    stats = jnp.concatenate([mean, scale_one, flowing, flowing], 1)
    mix_vec = vectors[:, :8].T
    first_values, stats = lax.optimization_barrier((first_layer_values, stats))
    first_given = exchange(
        first_values.reshape(rows, seqs, own_width).transpose(1, 0, 2), "seq"
    ).reshape(group, own_width)
    recept, keys, values, downs, hidden = run_project(balanced, stats, mix_vec, weights, own_width, parts)
    teacher_late, recept, first_given = lax.optimization_barrier((teacher, recept, first_given))
    first = dot(permute, first_given).astype(BF16)
    teacher_rows = exchange(dot(arrange, teacher_late).astype(BF16).reshape(seqs, rows // seqs, width), "seq")
    inputs = (recept, keys, values, hidden, first, up, vec, segments)
    mixed_out, *saved = run_forward(*inputs)
    teacher_rows, mixed_out, total_valid = lax.optimization_barrier((teacher_rows, mixed_out, total_valid))
    target = dot(settle, teacher_rows.reshape(rows, width))

    mixed_rows = deal(mixed_out, False)
    own = lax.dynamic_slice_in_dim(balanced, me * rows, rows, 0).astype(F32)
    own_starts = lax.dynamic_slice_in_dim(starts, me * rows, rows, 0)
    own_flowing = (1.0 - own_starts)[:, None]
    own_valid = dot(own_rows, tails)[:, 2]
    residual = own + dot(mixed_rows, w_out)
    standard_two, scale_two = norm_stats(residual)
    normed_two = standard_two * vectors[:, 16] + vectors[:, 17]
    carried_two = from_behind(normed_two[-1:], "seq", 1)
    delta_two = jnp.concatenate([carried_two, normed_two[:-1]], 0) * own_flowing - normed_two
    channel_in = (normed_two + delta_two * vectors[:, 18]).astype(BF16)
    paired = near and seqs == 8
    if paired:
        summed, channel, hidden_mine, hidden_other, active = channel_stage(
            channel_in, channel_key_weight, channel_value_weight, None
        )
    else:
        channel = gather_near(channel_in)
        active = jax.nn.relu(dot(channel, channel_key_weight, NT))
        hidden_rows = jnp.square(active).astype(BF16)
        summed = near_sum(dot(hidden_rows, channel_value_weight))
    result = residual + summed
    total_tokens = group * parts
    cotangent = (result - target) * (own_valid * (total_tokens / total_valid))[:, None]
    cot_low = cotangent.astype(BF16)

    result_back = exchange(dot(settle, result.astype(BF16), TN).astype(BF16).reshape(seqs, rows // seqs, width), "seq")
    if paired:
        grad_channel, cot, pre_mine, cot_other, pre_spare = channel_stage(
            cot_low, channel_value_weight, channel_key_weight, active
        )
    else:
        cot = gather_near(cot_low)
        grad_pre = (dot(cot, channel_value_weight, NT) * 2.0 * active).astype(BF16)
        grad_channel = near_sum(dot(grad_pre, channel_key_weight))
    if paired:
        value_part = (dot(hidden_mine, cot, TN) + dot(hidden_other, cot_other, TN)).astype(BF16)
    else:
        value_part = dot(hidden_rows, cot, TN).astype(BF16)
    result_back, grad_channel, value_part = lax.optimization_barrier((result_back, grad_channel, value_part))
    output = dot(arrange, result_back.reshape(rows, width), TN).astype(BF16)
    grad_vec_mix_two = jnp.sum(grad_channel * delta_two, 0)
    shifted = grad_channel * vectors[:, 18] * own_flowing
    behind = from_behind(shifted[:1], "seq", -1)
    grad_normed_two = grad_channel * (1.0 - vectors[:, 18]) + jnp.concatenate([shifted[1:], behind], 0)
    grad_residual = cotangent + norm_back(grad_normed_two, standard_two, scale_two, vectors[:, 16])
    grad_low = grad_residual.astype(BF16)

    grad_posted = dot(grad_low, w_out, NT).astype(BF16)
    grad_heads = deal(grad_posted, True)
    if paired:
        grad_heads, value_part, mixed_late, channel, pre_spare = lax.optimization_barrier(
            (grad_heads, value_part, mixed_rows, channel, pre_spare)
        )
        channel_other, pre_other = beside(channel), beside(pre_spare)
    else:
        grad_heads, mixed_late = lax.optimization_barrier((grad_heads, mixed_rows))
    lefts = exchange(mixed_late.reshape(rows, seqs, parts, piece).transpose(2, 0, 1, 3), "wsh")
    near_grad = (swap(grad_low, 1), swap(grad_low, 2)) if near else gather_near(grad_low)
    recept_low, keys_low, values_low, ups_low, grad_first, grad_vec_heads = run_backward(grad_heads, *inputs, saved)
    if paired:
        channel_other, pre_mine, pre_other, lefts, near_grad, recept_low = lax.optimization_barrier(
            (channel_other, pre_mine, pre_other, lefts, near_grad, recept_low)
        )
        key_part = (dot(pre_mine, channel, TN) + dot(pre_other, channel_other, TN)).astype(BF16)
    else:
        lefts, near_grad, recept_low = lax.optimization_barrier((lefts, near_grad, recept_low))
        key_part = dot(grad_pre, channel, TN).astype(BF16)
    if near:
        near_grad = gathered_near(grad_low, *near_grad)
        lefts = jnp.stack([lax.dynamic_index_in_dim(lefts, lax.axis_index("wsh") ^ k, 0, keepdims=False) for k in range(4)])
    out_part = dot(lefts.reshape(rows * parts, -1), near_grad, TN).astype(BF16)

    moved = exchange(dot(permute, grad_first, TN).astype(BF16).reshape(seqs, rows, own_width), "seq")
    recept_low, key_part, out_part = lax.optimization_barrier((recept_low, key_part, out_part))
    if paired:
        lines = [[0, 2, 4, 6], [1, 3, 5, 7]]
        def along(part):
            return lax.psum_scatter(part, "seq", scatter_dimension=0, tiled=True, axis_index_groups=lines)

        halves_out = out_part.reshape(seqs // 2, 2, piece, width)
        x_side = me % 2
        out_mine = lax.dynamic_index_in_dim(halves_out, x_side, 1, keepdims=False).astype(F32)
        out_other = beside(lax.dynamic_index_in_dim(halves_out, 1 - x_side, 1, keepdims=False))
        value_sum, key_sum = along(value_part), along(key_part)
    else:
        moves = [(s * parts + w, w * seqs + s) for s in range(seqs) for w in range(parts)]

        def ffn_grad(part):
            part = lax.psum_scatter(part, "seq", scatter_dimension=0, tiled=True)
            return lax.ppermute(part, ("seq", "wsh"), moves).astype(F32)

        grad_ffn_value, grad_ffn_key = ffn_grad(value_part), ffn_grad(key_part)
        grad_out = lax.psum_scatter(out_part, "seq", scatter_dimension=0, tiled=True)

    heads_part = lax.dynamic_update_slice_in_dim(jnp.zeros((width, 8), F32), grad_vec_heads.T, column, 0)
    vec_two = jnp.stack(
        [jnp.sum(grad_normed_two * standard_two, 0), jnp.sum(grad_normed_two, 0), grad_vec_mix_two], 1
    )
    others = jnp.concatenate([heads_part, jnp.pad(vec_two, ((0, 0), (0, 13)))], 1)
    scaled_grad, sums, wide, up_grad = run_unproject(
        balanced, stats, mix_vec, weights, others, (recept_low, keys_low, values_low), ups_low, hidden, downs, up, parts
    )
    if paired:
        moved, value_sum, out_other, scaled_grad, sums, wide, up_grad = lax.optimization_barrier(
            (moved, value_sum, out_other, scaled_grad, sums, wide, up_grad)
        )
        out_half = (out_mine + out_other.astype(F32)).astype(BF16).reshape(-1, width)
        out_half, sums = lax.optimization_barrier((out_half, sums))
        grad_out = along(out_half)
    else:
        moved, scaled_grad, sums, wide = lax.optimization_barrier((moved, scaled_grad, sums, wide))
    grad_first_rows = moved.transpose(1, 0, 2).reshape(rows, width)

    standard = (balanced.astype(F32) - mean) * scale_one
    grad_balanced = scale_one * (scaled_grad - sums[:, :1] * (1.0 / width) - standard * (sums[:, 1:] * (1.0 / width)))
    mine_rows = lax.dynamic_slice_in_dim(grad_balanced, me * rows, rows, 0) + grad_residual
    grad_balanced = lax.dynamic_update_slice_in_dim(grad_balanced, mine_rows, me * rows, 0)
    grad_given = dot(permute, grad_balanced.astype(BF16), TN).astype(BF16).reshape(seqs, rows, width)
    if near:
        kept_part, far = block_halves(wide)
        kept_up, far_up = block_halves(up_grad.reshape(parts, piece, WIDE))
        if paired:
            grad_given, far, far_up, key_sum = lax.optimization_barrier((grad_given, far, far_up, key_sum))
        wide_part, across_up = kept_part + swap(far, 2).astype(F32), swap(far_up, 2)
    else:
        wide_part = block_sum(wide)
    if paired:
        grad_tokens, value_all = reduce_seq(grad_given, value_sum.reshape(4, -1, width))
        wide_part, grad_tokens, grad_out, across_up = lax.optimization_barrier(
            (wide_part, grad_tokens, grad_out, across_up)
        )
        wide_all, key_all = finish(wide_part.astype(BF16), key_sum.reshape(4, -1, width))
        wide_all = wide_all.astype(F32)
        grad_ffn_key, grad_ffn_value = [x.reshape(-1, width).astype(F32) for x in (key_all, value_all)]
    else:
        grad_tokens = jnp.sum(exchange(grad_given, "seq").astype(F32), 0)
        wide_all = exchange(wide_part.astype(BF16), "seq").astype(F32)

    def square(at):
        taken = wide_all[:, :, at * own_width : (at + 1) * own_width]
        return taken.transpose(1, 0, 2).reshape(piece, width)

    narrow = jnp.sum(wide_all[:, :, 3 * own_width :], 0)
    grad_down = unpad_ranks(narrow)
    grad_vectors = narrow[:, RANKS[0] : RANKS[0] + vectors.shape[1]]
    up_part = unpad_ranks(kept_up + across_up.astype(F32) if near else block_sum(up_grad.reshape(parts, piece, WIDE)))

    return (
        output, grad_tokens.astype(BF16), grad_first_rows,
        square(0), square(1), square(2),
        grad_out.astype(F32), grad_down, up_part,
        grad_ffn_key, grad_ffn_value, grad_vectors,
    )


def solution(mesh):
    both, shard = P(("seq", "wsh"), None), P("wsh", None)
    flat = P(("seq", "wsh"))
    return jax.shard_map(
        local,
        mesh=mesh,
        in_specs=(both, both, both, flat, flat) + (shard,) * 9 + (P(),),
        out_specs=(both,) * 12,
        check_vma=False,
    )
```

```python
import functools

import jax
import jax.numpy as jnp
from jax import lax
from jax.experimental import pallas as pl
from jax.experimental.pallas import tpu as pltpu
from jax.sharding import PartitionSpec as P

HEAD = 64
BLOCK = 64
RANKS = (96, 96, 64, 256)
PADDED = (128, 128, 128, 256)
OFFSETS = (0, 128, 256, 384)
WIDE = 640
EXTRA = 128
DIGIT = 64

F32 = jnp.float32
BF16 = jnp.bfloat16

NN = (((1,), (0,)), ((), ()))
NT = (((1,), (1,)), ((), ()))
TN = (((0,), (0,)), ((), ()))


def dot(a, b, dims=NN):
    return lax.dot_general(a, b, dims, preferred_element_type=F32)


def halves(x):
    high = x.astype(BF16)
    return high, (x - high.astype(F32)).astype(BF16)


def dot3(a, b, dims=NN):
    a_high, a_low = halves(a)
    b_high, b_low = halves(b)
    return dot(a_high, b_high, dims) + (dot(a_high, b_low, dims) + dot(a_low, b_high, dims))


def sum_left(mask, x):
    high, low = halves(x)
    low_two = (x - high.astype(F32) - low.astype(F32)).astype(BF16)
    return dot(mask, high) + (dot(mask, low) + dot(mask, low_two))


def head_sum(x, ones):
    high, low = halves(x)
    return dot(high, ones) + dot(low, ones)


def low(x):
    return x.astype(BF16).astype(F32)


def iotas(rows, columns):
    return (
        lax.broadcasted_iota(jnp.int32, (rows, columns), 0),
        lax.broadcasted_iota(jnp.int32, (rows, columns), 1),
    )


def head_ones(width):
    i, j = iotas(width, width)
    return jnp.where((i >> 6) == (j >> 6), 1.0, 0.0).astype(BF16)


def front(keys, values, hidden, up, first, vec, ones):
    z = vec[0:1] + dot(hidden[:, 0:128], up[0:128])
    decay_log = -(jnp.maximum(-z, 0.0) + jnp.log1p(jnp.exp(-jnp.abs(z)))) - 0.5
    rate = jax.nn.sigmoid(vec[1:2] + dot(hidden[:, 128:256], up[128:256]))
    blend = jax.nn.sigmoid(vec[2:3] + dot(hidden[:, 256:384], up[256:384]))
    gate = dot(hidden[:, 384:640], up[384:640])
    mixed_value = values + (first - values) * blend
    scaled = keys * vec[3:4]
    scale = lax.rsqrt(head_sum(scaled * scaled, ones) + 1e-06)
    key_dir = scaled * scale
    key_mod = keys * (1.0 + (rate - 1.0) * vec[4:5])
    return z, decay_log, rate, blend, gate, mixed_value, scale, key_dir, key_mod


def block_masks(segments):
    i, j = iotas(BLOCK, BLOCK)
    across = jnp.broadcast_to(segments[0:1], (BLOCK, BLOCK))
    down = across.T
    before = jnp.broadcast_to(segments[1:2], (BLOCK, BLOCK))
    last = jnp.broadcast_to(segments[2:3], (BLOCK, BLOCK))
    same = across == down
    strict = jnp.where(same & (i > j), 1.0, 0.0)
    closed = jnp.where(same & (i >= j), 1.0, 0.0)
    carry = jnp.where(down == before, 1.0, 0.0)
    tail = jnp.where(down == last, 1.0, 0.0)
    keep = jnp.where(segments[2:3] == segments[1:2], 1.0, 0.0)
    quad = jnp.concatenate(
        [jnp.concatenate([strict, strict], 1), jnp.concatenate([closed, closed], 1)], 0
    )
    return quad, carry, tail, keep


def tile_heads(x, heads):
    return jnp.concatenate([x] * heads, 1) if heads > 1 else x


def join(pieces, axis):
    return jnp.concatenate(pieces, axis) if len(pieces) > 1 else pieces[0]


def decayed(decay_low, key_low, dir_low, rate_low, recept_low, carry, tail):
    i, j = iotas(BLOCK, BLOCK)
    lower = jnp.where(i >= j, 1.0, 0.0).astype(BF16)
    log_step = -jnp.exp(decay_low)
    total = sum_left(lower, log_step)
    before = jnp.exp(total - log_step)
    grown = jnp.exp(total)
    shrunk = jnp.exp(-total)
    end = total[BLOCK - 1 : BLOCK]
    tail_decay = jnp.exp(end - total) * tail
    alpha = -dir_low * before
    beta_plain = dir_low * rate_low
    beta = beta_plain * shrunk
    key = key_low * shrunk
    recept = recept_low * grown
    return dict(
        log_step=log_step, before=before, grown=grown, shrunk=shrunk, end=jnp.exp(end), tail=tail_decay,
        alpha=alpha, beta_plain=beta_plain, beta=beta, key=key, recept=recept,
        beta_end=beta_plain * tail_decay, key_end=key_low * tail_decay,
        alpha_in=alpha * carry, recept_in=recept * carry,
    )


def unit_inverses(lowers):
    i, j = iotas(BLOCK, BLOCK)
    eye = jnp.where(i == j, 1.0, 0.0)

    def within(size):
        return (i // size) == (j // size)

    smalls = [jnp.where(within(4), x, 0.0) for x in lowers]
    low_smalls = [x.astype(BF16) for x in smalls]
    twos = [dot(x, x) for x in low_smalls]
    inverses = [eye + x for x in smalls]
    inverses = [x + dot(x.astype(BF16), y.astype(BF16)) for x, y in zip(inverses, twos)]
    for size in (8, 16, 32, 64):
        mask = within(size) & ~within(size // 2)
        offs = [jnp.where(mask, x, 0.0).astype(BF16) for x in lowers]
        lows = [x.astype(BF16) for x in inverses]
        inner = [dot(x, y).astype(BF16) for x, y in zip(offs, lows)]
        inverses = [x + dot(y, z) for x, y, z in zip(inverses, lows, inner)]
    errors = [eye - x + dot3(y, x) for x, y in zip(inverses, lowers)]
    return [x + dot(x.astype(BF16), y.astype(BF16)) for x, y in zip(inverses, errors)]


def post_norm(head_low, ones):
    centered = head_low - head_sum(head_low, ones) * (1.0 / HEAD)
    spread = lax.rsqrt(head_sum(centered * centered, ones) * (1.0 / HEAD) + HEAD * 1e-05)
    return centered * spread, spread


def forward_kernel(
    count, recept_ref, keys_ref, values_ref, hidden_ref, first_ref, up_ref, vec_ref, segment_ref,
    mixed_ref, head_ref, state_ref, inverse_ref, removed_ref, state,
):
    width = recept_ref.shape[1]
    heads = width // HEAD

    @pl.when(pl.program_id(0) == 0)
    def _():
        state[...] = jnp.zeros_like(state)

    ones = head_ones(width)
    vec = vec_ref[...]
    up = up_ref[...]
    columns = [slice(head * HEAD, (head + 1) * HEAD) for head in range(heads)]
    done = []
    for block in range(count):
        rows = slice(block * BLOCK, (block + 1) * BLOCK)
        recept, keys, values = recept_ref[rows], keys_ref[rows], values_ref[rows]
        _, decay_log, rate, _, gate, mixed_value, _, key_dir, key_mod = front(
            keys, values, hidden_ref[rows], up, first_ref[rows].astype(F32), vec, ones
        )
        quad, carry, tail, keep = block_masks(segment_ref[block * 8 : block * 8 + 8])
        parts = decayed(
            low(decay_log), low(key_mod), low(key_dir), low(rate), low(recept),
            tile_heads(carry, heads), tile_heads(tail, heads),
        )
        lefts = [jnp.concatenate([parts["alpha"][:, c], parts["recept"][:, c]], 0) for c in columns]
        rights = [jnp.concatenate([parts["beta"][:, c], parts["key"][:, c]], 0) for c in columns]
        pairs = [quad * dot3(x, y, NT) for x, y in zip(lefts, rights)]
        done.append((rows, recept, key_mod, gate, mixed_value, keep, parts, pairs))
    inverses = unit_inverses([x[:BLOCK, :BLOCK] for item in done for x in item[-1]])
    for block, (rows, recept, key_mod, gate, mixed_value, keep, parts, pairs) in enumerate(done):
        mine = inverses[block * heads : (block + 1) * heads]
        value_low = low(mixed_value)
        owns = [value_low[:, c] for c in columns]
        by_values = [dot3(x[:, BLOCK:], y) for x, y in zip(pairs, owns)]
        ends = [jnp.concatenate([parts["beta_end"][:, c], parts["key_end"][:, c]], 0) for c in columns]
        inners = [jnp.concatenate([parts["alpha_in"][:, c], parts["recept_in"][:, c]], 0) for c in columns]
        entering = state[...]
        state_ref[rows] = entering
        nows = [entering[:, c] for c in columns]
        inwards = [dot3(x, y, NT) for x, y in zip(inners, nows)]
        removals = [dot3(x, y[:BLOCK] + z[:BLOCK]) for x, y, z in zip(mine, inwards, by_values)]
        outs = [
            y[BLOCK:] + z[BLOCK:] + dot3(x[BLOCK:, :BLOCK], r)
            for x, y, z, r in zip(pairs, inwards, by_values, removals)
        ]
        leaving = [
            x * (parts["end"][:, c] * keep) + dot3(jnp.concatenate([r, v], 0), e, TN)
            for x, c, r, v, e in zip(nows, columns, removals, owns, ends)
        ]
        state[...] = join(leaving, 1)
        inverse_ref[rows] = join(mine, 1)
        removed_ref[rows] = join(removals, 1)
        head_low = join(outs, 1).astype(BF16)
        head_ref[rows] = head_low
        normed, _ = post_norm(head_low.astype(F32), ones)
        bonus = head_sum(recept * key_mod * vec[5:6], ones) * mixed_value
        mixed_ref[rows] = ((normed * vec[6:7] + vec[7:8] + bonus) * gate).astype(BF16)


def backward_kernel(
    count, grad_ref, recept_ref, keys_ref, values_ref, hidden_ref, first_ref, up_ref, vec_ref, segment_ref,
    head_ref, state_ref, inverse_ref, removed_ref,
    recept_out, keys_out, values_out, ups_out, first_out, vec_out, state,
):
    width = recept_ref.shape[1]
    heads = width // HEAD

    @pl.when(pl.program_id(0) == 0)
    def _():
        state[...] = jnp.zeros_like(state)
        vec_out[...] = jnp.zeros_like(vec_out)

    ones = head_ones(width)
    vec = vec_ref[...]
    up = up_ref[...]
    i, j = iotas(BLOCK, BLOCK)
    upper = jnp.where(i <= j, 1.0, 0.0).astype(BF16)
    columns = [slice(head * HEAD, (head + 1) * HEAD) for head in range(heads)]
    order = range(count - 1, -1, -1)
    kept = {}
    for block in order:
        rows = slice(block * BLOCK, (block + 1) * BLOCK)
        recept, keys, values = recept_ref[rows], keys_ref[rows], values_ref[rows]
        first = first_ref[rows].astype(F32)
        z, decay_log, rate, blend, gate, mixed_value, scale, key_dir, key_mod = front(
            keys, values, hidden_ref[rows], up, first, vec, ones
        )
        quad, carry, tail, keep = block_masks(segment_ref[block * 8 : block * 8 + 8])
        rate_low, dir_low = low(rate), low(key_dir)
        parts = decayed(
            low(decay_log), low(key_mod), dir_low, rate_low, low(recept),
            tile_heads(carry, heads), tile_heads(tail, heads),
        )
        value_low = low(mixed_value)

        grad = grad_ref[rows].astype(F32)
        normed, spread = post_norm(head_ref[rows].astype(F32), ones)
        product = recept * key_mod
        coefficient = head_sum(product * vec[5:6], ones)
        grad_gate = grad * (normed * vec[6:7] + vec[7:8] + coefficient * mixed_value)
        opened = grad * gate
        grad_normed = opened * vec[6:7]
        grad_head = spread * (
            grad_normed
            - head_sum(grad_normed, ones) * (1.0 / HEAD)
            - normed * (head_sum(grad_normed * normed, ones) * (1.0 / HEAD))
        )
        grad_coefficient = head_sum(opened * mixed_value, ones)
        weighted = grad_coefficient * vec[5:6]
        head_grad = low(grad_head)

        lefts = [jnp.concatenate([parts["alpha"][:, c], parts["recept"][:, c]], 0) for c in columns]
        rights = [jnp.concatenate([parts["beta"][:, c], parts["key"][:, c]], 0) for c in columns]
        ends = [jnp.concatenate([parts["beta_end"][:, c], parts["key_end"][:, c]], 0) for c in columns]
        inners = [jnp.concatenate([parts["alpha_in"][:, c], parts["recept_in"][:, c]], 0) for c in columns]
        pairs = [quad * dot3(x, y, NT) for x, y in zip(lefts, rights)]
        out_grads = [head_grad[:, c] for c in columns]
        through = [dot3(x[BLOCK:, :BLOCK], y, TN) for x, y in zip(pairs, out_grads)]
        kept[block] = dict(
            rows=rows, recept=recept, keys=keys, values=values, first=first, z=z, rate=rate, blend=blend,
            mixed_value=mixed_value, scale=scale, key_dir=key_dir, key_mod=key_mod, quad=quad, carry=carry, keep=keep,
            rate_low=rate_low, dir_low=dir_low, parts=parts, value_low=value_low, normed=normed, product=product,
            grad_gate=grad_gate, opened=opened, grad_coefficient=grad_coefficient,
            grad_mixed_value=opened * coefficient, grad_recept=weighted * key_mod, grad_key_mod=weighted * recept,
            lefts=lefts, rights=rights, ends=ends, inners=inners, pairs=pairs, out_grads=out_grads, through=through,
        )
    for block in order:
        k = kept[block]
        after, entering, inverse_all = state[...], state_ref[k["rows"]], inverse_ref[k["rows"]]
        laters, nows = [after[:, c] for c in columns], [entering[:, c] for c in columns]
        from_ends = [dot3(x, y, NT) for x, y in zip(k["ends"], laters)]
        inner_grads = [
            dot3(inverse_all[:, c], x + y[:BLOCK], TN) for c, x, y in zip(columns, k["through"], from_ends)
        ]
        boths = [jnp.concatenate([x, y], 0) for x, y in zip(inner_grads, k["out_grads"])]
        stays = [x * (k["parts"]["end"][:, c] * k["keep"]) for x, c in zip(laters, columns)]
        state[...] = join([x + dot3(y, z, TN) for x, y, z in zip(stays, boths, k["inners"])], 1)
        k.update(
            laters=laters, nows=nows, from_ends=from_ends, boths=boths,
            end_sum=join([jnp.sum(x * y, 0, keepdims=True) for x, y in zip(nows, stays)], 1),
        )
    vec_total = jnp.zeros_like(vec)
    for block in order:
        k = kept[block]
        rows, parts, quad = k["rows"], k["parts"], k["quad"]
        removed_all = removed_ref[rows]
        carry_two = jnp.concatenate([k["carry"], k["carry"]], 0)
        sources = [jnp.concatenate([removed_all[:, c], k["value_low"][:, c]], 0) for c in columns]
        grad_pairs = [quad * dot3(x, y, NT) for x, y in zip(k["boths"], sources)]
        grad_values = [
            dot3(x[:, BLOCK:], y, TN) + z[BLOCK:] for x, y, z in zip(k["pairs"], k["boths"], k["from_ends"])
        ]
        grad_ends = [dot3(x, y) for x, y in zip(sources, k["laters"])]
        to_state = [carry_two * dot3(x, y) for x, y in zip(k["boths"], k["nows"])]
        grad_lefts = [dot3(x, y) + z for x, y, z in zip(grad_pairs, k["rights"], to_state)]
        grad_rights = [dot3(x, y, TN) for x, y in zip(grad_pairs, k["lefts"])]
        d_alpha, d_recept = join([x[:BLOCK] for x in grad_lefts], 1), join([x[BLOCK:] for x in grad_lefts], 1)
        d_beta, d_key = join([x[:BLOCK] for x in grad_rights], 1), join([x[BLOCK:] for x in grad_rights], 1)
        d_beta_end, d_key_end = join([x[:BLOCK] for x in grad_ends], 1), join([x[BLOCK:] for x in grad_ends], 1)
        ended = parts["beta_end"] * d_beta_end + parts["key_end"] * d_key_end
        alphas = parts["alpha"] * d_alpha
        d_total = parts["recept"] * d_recept - parts["beta"] * d_beta - parts["key"] * d_key - ended + alphas
        d_step = sum_left(upper, d_total) + (jnp.sum(ended, 0, keepdims=True) + k["end_sum"]) - alphas
        d_beta_plain = d_beta * parts["shrunk"] + d_beta_end * parts["tail"]
        copy_decay = low(d_step * parts["log_step"])
        copy_dir = low(d_beta_plain * k["rate_low"] - d_alpha * parts["before"])
        copy_rate = low(d_beta_plain * k["dir_low"])

        keys, values, rate, blend = k["keys"], k["values"], k["rate"], k["blend"]
        grad_recept = k["grad_recept"] + low(d_recept * parts["grown"])
        grad_key_mod = k["grad_key_mod"] + low(d_key * parts["shrunk"] + d_key_end * parts["tail"])
        grad_mixed_value = k["grad_mixed_value"] + low(join(grad_values, 1))
        grad_z = copy_decay * jax.nn.sigmoid(-k["z"])
        factor = 1.0 + (rate - 1.0) * vec[4:5]
        keyed = grad_key_mod * keys
        grad_rate = copy_rate + keyed * vec[4:5]
        grad_scaled = k["scale"] * (copy_dir - k["key_dir"] * head_sum(copy_dir * k["key_dir"], ones))
        grad_keys = grad_key_mod * factor + grad_scaled * vec[3:4]
        grad_rate_up = grad_rate * rate * (1.0 - rate)
        grad_value_up = grad_mixed_value * (k["first"] - values) * blend * (1.0 - blend)
        recept_out[rows] = grad_recept.astype(BF16)
        keys_out[rows] = grad_keys.astype(BF16)
        values_out[rows] = (grad_mixed_value * (1.0 - blend)).astype(BF16)
        first_out[rows] = (grad_mixed_value * blend).astype(BF16)
        ups_out[0, rows] = grad_z.astype(BF16)
        ups_out[1, rows] = grad_rate_up.astype(BF16)
        ups_out[2, rows] = grad_value_up.astype(BF16)
        ups_out[3, rows] = k["grad_gate"].astype(BF16)

        def total(x):
            return jnp.sum(x, 0, keepdims=True)

        vec_total = vec_total + jnp.concatenate(
            [
                total(grad_z), total(grad_rate_up), total(grad_value_up), total(grad_scaled * keys),
                total(keyed * (rate - 1.0)), total(k["grad_coefficient"] * k["product"]),
                total(k["opened"] * k["normed"]), total(k["opened"]),
            ],
            0,
        )
    vec_out[...] += vec_total


def kernel_cost(rows, width, passes):
    return pl.CostEstimate(flops=2 * rows * width * width, bytes_accessed=4 * rows * width * passes, transcendentals=0)


def per_step(rows, most):
    return most if (rows // BLOCK) % most == 0 else 1


def run_forward(recept, keys, values, hidden, first, up, vec, segments):
    rows, width = recept.shape
    count = per_step(rows, 4)
    step = count * BLOCK

    def spec(columns):
        return pl.BlockSpec((step, columns), lambda i: (i, 0))

    def whole(array):
        return pl.BlockSpec(array.shape, lambda i: (0, 0))

    return pl.pallas_call(
        functools.partial(forward_kernel, count),
        grid=(rows // step,),
        in_specs=[
            spec(width), spec(width), spec(width), spec(WIDE), spec(width), whole(up), whole(vec),
            pl.BlockSpec((count * 8, BLOCK), lambda i: (i, 0)),
        ],
        out_specs=[spec(width)] * 5,
        out_shape=[jax.ShapeDtypeStruct((rows, width), d) for d in (BF16, BF16, F32, F32, F32)],
        scratch_shapes=[pltpu.VMEM((BLOCK, width), F32)],
        compiler_params=pltpu.CompilerParams(vmem_limit_bytes=48 << 20),
        cost_estimate=kernel_cost(rows, width, 110),
        name="mix_forward",
    )(recept, keys, values, hidden, first, up, vec, segments)


def run_backward(grad, recept, keys, values, hidden, first, up, vec, segments, saved):
    rows, width = recept.shape
    count = per_step(rows, 2)
    step = count * BLOCK
    last = rows // step - 1

    def spec(columns):
        return pl.BlockSpec((step, columns), lambda i: (last - i, 0))

    def whole(array):
        return pl.BlockSpec(array.shape, lambda i: (0, 0))

    return pl.pallas_call(
        functools.partial(backward_kernel, count),
        grid=(rows // step,),
        in_specs=[
            spec(width), spec(width), spec(width), spec(width), spec(WIDE), spec(width), whole(up), whole(vec),
            pl.BlockSpec((count * 8, BLOCK), lambda i: (last - i, 0)),
            spec(width), spec(width), spec(width), spec(width),
        ],
        out_specs=[
            spec(width), spec(width), spec(width),
            pl.BlockSpec((4, step, width), lambda i: (0, last - i, 0)),
            spec(width), pl.BlockSpec((8, width), lambda i: (0, 0)),
        ],
        out_shape=[
            jax.ShapeDtypeStruct((rows, width), BF16), jax.ShapeDtypeStruct((rows, width), BF16),
            jax.ShapeDtypeStruct((rows, width), BF16), jax.ShapeDtypeStruct((4, rows, width), BF16),
            jax.ShapeDtypeStruct((rows, width), BF16), jax.ShapeDtypeStruct((8, width), F32),
        ],
        scratch_shapes=[pltpu.VMEM((BLOCK, width), F32)],
        compiler_params=pltpu.CompilerParams(vmem_limit_bytes=48 << 20),
        cost_estimate=kernel_cost(rows, width, 150),
        name="mix_backward",
    )(grad, recept, keys, values, hidden, first, up, vec, segments, *saved)


def mix_norm(block_ref, stats_ref, vec_ref):
    stats = stats_ref[...]
    flowing = stats[:, 2:3]
    standard = (block_ref[...].astype(F32) - stats[:, 0:1]) * stats[:, 1:2]
    normed = standard * vec_ref[0:1] + vec_ref[1:2]
    delta = pltpu.roll(normed, 1, 0) * flowing - normed
    return standard, normed, delta, flowing


def project_kernel(
    width, block_ref, stats_ref, vec_ref, weight_ref,
    recept_ref, keys_ref, values_ref, downs_ref, hidden_ref,
):
    base = 3 * width
    _, normed, delta, _ = mix_norm(block_ref, stats_ref, vec_ref)
    weight = weight_ref[...]
    uses = (
        ((recept_ref, 0, width, 0),),
        ((downs_ref, base + OFFSETS[0], PADDED[0], OFFSETS[0]),),
        ((keys_ref, width, width, 0),),
        ((values_ref, 2 * width, width, 0), (downs_ref, base + OFFSETS[2], PADDED[2], OFFSETS[2])),
        ((downs_ref, base + OFFSETS[1], PADDED[1], OFFSETS[1]),),
        ((downs_ref, base + OFFSETS[3], PADDED[3], OFFSETS[3]),),
    )

    @pl.when(pl.program_id(0) == 0)
    def _():
        for ref in (recept_ref, keys_ref, values_ref, downs_ref):
            ref[...] = jnp.zeros_like(ref)

    for c, targets in enumerate(uses):
        mixed = (normed + delta * vec_ref[2 + c : 3 + c]).astype(BF16)
        for ref, start, size, at in targets:
            ref[:, at : at + size] += dot(mixed, weight[:, start : start + size])

    @pl.when(pl.program_id(0) == pl.num_programs(0) - 1)
    def _():
        hidden_ref[:, 0:128] = jnp.tanh(downs_ref[:, 0:128]).astype(BF16)
        hidden_ref[:, 128:384] = downs_ref[:, 128:384].astype(BF16)
        hidden_ref[:, 384:640] = jax.nn.sigmoid(downs_ref[:, 384:640]).astype(BF16)


def unproject_kernel(
    width, parts, piece, block_ref, stats_ref, vec_ref, weight_ref,
    other_ref, recept_ref, keys_ref, values_ref, ups_ref, hidden_ref, downs_ref, up_ref,
    grad_ref, sums_ref, wide_ref, up_out, down_lows,
):
    rows = block_ref.shape[0]
    base = 3 * width

    @pl.when(pl.program_id(0) == 0)
    def _():
        sums_ref[...] = jnp.zeros_like(sums_ref)
        for k, (at, size) in enumerate(zip(OFFSETS, PADDED)):
            cols = slice(at, at + size)
            grad = dot(ups_ref[k], up_ref[cols], NT)
            if k == 0:
                grad = grad * (1.0 - jnp.square(jnp.tanh(downs_ref[:, cols])))
            if k == 3:
                opening = jax.nn.sigmoid(downs_ref[:, cols])
                grad = grad * opening * (1.0 - opening)
            down_lows[:, cols] = grad.astype(BF16)
            up_out[:, cols] = dot(ups_ref[k], hidden_ref[:, cols], TN).astype(BF16)

    standard, normed, delta, flowing = mix_norm(block_ref, stats_ref, vec_ref)
    weight = weight_ref[...]

    def down(k):
        return (down_lows[:, OFFSETS[k] : OFFSETS[k] + PADDED[k]], base + OFFSETS[k], PADDED[k])

    uses = (
        ((recept_ref[...], 0, width),),
        (down(0),),
        ((keys_ref[...], width, width),),
        ((values_ref[...], 2 * width, width), down(2)),
        (down(1),),
        (down(3),),
    )
    kept, sent, vec_rows = None, None, []
    per_seq = parts * piece
    for c, sources in enumerate(uses):
        share = vec_ref[2 + c : 3 + c]
        mixed = (normed + delta * share).astype(BF16)
        grad = None
        for source, start, size in sources:
            part = dot(source, weight[:, start : start + size], NT)
            grad = part if grad is None else grad + part
            product = dot(mixed, source, TN).astype(BF16)
            for number in range(product.shape[0] // per_seq):
                for w in range(parts):
                    at = number * per_seq + w * piece
                    wide_ref[w, number, :, start : start + size] = product[at : at + piece]
        vec_rows.append(jnp.sum(grad * delta, 0, keepdims=True))
        moved = grad * share
        kept = grad - moved if kept is None else kept + (grad - moved)
        sent = moved if sent is None else sent + moved
    grad = kept + pltpu.roll(sent * flowing, rows - 1, 0)
    vec_rows = jnp.concatenate(
        [jnp.sum(grad * standard, 0, keepdims=True), jnp.sum(grad, 0, keepdims=True)] + vec_rows, 0
    )
    spare = jnp.concatenate([vec_rows.T, other_ref[...]], 1).astype(BF16)
    for number in range(spare.shape[0] // per_seq):
        for w in range(parts):
            at = number * per_seq + w * piece
            wide_ref[w, number, :, base + RANKS[0] : base + PADDED[0]] = spare[at : at + piece]
    scaled = grad * vec_ref[0:1]
    sums_ref[:, 0:1] += jnp.sum(scaled, 1, keepdims=True)
    sums_ref[:, 1:2] += jnp.sum(scaled * standard, 1, keepdims=True)
    grad_ref[...] = scaled


def mix_specs(rows, width, own_width, parts):
    block = 256 if rows <= 1024 else 128

    def columns(height):
        return pl.BlockSpec((height, block), lambda j: (0, j))

    def whole(shape):
        return pl.BlockSpec(shape, lambda j: (0,) * len(shape))

    def weights(array):
        size = array.shape[1] if rows > 1024 else 3 * own_width + WIDE
        return pl.BlockSpec((block, size), lambda j: (j, 0))

    return block, columns, whole, weights


def run_project(balanced, stats, vec, weights, own_width, parts):
    rows, width = balanced.shape
    block, columns, whole, weight_spec = mix_specs(rows, width, own_width, parts)
    shapes = [(rows, own_width)] * 3 + [(rows, WIDE)] * 2
    return pl.pallas_call(
        functools.partial(project_kernel, own_width),
        grid_spec=pltpu.PrefetchScalarGridSpec(
            num_scalar_prefetch=0,
            grid=(width // block,),
            in_specs=[columns(rows), whole(stats.shape), columns(8), weight_spec(weights)],
            out_specs=[whole(s) for s in shapes],
        ),
        out_shape=[jax.ShapeDtypeStruct(s, d) for s, d in zip(shapes, (F32, F32, F32, F32, BF16))],
        compiler_params=pltpu.CompilerParams(vmem_limit_bytes=60 << 20),
        cost_estimate=kernel_cost(rows, own_width, 60),
        name="mix_project",
    )(balanced, stats, vec, weights)


def run_unproject(balanced, stats, vec, weights, others, lows, ups, hidden, downs, up, parts):
    rows, width = balanced.shape
    own_width = lows[0].shape[1]
    seqs = width // own_width
    piece = own_width // parts
    block, columns, whole, weight_spec = mix_specs(rows, width, own_width, parts)
    taken = block // own_width
    total = 3 * own_width + WIDE
    return pl.pallas_call(
        functools.partial(unproject_kernel, own_width, parts, piece),
        grid_spec=pltpu.PrefetchScalarGridSpec(
            num_scalar_prefetch=0,
            grid=(width // block,),
            in_specs=[
                columns(rows), whole(stats.shape), columns(8), weight_spec(weights),
                pl.BlockSpec((block, others.shape[1]), lambda j: (j, 0)),
            ]
            + [whole(a.shape) for a in (*lows, ups, hidden, downs, up)],
            out_specs=[
                columns(rows), whole((rows, 2)),
                pl.BlockSpec((parts, taken, piece, total), lambda j: (0, j, 0, 0)),
                whole((own_width, WIDE)),
            ],
            scratch_shapes=[pltpu.VMEM((rows, WIDE), BF16)],
        ),
        out_shape=[
            jax.ShapeDtypeStruct((rows, width), F32), jax.ShapeDtypeStruct((rows, 2), F32),
            jax.ShapeDtypeStruct((parts, seqs, piece, total), BF16),
            jax.ShapeDtypeStruct((own_width, WIDE), BF16),
        ],
        compiler_params=pltpu.CompilerParams(vmem_limit_bytes=60 << 20),
        cost_estimate=kernel_cost(rows, own_width, 120),
        name="mix_unproject",
    )(balanced, stats, vec, weights, others, *lows, ups, hidden, downs, up)


def norm_stats(values):
    centered = values - jnp.mean(values, -1, keepdims=True)
    scale = lax.rsqrt(jnp.mean(centered * centered, -1, keepdims=True) + 1e-05)
    return centered * scale, scale


def norm_back(grad, standard, scale, gain):
    scaled = grad * gain
    return scale * (
        scaled
        - jnp.mean(scaled, -1, keepdims=True)
        - standard * jnp.mean(scaled * standard, -1, keepdims=True)
    )


def pad_ranks(matrix):
    pieces, start = [], 0
    for rank, padded in zip(RANKS, PADDED):
        pieces.append(jnp.pad(matrix[:, start : start + rank], ((0, 0), (0, padded - rank))))
        start += rank
    return jnp.concatenate(pieces, 1)


def unpad_ranks(matrix):
    return jnp.concatenate([matrix[..., o : o + r] for o, r in zip(OFFSETS, RANKS)], -1)


MESH_ID = pl.DeviceIdType.MESH


def places():
    s, w = lax.axis_index("seq"), lax.axis_index("wsh")
    side = s % 2
    return s, w, side, s // 2, (s + 1 - 2 * side, w), (s, w + 1 - 2 * (w % 2)), (s, w + 2 - 4 * (w // 2))


def greet(neighbours, number):
    barrier = pltpu.get_barrier_semaphore()
    for there, device in neighbours:
        if there is None:
            pl.semaphore_signal(barrier, inc=1, device_id=device, device_id_type=MESH_ID)
        else:

            @pl.when(there)
            def _(device=device):
                pl.semaphore_signal(barrier, inc=1, device_id=device, device_id_type=MESH_ID)

    pl.semaphore_wait(barrier, number)


def send(source, target, send_sem, recv_sem, device):
    return pltpu.make_async_remote_copy(
        src_ref=source, dst_ref=target, send_sem=send_sem, recv_sem=recv_sem, device_id=device, device_id_type=MESH_ID
    )


def line_ends(z):
    return jnp.where(z > 0, 1, 0) + jnp.where(z < 3, 1, 0)


def gather_kernel(
    own_ref, tail_ref, weight_ref, out_ref, tails_ref, weights_ref,
    copy_sem, right_send, right_recv, left_send, left_recv, x_send, x_recv, c_send, c_recv, y_send, y_recv,
):
    s, w, side, z, x_device, core_device, y_device = places()
    up, down = (s + 2, w), (s - 2, w)
    across = w + 2 - 4 * (w // 2)
    kinds = ((own_ref, out_ref), (tail_ref, tails_ref))
    copies = [pltpu.make_async_copy(own, out.at[s], copy_sem.at[k]) for k, (own, out) in enumerate(kinds)]
    copies.append(pltpu.make_async_copy(weight_ref, weights_ref.at[w], copy_sem.at[2]))
    for copy in copies:
        copy.start()
    greet(((None, x_device), (None, core_device), (None, y_device), (z < 3, up), (z > 0, down)), 3 + line_ends(z))

    weight_y = send(weight_ref, weights_ref.at[w], y_send, y_recv, y_device)
    weight_core = send(weight_ref, weights_ref.at[w], c_send.at[0], c_recv.at[0], core_device)
    weight_on = send(weights_ref.at[across], weights_ref.at[across], c_send.at[1], c_recv.at[1], core_device)
    weight_y.start()
    weight_core.start()

    def to_right(j, k, source, number):
        return send(source, kinds[k][1].at[number], right_send.at[j, k], right_recv.at[j, k], up)

    def to_left(j, k, source, number):
        return send(source, kinds[k][1].at[number], left_send.at[j, k], left_recv.at[j, k], down)

    def to_x(at, k, source, number):
        return send(source, kinds[k][1].at[number], x_send.at[at, k], x_recv.at[at, k], x_device)

    for k, (own, _) in enumerate(kinds):

        @pl.when(z < 3)
        def _(k=k, own=own):
            to_right(0, k, own, s).start()

        @pl.when(z > 0)
        def _(k=k, own=own):
            to_left(0, k, own, s).start()

        to_x(z, k, own, s).start()
    for j in (1, 2, 3):
        lower, upper = s - 2 * j, s + 2 * j
        for k, (_, out) in enumerate(kinds):

            @pl.when(z >= j)
            def _(j=j, k=k, out=out, lower=lower):
                block = out.at[lower]
                to_right(j - 1, k, block, lower).wait_recv()

                @pl.when(z < 3)
                def _():
                    to_right(j, k, block, lower).start()

                to_x(z - j, k, block, lower).start()

            @pl.when(z + j <= 3)
            def _(j=j, k=k, out=out, upper=upper):
                block = out.at[upper]
                to_left(j - 1, k, block, upper).wait_recv()

                @pl.when(z > 0)
                def _():
                    to_left(j, k, block, upper).start()

                to_x(z + j, k, block, upper).start()

    weight_y.wait_recv()
    weight_on.start()
    for k, (own, _) in enumerate(kinds):
        for number in range(4):
            done = to_x(number, k, own, s)
            done.wait_send()
            done.wait_recv()
        for j in range(3):

            @pl.when((z >= j) & (z < 3))
            def _(j=j, k=k, own=own):
                to_right(j, k, own, s).wait_send()

            @pl.when((z + j <= 3) & (z > 0))
            def _(j=j, k=k, own=own):
                to_left(j, k, own, s).wait_send()

    weight_core.wait_recv()
    weight_on.wait_recv()
    for copy in (weight_y, weight_core, weight_on):
        copy.wait_send()
    for copy in copies:
        copy.wait()


def gather_first(own, tail, weight):
    seqs, parts = lax.axis_size("seq"), lax.axis_size("wsh")
    if seqs != 8 or parts != 4:
        return (
            lax.all_gather(own, "seq", axis=0, tiled=False),
            lax.all_gather(tail, "seq", axis=0, tiled=False),
            lax.all_gather(weight, "wsh", axis=0, tiled=False),
        )
    dma = pltpu.SemaphoreType.DMA
    given = ((seqs, own), (seqs, tail), (parts, weight))
    return pl.pallas_call(
        gather_kernel,
        in_specs=[pl.BlockSpec(memory_space=pltpu.VMEM)] * 3,
        out_specs=[pl.BlockSpec(memory_space=pl.ANY)] * 3,
        out_shape=[jax.ShapeDtypeStruct((n,) + x.shape, x.dtype) for n, x in given],
        scratch_shapes=[dma((3,))] + [dma((3, 2))] * 4 + [dma((4, 2))] * 2 + [dma((2,))] * 2 + [dma] * 2,
        compiler_params=pltpu.CompilerParams(collective_id=1, has_side_effects=True),
        cost_estimate=pl.CostEstimate(flops=0, bytes_accessed=100 << 20, transcendentals=0),
        name="gather_first",
    )(own, tail, weight)


def reduce_kernel(
    splits, x_ref, out_ref, x_buf, right_buf, left_buf, right_out, left_out,
    x_send, x_recv, right_send, right_recv, left_send, left_recv,
):
    s, w, side, z, x_device, _, _ = places()
    up, down = (s + 2, w), (s - 2, w)
    size = x_ref.shape[2] // splits
    columns = [slice(c * size, (c + 1) * size) for c in range(splits)]
    greet(((None, x_device), (z < 3, up), (z > 0, down)), 1 + line_ends(z))

    def to_x(target, c):
        return send(
            x_ref.at[target * 2 + 1 - side, :, columns[c]], x_buf.at[target, :, columns[c]],
            x_send.at[target, c], x_recv.at[target, c], x_device,
        )

    def start_x(target):
        for c in range(splits):
            to_x(target, c).start()

    def to_right(k, c):
        return send(
            right_out.at[k - 1, :, columns[c]], right_buf.at[k - 1, :, columns[c]],
            right_send.at[k - 1, c], right_recv.at[k - 1, c], up,
        )

    def to_left(k, c):
        return send(
            left_out.at[k - 1, :, columns[c]], left_buf.at[k - 1, :, columns[c]],
            left_send.at[k - 1, c], left_recv.at[k - 1, c], down,
        )

    def pair(target, c):
        to_x(target, c).wait_recv()
        return x_ref[target * 2 + side, :, columns[c]].astype(F32) + x_buf[target, :, columns[c]].astype(F32)

    for k in (3, 2, 1):

        @pl.when(z + k <= 3)
        def _(k=k):
            start_x(z + k)

        @pl.when(z >= k)
        def _(k=k):
            start_x(z - k)

    start_x(z)
    for k in (3, 2, 1):
        for c in range(splits):

            @pl.when(z + k <= 3)
            def _(k=k, c=c):
                right_out[k - 1, :, columns[c]] = pair(z + k, c).astype(BF16)
                if k < 3:

                    @pl.when(z > 0)
                    def _():
                        to_right(k + 1, c).wait_recv()
                        right_out[k - 1, :, columns[c]] = (
                            right_out[k - 1, :, columns[c]].astype(F32) + right_buf[k, :, columns[c]].astype(F32)
                        ).astype(BF16)

                to_right(k, c).start()

            @pl.when(z >= k)
            def _(k=k, c=c):
                left_out[k - 1, :, columns[c]] = pair(z - k, c).astype(BF16)
                if k < 3:

                    @pl.when(z < 3)
                    def _():
                        to_left(k + 1, c).wait_recv()
                        left_out[k - 1, :, columns[c]] = (
                            left_out[k - 1, :, columns[c]].astype(F32) + left_buf[k, :, columns[c]].astype(F32)
                        ).astype(BF16)

                to_left(k, c).start()

    for c in range(splits):
        out_ref[:, columns[c]] = pair(z, c)

        @pl.when(z > 0)
        def _(c=c):
            to_right(1, c).wait_recv()
            out_ref[:, columns[c]] += right_buf[0, :, columns[c]].astype(F32)

        @pl.when(z < 3)
        def _(c=c):
            to_left(1, c).wait_recv()
            out_ref[:, columns[c]] += left_buf[0, :, columns[c]].astype(F32)

    for c in range(splits):
        for target in range(4):
            to_x(target, c).wait_send()
        for k in (3, 2, 1):

            @pl.when(z + k <= 3)
            def _(k=k, c=c):
                to_right(k, c).wait_send()

            @pl.when(z >= k)
            def _(k=k, c=c):
                to_left(k, c).wait_send()


def reduce_seq(x):
    seqs, rows, width = x.shape
    splits = 2
    vmem = pl.BlockSpec(memory_space=pltpu.VMEM)
    dma = pltpu.SemaphoreType.DMA
    return pl.pallas_call(
        functools.partial(reduce_kernel, splits),
        in_specs=[vmem],
        out_specs=vmem,
        out_shape=jax.ShapeDtypeStruct((rows, width), F32),
        scratch_shapes=[pltpu.VMEM((4, rows, width), BF16)]
        + [pltpu.VMEM((3, rows, width), BF16)] * 4
        + [dma((4, splits))] * 2 + [dma((3, splits))] * 4,
        compiler_params=pltpu.CompilerParams(collective_id=2, has_side_effects=True, vmem_limit_bytes=40 << 20),
        cost_estimate=pl.CostEstimate(flops=0, bytes_accessed=1 << 20, transcendentals=0),
        name="reduce_seq",
    )(x)


def deal_kernel(to_heads, x_ref, out_ref, send_sem, recv_sem):
    s, w, _, _, _, _, _ = places()
    tall, thin = (out_ref, x_ref) if to_heads else (x_ref, out_ref)
    columns, rows = tall.shape[1], thin.shape[0]

    def column(number):
        return pl.ds(pl.multiple_of(number * columns, columns), columns)

    def row(number):
        return pl.ds(pl.multiple_of(number * rows, rows), rows)

    greet(tuple((None, ((s + d) % 8, w)) for d in range(1, 8)), 7)

    def copy(d):
        target = (s + d) % 8
        if to_heads:
            source, goal = x_ref.at[:, column(target)], out_ref.at[row(s)]
        else:
            source, goal = x_ref.at[row(target)], out_ref.at[:, column(s)]
        return send(source, goal, send_sem.at[d - 1], recv_sem.at[d - 1], (target, w))

    for d in (4, 3, 5, 2, 6, 1, 7):
        copy(d).start()
    if to_heads:
        out_ref[row(s), :] = x_ref[:, column(s)]
    else:
        out_ref[:, column(s)] = x_ref[row(s), :]
    for d in range(1, 8):
        copy(d).wait_recv()
        copy(d).wait_send()


def deal(x, to_heads):
    seqs = lax.axis_size("seq")
    if seqs != 8 or lax.axis_size("wsh") != 4:
        if to_heads:
            split = x.reshape(x.shape[0], seqs, -1).transpose(1, 0, 2)
            return exchange(split, "seq").reshape(x.shape[0] * seqs, -1)
        moved = exchange(x.reshape(seqs, x.shape[0] // seqs, -1), "seq")
        return moved.transpose(1, 0, 2).reshape(x.shape[0] // seqs, -1)
    shape = (x.shape[0] * seqs, x.shape[1] // seqs) if to_heads else (x.shape[0] // seqs, x.shape[1] * seqs)
    vmem, dma = pl.BlockSpec(memory_space=pltpu.VMEM), pltpu.SemaphoreType.DMA
    return pl.pallas_call(
        functools.partial(deal_kernel, to_heads),
        in_specs=[vmem],
        out_specs=vmem,
        out_shape=jax.ShapeDtypeStruct(shape, x.dtype),
        scratch_shapes=[dma((7,)), dma((7,))],
        compiler_params=pltpu.CompilerParams(collective_id=6 if to_heads else 7, has_side_effects=True),
        cost_estimate=pl.CostEstimate(flops=0, bytes_accessed=60 << 20, transcendentals=0),
        name="deal_heads" if to_heads else "deal_rows",
    )(x)


def channel_kernel(
    forward, x_ref, first_hbm, second_hbm, active_hbm,
    sum_ref, all_hbm, mine_hbm, other_hbm, extra_hbm,
    first, second, rows_all, middle, active, part, core_buf, far_out, far_buf,
    load_sem, store_sem, core_send, core_recv, y_send, y_recv, x_send, x_recv, r_send, r_recv, f_send, f_recv,
):
    s, w, side, z, x_device, core_device, y_device = places()
    rows, width = x_ref.shape
    units = first.shape[0]
    half = units // 2
    loads = [
        pltpu.make_async_copy(first_hbm, first, load_sem.at[0]),
        pltpu.make_async_copy(second_hbm, second, load_sem.at[1]),
    ]
    for load in loads:
        load.start()
    if not forward:
        loads.append(pltpu.make_async_copy(active_hbm, active, load_sem.at[2]))
        loads[2].start()
    rows_all[0:rows] = x_ref[...]
    greet(((None, x_device), (None, core_device), (None, y_device)), 3)

    def block(number):
        return rows_all.at[pl.ds(number * rows, rows)]

    to_core = [
        send(block(0), block(1), core_send.at[0], core_recv.at[0], core_device),
        send(block(2), block(3), core_send.at[1], core_recv.at[1], core_device),
    ]
    to_y = send(block(0), block(2), y_send, y_recv, y_device)
    if forward:
        to_x = [
            send(
                middle.at[1 - side, pl.ds(2 * n * rows, 2 * rows)], other_hbm.at[pl.ds(2 * n * rows, 2 * rows)],
                x_send.at[n], x_recv.at[n], x_device,
            )
            for n in range(2)
        ]
    else:
        to_x = [
            send(block(n), other_hbm.at[pl.ds(n * rows, rows)], x_send.at[n], x_recv.at[n], x_device) for n in range(4)
        ]
    sums_core = [
        send(part.at[pl.ds((2 * n + 1) * rows, rows)], core_buf.at[n], r_send.at[n], r_recv.at[n], core_device)
        for n in range(2)
    ]
    far = send(far_out, far_buf, f_send, f_recv, y_device)
    stores = [
        pltpu.make_async_copy(rows_all, all_hbm, store_sem.at[0]),
        pltpu.make_async_copy(middle.at[side], mine_hbm, store_sem.at[1]),
        pltpu.make_async_copy(active if forward else middle.at[1 - side], extra_hbm, store_sem.at[2]),
    ]

    def pass_on(number):
        if not forward:
            to_x[number].start()

    to_y.start()
    to_core[0].start()
    pass_on(0)
    tile = min(512, half)

    def multiply(number):
        two = pl.ds(2 * number * rows, 2 * rows)

        def up(t, carry):
            for side_units in range(2):
                at = pl.multiple_of(t * tile, tile)
                unit = pl.multiple_of(side_units * half + at, tile)
                raw = dot(rows_all[two, :], first[pl.ds(unit, tile), :], NT)
                if forward:
                    raw = jnp.maximum(raw, 0.0)
                    active[two, pl.ds(unit, tile)] = raw
                    mid = raw * raw
                else:
                    mid = raw * 2.0 * active[two, pl.ds(unit, tile)]
                middle[side_units, two, pl.ds(at, tile)] = mid.astype(BF16)
            return carry

        lax.fori_loop(0, half // tile, up, 0)
        if forward:
            to_x[number].start()
        if number == 0:
            loads[1].wait()

        def down(t, carry):
            at = pl.multiple_of(t * tile, tile)
            part[two, pl.ds(at, tile)] = dot(middle[0, two, :], second[0:half, pl.ds(at, tile)]) + dot(
                middle[1, two, :], second[half:units, pl.ds(at, tile)]
            )
            return carry

        lax.fori_loop(0, width // tile, down, 0)
        sums_core[number].start()

    loads[0].wait()
    if not forward:
        loads[2].wait()
    to_core[0].wait_recv()
    pass_on(1)
    multiply(0)
    to_y.wait_recv()
    to_core[1].start()
    pass_on(2)
    to_core[1].wait_recv()
    pass_on(3)
    stores[0].start()
    multiply(1)
    for store in stores[1:]:
        store.start()
    sums_core[1].wait_recv()
    far_out[...] = (part[2 * rows : 3 * rows] + core_buf[1]).astype(BF16)
    far.start()
    sums_core[0].wait_recv()
    sum_ref[...] = part[0:rows] + core_buf[0]
    far.wait_recv()
    sum_ref[...] += far_buf[...].astype(F32)
    for copy in to_x:
        copy.wait_recv()
    for copy in to_x + to_core + sums_core + [to_y, far]:
        copy.wait_send()
    for store in stores:
        store.wait()


def channel_stage(x, first, second, active):
    rows, width = x.shape
    units = first.shape[0]
    forward = active is None
    given = (x, first, second) if forward else (x, first, second, active)
    everything = pl.BlockSpec(memory_space=pl.ANY)
    shapes = [
        ((rows, width), F32), ((4 * rows, width), BF16), ((4 * rows, units // 2), BF16),
        ((4 * rows, units // 2 if forward else width), BF16),
        ((4 * rows, units), F32) if forward else ((4 * rows, units // 2), BF16),
    ]

    def body(*refs):
        refs = list(refs)
        if forward:
            refs.insert(3, None)
        channel_kernel(forward, *refs)

    dma = pltpu.SemaphoreType.DMA
    return pl.pallas_call(
        body,
        in_specs=[pl.BlockSpec(memory_space=pltpu.VMEM)] + [everything] * (len(given) - 1),
        out_specs=[pl.BlockSpec(memory_space=pltpu.VMEM)] + [everything] * (len(shapes) - 1),
        out_shape=[jax.ShapeDtypeStruct(s, d) for s, d in shapes],
        scratch_shapes=[
            pltpu.VMEM((units, width), BF16), pltpu.VMEM((units, width), BF16), pltpu.VMEM((4 * rows, width), BF16),
            pltpu.VMEM((2, 4 * rows, units // 2), BF16), pltpu.VMEM((4 * rows, units), F32),
            pltpu.VMEM((4 * rows, width), F32), pltpu.VMEM((2, rows, width), F32),
            pltpu.VMEM((rows, width), BF16), pltpu.VMEM((rows, width), BF16),
            dma((3,)), dma((3,)), dma((2,)), dma((2,)), dma, dma, dma((4,)), dma((4,)), dma((2,)), dma((2,)),
            dma, dma,
        ],
        compiler_params=pltpu.CompilerParams(
            collective_id=3 if forward else 4, has_side_effects=True, vmem_limit_bytes=60 << 20
        ),
        cost_estimate=pl.CostEstimate(flops=0, bytes_accessed=100 << 20, transcendentals=0),
        name="channel_forward" if forward else "channel_backward",
    )(*given)


def from_behind(x, axis, by):
    size = lax.axis_size(axis)
    pairs = [(i, i + by) for i in range(size) if 0 <= i + by < size]
    return lax.ppermute(x, axis, pairs)


def exchange(x, axis):
    return lax.all_to_all(x, axis, split_axis=0, concat_axis=0, tiled=True)


def swap(x, by):
    size = lax.axis_size("wsh")
    return lax.ppermute(x, "wsh", [(i, i ^ by) for i in range(size)])


def gather_near(x):
    if lax.axis_size("wsh") != 4:
        return lax.all_gather(x, "wsh", axis=0, tiled=True)
    return gathered_near(x, swap(x, 1), swap(x, 2))


def gathered_near(x, beside, across):
    return jnp.concatenate([x, beside, across, swap(across, 1)], 0)


def beside(x):
    return lax.ppermute(x, "seq", [(i, i ^ 1) for i in range(lax.axis_size("seq"))])


def scalar_sum(x):
    if lax.axis_size("wsh") != 4:
        return jnp.sum(lax.all_gather(x.reshape(1), "wsh", axis=0, tiled=True))
    x = jnp.full((8, 128), x)
    x = x + swap(x, 1)
    return (x + swap(x, 2))[0, 0]


def near_sum(x):
    if lax.axis_size("wsh") != 4:
        return lax.psum_scatter(x, "wsh", scatter_dimension=0, tiled=True)
    rows = x.shape[0] // 4
    beside = swap(jnp.concatenate([x[rows : 2 * rows], x[3 * rows :]], 0), 1)
    far = x[2 * rows : 3 * rows] + beside[rows:]
    return x[:rows] + beside[:rows] + swap(far.astype(BF16), 2).astype(F32)


def block_sum(x):
    if lax.axis_size("wsh") != 4:
        return lax.psum_scatter(x, "wsh", scatter_dimension=0, tiled=False).astype(F32)
    kept, far = block_halves(x)
    return kept + swap(far, 2).astype(F32)


def block_halves(x):
    number = lax.axis_index("wsh")

    def block(by):
        return lax.dynamic_index_in_dim(x, number ^ by, 0, keepdims=False)

    beside = swap(jnp.stack([block(1), block(3)]), 1).astype(F32)
    return block(0).astype(F32) + beside[0], (block(2).astype(F32) + beside[1]).astype(BF16)


def local(
    tokens, first_layer_values, teacher, valid, destination, lengths,
    receptance_matrix, key_matrix, value_matrix, output_matrix,
    lowrank_down_weight, lowrank_up_weight, channel_key_weight, channel_value_weight, vectors,
):
    rows, width = tokens.shape
    seqs, parts = lax.axis_size("seq"), lax.axis_size("wsh")
    me = lax.axis_index("seq")
    group = rows * seqs
    own_width = width // seqs
    shard = width // parts
    piece = shard // seqs
    column = me * own_width

    def own_columns(matrix):
        return lax.dynamic_slice_in_dim(matrix, column, own_width, 1)

    near = parts == 4
    up_piece = lax.dynamic_slice_in_dim(lowrank_up_weight, column % shard, own_width, 0)
    total = 3 * own_width + WIDE
    own_weights = jnp.concatenate(
        [
            own_columns(receptance_matrix), own_columns(key_matrix), own_columns(value_matrix),
            pad_ranks(lowrank_down_weight), up_piece.reshape(shard, -1),
        ],
        1,
    )

    dest_seq = destination // rows // parts
    position = dest_seq * rows + destination % rows
    digits = jnp.stack([position // DIGIT, position % DIGIT, valid], 1).astype(BF16)
    tail = jnp.pad(digits, ((0, 0), (0, EXTRA - 3)))
    given, tails, weights = gather_first(tokens, tail, own_weights)
    given, tails, weights = given.reshape(group, width), tails.reshape(group, EXTRA), weights.reshape(width, -1)
    info = tails[:, :3].astype(F32)
    places = (info[:, 0] * DIGIT + info[:, 1]).astype(jnp.int32)
    numbers = jnp.arange(group, dtype=jnp.int32)
    permute = (numbers[:, None] == places[None, :]).astype(BF16)
    total_valid = scalar_sum(jnp.sum(info[:, 2]))

    index = jnp.arange(rows, dtype=jnp.int32)
    same_dest = (dest_seq[:, None] == dest_seq[None, :]) & (index[None, :] < index[:, None])
    slot = dest_seq * (rows // seqs) + jnp.sum(same_dest.astype(jnp.int32), 1)
    arrange = (index[:, None] == slot[None, :]).astype(BF16)
    mine = (places // rows) == me
    arrival = jnp.cumsum(mine.astype(jnp.int32)) - 1
    own_rows = ((index[:, None] + me * rows) == places[None, :]).astype(BF16)
    settle = dot(own_rows, (mine[:, None] & (arrival[:, None] == index[None, :])).astype(BF16)).astype(BF16)

    offsets = jnp.cumsum(lengths[0]) - lengths[0]
    starts = jnp.any(numbers[:, None] == offsets[None, :], 1).astype(F32)
    segment_ids = jnp.cumsum(starts).reshape(-1, BLOCK)
    before = segment_ids[:, :1] - starts.reshape(-1, BLOCK)[:, :1]
    segments = jnp.stack(
        [segment_ids, jnp.broadcast_to(before, segment_ids.shape), jnp.broadcast_to(segment_ids[:, -1:], segment_ids.shape)]
        + [jnp.zeros_like(segment_ids)] * 5,
        1,
    ).reshape(-1, BLOCK)
    flowing = (1.0 - starts)[:, None]

    up = pad_ranks(
        lax.dynamic_slice(
            weights, (column // shard * shard, total), (shard, weights.shape[1] - total)
        ).reshape(own_width, -1)
    ).T
    vec = lax.dynamic_slice_in_dim(vectors, column, own_width, 0)[:, 8:16].T

    output_late, given = lax.optimization_barrier((output_matrix, given))
    w_out = lax.all_gather(output_late, "wsh", axis=0, tiled=True)
    balanced = dot(permute, given).astype(BF16)
    wide_rows = balanced.astype(F32)
    mean = jnp.mean(wide_rows, -1, keepdims=True)
    scale_one = lax.rsqrt(jnp.mean(jnp.square(wide_rows - mean), -1, keepdims=True) + 1e-05)
    stats = jnp.concatenate([mean, scale_one, flowing, flowing], 1)
    mix_vec = vectors[:, :8].T
    first_values, stats = lax.optimization_barrier((first_layer_values, stats))
    first_given = exchange(
        first_values.reshape(rows, seqs, own_width).transpose(1, 0, 2), "seq"
    ).reshape(group, own_width)
    recept, keys, values, downs, hidden = run_project(balanced, stats, mix_vec, weights, own_width, parts)
    teacher_late, recept, first_given = lax.optimization_barrier((teacher, recept, first_given))
    first = dot(permute, first_given).astype(BF16)
    teacher_rows = exchange(dot(arrange, teacher_late).astype(BF16).reshape(seqs, rows // seqs, width), "seq")
    inputs = (recept, keys, values, hidden, first, up, vec, segments)
    mixed_out, *saved = run_forward(*inputs)
    teacher_rows, mixed_out, total_valid = lax.optimization_barrier((teacher_rows, mixed_out, total_valid))
    target = dot(settle, teacher_rows.reshape(rows, width))

    mixed_rows = deal(mixed_out, False)
    own = lax.dynamic_slice_in_dim(balanced, me * rows, rows, 0).astype(F32)
    own_starts = lax.dynamic_slice_in_dim(starts, me * rows, rows, 0)
    own_flowing = (1.0 - own_starts)[:, None]
    own_valid = dot(own_rows, tails)[:, 2]
    residual = own + dot(mixed_rows, w_out)
    standard_two, scale_two = norm_stats(residual)
    normed_two = standard_two * vectors[:, 16] + vectors[:, 17]
    carried_two = from_behind(normed_two[-1:], "seq", 1)
    delta_two = jnp.concatenate([carried_two, normed_two[:-1]], 0) * own_flowing - normed_two
    channel_in = (normed_two + delta_two * vectors[:, 18]).astype(BF16)
    paired = near and seqs == 8
    if paired:
        summed, channel, hidden_mine, hidden_other, active = channel_stage(
            channel_in, channel_key_weight, channel_value_weight, None
        )
    else:
        channel = gather_near(channel_in)
        active = jax.nn.relu(dot(channel, channel_key_weight, NT))
        hidden_rows = jnp.square(active).astype(BF16)
        summed = near_sum(dot(hidden_rows, channel_value_weight))
    result = residual + summed
    total_tokens = group * parts
    cotangent = (result - target) * (own_valid * (total_tokens / total_valid))[:, None]
    cot_low = cotangent.astype(BF16)

    result_back = exchange(dot(settle, result.astype(BF16), TN).astype(BF16).reshape(seqs, rows // seqs, width), "seq")
    if paired:
        grad_channel, cot, pre_mine, cot_other, pre_spare = channel_stage(
            cot_low, channel_value_weight, channel_key_weight, active
        )
    else:
        cot = gather_near(cot_low)
        grad_pre = (dot(cot, channel_value_weight, NT) * 2.0 * active).astype(BF16)
        grad_channel = near_sum(dot(grad_pre, channel_key_weight))
    if paired:
        value_part = (dot(hidden_mine, cot, TN) + dot(hidden_other, cot_other, TN)).astype(BF16)
    else:
        value_part = dot(hidden_rows, cot, TN).astype(BF16)
    result_back, grad_channel, value_part = lax.optimization_barrier((result_back, grad_channel, value_part))
    output = dot(arrange, result_back.reshape(rows, width), TN).astype(BF16)
    grad_vec_mix_two = jnp.sum(grad_channel * delta_two, 0)
    shifted = grad_channel * vectors[:, 18] * own_flowing
    behind = from_behind(shifted[:1], "seq", -1)
    grad_normed_two = grad_channel * (1.0 - vectors[:, 18]) + jnp.concatenate([shifted[1:], behind], 0)
    grad_residual = cotangent + norm_back(grad_normed_two, standard_two, scale_two, vectors[:, 16])
    grad_low = grad_residual.astype(BF16)

    grad_posted = dot(grad_low, w_out, NT).astype(BF16)
    grad_heads = deal(grad_posted, True)
    if paired:
        grad_heads, value_part, mixed_late, channel, pre_spare = lax.optimization_barrier(
            (grad_heads, value_part, mixed_rows, channel, pre_spare)
        )
        channel_other, pre_other = beside(channel), beside(pre_spare)
    else:
        grad_heads, mixed_late = lax.optimization_barrier((grad_heads, mixed_rows))
    lefts = exchange(mixed_late.reshape(rows, seqs, parts, piece).transpose(2, 0, 1, 3), "wsh")
    near_grad = (swap(grad_low, 1), swap(grad_low, 2)) if near else gather_near(grad_low)
    recept_low, keys_low, values_low, ups_low, grad_first, grad_vec_heads = run_backward(grad_heads, *inputs, saved)
    if paired:
        channel_other, pre_mine, pre_other, lefts, near_grad, recept_low = lax.optimization_barrier(
            (channel_other, pre_mine, pre_other, lefts, near_grad, recept_low)
        )
        key_part = (dot(pre_mine, channel, TN) + dot(pre_other, channel_other, TN)).astype(BF16)
    else:
        lefts, near_grad, recept_low = lax.optimization_barrier((lefts, near_grad, recept_low))
        key_part = dot(grad_pre, channel, TN).astype(BF16)
    if near:
        near_grad = gathered_near(grad_low, *near_grad)
        lefts = jnp.stack([lax.dynamic_index_in_dim(lefts, lax.axis_index("wsh") ^ k, 0, keepdims=False) for k in range(4)])
    out_part = dot(lefts.reshape(rows * parts, -1), near_grad, TN).astype(BF16)

    moved = exchange(dot(permute, grad_first, TN).astype(BF16).reshape(seqs, rows, own_width), "seq")
    recept_low, key_part, out_part = lax.optimization_barrier((recept_low, key_part, out_part))
    if paired:
        lines = [[0, 2, 4, 6], [1, 3, 5, 7]]
        def along(part):
            return lax.psum_scatter(part, "seq", scatter_dimension=0, tiled=True, axis_index_groups=lines)

        halves_out = out_part.reshape(seqs // 2, 2, piece, width)
        x_side = me % 2
        out_mine = lax.dynamic_index_in_dim(halves_out, x_side, 1, keepdims=False).astype(F32)
        out_other = beside(lax.dynamic_index_in_dim(halves_out, 1 - x_side, 1, keepdims=False))
        value_sum, key_sum = along(value_part), along(key_part)
    else:
        moves = [(s * parts + w, w * seqs + s) for s in range(seqs) for w in range(parts)]

        def ffn_grad(part):
            part = lax.psum_scatter(part, "seq", scatter_dimension=0, tiled=True)
            return lax.ppermute(part, ("seq", "wsh"), moves).astype(F32)

        grad_ffn_value, grad_ffn_key = ffn_grad(value_part), ffn_grad(key_part)
        grad_out = lax.psum_scatter(out_part, "seq", scatter_dimension=0, tiled=True)

    heads_part = lax.dynamic_update_slice_in_dim(jnp.zeros((width, 8), F32), grad_vec_heads.T, column, 0)
    vec_two = jnp.stack(
        [jnp.sum(grad_normed_two * standard_two, 0), jnp.sum(grad_normed_two, 0), grad_vec_mix_two], 1
    )
    others = jnp.concatenate([heads_part, jnp.pad(vec_two, ((0, 0), (0, 13)))], 1)
    scaled_grad, sums, wide, up_grad = run_unproject(
        balanced, stats, mix_vec, weights, others, (recept_low, keys_low, values_low), ups_low, hidden, downs, up, parts
    )
    if paired:
        moved, value_sum, out_other, scaled_grad, sums, wide, up_grad = lax.optimization_barrier(
            (moved, value_sum, out_other, scaled_grad, sums, wide, up_grad)
        )
        out_half = (out_mine + out_other.astype(F32)).astype(BF16).reshape(-1, width)
        out_half, sums = lax.optimization_barrier((out_half, sums))
        grad_out = along(out_half)
    else:
        moved, scaled_grad, sums, wide = lax.optimization_barrier((moved, scaled_grad, sums, wide))
    grad_first_rows = moved.transpose(1, 0, 2).reshape(rows, width)

    standard = (balanced.astype(F32) - mean) * scale_one
    grad_balanced = scale_one * (scaled_grad - sums[:, :1] * (1.0 / width) - standard * (sums[:, 1:] * (1.0 / width)))
    mine_rows = lax.dynamic_slice_in_dim(grad_balanced, me * rows, rows, 0) + grad_residual
    grad_balanced = lax.dynamic_update_slice_in_dim(grad_balanced, mine_rows, me * rows, 0)
    grad_given = dot(permute, grad_balanced.astype(BF16), TN).astype(BF16).reshape(seqs, rows, width)
    if near:
        kept_part, far = block_halves(wide)
        kept_up, far_up = block_halves(up_grad.reshape(parts, piece, WIDE))
        if paired:
            grad_given, far, far_up, key_sum = lax.optimization_barrier((grad_given, far, far_up, key_sum))
        wide_part, across_up = kept_part + swap(far, 2).astype(F32), swap(far_up, 2)
    else:
        wide_part = block_sum(wide)
    if paired:
        grad_tokens = reduce_seq(grad_given)
        turned = [
            ((z * 2 + x) * 4 + w, (w * 2 + x) * 4 + z) for z in range(4) for x in range(2) for w in range(4)
        ]
        value_turned = lax.ppermute(value_sum, ("seq", "wsh"), turned)
        wide_part, grad_tokens, grad_out, value_turned, across_up, key_sum = lax.optimization_barrier(
            (wide_part, grad_tokens, grad_out, value_turned, across_up, key_sum)
        )
        grad_ffn_key = lax.ppermute(key_sum, ("seq", "wsh"), turned).astype(F32)
        grad_ffn_value = value_turned.astype(F32)
    else:
        grad_tokens = jnp.sum(exchange(grad_given, "seq").astype(F32), 0)
    wide_all = exchange(wide_part.astype(BF16), "seq").astype(F32)

    def square(at):
        taken = wide_all[:, :, at * own_width : (at + 1) * own_width]
        return taken.transpose(1, 0, 2).reshape(piece, width)

    narrow = jnp.sum(wide_all[:, :, 3 * own_width :], 0)
    grad_down = unpad_ranks(narrow)
    grad_vectors = narrow[:, RANKS[0] : RANKS[0] + vectors.shape[1]]
    up_part = unpad_ranks(kept_up + across_up.astype(F32) if near else block_sum(up_grad.reshape(parts, piece, WIDE)))

    return (
        output, grad_tokens.astype(BF16), grad_first_rows,
        square(0), square(1), square(2),
        grad_out.astype(F32), grad_down, up_part,
        grad_ffn_key, grad_ffn_value, grad_vectors,
    )


def solution(mesh):
    both, shard = P(("seq", "wsh"), None), P("wsh", None)
    flat = P(("seq", "wsh"))
    return jax.shard_map(
        local,
        mesh=mesh,
        in_specs=(both, both, both, flat, flat) + (shard,) * 9 + (P(),),
        out_specs=(both,) * 12,
        check_vma=False,
    )
```

```python
import functools

import jax
import jax.numpy as jnp
from jax import lax
from jax.experimental import pallas as pl
from jax.experimental.pallas import tpu as pltpu
from jax.sharding import PartitionSpec as P

HEAD = 64
BLOCK = 64
RANKS = (96, 96, 64, 256)
PADDED = (128, 128, 128, 256)
OFFSETS = (0, 128, 256, 384)
WIDE = 640
EXTRA = 128
DIGIT = 64

F32 = jnp.float32
BF16 = jnp.bfloat16

NN = (((1,), (0,)), ((), ()))
NT = (((1,), (1,)), ((), ()))
TN = (((0,), (0,)), ((), ()))


def dot(a, b, dims=NN):
    return lax.dot_general(a, b, dims, preferred_element_type=F32)


def halves(x):
    high = x.astype(BF16)
    return high, (x - high.astype(F32)).astype(BF16)


def dot3(a, b, dims=NN):
    a_high, a_low = halves(a)
    b_high, b_low = halves(b)
    return dot(a_high, b_high, dims) + (dot(a_high, b_low, dims) + dot(a_low, b_high, dims))


def sum_left(mask, x):
    high, low = halves(x)
    low_two = (x - high.astype(F32) - low.astype(F32)).astype(BF16)
    return dot(mask, high) + (dot(mask, low) + dot(mask, low_two))


def head_sum(x, ones):
    high, low = halves(x)
    return dot(high, ones) + dot(low, ones)


def low(x):
    return x.astype(BF16).astype(F32)


def iotas(rows, columns):
    return (
        lax.broadcasted_iota(jnp.int32, (rows, columns), 0),
        lax.broadcasted_iota(jnp.int32, (rows, columns), 1),
    )


def head_ones(width):
    i, j = iotas(width, width)
    return jnp.where((i >> 6) == (j >> 6), 1.0, 0.0).astype(BF16)


def front(keys, values, hidden, up, first, vec, ones):
    z = vec[0:1] + dot(hidden[:, 0:128], up[0:128])
    decay_log = -(jnp.maximum(-z, 0.0) + jnp.log1p(jnp.exp(-jnp.abs(z)))) - 0.5
    rate = jax.nn.sigmoid(vec[1:2] + dot(hidden[:, 128:256], up[128:256]))
    blend = jax.nn.sigmoid(vec[2:3] + dot(hidden[:, 256:384], up[256:384]))
    gate = dot(hidden[:, 384:640], up[384:640])
    mixed_value = values + (first - values) * blend
    scaled = keys * vec[3:4]
    scale = lax.rsqrt(head_sum(scaled * scaled, ones) + 1e-06)
    key_dir = scaled * scale
    key_mod = keys * (1.0 + (rate - 1.0) * vec[4:5])
    return z, decay_log, rate, blend, gate, mixed_value, scale, key_dir, key_mod


def block_masks(segments):
    i, j = iotas(BLOCK, BLOCK)
    across = jnp.broadcast_to(segments[0:1], (BLOCK, BLOCK))
    down = across.T
    before = jnp.broadcast_to(segments[1:2], (BLOCK, BLOCK))
    last = jnp.broadcast_to(segments[2:3], (BLOCK, BLOCK))
    same = across == down
    strict = jnp.where(same & (i > j), 1.0, 0.0)
    closed = jnp.where(same & (i >= j), 1.0, 0.0)
    carry = jnp.where(down == before, 1.0, 0.0)
    tail = jnp.where(down == last, 1.0, 0.0)
    keep = jnp.where(segments[2:3] == segments[1:2], 1.0, 0.0)
    quad = jnp.concatenate(
        [jnp.concatenate([strict, strict], 1), jnp.concatenate([closed, closed], 1)], 0
    )
    return quad, carry, tail, keep


def tile_heads(x, heads):
    return jnp.concatenate([x] * heads, 1) if heads > 1 else x


def join(pieces, axis):
    return jnp.concatenate(pieces, axis) if len(pieces) > 1 else pieces[0]


def decayed(decay_low, key_low, dir_low, rate_low, recept_low, carry, tail):
    i, j = iotas(BLOCK, BLOCK)
    lower = jnp.where(i >= j, 1.0, 0.0).astype(BF16)
    log_step = -jnp.exp(decay_low)
    total = sum_left(lower, log_step)
    before = jnp.exp(total - log_step)
    grown = jnp.exp(total)
    shrunk = jnp.exp(-total)
    end = total[BLOCK - 1 : BLOCK]
    tail_decay = jnp.exp(end - total) * tail
    alpha = -dir_low * before
    beta_plain = dir_low * rate_low
    beta = beta_plain * shrunk
    key = key_low * shrunk
    recept = recept_low * grown
    return dict(
        log_step=log_step, before=before, grown=grown, shrunk=shrunk, end=jnp.exp(end), tail=tail_decay,
        alpha=alpha, beta_plain=beta_plain, beta=beta, key=key, recept=recept,
        beta_end=beta_plain * tail_decay, key_end=key_low * tail_decay,
        alpha_in=alpha * carry, recept_in=recept * carry,
    )


def unit_inverses(lowers):
    i, j = iotas(BLOCK, BLOCK)
    eye = jnp.where(i == j, 1.0, 0.0)

    def within(size):
        return (i // size) == (j // size)

    smalls = [jnp.where(within(4), x, 0.0) for x in lowers]
    low_smalls = [x.astype(BF16) for x in smalls]
    twos = [dot(x, x) for x in low_smalls]
    inverses = [eye + x for x in smalls]
    inverses = [x + dot(x.astype(BF16), y.astype(BF16)) for x, y in zip(inverses, twos)]
    for size in (8, 16, 32, 64):
        mask = within(size) & ~within(size // 2)
        offs = [jnp.where(mask, x, 0.0).astype(BF16) for x in lowers]
        lows = [x.astype(BF16) for x in inverses]
        inner = [dot(x, y).astype(BF16) for x, y in zip(offs, lows)]
        inverses = [x + dot(y, z) for x, y, z in zip(inverses, lows, inner)]
    errors = [eye - x + dot3(y, x) for x, y in zip(inverses, lowers)]
    return [x + dot(x.astype(BF16), y.astype(BF16)) for x, y in zip(inverses, errors)]


def post_norm(head_low, ones):
    centered = head_low - head_sum(head_low, ones) * (1.0 / HEAD)
    spread = lax.rsqrt(head_sum(centered * centered, ones) * (1.0 / HEAD) + HEAD * 1e-05)
    return centered * spread, spread


def forward_kernel(
    count, recept_ref, keys_ref, values_ref, hidden_ref, first_ref, up_ref, vec_ref, segment_ref,
    mixed_ref, head_ref, state_ref, inverse_ref, removed_ref, state,
):
    width = recept_ref.shape[1]
    heads = width // HEAD

    @pl.when(pl.program_id(0) == 0)
    def _():
        state[...] = jnp.zeros_like(state)

    ones = head_ones(width)
    vec = vec_ref[...]
    up = up_ref[...]
    columns = [slice(head * HEAD, (head + 1) * HEAD) for head in range(heads)]
    done = []
    for block in range(count):
        rows = slice(block * BLOCK, (block + 1) * BLOCK)
        recept, keys, values = recept_ref[rows], keys_ref[rows], values_ref[rows]
        _, decay_log, rate, _, gate, mixed_value, _, key_dir, key_mod = front(
            keys, values, hidden_ref[rows], up, first_ref[rows].astype(F32), vec, ones
        )
        quad, carry, tail, keep = block_masks(segment_ref[block * 8 : block * 8 + 8])
        parts = decayed(
            low(decay_log), low(key_mod), low(key_dir), low(rate), low(recept),
            tile_heads(carry, heads), tile_heads(tail, heads),
        )
        lefts = [jnp.concatenate([parts["alpha"][:, c], parts["recept"][:, c]], 0) for c in columns]
        rights = [jnp.concatenate([parts["beta"][:, c], parts["key"][:, c]], 0) for c in columns]
        pairs = [quad * dot3(x, y, NT) for x, y in zip(lefts, rights)]
        done.append((rows, recept, key_mod, gate, mixed_value, keep, parts, pairs))
    inverses = unit_inverses([x[:BLOCK, :BLOCK] for item in done for x in item[-1]])
    for block, (rows, recept, key_mod, gate, mixed_value, keep, parts, pairs) in enumerate(done):
        mine = inverses[block * heads : (block + 1) * heads]
        value_low = low(mixed_value)
        owns = [value_low[:, c] for c in columns]
        by_values = [dot3(x[:, BLOCK:], y) for x, y in zip(pairs, owns)]
        ends = [jnp.concatenate([parts["beta_end"][:, c], parts["key_end"][:, c]], 0) for c in columns]
        inners = [jnp.concatenate([parts["alpha_in"][:, c], parts["recept_in"][:, c]], 0) for c in columns]
        entering = state[...]
        state_ref[rows] = entering
        nows = [entering[:, c] for c in columns]
        inwards = [dot3(x, y, NT) for x, y in zip(inners, nows)]
        removals = [dot3(x, y[:BLOCK] + z[:BLOCK]) for x, y, z in zip(mine, inwards, by_values)]
        outs = [
            y[BLOCK:] + z[BLOCK:] + dot3(x[BLOCK:, :BLOCK], r)
            for x, y, z, r in zip(pairs, inwards, by_values, removals)
        ]
        leaving = [
            x * (parts["end"][:, c] * keep) + dot3(jnp.concatenate([r, v], 0), e, TN)
            for x, c, r, v, e in zip(nows, columns, removals, owns, ends)
        ]
        state[...] = join(leaving, 1)
        inverse_ref[rows] = join(mine, 1)
        removed_ref[rows] = join(removals, 1)
        head_low = join(outs, 1).astype(BF16)
        head_ref[rows] = head_low
        normed, _ = post_norm(head_low.astype(F32), ones)
        bonus = head_sum(recept * key_mod * vec[5:6], ones) * mixed_value
        mixed_ref[rows] = ((normed * vec[6:7] + vec[7:8] + bonus) * gate).astype(BF16)


def backward_kernel(
    count, grad_ref, recept_ref, keys_ref, values_ref, hidden_ref, first_ref, up_ref, vec_ref, segment_ref,
    head_ref, state_ref, inverse_ref, removed_ref,
    recept_out, keys_out, values_out, ups_out, first_out, vec_out, state,
):
    width = recept_ref.shape[1]
    heads = width // HEAD

    @pl.when(pl.program_id(0) == 0)
    def _():
        state[...] = jnp.zeros_like(state)
        vec_out[...] = jnp.zeros_like(vec_out)

    ones = head_ones(width)
    vec = vec_ref[...]
    up = up_ref[...]
    i, j = iotas(BLOCK, BLOCK)
    upper = jnp.where(i <= j, 1.0, 0.0).astype(BF16)
    columns = [slice(head * HEAD, (head + 1) * HEAD) for head in range(heads)]
    order = range(count - 1, -1, -1)
    kept = {}
    for block in order:
        rows = slice(block * BLOCK, (block + 1) * BLOCK)
        recept, keys, values = recept_ref[rows], keys_ref[rows], values_ref[rows]
        first = first_ref[rows].astype(F32)
        z, decay_log, rate, blend, gate, mixed_value, scale, key_dir, key_mod = front(
            keys, values, hidden_ref[rows], up, first, vec, ones
        )
        quad, carry, tail, keep = block_masks(segment_ref[block * 8 : block * 8 + 8])
        rate_low, dir_low = low(rate), low(key_dir)
        parts = decayed(
            low(decay_log), low(key_mod), dir_low, rate_low, low(recept),
            tile_heads(carry, heads), tile_heads(tail, heads),
        )
        value_low = low(mixed_value)

        grad = grad_ref[rows].astype(F32)
        normed, spread = post_norm(head_ref[rows].astype(F32), ones)
        product = recept * key_mod
        coefficient = head_sum(product * vec[5:6], ones)
        grad_gate = grad * (normed * vec[6:7] + vec[7:8] + coefficient * mixed_value)
        opened = grad * gate
        grad_normed = opened * vec[6:7]
        grad_head = spread * (
            grad_normed
            - head_sum(grad_normed, ones) * (1.0 / HEAD)
            - normed * (head_sum(grad_normed * normed, ones) * (1.0 / HEAD))
        )
        grad_coefficient = head_sum(opened * mixed_value, ones)
        weighted = grad_coefficient * vec[5:6]
        head_grad = low(grad_head)

        lefts = [jnp.concatenate([parts["alpha"][:, c], parts["recept"][:, c]], 0) for c in columns]
        rights = [jnp.concatenate([parts["beta"][:, c], parts["key"][:, c]], 0) for c in columns]
        ends = [jnp.concatenate([parts["beta_end"][:, c], parts["key_end"][:, c]], 0) for c in columns]
        inners = [jnp.concatenate([parts["alpha_in"][:, c], parts["recept_in"][:, c]], 0) for c in columns]
        pairs = [quad * dot3(x, y, NT) for x, y in zip(lefts, rights)]
        out_grads = [head_grad[:, c] for c in columns]
        through = [dot3(x[BLOCK:, :BLOCK], y, TN) for x, y in zip(pairs, out_grads)]
        kept[block] = dict(
            rows=rows, recept=recept, keys=keys, values=values, first=first, z=z, rate=rate, blend=blend,
            mixed_value=mixed_value, scale=scale, key_dir=key_dir, key_mod=key_mod, quad=quad, carry=carry, keep=keep,
            rate_low=rate_low, dir_low=dir_low, parts=parts, value_low=value_low, normed=normed, product=product,
            grad_gate=grad_gate, opened=opened, grad_coefficient=grad_coefficient,
            grad_mixed_value=opened * coefficient, grad_recept=weighted * key_mod, grad_key_mod=weighted * recept,
            lefts=lefts, rights=rights, ends=ends, inners=inners, pairs=pairs, out_grads=out_grads, through=through,
        )
    for block in order:
        k = kept[block]
        after, entering, inverse_all = state[...], state_ref[k["rows"]], inverse_ref[k["rows"]]
        laters, nows = [after[:, c] for c in columns], [entering[:, c] for c in columns]
        from_ends = [dot3(x, y, NT) for x, y in zip(k["ends"], laters)]
        inner_grads = [
            dot3(inverse_all[:, c], x + y[:BLOCK], TN) for c, x, y in zip(columns, k["through"], from_ends)
        ]
        boths = [jnp.concatenate([x, y], 0) for x, y in zip(inner_grads, k["out_grads"])]
        stays = [x * (k["parts"]["end"][:, c] * k["keep"]) for x, c in zip(laters, columns)]
        state[...] = join([x + dot3(y, z, TN) for x, y, z in zip(stays, boths, k["inners"])], 1)
        k.update(
            laters=laters, nows=nows, from_ends=from_ends, boths=boths,
            end_sum=join([jnp.sum(x * y, 0, keepdims=True) for x, y in zip(nows, stays)], 1),
        )
    vec_total = jnp.zeros_like(vec)
    for block in order:
        k = kept[block]
        rows, parts, quad = k["rows"], k["parts"], k["quad"]
        removed_all = removed_ref[rows]
        carry_two = jnp.concatenate([k["carry"], k["carry"]], 0)
        sources = [jnp.concatenate([removed_all[:, c], k["value_low"][:, c]], 0) for c in columns]
        grad_pairs = [quad * dot3(x, y, NT) for x, y in zip(k["boths"], sources)]
        grad_values = [
            dot3(x[:, BLOCK:], y, TN) + z[BLOCK:] for x, y, z in zip(k["pairs"], k["boths"], k["from_ends"])
        ]
        grad_ends = [dot3(x, y) for x, y in zip(sources, k["laters"])]
        to_state = [carry_two * dot3(x, y) for x, y in zip(k["boths"], k["nows"])]
        grad_lefts = [dot3(x, y) + z for x, y, z in zip(grad_pairs, k["rights"], to_state)]
        grad_rights = [dot3(x, y, TN) for x, y in zip(grad_pairs, k["lefts"])]
        d_alpha, d_recept = join([x[:BLOCK] for x in grad_lefts], 1), join([x[BLOCK:] for x in grad_lefts], 1)
        d_beta, d_key = join([x[:BLOCK] for x in grad_rights], 1), join([x[BLOCK:] for x in grad_rights], 1)
        d_beta_end, d_key_end = join([x[:BLOCK] for x in grad_ends], 1), join([x[BLOCK:] for x in grad_ends], 1)
        ended = parts["beta_end"] * d_beta_end + parts["key_end"] * d_key_end
        alphas = parts["alpha"] * d_alpha
        d_total = parts["recept"] * d_recept - parts["beta"] * d_beta - parts["key"] * d_key - ended + alphas
        d_step = sum_left(upper, d_total) + (jnp.sum(ended, 0, keepdims=True) + k["end_sum"]) - alphas
        d_beta_plain = d_beta * parts["shrunk"] + d_beta_end * parts["tail"]
        copy_decay = low(d_step * parts["log_step"])
        copy_dir = low(d_beta_plain * k["rate_low"] - d_alpha * parts["before"])
        copy_rate = low(d_beta_plain * k["dir_low"])

        keys, values, rate, blend = k["keys"], k["values"], k["rate"], k["blend"]
        grad_recept = k["grad_recept"] + low(d_recept * parts["grown"])
        grad_key_mod = k["grad_key_mod"] + low(d_key * parts["shrunk"] + d_key_end * parts["tail"])
        grad_mixed_value = k["grad_mixed_value"] + low(join(grad_values, 1))
        grad_z = copy_decay * jax.nn.sigmoid(-k["z"])
        factor = 1.0 + (rate - 1.0) * vec[4:5]
        keyed = grad_key_mod * keys
        grad_rate = copy_rate + keyed * vec[4:5]
        grad_scaled = k["scale"] * (copy_dir - k["key_dir"] * head_sum(copy_dir * k["key_dir"], ones))
        grad_keys = grad_key_mod * factor + grad_scaled * vec[3:4]
        grad_rate_up = grad_rate * rate * (1.0 - rate)
        grad_value_up = grad_mixed_value * (k["first"] - values) * blend * (1.0 - blend)
        recept_out[rows] = grad_recept.astype(BF16)
        keys_out[rows] = grad_keys.astype(BF16)
        values_out[rows] = (grad_mixed_value * (1.0 - blend)).astype(BF16)
        first_out[rows] = (grad_mixed_value * blend).astype(BF16)
        ups_out[0, rows] = grad_z.astype(BF16)
        ups_out[1, rows] = grad_rate_up.astype(BF16)
        ups_out[2, rows] = grad_value_up.astype(BF16)
        ups_out[3, rows] = k["grad_gate"].astype(BF16)

        def total(x):
            return jnp.sum(x, 0, keepdims=True)

        vec_total = vec_total + jnp.concatenate(
            [
                total(grad_z), total(grad_rate_up), total(grad_value_up), total(grad_scaled * keys),
                total(keyed * (rate - 1.0)), total(k["grad_coefficient"] * k["product"]),
                total(k["opened"] * k["normed"]), total(k["opened"]),
            ],
            0,
        )
    vec_out[...] += vec_total


def kernel_cost(rows, width, passes):
    return pl.CostEstimate(flops=2 * rows * width * width, bytes_accessed=4 * rows * width * passes, transcendentals=0)


def per_step(rows, most):
    return most if (rows // BLOCK) % most == 0 else 1


def run_forward(recept, keys, values, hidden, first, up, vec, segments):
    rows, width = recept.shape
    count = per_step(rows, 4)
    step = count * BLOCK

    def spec(columns):
        return pl.BlockSpec((step, columns), lambda i: (i, 0))

    def whole(array):
        return pl.BlockSpec(array.shape, lambda i: (0, 0))

    return pl.pallas_call(
        functools.partial(forward_kernel, count),
        grid=(rows // step,),
        in_specs=[
            spec(width), spec(width), spec(width), spec(WIDE), spec(width), whole(up), whole(vec),
            pl.BlockSpec((count * 8, BLOCK), lambda i: (i, 0)),
        ],
        out_specs=[spec(width)] * 5,
        out_shape=[jax.ShapeDtypeStruct((rows, width), d) for d in (BF16, BF16, F32, F32, F32)],
        scratch_shapes=[pltpu.VMEM((BLOCK, width), F32)],
        compiler_params=pltpu.CompilerParams(vmem_limit_bytes=48 << 20),
        cost_estimate=kernel_cost(rows, width, 110),
        name="mix_forward",
    )(recept, keys, values, hidden, first, up, vec, segments)


def run_backward(grad, recept, keys, values, hidden, first, up, vec, segments, saved):
    rows, width = recept.shape
    count = per_step(rows, 2)
    step = count * BLOCK
    last = rows // step - 1

    def spec(columns):
        return pl.BlockSpec((step, columns), lambda i: (last - i, 0))

    def whole(array):
        return pl.BlockSpec(array.shape, lambda i: (0, 0))

    return pl.pallas_call(
        functools.partial(backward_kernel, count),
        grid=(rows // step,),
        in_specs=[
            spec(width), spec(width), spec(width), spec(width), spec(WIDE), spec(width), whole(up), whole(vec),
            pl.BlockSpec((count * 8, BLOCK), lambda i: (last - i, 0)),
            spec(width), spec(width), spec(width), spec(width),
        ],
        out_specs=[
            spec(width), spec(width), spec(width),
            pl.BlockSpec((4, step, width), lambda i: (0, last - i, 0)),
            spec(width), pl.BlockSpec((8, width), lambda i: (0, 0)),
        ],
        out_shape=[
            jax.ShapeDtypeStruct((rows, width), BF16), jax.ShapeDtypeStruct((rows, width), BF16),
            jax.ShapeDtypeStruct((rows, width), BF16), jax.ShapeDtypeStruct((4, rows, width), BF16),
            jax.ShapeDtypeStruct((rows, width), BF16), jax.ShapeDtypeStruct((8, width), F32),
        ],
        scratch_shapes=[pltpu.VMEM((BLOCK, width), F32)],
        compiler_params=pltpu.CompilerParams(vmem_limit_bytes=48 << 20),
        cost_estimate=kernel_cost(rows, width, 150),
        name="mix_backward",
    )(grad, recept, keys, values, hidden, first, up, vec, segments, *saved)


def mix_norm(block_ref, stats_ref, vec_ref):
    stats = stats_ref[...]
    flowing = stats[:, 2:3]
    standard = (block_ref[...].astype(F32) - stats[:, 0:1]) * stats[:, 1:2]
    normed = standard * vec_ref[0:1] + vec_ref[1:2]
    delta = pltpu.roll(normed, 1, 0) * flowing - normed
    return standard, normed, delta, flowing


def project_kernel(
    width, block_ref, stats_ref, vec_ref, weight_ref,
    recept_ref, keys_ref, values_ref, downs_ref, hidden_ref,
):
    base = 3 * width
    _, normed, delta, _ = mix_norm(block_ref, stats_ref, vec_ref)
    weight = weight_ref[...]
    uses = (
        ((recept_ref, 0, width, 0),),
        ((downs_ref, base + OFFSETS[0], PADDED[0], OFFSETS[0]),),
        ((keys_ref, width, width, 0),),
        ((values_ref, 2 * width, width, 0), (downs_ref, base + OFFSETS[2], PADDED[2], OFFSETS[2])),
        ((downs_ref, base + OFFSETS[1], PADDED[1], OFFSETS[1]),),
        ((downs_ref, base + OFFSETS[3], PADDED[3], OFFSETS[3]),),
    )

    @pl.when(pl.program_id(0) == 0)
    def _():
        for ref in (recept_ref, keys_ref, values_ref, downs_ref):
            ref[...] = jnp.zeros_like(ref)

    for c, targets in enumerate(uses):
        mixed = (normed + delta * vec_ref[2 + c : 3 + c]).astype(BF16)
        for ref, start, size, at in targets:
            ref[:, at : at + size] += dot(mixed, weight[:, start : start + size])

    @pl.when(pl.program_id(0) == pl.num_programs(0) - 1)
    def _():
        hidden_ref[:, 0:128] = jnp.tanh(downs_ref[:, 0:128]).astype(BF16)
        hidden_ref[:, 128:384] = downs_ref[:, 128:384].astype(BF16)
        hidden_ref[:, 384:640] = jax.nn.sigmoid(downs_ref[:, 384:640]).astype(BF16)


def unproject_kernel(
    width, parts, piece, block_ref, stats_ref, vec_ref, weight_ref,
    other_ref, recept_ref, keys_ref, values_ref, ups_ref, hidden_ref, downs_ref, up_ref,
    grad_ref, sums_ref, wide_ref, up_out, down_lows,
):
    rows = block_ref.shape[0]
    base = 3 * width

    @pl.when(pl.program_id(0) == 0)
    def _():
        sums_ref[...] = jnp.zeros_like(sums_ref)
        for k, (at, size) in enumerate(zip(OFFSETS, PADDED)):
            cols = slice(at, at + size)
            grad = dot(ups_ref[k], up_ref[cols], NT)
            if k == 0:
                grad = grad * (1.0 - jnp.square(jnp.tanh(downs_ref[:, cols])))
            if k == 3:
                opening = jax.nn.sigmoid(downs_ref[:, cols])
                grad = grad * opening * (1.0 - opening)
            down_lows[:, cols] = grad.astype(BF16)
            up_out[:, cols] = dot(ups_ref[k], hidden_ref[:, cols], TN).astype(BF16)

    standard, normed, delta, flowing = mix_norm(block_ref, stats_ref, vec_ref)
    weight = weight_ref[...]

    def down(k):
        return (down_lows[:, OFFSETS[k] : OFFSETS[k] + PADDED[k]], base + OFFSETS[k], PADDED[k])

    uses = (
        ((recept_ref[...], 0, width),),
        (down(0),),
        ((keys_ref[...], width, width),),
        ((values_ref[...], 2 * width, width), down(2)),
        (down(1),),
        (down(3),),
    )
    kept, sent, vec_rows = None, None, []
    per_seq = parts * piece
    for c, sources in enumerate(uses):
        share = vec_ref[2 + c : 3 + c]
        mixed = (normed + delta * share).astype(BF16)
        grad = None
        for source, start, size in sources:
            part = dot(source, weight[:, start : start + size], NT)
            grad = part if grad is None else grad + part
            product = dot(mixed, source, TN).astype(BF16)
            for number in range(product.shape[0] // per_seq):
                for w in range(parts):
                    at = number * per_seq + w * piece
                    wide_ref[w, number, :, start : start + size] = product[at : at + piece]
        vec_rows.append(jnp.sum(grad * delta, 0, keepdims=True))
        moved = grad * share
        kept = grad - moved if kept is None else kept + (grad - moved)
        sent = moved if sent is None else sent + moved
    grad = kept + pltpu.roll(sent * flowing, rows - 1, 0)
    vec_rows = jnp.concatenate(
        [jnp.sum(grad * standard, 0, keepdims=True), jnp.sum(grad, 0, keepdims=True)] + vec_rows, 0
    )
    spare = jnp.concatenate([vec_rows.T, other_ref[...]], 1).astype(BF16)
    for number in range(spare.shape[0] // per_seq):
        for w in range(parts):
            at = number * per_seq + w * piece
            wide_ref[w, number, :, base + RANKS[0] : base + PADDED[0]] = spare[at : at + piece]
    scaled = grad * vec_ref[0:1]
    sums_ref[:, 0:1] += jnp.sum(scaled, 1, keepdims=True)
    sums_ref[:, 1:2] += jnp.sum(scaled * standard, 1, keepdims=True)
    grad_ref[...] = scaled


def mix_specs(rows, width, own_width, parts):
    block = 256 if rows <= 1024 else 128

    def columns(height):
        return pl.BlockSpec((height, block), lambda j: (0, j))

    def whole(shape):
        return pl.BlockSpec(shape, lambda j: (0,) * len(shape))

    def weights(array):
        size = array.shape[1] if rows > 1024 else 3 * own_width + WIDE
        return pl.BlockSpec((block, size), lambda j: (j, 0))

    return block, columns, whole, weights


def run_project(balanced, stats, vec, weights, own_width, parts):
    rows, width = balanced.shape
    block, columns, whole, weight_spec = mix_specs(rows, width, own_width, parts)
    shapes = [(rows, own_width)] * 3 + [(rows, WIDE)] * 2
    return pl.pallas_call(
        functools.partial(project_kernel, own_width),
        grid_spec=pltpu.PrefetchScalarGridSpec(
            num_scalar_prefetch=0,
            grid=(width // block,),
            in_specs=[columns(rows), whole(stats.shape), columns(8), weight_spec(weights)],
            out_specs=[whole(s) for s in shapes],
        ),
        out_shape=[jax.ShapeDtypeStruct(s, d) for s, d in zip(shapes, (F32, F32, F32, F32, BF16))],
        compiler_params=pltpu.CompilerParams(vmem_limit_bytes=60 << 20),
        cost_estimate=kernel_cost(rows, own_width, 60),
        name="mix_project",
    )(balanced, stats, vec, weights)


def run_unproject(balanced, stats, vec, weights, others, lows, ups, hidden, downs, up, parts):
    rows, width = balanced.shape
    own_width = lows[0].shape[1]
    seqs = width // own_width
    piece = own_width // parts
    block, columns, whole, weight_spec = mix_specs(rows, width, own_width, parts)
    taken = block // own_width
    total = 3 * own_width + WIDE
    return pl.pallas_call(
        functools.partial(unproject_kernel, own_width, parts, piece),
        grid_spec=pltpu.PrefetchScalarGridSpec(
            num_scalar_prefetch=0,
            grid=(width // block,),
            in_specs=[
                columns(rows), whole(stats.shape), columns(8), weight_spec(weights),
                pl.BlockSpec((block, others.shape[1]), lambda j: (j, 0)),
            ]
            + [whole(a.shape) for a in (*lows, ups, hidden, downs, up)],
            out_specs=[
                columns(rows), whole((rows, 2)),
                pl.BlockSpec((parts, taken, piece, total), lambda j: (0, j, 0, 0)),
                whole((own_width, WIDE)),
            ],
            scratch_shapes=[pltpu.VMEM((rows, WIDE), BF16)],
        ),
        out_shape=[
            jax.ShapeDtypeStruct((rows, width), F32), jax.ShapeDtypeStruct((rows, 2), F32),
            jax.ShapeDtypeStruct((parts, seqs, piece, total), BF16),
            jax.ShapeDtypeStruct((own_width, WIDE), BF16),
        ],
        compiler_params=pltpu.CompilerParams(vmem_limit_bytes=60 << 20),
        cost_estimate=kernel_cost(rows, own_width, 120),
        name="mix_unproject",
    )(balanced, stats, vec, weights, others, *lows, ups, hidden, downs, up)


def norm_stats(values):
    centered = values - jnp.mean(values, -1, keepdims=True)
    scale = lax.rsqrt(jnp.mean(centered * centered, -1, keepdims=True) + 1e-05)
    return centered * scale, scale


def norm_back(grad, standard, scale, gain):
    scaled = grad * gain
    return scale * (
        scaled
        - jnp.mean(scaled, -1, keepdims=True)
        - standard * jnp.mean(scaled * standard, -1, keepdims=True)
    )


def pad_ranks(matrix):
    pieces, start = [], 0
    for rank, padded in zip(RANKS, PADDED):
        pieces.append(jnp.pad(matrix[:, start : start + rank], ((0, 0), (0, padded - rank))))
        start += rank
    return jnp.concatenate(pieces, 1)


def unpad_ranks(matrix):
    return jnp.concatenate([matrix[..., o : o + r] for o, r in zip(OFFSETS, RANKS)], -1)


MESH_ID = pl.DeviceIdType.MESH


def places():
    s, w = lax.axis_index("seq"), lax.axis_index("wsh")
    side = s % 2
    return s, w, side, s // 2, (s + 1 - 2 * side, w), (s, w + 1 - 2 * (w % 2)), (s, w + 2 - 4 * (w // 2))


def greet(neighbours, number):
    barrier = pltpu.get_barrier_semaphore()
    for there, device in neighbours:
        if there is None:
            pl.semaphore_signal(barrier, inc=1, device_id=device, device_id_type=MESH_ID)
        else:

            @pl.when(there)
            def _(device=device):
                pl.semaphore_signal(barrier, inc=1, device_id=device, device_id_type=MESH_ID)

    pl.semaphore_wait(barrier, number)


def send(source, target, send_sem, recv_sem, device):
    return pltpu.make_async_remote_copy(
        src_ref=source, dst_ref=target, send_sem=send_sem, recv_sem=recv_sem, device_id=device, device_id_type=MESH_ID
    )


def line_ends(z):
    return jnp.where(z > 0, 1, 0) + jnp.where(z < 3, 1, 0)


def gather_kernel(
    own_ref, tail_ref, weight_ref, out_ref, tails_ref, weights_ref,
    copy_sem, right_send, right_recv, left_send, left_recv, x_send, x_recv, c_send, c_recv, y_send, y_recv,
):
    s, w, side, z, x_device, core_device, y_device = places()
    up, down = (s + 2, w), (s - 2, w)
    across = w + 2 - 4 * (w // 2)
    kinds = ((own_ref, out_ref), (tail_ref, tails_ref))
    copies = [pltpu.make_async_copy(own, out.at[s], copy_sem.at[k]) for k, (own, out) in enumerate(kinds)]
    copies.append(pltpu.make_async_copy(weight_ref, weights_ref.at[w], copy_sem.at[2]))
    for copy in copies:
        copy.start()
    greet(((None, x_device), (None, core_device), (None, y_device), (z < 3, up), (z > 0, down)), 3 + line_ends(z))

    weight_y = send(weight_ref, weights_ref.at[w], y_send, y_recv, y_device)
    weight_core = send(weight_ref, weights_ref.at[w], c_send.at[0], c_recv.at[0], core_device)
    weight_on = send(weights_ref.at[across], weights_ref.at[across], c_send.at[1], c_recv.at[1], core_device)
    weight_y.start()
    weight_core.start()

    def to_right(j, k, source, number):
        return send(source, kinds[k][1].at[number], right_send.at[j, k], right_recv.at[j, k], up)

    def to_left(j, k, source, number):
        return send(source, kinds[k][1].at[number], left_send.at[j, k], left_recv.at[j, k], down)

    def to_x(at, k, source, number):
        return send(source, kinds[k][1].at[number], x_send.at[at, k], x_recv.at[at, k], x_device)

    for k, (own, _) in enumerate(kinds):

        @pl.when(z < 3)
        def _(k=k, own=own):
            to_right(0, k, own, s).start()

        @pl.when(z > 0)
        def _(k=k, own=own):
            to_left(0, k, own, s).start()

        to_x(z, k, own, s).start()
    for j in (1, 2, 3):
        lower, upper = s - 2 * j, s + 2 * j
        for k, (_, out) in enumerate(kinds):

            @pl.when(z >= j)
            def _(j=j, k=k, out=out, lower=lower):
                block = out.at[lower]
                to_right(j - 1, k, block, lower).wait_recv()

                @pl.when(z < 3)
                def _():
                    to_right(j, k, block, lower).start()

                to_x(z - j, k, block, lower).start()

            @pl.when(z + j <= 3)
            def _(j=j, k=k, out=out, upper=upper):
                block = out.at[upper]
                to_left(j - 1, k, block, upper).wait_recv()

                @pl.when(z > 0)
                def _():
                    to_left(j, k, block, upper).start()

                to_x(z + j, k, block, upper).start()

    weight_y.wait_recv()
    weight_on.start()
    for k, (own, _) in enumerate(kinds):
        for number in range(4):
            done = to_x(number, k, own, s)
            done.wait_send()
            done.wait_recv()
        for j in range(3):

            @pl.when((z >= j) & (z < 3))
            def _(j=j, k=k, own=own):
                to_right(j, k, own, s).wait_send()

            @pl.when((z + j <= 3) & (z > 0))
            def _(j=j, k=k, own=own):
                to_left(j, k, own, s).wait_send()

    weight_core.wait_recv()
    weight_on.wait_recv()
    for copy in (weight_y, weight_core, weight_on):
        copy.wait_send()
    for copy in copies:
        copy.wait()


def gather_first(own, tail, weight):
    seqs, parts = lax.axis_size("seq"), lax.axis_size("wsh")
    if seqs != 8 or parts != 4:
        return (
            lax.all_gather(own, "seq", axis=0, tiled=False),
            lax.all_gather(tail, "seq", axis=0, tiled=False),
            lax.all_gather(weight, "wsh", axis=0, tiled=False),
        )
    dma = pltpu.SemaphoreType.DMA
    given = ((seqs, own), (seqs, tail), (parts, weight))
    return pl.pallas_call(
        gather_kernel,
        in_specs=[pl.BlockSpec(memory_space=pltpu.VMEM)] * 3,
        out_specs=[pl.BlockSpec(memory_space=pl.ANY)] * 3,
        out_shape=[jax.ShapeDtypeStruct((n,) + x.shape, x.dtype) for n, x in given],
        scratch_shapes=[dma((3,))] + [dma((3, 2))] * 4 + [dma((4, 2))] * 2 + [dma((2,))] * 2 + [dma] * 2,
        compiler_params=pltpu.CompilerParams(collective_id=1, has_side_effects=True),
        cost_estimate=pl.CostEstimate(flops=0, bytes_accessed=100 << 20, transcendentals=0),
        name="gather_first",
    )(own, tail, weight)


def reduce_kernel(
    splits, x_ref, out_ref, x_buf, right_buf, left_buf, right_out, left_out,
    x_send, x_recv, right_send, right_recv, left_send, left_recv,
):
    s, w, side, z, x_device, _, _ = places()
    up, down = (s + 2, w), (s - 2, w)
    size = x_ref.shape[2] // splits
    columns = [slice(c * size, (c + 1) * size) for c in range(splits)]
    greet(((None, x_device), (z < 3, up), (z > 0, down)), 1 + line_ends(z))

    def to_x(target, c):
        return send(
            x_ref.at[target * 2 + 1 - side, :, columns[c]], x_buf.at[target, :, columns[c]],
            x_send.at[target, c], x_recv.at[target, c], x_device,
        )

    def start_x(target):
        for c in range(splits):
            to_x(target, c).start()

    def to_right(k, c):
        return send(
            right_out.at[k - 1, :, columns[c]], right_buf.at[k - 1, :, columns[c]],
            right_send.at[k - 1, c], right_recv.at[k - 1, c], up,
        )

    def to_left(k, c):
        return send(
            left_out.at[k - 1, :, columns[c]], left_buf.at[k - 1, :, columns[c]],
            left_send.at[k - 1, c], left_recv.at[k - 1, c], down,
        )

    def pair(target, c):
        to_x(target, c).wait_recv()
        return x_ref[target * 2 + side, :, columns[c]].astype(F32) + x_buf[target, :, columns[c]].astype(F32)

    for k in (3, 2, 1):

        @pl.when(z + k <= 3)
        def _(k=k):
            start_x(z + k)

        @pl.when(z >= k)
        def _(k=k):
            start_x(z - k)

    start_x(z)
    for k in (3, 2, 1):
        for c in range(splits):

            @pl.when(z + k <= 3)
            def _(k=k, c=c):
                right_out[k - 1, :, columns[c]] = pair(z + k, c).astype(BF16)
                if k < 3:

                    @pl.when(z > 0)
                    def _():
                        to_right(k + 1, c).wait_recv()
                        right_out[k - 1, :, columns[c]] = (
                            right_out[k - 1, :, columns[c]].astype(F32) + right_buf[k, :, columns[c]].astype(F32)
                        ).astype(BF16)

                to_right(k, c).start()

            @pl.when(z >= k)
            def _(k=k, c=c):
                left_out[k - 1, :, columns[c]] = pair(z - k, c).astype(BF16)
                if k < 3:

                    @pl.when(z < 3)
                    def _():
                        to_left(k + 1, c).wait_recv()
                        left_out[k - 1, :, columns[c]] = (
                            left_out[k - 1, :, columns[c]].astype(F32) + left_buf[k, :, columns[c]].astype(F32)
                        ).astype(BF16)

                to_left(k, c).start()

    for c in range(splits):
        out_ref[:, columns[c]] = pair(z, c)

        @pl.when(z > 0)
        def _(c=c):
            to_right(1, c).wait_recv()
            out_ref[:, columns[c]] += right_buf[0, :, columns[c]].astype(F32)

        @pl.when(z < 3)
        def _(c=c):
            to_left(1, c).wait_recv()
            out_ref[:, columns[c]] += left_buf[0, :, columns[c]].astype(F32)

    for c in range(splits):
        for target in range(4):
            to_x(target, c).wait_send()
        for k in (3, 2, 1):

            @pl.when(z + k <= 3)
            def _(k=k, c=c):
                to_right(k, c).wait_send()

            @pl.when(z >= k)
            def _(k=k, c=c):
                to_left(k, c).wait_send()


def reduce_seq(x):
    seqs, rows, width = x.shape
    if seqs != 8 or lax.axis_size("wsh") != 4:
        return jnp.sum(exchange(x, "seq").astype(F32), 0)
    splits = 2
    return pl.pallas_call(
        functools.partial(reduce_kernel, splits),
        in_specs=[pl.BlockSpec(memory_space=pltpu.VMEM)],
        out_specs=pl.BlockSpec(memory_space=pltpu.VMEM),
        out_shape=jax.ShapeDtypeStruct((rows, width), F32),
        scratch_shapes=[pltpu.VMEM((4, rows, width), BF16)]
        + [pltpu.VMEM((3, rows, width), BF16)] * 4
        + [pltpu.SemaphoreType.DMA((4, splits))] * 2
        + [pltpu.SemaphoreType.DMA((3, splits))] * 4,
        compiler_params=pltpu.CompilerParams(collective_id=2, has_side_effects=True, vmem_limit_bytes=40 << 20),
        cost_estimate=pl.CostEstimate(flops=0, bytes_accessed=1 << 20, transcendentals=0),
        name="reduce_seq",
    )(x)


def channel_kernel(
    forward, x_ref, first_hbm, second_hbm, active_hbm,
    sum_ref, all_hbm, mine_hbm, other_hbm, extra_hbm,
    first, second, rows_all, middle, active, part, core_buf, far_out, far_buf,
    load_sem, store_sem, core_send, core_recv, y_send, y_recv, x_send, x_recv, r_send, r_recv, f_send, f_recv,
):
    s, w, side, z, x_device, core_device, y_device = places()
    rows, width = x_ref.shape
    units = first.shape[0]
    half = units // 2
    loads = [
        pltpu.make_async_copy(first_hbm, first, load_sem.at[0]),
        pltpu.make_async_copy(second_hbm, second, load_sem.at[1]),
    ]
    if not forward:
        loads.append(pltpu.make_async_copy(active_hbm, active, load_sem.at[2]))
    for load in loads:
        load.start()
    rows_all[0:rows] = x_ref[...]
    greet(((None, x_device), (None, core_device), (None, y_device)), 3)

    def block(number):
        return rows_all.at[pl.ds(number * rows, rows)]

    to_core = [
        send(block(0), block(1), core_send.at[0], core_recv.at[0], core_device),
        send(block(2), block(3), core_send.at[1], core_recv.at[1], core_device),
    ]
    to_y = send(block(0), block(2), y_send, y_recv, y_device)
    if forward:
        to_x = [
            send(
                middle.at[1 - side, pl.ds(2 * n * rows, 2 * rows)], other_hbm.at[pl.ds(2 * n * rows, 2 * rows)],
                x_send.at[n], x_recv.at[n], x_device,
            )
            for n in range(2)
        ]
    else:
        to_x = [
            send(block(n), other_hbm.at[pl.ds(n * rows, rows)], x_send.at[n], x_recv.at[n], x_device) for n in range(4)
        ]
    sums_core = [
        send(part.at[pl.ds((2 * n + 1) * rows, rows)], core_buf.at[n], r_send.at[n], r_recv.at[n], core_device)
        for n in range(2)
    ]
    far = send(far_out, far_buf, f_send, f_recv, y_device)
    stores = [
        pltpu.make_async_copy(rows_all, all_hbm, store_sem.at[0]),
        pltpu.make_async_copy(middle.at[side], mine_hbm, store_sem.at[1]),
        pltpu.make_async_copy(active if forward else middle.at[1 - side], extra_hbm, store_sem.at[2]),
    ]

    def pass_on(number):
        if not forward:
            to_x[number].start()

    to_y.start()
    to_core[0].start()
    pass_on(0)
    tile = min(512, half)

    def multiply(number):
        two = pl.ds(2 * number * rows, 2 * rows)

        def up(t, carry):
            for side_units in range(2):
                at = pl.multiple_of(t * tile, tile)
                unit = pl.multiple_of(side_units * half + at, tile)
                raw = dot(rows_all[two, :], first[pl.ds(unit, tile), :], NT)
                if forward:
                    raw = jnp.maximum(raw, 0.0)
                    active[two, pl.ds(unit, tile)] = raw
                    mid = raw * raw
                else:
                    mid = raw * 2.0 * active[two, pl.ds(unit, tile)]
                middle[side_units, two, pl.ds(at, tile)] = mid.astype(BF16)
            return carry

        lax.fori_loop(0, half // tile, up, 0)
        if forward:
            to_x[number].start()
        if number == 0:
            loads[1].wait()

        def down(t, carry):
            at = pl.multiple_of(t * tile, tile)
            part[two, pl.ds(at, tile)] = dot(middle[0, two, :], second[0:half, pl.ds(at, tile)]) + dot(
                middle[1, two, :], second[half:units, pl.ds(at, tile)]
            )
            return carry

        lax.fori_loop(0, width // tile, down, 0)
        sums_core[number].start()

    loads[0].wait()
    if not forward:
        loads[2].wait()
    to_core[0].wait_recv()
    pass_on(1)
    multiply(0)
    to_y.wait_recv()
    to_core[1].start()
    pass_on(2)
    to_core[1].wait_recv()
    pass_on(3)
    stores[0].start()
    multiply(1)
    for store in stores[1:]:
        store.start()
    sums_core[1].wait_recv()
    far_out[...] = (part[2 * rows : 3 * rows] + core_buf[1]).astype(BF16)
    far.start()
    sums_core[0].wait_recv()
    sum_ref[...] = part[0:rows] + core_buf[0]
    far.wait_recv()
    sum_ref[...] += far_buf[...].astype(F32)
    for copy in to_x:
        copy.wait_recv()
    for copy in to_x + to_core + sums_core + [to_y, far]:
        copy.wait_send()
    for store in stores:
        store.wait()


def channel_stage(x, first, second, active):
    rows, width = x.shape
    units = first.shape[0]
    forward = active is None
    given = (x, first, second) if forward else (x, first, second, active)
    everything = pl.BlockSpec(memory_space=pl.ANY)
    shapes = [
        ((rows, width), F32), ((4 * rows, width), BF16), ((4 * rows, units // 2), BF16),
        ((4 * rows, units // 2 if forward else width), BF16),
        ((4 * rows, units), F32) if forward else ((4 * rows, units // 2), BF16),
    ]

    def body(*refs):
        refs = list(refs)
        if forward:
            refs.insert(3, None)
        channel_kernel(forward, *refs)

    dma = pltpu.SemaphoreType.DMA
    return pl.pallas_call(
        body,
        in_specs=[pl.BlockSpec(memory_space=pltpu.VMEM)] + [everything] * (len(given) - 1),
        out_specs=[pl.BlockSpec(memory_space=pltpu.VMEM)] + [everything] * (len(shapes) - 1),
        out_shape=[jax.ShapeDtypeStruct(s, d) for s, d in shapes],
        scratch_shapes=[
            pltpu.VMEM((units, width), BF16), pltpu.VMEM((units, width), BF16), pltpu.VMEM((4 * rows, width), BF16),
            pltpu.VMEM((2, 4 * rows, units // 2), BF16), pltpu.VMEM((4 * rows, units), F32),
            pltpu.VMEM((4 * rows, width), F32), pltpu.VMEM((2, rows, width), F32),
            pltpu.VMEM((rows, width), BF16), pltpu.VMEM((rows, width), BF16),
            dma((3,)), dma((3,)), dma((2,)), dma((2,)), dma, dma, dma((4,)), dma((4,)), dma((2,)), dma((2,)),
            dma, dma,
        ],
        compiler_params=pltpu.CompilerParams(
            collective_id=3 if forward else 4, has_side_effects=True, vmem_limit_bytes=60 << 20
        ),
        cost_estimate=pl.CostEstimate(flops=0, bytes_accessed=100 << 20, transcendentals=0),
        name="channel_forward" if forward else "channel_backward",
    )(*given)


def from_behind(x, axis, by):
    size = lax.axis_size(axis)
    pairs = [(i, i + by) for i in range(size) if 0 <= i + by < size]
    return lax.ppermute(x, axis, pairs)


def exchange(x, axis):
    return lax.all_to_all(x, axis, split_axis=0, concat_axis=0, tiled=True)


def swap(x, by):
    size = lax.axis_size("wsh")
    return lax.ppermute(x, "wsh", [(i, i ^ by) for i in range(size)])


def gather_near(x):
    if lax.axis_size("wsh") != 4:
        return lax.all_gather(x, "wsh", axis=0, tiled=True)
    return gathered_near(x, swap(x, 1), swap(x, 2))


def gathered_near(x, beside, across):
    return jnp.concatenate([x, beside, across, swap(across, 1)], 0)


def beside(x):
    return lax.ppermute(x, "seq", [(i, i ^ 1) for i in range(lax.axis_size("seq"))])


def scalar_sum(x):
    if lax.axis_size("wsh") != 4:
        return jnp.sum(lax.all_gather(x.reshape(1), "wsh", axis=0, tiled=True))
    x = jnp.full((8, 128), x)
    x = x + swap(x, 1)
    return (x + swap(x, 2))[0, 0]


def near_sum(x):
    if lax.axis_size("wsh") != 4:
        return lax.psum_scatter(x, "wsh", scatter_dimension=0, tiled=True)
    rows = x.shape[0] // 4
    beside = swap(jnp.concatenate([x[rows : 2 * rows], x[3 * rows :]], 0), 1)
    far = x[2 * rows : 3 * rows] + beside[rows:]
    return x[:rows] + beside[:rows] + swap(far.astype(BF16), 2).astype(F32)


def block_sum(x):
    if lax.axis_size("wsh") != 4:
        return lax.psum_scatter(x, "wsh", scatter_dimension=0, tiled=False).astype(F32)
    kept, far = block_halves(x)
    return kept + swap(far, 2).astype(F32)


def block_halves(x):
    number = lax.axis_index("wsh")

    def block(by):
        return lax.dynamic_index_in_dim(x, number ^ by, 0, keepdims=False)

    beside = swap(jnp.stack([block(1), block(3)]), 1).astype(F32)
    return block(0).astype(F32) + beside[0], (block(2).astype(F32) + beside[1]).astype(BF16)


def local(
    tokens, first_layer_values, teacher, valid, destination, lengths,
    receptance_matrix, key_matrix, value_matrix, output_matrix,
    lowrank_down_weight, lowrank_up_weight, channel_key_weight, channel_value_weight, vectors,
):
    rows, width = tokens.shape
    seqs, parts = lax.axis_size("seq"), lax.axis_size("wsh")
    me = lax.axis_index("seq")
    group = rows * seqs
    own_width = width // seqs
    shard = width // parts
    piece = shard // seqs
    column = me * own_width

    def own_columns(matrix):
        return lax.dynamic_slice_in_dim(matrix, column, own_width, 1)

    near = parts == 4
    up_piece = lax.dynamic_slice_in_dim(lowrank_up_weight, column % shard, own_width, 0)
    total = 3 * own_width + WIDE
    own_weights = jnp.concatenate(
        [
            own_columns(receptance_matrix), own_columns(key_matrix), own_columns(value_matrix),
            pad_ranks(lowrank_down_weight), up_piece.reshape(shard, -1),
        ],
        1,
    )

    dest_seq = destination // rows // parts
    position = dest_seq * rows + destination % rows
    digits = jnp.stack([position // DIGIT, position % DIGIT, valid], 1).astype(BF16)
    tail = jnp.pad(digits, ((0, 0), (0, EXTRA - 3)))
    given, tails, weights = gather_first(tokens, tail, own_weights)
    given, tails, weights = given.reshape(group, width), tails.reshape(group, EXTRA), weights.reshape(width, -1)
    info = tails[:, :3].astype(F32)
    places = (info[:, 0] * DIGIT + info[:, 1]).astype(jnp.int32)
    numbers = jnp.arange(group, dtype=jnp.int32)
    permute = (numbers[:, None] == places[None, :]).astype(BF16)
    total_valid = scalar_sum(jnp.sum(info[:, 2]))

    index = jnp.arange(rows, dtype=jnp.int32)
    same_dest = (dest_seq[:, None] == dest_seq[None, :]) & (index[None, :] < index[:, None])
    slot = dest_seq * (rows // seqs) + jnp.sum(same_dest.astype(jnp.int32), 1)
    arrange = (index[:, None] == slot[None, :]).astype(BF16)
    mine = (places // rows) == me
    arrival = jnp.cumsum(mine.astype(jnp.int32)) - 1
    own_rows = ((index[:, None] + me * rows) == places[None, :]).astype(BF16)
    settle = dot(own_rows, (mine[:, None] & (arrival[:, None] == index[None, :])).astype(BF16)).astype(BF16)

    offsets = jnp.cumsum(lengths[0]) - lengths[0]
    starts = jnp.any(numbers[:, None] == offsets[None, :], 1).astype(F32)
    segment_ids = jnp.cumsum(starts).reshape(-1, BLOCK)
    before = segment_ids[:, :1] - starts.reshape(-1, BLOCK)[:, :1]
    segments = jnp.stack(
        [segment_ids, jnp.broadcast_to(before, segment_ids.shape), jnp.broadcast_to(segment_ids[:, -1:], segment_ids.shape)]
        + [jnp.zeros_like(segment_ids)] * 5,
        1,
    ).reshape(-1, BLOCK)
    flowing = (1.0 - starts)[:, None]

    up = pad_ranks(
        lax.dynamic_slice(
            weights, (column // shard * shard, total), (shard, weights.shape[1] - total)
        ).reshape(own_width, -1)
    ).T
    vec = lax.dynamic_slice_in_dim(vectors, column, own_width, 0)[:, 8:16].T

    output_late, given = lax.optimization_barrier((output_matrix, given))
    w_out = lax.all_gather(output_late, "wsh", axis=0, tiled=True)
    balanced = dot(permute, given).astype(BF16)
    wide_rows = balanced.astype(F32)
    mean = jnp.mean(wide_rows, -1, keepdims=True)
    scale_one = lax.rsqrt(jnp.mean(jnp.square(wide_rows - mean), -1, keepdims=True) + 1e-05)
    stats = jnp.concatenate([mean, scale_one, flowing, flowing], 1)
    mix_vec = vectors[:, :8].T
    first_values, stats = lax.optimization_barrier((first_layer_values, stats))
    first_given = exchange(
        first_values.reshape(rows, seqs, own_width).transpose(1, 0, 2), "seq"
    ).reshape(group, own_width)
    recept, keys, values, downs, hidden = run_project(balanced, stats, mix_vec, weights, own_width, parts)
    teacher_late, recept, first_given = lax.optimization_barrier((teacher, recept, first_given))
    first = dot(permute, first_given).astype(BF16)
    teacher_rows = exchange(dot(arrange, teacher_late).astype(BF16).reshape(seqs, rows // seqs, width), "seq")
    inputs = (recept, keys, values, hidden, first, up, vec, segments)
    mixed_out, *saved = run_forward(*inputs)
    teacher_rows, mixed_out = lax.optimization_barrier((teacher_rows, mixed_out))
    target = dot(settle, teacher_rows.reshape(rows, width))

    mixed_rows = exchange(mixed_out.reshape(seqs, rows, own_width), "seq").transpose(1, 0, 2).reshape(rows, width)
    own = lax.dynamic_slice_in_dim(balanced, me * rows, rows, 0).astype(F32)
    own_starts = lax.dynamic_slice_in_dim(starts, me * rows, rows, 0)
    own_flowing = (1.0 - own_starts)[:, None]
    own_valid = dot(own_rows, tails)[:, 2]
    residual = own + dot(mixed_rows, w_out)
    standard_two, scale_two = norm_stats(residual)
    normed_two = standard_two * vectors[:, 16] + vectors[:, 17]
    carried_two = from_behind(normed_two[-1:], "seq", 1)
    delta_two = jnp.concatenate([carried_two, normed_two[:-1]], 0) * own_flowing - normed_two
    channel_in = (normed_two + delta_two * vectors[:, 18]).astype(BF16)
    paired = near and seqs == 8
    if paired:
        summed, channel, hidden_mine, hidden_other, active = channel_stage(
            channel_in, channel_key_weight, channel_value_weight, None
        )
    else:
        channel = gather_near(channel_in)
        active = jax.nn.relu(dot(channel, channel_key_weight, NT))
        hidden_rows = jnp.square(active).astype(BF16)
        summed = near_sum(dot(hidden_rows, channel_value_weight))
    result = residual + summed
    total_tokens = group * parts
    cotangent = (result - target) * (own_valid * (total_tokens / total_valid))[:, None]
    cot_low = cotangent.astype(BF16)

    if paired:
        grad_channel, cot, pre_mine, cot_other, pre_spare = channel_stage(
            cot_low, channel_value_weight, channel_key_weight, active
        )
        channel_other, pre_other = beside(channel), beside(pre_spare)
    else:
        cot = gather_near(cot_low)
        grad_pre = (dot(cot, channel_value_weight, NT) * 2.0 * active).astype(BF16)
        grad_channel = near_sum(dot(grad_pre, channel_key_weight))
    grad_vec_mix_two = jnp.sum(grad_channel * delta_two, 0)
    shifted = grad_channel * vectors[:, 18] * own_flowing
    behind = from_behind(shifted[:1], "seq", -1)
    grad_normed_two = grad_channel * (1.0 - vectors[:, 18]) + jnp.concatenate([shifted[1:], behind], 0)
    grad_residual = cotangent + norm_back(grad_normed_two, standard_two, scale_two, vectors[:, 16])
    grad_low = grad_residual.astype(BF16)

    grad_posted = dot(grad_low, w_out, NT).astype(BF16)
    if paired:
        hidden_mine, grad_posted = lax.optimization_barrier((hidden_mine, grad_posted))
        value_part = (dot(hidden_mine, cot, TN) + dot(hidden_other, cot_other, TN)).astype(BF16)
    else:
        value_part = dot(hidden_rows, cot, TN).astype(BF16)
    grad_heads = exchange(grad_posted.reshape(rows, seqs, own_width).transpose(1, 0, 2), "seq").reshape(group, own_width)
    grad_heads, value_part, mixed_late = lax.optimization_barrier((grad_heads, value_part, mixed_rows))
    lefts = exchange(mixed_late.reshape(rows, seqs, parts, piece).transpose(2, 0, 1, 3), "wsh")
    near_grad = (swap(grad_low, 1), swap(grad_low, 2)) if near else gather_near(grad_low)
    recept_low, keys_low, values_low, ups_low, grad_first, grad_vec_heads = run_backward(grad_heads, *inputs, saved)
    if paired:
        channel_other, pre_other, lefts, near_grad, recept_low = lax.optimization_barrier(
            (channel_other, pre_other, lefts, near_grad, recept_low)
        )
        key_part = (dot(pre_mine, channel, TN) + dot(pre_other, channel_other, TN)).astype(BF16)
    else:
        lefts, near_grad, recept_low = lax.optimization_barrier((lefts, near_grad, recept_low))
        key_part = dot(grad_pre, channel, TN).astype(BF16)
    if near:
        near_grad = gathered_near(grad_low, *near_grad)
        lefts = jnp.stack([lax.dynamic_index_in_dim(lefts, lax.axis_index("wsh") ^ k, 0, keepdims=False) for k in range(4)])
    out_part = dot(lefts.reshape(rows * parts, -1), near_grad, TN).astype(BF16)

    result_back = dot(settle, result.astype(BF16), TN).astype(BF16).reshape(seqs, rows // seqs, width)
    first_back = dot(permute, grad_first, TN).astype(BF16).reshape(seqs, rows // seqs, width)
    moved = exchange(jnp.concatenate([result_back, first_back], 1), "seq")
    recept_low, key_part, out_part = lax.optimization_barrier((recept_low, key_part, out_part))
    if paired:
        lines = [[0, 2, 4, 6], [1, 3, 5, 7]]
        turned = [
            ((z * 2 + x) * 4 + w, (w * 2 + x) * 4 + z) for z in range(4) for x in range(2) for w in range(4)
        ]

        def along(part):
            return lax.psum_scatter(part, "seq", scatter_dimension=0, tiled=True, axis_index_groups=lines)

        def turn(part):
            return lax.ppermute(part, ("seq", "wsh"), turned)

        halves_out = out_part.reshape(seqs // 2, 2, piece, width)
        x_side = me % 2
        out_mine = lax.dynamic_index_in_dim(halves_out, x_side, 1, keepdims=False).astype(F32)
        out_other = beside(lax.dynamic_index_in_dim(halves_out, 1 - x_side, 1, keepdims=False))
        value_turned, key_sum = turn(along(value_part)), along(key_part)
    else:
        moves = [(s * parts + w, w * seqs + s) for s in range(seqs) for w in range(parts)]

        def ffn_grad(part):
            part = lax.psum_scatter(part, "seq", scatter_dimension=0, tiled=True)
            return lax.ppermute(part, ("seq", "wsh"), moves).astype(F32)

        grad_ffn_value, grad_ffn_key = ffn_grad(value_part), ffn_grad(key_part)
        grad_out = lax.psum_scatter(out_part, "seq", scatter_dimension=0, tiled=True)

    heads_part = lax.dynamic_update_slice_in_dim(jnp.zeros((width, 8), F32), grad_vec_heads.T, column, 0)
    vec_two = jnp.stack(
        [jnp.sum(grad_normed_two * standard_two, 0), jnp.sum(grad_normed_two, 0), grad_vec_mix_two], 1
    )
    others = jnp.concatenate([heads_part, jnp.pad(vec_two, ((0, 0), (0, 13)))], 1)
    scaled_grad, sums, wide, up_grad = run_unproject(
        balanced, stats, mix_vec, weights, others, (recept_low, keys_low, values_low), ups_low, hidden, downs, up, parts
    )
    if paired:
        moved, value_turned, out_other, scaled_grad, sums, wide, up_grad = lax.optimization_barrier(
            (moved, value_turned, out_other, scaled_grad, sums, wide, up_grad)
        )
        out_half = (out_mine + out_other.astype(F32)).astype(BF16).reshape(-1, width)
        out_half, sums = lax.optimization_barrier((out_half, sums))
        grad_out = along(out_half)
        grad_ffn_value, grad_ffn_key = value_turned.astype(F32), turn(key_sum).astype(F32)
    else:
        moved, scaled_grad, sums, wide = lax.optimization_barrier((moved, scaled_grad, sums, wide))
    output = dot(arrange, moved[:, : rows // seqs].reshape(rows, width), TN).astype(BF16)
    grad_first_rows = moved[:, rows // seqs :].reshape(seqs, rows, own_width).transpose(1, 0, 2).reshape(rows, width)

    standard = (balanced.astype(F32) - mean) * scale_one
    grad_balanced = scale_one * (scaled_grad - sums[:, :1] * (1.0 / width) - standard * (sums[:, 1:] * (1.0 / width)))
    mine_rows = lax.dynamic_slice_in_dim(grad_balanced, me * rows, rows, 0) + grad_residual
    grad_balanced = lax.dynamic_update_slice_in_dim(grad_balanced, mine_rows, me * rows, 0)
    grad_given = dot(permute, grad_balanced.astype(BF16), TN).astype(BF16).reshape(seqs, rows, width)
    if near:
        kept_part, far = block_halves(wide)
        grad_given, far = lax.optimization_barrier((grad_given, far))
        wide_part = kept_part + swap(far, 2).astype(F32)
    else:
        wide_part = block_sum(wide)
    grad_tokens = reduce_seq(grad_given).astype(BF16)
    wide_part, grad_tokens, grad_out = lax.optimization_barrier((wide_part, grad_tokens, grad_out))
    wide_all = exchange(wide_part.astype(BF16), "seq").astype(F32)

    def square(at):
        taken = wide_all[:, :, at * own_width : (at + 1) * own_width]
        return taken.transpose(1, 0, 2).reshape(piece, width)

    narrow = jnp.sum(wide_all[:, :, 3 * own_width :], 0)
    grad_down = unpad_ranks(narrow)
    grad_vectors = narrow[:, RANKS[0] : RANKS[0] + vectors.shape[1]]
    up_part = unpad_ranks(block_sum(up_grad.reshape(parts, piece, WIDE)))

    return (
        output, grad_tokens, grad_first_rows,
        square(0), square(1), square(2),
        grad_out.astype(F32), grad_down, up_part,
        grad_ffn_key, grad_ffn_value, grad_vectors,
    )


def solution(mesh):
    both, shard = P(("seq", "wsh"), None), P("wsh", None)
    flat = P(("seq", "wsh"))
    return jax.shard_map(
        local,
        mesh=mesh,
        in_specs=(both, both, both, flat, flat) + (shard,) * 9 + (P(),),
        out_specs=(both,) * 12,
        check_vma=False,
    )
```
